32 devices in a mesh: dp: 4 (over y, core), mp: 8 (over z, x).
Axes of the slice: x: 2, y: 2, z: 4, core: 2. Of those that a mesh axis runs over, the one named last changes fastest.
Arguments:
- query_rows: bfloat16 [8192, 16, 128], P('dp', 'mp'), may hold values from -8 to 8
- key_rows: bfloat16 [8192, 16, 128], P('dp', 'mp'), may hold values from -8 to 8
- value_rows: bfloat16 [8192, 16, 128], P('dp', 'mp'), may hold values from -6 to 6
- residual: bfloat16 [4096, 8, 768], P('dp', 'mp'), may hold values from -40 to 40
- lengths: int32 [64], replicated, may hold values from 1 to 256, as said below
- assignment: int32 [64], replicated, may hold values from 0 to 3, as said below
- out_proj: bfloat16 [1024, 1536], P(None, 'mp'), may hold values from -0.1875 to 0.1875
- norm_gain: float32 [1536], replicated, may hold values from 0.5 to 1.5
- norm_bias: float32 [1536], replicated, may hold values from -3 to 3
- glu_proj: bfloat16 [1536, 3072], P(None, 'mp'), may hold values from -0.15625 to 0.15625
- conv_taps: float32 [31, 1536], replicated, may hold values from -1 to 1
- batch_scale: float32 [1536], replicated, may hold values from 0.25 to 1.75
- batch_shift: float32 [1536], replicated, may hold values from -3 to 3
- down_proj: bfloat16 [1536, 1536], P(None, 'mp'), may hold values from -0.15625 to 0.15625
Outputs:
- encoded: bfloat16 [16384, 1536], P(('dp', 'mp'))
The draws below stay inside these ranges and needn't reach their ends.
Inputs may be any that keep to these rules, and one draw needn't show every extreme that they name: `lengths`: utterance u starts in data group u // 16; a data group holds its utterances in order of u from its first frame on, and its frames after them are padding. In every draw every data group sends exactly 256 frames in each of its 4 utterances to one and the same data group, so that this group receives 4 * 256 frames from every data group; the utterances one data group sends to one data group never have more frames together. `assignment`: every data group sends exactly 4 of its utterances to each data group, itself included. In its new group an utterance lies after those of lower number, from the first frame on, and the frames after them are padding.
All inputs are finite; a program needn't handle non-finite values.
Results may differ from the reference program's by a relative error of at most 0.0034.
Values may be sent and summed in bfloat16 or wider, within the bound.
A program may use at most 128 MiB of HBM per device.

```python
import math
import jax
import jax.numpy as jnp
from jax import lax

D = 1536
HEADS = 16
HD = 64
KERNEL = 31
HALF = 15
MAXLEN = 256
PIECES = 4
QBLK = 512
FEAT_DEV = 192
ROWS_G = 4096
ROWS = 16384
UTT_G = 16
UTTS = 64
N_DP = 4


def routing_tables(key):
    groups = UTTS // UTT_G
    routing_key = jax.random.fold_in(key, 7001)
    order_keys = jax.random.split(jax.random.fold_in(routing_key, 1), groups)
    orders = jax.vmap(lambda order_key: jax.random.permutation(order_key, UTT_G))(order_keys)
    targets = (orders // PIECES).reshape(UTTS).astype(jnp.int32)
    factor = jax.random.randint(jax.random.fold_in(routing_key, 2), (groups,), 1, 5)
    spread = jax.random.randint(jax.random.fold_in(routing_key, 3), (UTTS,), MAXLEN // 4, MAXLEN // 2 + 1)
    owner_group = jnp.arange(UTTS) // UTT_G
    spans_drawn = jnp.minimum(MAXLEN, factor[owner_group] * spread // 2)
    filled_group = jax.random.randint(jax.random.fold_in(routing_key, 4), (), 0, groups)
    heavy_group = (filled_group + 1) % groups
    spans_drawn = jnp.where(targets == heavy_group, MAXLEN - 1, spans_drawn)
    spans_drawn = jnp.where(targets == filled_group, MAXLEN, spans_drawn).astype(jnp.int32)
    return (spans_drawn, targets)


def draw_lengths(key, part):
    return routing_tables(key)[0]


def draw_assignment(key, part):
    return routing_tables(key)[1]


def pack_pairs(flat):
    return flat.reshape(ROWS // 2, 2, HEADS, HD).transpose(0, 2, 1, 3).reshape(ROWS // 2, HEADS, 2 * HD)


def drawn_pair(key):
    shape = (ROWS, HEADS * HD)
    query_key = jax.random.fold_in(key, 501)
    keys_key = jax.random.fold_in(key, 502)
    queries = jax.random.truncated_normal(query_key, -4.0, 4.0, shape, jnp.float32)
    keyset = jax.random.truncated_normal(keys_key, -4.0, 4.0, shape, jnp.float32)
    return (queries, keyset)


def draw_query_rows(key, part):
    return pack_pairs(drawn_pair(key)[0]).astype(jnp.bfloat16)


def draw_key_rows(key, part):
    return pack_pairs(drawn_pair(key)[1]).astype(jnp.bfloat16)


def draw_residual(key, part):
    row_scale = 0.3 * jnp.exp(jax.random.uniform(jax.random.fold_in(key, 601), (ROWS, 1), jnp.float32, 0.0, math.log(10.0)))
    column_scale = 0.3 * jnp.exp(jax.random.uniform(jax.random.fold_in(key, 602), (1, D), jnp.float32, 0.0, math.log(10.0)))
    basis = jax.random.truncated_normal(jax.random.fold_in(key, 605), -4.0, 4.0, (ROWS, D), jnp.float32)
    flat = basis * row_scale * column_scale
    blocks = D // FEAT_DEV
    packed = flat.reshape(ROWS // 4, 4, blocks, FEAT_DEV).transpose(0, 2, 1, 3).reshape(ROWS // 4, blocks, 4 * FEAT_DEV)
    return packed.astype(jnp.bfloat16)


def levels(rng, shape, shards, smallest, high):
    gain, own = 1.0, jax.random.fold_in(rng, 6)
    for dim, shards_of in shards:
        steps = jnp.exp(jax.random.uniform(jax.random.fold_in(own, dim), (shards_of,), jnp.float32, smallest / len(shards), high / len(shards)))
        gain = gain * jnp.repeat(steps, shape[dim] // shards_of).reshape([-1 if axis == dim else 1 for axis in range(len(shape))])
    return gain


def bell_draw(stream_key, extent, deviation, most, pieces=(), held_as=jnp.bfloat16):
    values = jax.random.normal(stream_key, extent, jnp.float32) * deviation
    if len(pieces) > 0:
        values = levels(stream_key, extent, pieces, -0.22, 0.18) * values
    return jnp.clip(values, min=-most, max=most).astype(held_as)


def setup_inputs(seed: int = 0) -> dict:
    seeds = jax.random.split(jax.random.key(seed), 15)
    query_rows = draw_query_rows(jax.random.fold_in(seeds[14], 71), 0)
    key_rows = draw_key_rows(jax.random.fold_in(seeds[14], 71), 0)
    value_rows = bell_draw(seeds[2], (ROWS // 2, HEADS, 2 * HD), 1.0, 6.0, ((0, 4), (1, 8)))
    residual = draw_residual(jax.random.fold_in(seeds[14], 71), 0)
    lengths = draw_lengths(jax.random.fold_in(seeds[14], 71), 0)
    assignment = draw_assignment(jax.random.fold_in(seeds[14], 71), 0)
    out_proj = bell_draw(seeds[6], (HEADS * HD, D), (HEADS * HD) ** -0.5, 0.1875, ((1, 8),))
    norm_gain = jnp.clip(1.0 + 0.1 * jax.random.normal(seeds[7], (D,), jnp.float32), 0.5, 1.5)
    norm_bias = bell_draw(seeds[8], (D,), 0.5, 3.0, (), jnp.float32)
    glu_proj = bell_draw(seeds[9], (D, 2 * D), D ** -0.5, 0.15625, ((1, 8),))
    conv_taps = bell_draw(seeds[10], (KERNEL, D), KERNEL ** -0.5, 1.0, (), jnp.float32)
    batch_scale = jnp.clip(1.0 + 0.15 * jax.random.normal(seeds[11], (D,), jnp.float32), 0.25, 1.75)
    batch_shift = bell_draw(seeds[12], (D,), 0.5, 3.0, (), jnp.float32)
    down_proj = bell_draw(seeds[13], (D, D), D ** -0.5, 0.15625, ((1, 8),))
    return dict(query_rows=query_rows, key_rows=key_rows, value_rows=value_rows, residual=residual, lengths=lengths, assignment=assignment, out_proj=out_proj, norm_gain=norm_gain, norm_bias=norm_bias, glu_proj=glu_proj, conv_taps=conv_taps, batch_scale=batch_scale, batch_shift=batch_shift, down_proj=down_proj)


EPS = 1e-05
MASKED = -1e+30

def unpack_pairs(packed):
    pair_rows, head_count, pair_width = packed.shape
    width = pair_width // 2
    return packed.reshape(pair_rows, head_count, 2, width).transpose(0, 2, 1, 3).reshape(pair_rows * 2, head_count * width)

def unpack_fours(packed):
    four_rows, block_count, four_width = packed.shape
    width = four_width // 4
    return packed.reshape(four_rows, block_count, 4, width).transpose(0, 2, 1, 3).reshape(four_rows * 4, block_count * width)

def utterance_tables(lengths, assignment):
    utterance = jnp.arange(UTTS, dtype=jnp.int32)
    source = utterance // UTT_G
    earlier = utterance[None, :] < utterance[:, None]
    same_source = source[None, :] == source[:, None]
    same_target = assignment[None, :] == assignment[:, None]
    span_table = jnp.broadcast_to(lengths[None, :], (UTTS, UTTS))
    nothing = jnp.zeros_like(span_table)
    before_start = lax.optimization_barrier(jnp.sum(jnp.where(earlier & same_source, span_table, nothing), axis=1))
    after_start = lax.optimization_barrier(jnp.sum(jnp.where(earlier & same_target, span_table, nothing), axis=1))
    return (source, before_start, after_start)

def find_frames(data_group, owner_group, first_frame, lengths, frames, lookup):
    position = jnp.arange(frames, dtype=jnp.int32)[:, None]
    matches = (owner_group[None, :] == data_group) & (position >= first_frame[None, :]) & (position < first_frame[None, :] + lengths[None, :])
    utterance = jnp.arange(lengths.shape[0], dtype=jnp.int32)[None, :]
    occupied_slots = jnp.any(matches, axis=1)
    segment = jnp.where(occupied_slots, lax.optimization_barrier(jnp.sum(jnp.where(matches, utterance, 0), axis=1)), -1).astype(jnp.int32)
    shifted = lax.optimization_barrier(jnp.sum(jnp.where(matches, lookup[None, :] - first_frame[None, :], 0), axis=1))
    source_row = jnp.where(occupied_slots, jnp.arange(frames, dtype=jnp.int32) + shifted, 0).astype(jnp.int32)
    return (segment, occupied_slots, source_row)

def attend(query_rows, key_rows, value_rows, segment):
    group_rows, width_per_head = query_rows.shape
    head_count = width_per_head // HD
    window = QBLK + 2 * MAXLEN
    score_scale = HD ** (-0.5)
    queries = query_rows.reshape(group_rows, head_count, HD).astype(jnp.float32)
    keyset = key_rows.reshape(group_rows, head_count, HD).astype(jnp.float32)
    valueset = value_rows.reshape(group_rows, head_count, HD).astype(jnp.float32)

    def attend_block(block_index, context):
        first_row = (block_index * QBLK).astype(jnp.int32)
        window_low = jnp.clip(first_row - MAXLEN, 0, group_rows - window).astype(jnp.int32)
        query_block = lax.dynamic_slice_in_dim(queries, first_row, QBLK, 0)
        key_block = lax.dynamic_slice_in_dim(keyset, window_low, window, 0)
        value_block = lax.dynamic_slice_in_dim(valueset, window_low, window, 0)
        segment_query = lax.dynamic_slice_in_dim(segment, first_row, QBLK, 0)
        segment_key = lax.dynamic_slice_in_dim(segment, window_low, window, 0)
        allowed = (segment_query[:, None] == segment_key[None, :]) & (segment_key[None, :] >= 0)
        scores = jnp.einsum('qhd,khd->hqk', query_block, key_block) * score_scale
        scores = jnp.where(allowed[None], scores, MASKED)
        highest = lax.optimization_barrier(jnp.max(scores, axis=2, keepdims=True))
        exponentials = jnp.exp(scores - highest)
        denominator = lax.optimization_barrier(jnp.sum(exponentials, axis=2, keepdims=True))
        weights = (exponentials / denominator).astype(jnp.bfloat16)
        blended = jnp.einsum('hqk,khd->qhd', weights.astype(jnp.float32), value_block)
        blended = jnp.where((segment_query >= 0)[:, None, None], blended, 0.0).astype(jnp.bfloat16)
        return lax.dynamic_update_slice_in_dim(context, blended.reshape(QBLK, width_per_head), first_row, 0)
    return lax.fori_loop(0, group_rows // QBLK, attend_block, jnp.zeros((group_rows, width_per_head), jnp.bfloat16))

def depthwise(gated_rows, segment, conv_taps):
    output_rows = gated_rows.shape[0] - 2 * HALF
    centre = segment[HALF:HALF + output_rows]
    accumulated = jnp.zeros((output_rows, gated_rows.shape[1]), jnp.float32)
    for tap_index in range(KERNEL):
        same_segment = (segment[tap_index:tap_index + output_rows] == centre)[:, None]
        term = jnp.where(same_segment, gated_rows[tap_index:tap_index + output_rows].astype(jnp.float32), 0.0)
        accumulated = accumulated + term * conv_taps[tap_index]
    return accumulated

def reference(query_rows, key_rows, value_rows, residual, lengths, assignment, out_proj, norm_gain, norm_bias, glu_proj, conv_taps, batch_scale, batch_shift, down_proj):
    query_flat = unpack_pairs(query_rows)
    key_flat = unpack_pairs(key_rows)
    value_flat = unpack_pairs(value_rows)
    residual_flat = unpack_fours(residual)
    source, before_start, after_start = utterance_tables(lengths, assignment)
    lookup = source * ROWS_G + before_start

    def one_group(data_group):
        segment, occupied_slots, source_row = find_frames(data_group, assignment, after_start, lengths, ROWS_G, lookup)

        def bring(array):
            picked = jnp.take(array, source_row, axis=0)
            return jnp.where(occupied_slots[:, None], picked, jnp.zeros((), array.dtype))
        context = attend(bring(query_flat), bring(key_flat), bring(value_flat), segment)
        carried = bring(residual_flat).astype(jnp.float32) + jnp.dot(context, out_proj, preferred_element_type=jnp.float32)
        average = lax.optimization_barrier(jnp.mean(carried, axis=1, keepdims=True))
        centred = carried - average
        variance = lax.optimization_barrier(jnp.mean(centred * centred, axis=1, keepdims=True))
        normed = (centred * lax.rsqrt(variance + EPS) * norm_gain + norm_bias).astype(jnp.bfloat16)
        halves = jnp.dot(normed, glu_proj, preferred_element_type=jnp.float32)
        gated_rows = (halves[:, :D] * jax.nn.sigmoid(halves[:, D:])).astype(jnp.bfloat16)
        padded = jnp.pad(gated_rows, ((HALF, HALF), (0, 0)))
        wide_segment = jnp.pad(segment, (HALF, HALF), constant_values=-2)
        convolved = depthwise(padded, wide_segment, conv_taps)
        affine = convolved * batch_scale + batch_shift
        swished = (affine * jax.nn.sigmoid(affine)).astype(jnp.bfloat16)
        lowered = jnp.dot(swished, down_proj, preferred_element_type=jnp.float32)
        return jnp.where((segment >= 0)[:, None], carried + lowered, 0.0).astype(jnp.bfloat16)
    encoded = lax.map(one_group, jnp.arange(N_DP, dtype=jnp.int32))
    return encoded.reshape(ROWS, D)
```

```python
import functools

import jax
import jax.numpy as jnp
from jax import lax
from jax.experimental import pallas as pl
from jax.experimental.pallas import tpu as pltpu
from jax.sharding import PartitionSpec as P

HD = 64
KERNEL = 31
HALF = 15
MAXLEN = 256
PIECES = 4
LANES = 128
HALO = 16
CONV_ROWS = 64

EPS = 1e-05
MASKED = -1e30
VMEM_LIMIT = 60 * 1024 * 1024


def params():
    return pltpu.CompilerParams(vmem_limit_bytes=VMEM_LIMIT)


def whole_spec():
    return pl.BlockSpec(memory_space=pltpu.VMEM)


def smem_spec():
    return pl.BlockSpec(memory_space=pltpu.SMEM)


def attention_kernel(
    heads, start_ref, span_ref, q_ref, k_ref, v_ref, out_ref, q_rows, k_rows, v_rows
):
    pairs = q_ref.shape[0]
    step = 256
    lane = lax.broadcasted_iota(jnp.int32, (step, LANES), 1)
    low = lane < HD

    def unpack(chunk, carry):
        first = pl.multiple_of(chunk * step, step)
        for packed, rows in ((q_ref, q_rows), (k_ref, k_rows), (v_ref, v_rows)):
            one = packed[pl.ds(first, step), 0:LANES].astype(jnp.float32)
            if heads == 2:
                two = packed[pl.ds(first, step), LANES : 2 * LANES].astype(jnp.float32)
                even = jnp.where(low, one, pltpu.roll(two, HD, 1))
                odd = jnp.where(low, pltpu.roll(one, HD, 1), two)
            else:
                even = one
                odd = pltpu.roll(one, HD, 1)
            rows[pl.ds(2 * first, step, stride=2), :] = even
            rows[pl.ds(2 * first + 1, step, stride=2), :] = odd
        return carry

    lax.fori_loop(0, pairs // step, unpack, 0)
    for rows in (q_rows, k_rows, v_rows):
        rows[pl.ds(2 * pairs, MAXLEN), :] = jnp.zeros((MAXLEN, LANES), jnp.float32)

    column = lax.broadcasted_iota(jnp.int32, (MAXLEN, MAXLEN), 1)
    head_lane = lax.broadcasted_iota(jnp.int32, (MAXLEN, LANES), 1) // HD

    def slot_body(slot, carry):
        start = start_ref[slot]
        allowed = column < span_ref[slot]
        queries = q_rows[pl.ds(start, MAXLEN), :]
        keys = k_rows[pl.ds(start, MAXLEN), :].astype(jnp.bfloat16)
        values = v_rows[pl.ds(start, MAXLEN), :].astype(jnp.bfloat16)
        result = None
        for head in range(heads):
            own = jnp.where(head_lane == head, queries, 0.0).astype(jnp.bfloat16)
            scores = (
                lax.dot_general(
                    own, keys, (((1,), (1,)), ((), ())), preferred_element_type=jnp.float32
                )
                * HD ** (-0.5)
            )
            scores = jnp.where(allowed, scores, MASKED)
            highest = jnp.max(scores, axis=1, keepdims=True)
            exponentials = jnp.exp(scores - highest)
            denominator = jnp.sum(exponentials, axis=1, keepdims=True)
            weights = (exponentials / denominator).astype(jnp.bfloat16)
            blended = jnp.dot(weights, values, preferred_element_type=jnp.float32)
            result = blended if head == 0 else jnp.where(head_lane == head, blended, result)
        out_ref[slot] = result.astype(jnp.bfloat16)
        return carry

    lax.fori_loop(0, start_ref.shape[0], slot_body, 0)


def attend(start, span, query_rows, key_rows, value_rows):
    pairs, heads, _ = query_rows.shape
    slots = start.shape[0]
    flat = [a.reshape(pairs, heads * LANES) for a in (query_rows, key_rows, value_rows)]
    return pl.pallas_call(
        functools.partial(attention_kernel, heads),
        out_shape=jax.ShapeDtypeStruct((slots, MAXLEN, LANES), jnp.bfloat16),
        in_specs=[smem_spec()] * 2 + [whole_spec()] * 3,
        out_specs=whole_spec(),
        scratch_shapes=[pltpu.VMEM((2 * pairs + MAXLEN, LANES), jnp.float32)] * 3,
        compiler_params=params(),
        cost_estimate=pl.CostEstimate(
            flops=slots * heads * MAXLEN * MAXLEN * LANES * 4,
            bytes_accessed=pairs * heads * LANES * 8,
            transcendentals=slots * heads * MAXLEN * MAXLEN,
        ),
    )(start, span, *flat)


def lane_tiles(width):
    return [(first, min(LANES, width - first)) for first in range(0, width, LANES)]


def pairable(width):
    return width == LANES + LANES // 2


def join_pair(one, two):
    half = LANES // 2
    low = lax.broadcasted_iota(jnp.int32, one[0].shape, 1) < half
    turned = pltpu.roll(two[0], half, 1)
    return (
        one[0],
        jnp.where(low, one[1], turned),
        jnp.where(low, turned, pltpu.roll(two[1], half, 1)),
    )


def split_pair(tiles):
    half = LANES // 2
    low = lax.broadcasted_iota(jnp.int32, tiles[0].shape, 1) < half
    middle = pltpu.roll(tiles[1], half, 1)
    last = pltpu.roll(tiles[2], half, 1)
    return (tiles[0], tiles[1]), (jnp.where(low, middle, last), last)


def slots_kernel(start_ref, rows_ref, out_ref, *held):
    count, width = rows_ref.shape
    for (first, size), rows in zip(lane_tiles(width), held):

        def widen(chunk, carry):
            at = pl.multiple_of(chunk * MAXLEN, MAXLEN)
            rows[pl.ds(at, MAXLEN), 0:size] = rows_ref[
                pl.ds(at, MAXLEN), first : first + size
            ].astype(jnp.float32)
            return carry

        lax.fori_loop(0, count // MAXLEN, widen, 0)
        rows[pl.ds(count, MAXLEN), :] = jnp.zeros((MAXLEN, LANES), jnp.float32)

    def slot_body(slot, carry):
        if pairable(width):
            pair = [
                [rows[pl.ds(start_ref[2 * slot + side], MAXLEN), :] for rows in held]
                for side in range(2)
            ]
            tiles = join_pair(*pair)
        else:
            tiles = [rows[pl.ds(start_ref[slot], MAXLEN), :] for rows in held]
        for index, tile in enumerate(tiles):
            out_ref[slot, :, index * LANES : (index + 1) * LANES] = tile.astype(jnp.bfloat16)
        return carry

    lax.fori_loop(0, out_ref.shape[0], slot_body, 0)


def into_slots(start, rows):
    count, width = rows.shape
    slots = start.shape[0]
    tiles = len(lane_tiles(width))
    shape = (slots, MAXLEN, tiles * LANES)
    if pairable(width):
        shape = (slots // 2, MAXLEN, 2 * width)
    return pl.pallas_call(
        slots_kernel,
        out_shape=jax.ShapeDtypeStruct(shape, jnp.bfloat16),
        in_specs=[smem_spec(), whole_spec()],
        out_specs=whole_spec(),
        scratch_shapes=[pltpu.VMEM((count + MAXLEN, LANES), jnp.float32)] * tiles,
        compiler_params=params(),
    )(start, rows)


def place_kernel(paired, after_ref, x_ref, context_ref, out_ref, context_rows, *x_rows):
    slots = context_ref.shape[0]
    slabs = out_ref.shape[0]
    tall = out_ref.shape[1] * (2 if paired else 1)
    slab_rows = tall - 2 * HALO
    total_rows = context_rows.shape[0]
    held = (context_rows,) + x_rows
    zeros = jnp.zeros((MAXLEN, LANES), jnp.float32)
    for rows in held:
        rows[pl.ds(0, HALO), :] = jnp.zeros((HALO, LANES), jnp.float32)

    def load(ref, slot, tile):
        return ref[slot, :, tile * LANES : (tile + 1) * LANES].astype(jnp.float32)

    def put(step, carry):
        if paired:
            sides = split_pair([load(x_ref, step, tile) for tile in range(3)])
            for side in range(2):
                slot = 2 * step + side
                where = pl.ds(HALO + after_ref[slot], MAXLEN)
                for rows, piece in zip(x_rows, sides[side]):
                    rows[where, :] = piece
                context_rows[where, :] = load(context_ref, slot, 0)
        else:
            where = pl.ds(HALO + after_ref[step], MAXLEN)
            for tile, rows in enumerate(x_rows):
                rows[where, :] = load(x_ref, step, tile)
            context_rows[where, :] = load(context_ref, step, 0)
        return carry

    lax.fori_loop(0, x_ref.shape[0], put, 0)
    live = after_ref[slots]

    def clear(step, carry):
        at = jnp.minimum(HALO + live + step * MAXLEN, total_rows - MAXLEN)
        for rows in held:
            rows[pl.ds(at, MAXLEN), :] = zeros
        return carry

    lax.fori_loop(0, (total_rows - HALO - live + MAXLEN - 1) // MAXLEN, clear, 0)

    def emit(slab, carry):
        at = pl.multiple_of(slab * slab_rows, slab_rows)
        if paired:
            half = tall // 2
            one = pl.ds(at, half)
            two = pl.ds(pl.multiple_of(at + half, 8), half)
            tiles = join_pair([rows[one, :] for rows in x_rows], [rows[two, :] for rows in x_rows])
            tiles = tiles + (context_rows[one, :], context_rows[two, :])
        else:
            tiles = [rows[pl.ds(at, tall), :] for rows in x_rows + (context_rows,)]
        for index, tile in enumerate(tiles):
            out_ref[slab, :, index * LANES : (index + 1) * LANES] = tile.astype(jnp.bfloat16)
        return carry

    lax.fori_loop(0, slabs, emit, 0)


def place(after, x_slots, context_slots, slabs, slab_rows, features):
    count = context_slots.shape[0]
    paired = pairable(features)
    tiles = len(lane_tiles(features))
    tall = slab_rows + 2 * HALO
    shape = (slabs, tall, (tiles + 1) * LANES)
    if paired:
        shape = (slabs, tall // 2, 2 * features + 2 * LANES)
    return pl.pallas_call(
        functools.partial(place_kernel, paired),
        out_shape=jax.ShapeDtypeStruct(shape, jnp.bfloat16),
        in_specs=[smem_spec(), whole_spec(), whole_spec()],
        out_specs=whole_spec(),
        scratch_shapes=[pltpu.VMEM((count * MAXLEN + HALO + MAXLEN, LANES), jnp.float32)]
        * (tiles + 1),
        compiler_params=params(),
    )(after, x_slots, context_slots)


def unplace_kernel(moved_ref, x_ref, context_ref):
    slabs, rows, _ = moved_ref.shape
    step = 16
    span = 3 * LANES

    def chunk(index, carry):
        at = pl.multiple_of(index * step, step)

        def load(slab, tile):
            cells = moved_ref[slab, pl.ds(at, step), tile * LANES : (tile + 1) * LANES]
            return cells.astype(jnp.float32)

        for pair in range(slabs // 2):
            split = [
                split_pair([load(2 * pair + member, tile) for tile in range(3)])
                for member in range(2)
            ]
            for side in range(2):
                to = pl.ds(pl.multiple_of(at + side * rows, step), step)
                for tile, cells in enumerate(join_pair(split[0][side], split[1][side])):
                    first = pair * span + tile * LANES
                    x_ref[to, first : first + LANES] = cells.astype(jnp.bfloat16)
        for slab in range(slabs):
            for side in range(2):
                to = pl.ds(pl.multiple_of(at + side * rows, step), step)
                first = span + side * LANES
                context_ref[to, slab * LANES : (slab + 1) * LANES] = moved_ref[
                    slab, pl.ds(at, step), first : first + LANES
                ]
        return carry

    lax.fori_loop(0, rows // step, chunk, 0)


def unplace(moved, features, context_width):
    slabs, rows, _ = moved.shape
    if not (pairable(features) and context_width == LANES):
        first = len(lane_tiles(features)) * LANES
        x = moved[:, :, :features].transpose(1, 0, 2).reshape(rows, -1)
        context = moved[:, :, first : first + context_width]
        return x, context.transpose(1, 0, 2).reshape(rows, -1)
    return pl.pallas_call(
        unplace_kernel,
        out_shape=(
            jax.ShapeDtypeStruct((2 * rows, slabs * features), jnp.bfloat16),
            jax.ShapeDtypeStruct((2 * rows, slabs * context_width), jnp.bfloat16),
        ),
        in_specs=[whole_spec()],
        out_specs=(whole_spec(), whole_spec()),
        compiler_params=params(),
    )(moved)


def conv_kernel(
    uniform_ref, gated_ref, segment_ref, taps_ref, scale_ref, shift_ref, out_ref, wide
):
    wide[...] = gated_ref[...].astype(jnp.float32)
    edge = HALO - HALF
    scale = scale_ref[...]
    shift = shift_ref[...]
    for chunk in range(out_ref.shape[0] // CONV_ROWS):
        base = chunk * CONV_ROWS

        def finish(total):
            affine = total * scale + shift
            out_ref[base : base + CONV_ROWS, :] = (affine * jax.nn.sigmoid(affine)).astype(
                jnp.bfloat16
            )

        @pl.when(uniform_ref[chunk] == 1)
        def _():
            total = jnp.zeros((CONV_ROWS, LANES), jnp.float32)
            for tap in range(KERNEL):
                total = total + wide[pl.ds(base + edge + tap, CONV_ROWS), :] * taps_ref[
                    tap : tap + 1, :
                ]
            finish(total)

        @pl.when(uniform_ref[chunk] == 0)
        def _():
            centre = segment_ref[pl.ds(base + HALO, CONV_ROWS), :]
            total = jnp.zeros((CONV_ROWS, LANES), jnp.float32)
            for tap in range(KERNEL):
                same = segment_ref[pl.ds(base + edge + tap, CONV_ROWS), :] == centre
                term = jnp.where(same, wide[pl.ds(base + edge + tap, CONV_ROWS), :], 0.0)
                total = total + term * taps_ref[tap : tap + 1, :]
            finish(total)


def convolve(gated_rows, segment, conv_taps, batch_scale, batch_shift):
    tall, width = gated_rows.shape
    rows = tall - 2 * HALO
    chunks = rows // CONV_ROWS
    windows = [segment[c * CONV_ROWS : c * CONV_ROWS + CONV_ROWS + 2 * HALO] for c in range(chunks)]
    windows = jnp.stack(windows)
    uniform = jnp.all(windows == windows[:, :1], axis=1).astype(jnp.int32)
    wide_segment = jnp.broadcast_to(segment[:, None], (tall, LANES))
    return pl.pallas_call(
        conv_kernel,
        grid=(width // LANES,),
        out_shape=jax.ShapeDtypeStruct((rows, width), jnp.bfloat16),
        in_specs=[
            smem_spec(),
            pl.BlockSpec((tall, LANES), lambda i: (0, i)),
            pl.BlockSpec((tall, LANES), lambda i: (0, 0)),
            pl.BlockSpec((KERNEL, LANES), lambda i: (0, i)),
            pl.BlockSpec((1, LANES), lambda i: (0, i)),
            pl.BlockSpec((1, LANES), lambda i: (0, i)),
        ],
        out_specs=pl.BlockSpec((rows, LANES), lambda i: (0, i)),
        scratch_shapes=[pltpu.VMEM((tall, LANES), jnp.float32)],
        compiler_params=params(),
        cost_estimate=pl.CostEstimate(
            flops=2 * rows * width * KERNEL, bytes_accessed=4 * rows * width, transcendentals=0
        ),
    )(
        uniform,
        gated_rows,
        wide_segment,
        conv_taps,
        batch_scale[None, :],
        batch_shift[None, :],
    )


MESH = pl.DeviceIdType.MESH
OUT, GLU_ONE, GLU_TWO, DOWN = range(4)


def any_spec():
    return pl.BlockSpec(memory_space=pl.ANY)


class Place:
    def __init__(self):
        self.dp = lax.axis_index("dp")
        self.mp = lax.axis_index("mp")
        self.y, self.c = self.dp // 2, self.dp % 2
        self.z, self.x = self.mp // 2, self.mp % 2
        self.across = 1 - self.x
        self.near = self.z + 1 - 2 * (self.z % 2)
        self.far_one = 2 - self.z // 2
        self.far_two = 3 - 3 * (self.z // 2)

    def x_side(self):
        return (self.dp, 2 * self.z + self.across)

    def y_side(self):
        return (2 * (1 - self.y) + self.c, self.mp)

    def core_side(self):
        return (2 * self.y + 1 - self.c, self.mp)

    def corner(self):
        return (2 * (1 - self.y) + 1 - self.c, self.mp)

    def above(self):
        return (self.dp, self.mp + 2)

    def below(self):
        return (self.dp, self.mp - 2)


def aligned(index, step):
    return pl.multiple_of(index * step, step)


def piece(weights, kind, z, x, y, c, both_y=False):
    shard = 2 * z + x
    if kind == OUT:
        return weights[0].at[pl.ds(aligned(shard, 192), 192), pl.ds(aligned(c, 512), 512)]
    if kind == GLU_ONE:
        return weights[1].at[pl.ds(aligned(c, 256), 256), pl.ds(aligned(shard, 384), 384)]
    if kind == GLU_TWO:
        if both_y:
            rows = pl.ds(pl.multiple_of(512 + c * 512, 256), 512)
        else:
            rows = pl.ds(pl.multiple_of(512 + (c * 2 + y) * 256, 256), 256)
        return weights[1].at[rows, pl.ds(aligned(shard, 384), 384)]
    if both_y:
        columns = pl.ds(aligned(c, 768), 768)
    else:
        columns = pl.ds(aligned(c * 2 + y, 384), 384)
    return weights[2].at[pl.ds(aligned(shard, 192), 192), columns]


def own_piece(shards, kind, y, c):
    if kind == OUT:
        return shards[0].at[:, pl.ds(aligned(c, 512), 512)]
    if kind == GLU_ONE:
        return shards[1].at[pl.ds(aligned(c, 256), 256), :]
    if kind == GLU_TWO:
        return shards[1].at[pl.ds(pl.multiple_of(512 + (c * 2 + y) * 256, 256), 256), :]
    return shards[2].at[:, pl.ds(aligned(c * 2 + y, 384), 384)]


class Mail:
    def __init__(self, send_sems, recv_sems):
        self.send_sems, self.recv_sems = send_sems, recv_sems
        self.used = 0
        self.sent = []

    def slot(self):
        self.used += 1
        return self.used - 1

    def copy(self, slot, source, target, device):
        return pltpu.make_async_remote_copy(
            src_ref=source,
            dst_ref=target,
            send_sem=self.send_sems.at[slot],
            recv_sem=self.recv_sems.at[slot],
            device_id=device,
            device_id_type=MESH,
        )

    def send(self, slot, source, target, device, when=None):
        copy = self.copy(slot, source, target, device)
        run_if(when, copy.start)
        self.sent.append((copy, when))

    def receive(self, slot, target, device, when=None):
        run_if(when, self.copy(slot, target, target, device).wait_recv)

    def finish(self):
        for copy, when in self.sent:
            run_if(when, copy.wait_send)


def run_if(when, action):
    if when is None:
        action()
    else:
        pl.when(when)(action)


def greet(devices):
    barrier = pltpu.get_barrier_semaphore()

    def hello(device):
        pl.semaphore_signal(barrier, inc=1, device_id=device, device_id_type=MESH)

    count = 0
    for device, when in devices:
        if when is None:
            hello(device)
            count = count + 1
        else:
            pl.when(when)(functools.partial(hello, device))
            count = count + when.astype(jnp.int32)
    pl.semaphore_wait(barrier, count)


KINDS = (GLU_ONE, OUT, GLU_TWO, DOWN)


def move_kernel(
    start_ref,
    span_ref,
    q_ref,
    k_ref,
    v_ref,
    residual_ref,
    out_shard,
    glu_shard,
    down_shard,
    x_got,
    context_got,
    out_all,
    glu_all,
    down_all,
    q_rows,
    k_rows,
    v_rows,
    x_low,
    x_high,
    x_send,
    context_send,
    send_sems,
    recv_sems,
    local_sems,
):
    here = Place()
    z, x, y, c = here.z, here.x, here.y, here.c
    weights = (out_all, glu_all, down_all)
    shards = (out_shard, glu_shard, down_shard)
    mail = Mail(send_sems, recv_sems)
    up, down = z < 3, z > 0
    partners = (here.y_side(), here.corner(), here.core_side())
    greet(
        [(device, None) for device in partners + (here.x_side(),)]
        + [(here.above(), up), (here.below(), down)]
    )

    def spot(kind, zz, xx):
        return piece(weights, kind, zz, xx, y, c)

    locals_ = [
        pltpu.make_async_copy(
            out_shard, out_all.at[pl.ds(aligned(here.mp, 192), 192), :], local_sems.at[0]
        ),
        pltpu.make_async_copy(
            glu_shard, glu_all.at[:, pl.ds(aligned(here.mp, 384), 384)], local_sems.at[1]
        ),
        pltpu.make_async_copy(
            down_shard, down_all.at[pl.ds(aligned(here.mp, 192), 192), :], local_sems.at[2]
        ),
    ]
    slots_up, slots_down, slots_x, slots_near = [
        {kind: mail.slot() for kind in KINDS} for _ in range(4)
    ]
    slots_up_two, slots_down_two = [{kind: mail.slot() for kind in KINDS} for _ in range(2)]
    for kind in KINDS:
        mine = own_piece(shards, kind, y, c)
        mail.send(slots_up[kind], mine, spot(kind, z, x), here.above(), up)
        mail.send(slots_down[kind], mine, spot(kind, z, x), here.below(), down)
        mail.send(slots_x[kind], mine, spot(kind, z, x), here.x_side())
    for copy in locals_:
        copy.start()

    count = 4 * residual_ref.shape[0]
    step = 128
    low = lax.broadcasted_iota(jnp.int32, (step, LANES), 1) < HD

    def open_rows(chunk, carry):
        first = pl.multiple_of(chunk * step, step)
        cells = [
            residual_ref[pl.ds(first, step), i * LANES : (i + 1) * LANES].astype(jnp.float32)
            for i in range(6)
        ]
        turned = [pltpu.roll(cells[i], HD, 1) for i in (1, 2, 4, 5)]
        frames = (
            (cells[0], cells[1]),
            (jnp.where(low, turned[0], turned[1]), turned[1]),
            (cells[3], cells[4]),
            (jnp.where(low, turned[2], turned[3]), turned[3]),
        )
        for j, (one, two) in enumerate(frames):
            at = pl.ds(4 * first + j, step, stride=4)
            x_low[at, :] = one
            x_high[at, :] = two
        return carry

    lax.fori_loop(0, residual_ref.shape[0] // step, open_rows, 0)
    for rows in (x_low, x_high):
        rows[pl.ds(count, MAXLEN), :] = jnp.zeros((MAXLEN, LANES), jnp.float32)

    targets = partners + ((here.dp, here.mp),)
    half = PIECES // 2
    x_slots = [mail.slot() for _ in partners]
    context_slots = [mail.slot() for _ in partners]
    for index, target in enumerate(targets):
        group = target[0]

        def fill(pair, carry):
            at = group * half + pair
            both = [
                [
                    rows[pl.ds(start_ref[2 * at + side], MAXLEN), :]
                    for rows in (x_low, x_high)
                ]
                for side in range(2)
            ]
            for tile, cells in enumerate(join_pair(*both)):
                x_send[at, :, tile * LANES : (tile + 1) * LANES] = cells.astype(jnp.bfloat16)
            return carry

        lax.fori_loop(0, half, fill, 0)
        source = x_send.at[pl.ds(group * half, half)]
        landing = x_got.at[pl.ds(here.dp * half, half)]
        if index < 3:
            mail.send(x_slots[index], source, landing, target)
        else:
            copy = pltpu.make_async_copy(source, landing, local_sems.at[3])
            copy.start()
            locals_.append(copy)

    pairs = q_ref.shape[0]
    wide_low = lax.broadcasted_iota(jnp.int32, (256, LANES), 1) < HD

    def unpack(chunk, carry):
        first = pl.multiple_of(chunk * 256, 256)
        for packed, rows in ((q_ref, q_rows), (k_ref, k_rows), (v_ref, v_rows)):
            one = packed[pl.ds(first, 256), 0:LANES].astype(jnp.float32)
            two = packed[pl.ds(first, 256), LANES : 2 * LANES].astype(jnp.float32)
            rows[pl.ds(2 * first, 256, stride=2), :] = jnp.where(
                wide_low, one, pltpu.roll(two, HD, 1)
            )
            rows[pl.ds(2 * first + 1, 256, stride=2), :] = jnp.where(
                wide_low, pltpu.roll(one, HD, 1), two
            )
        return carry

    lax.fori_loop(0, pairs // 256, unpack, 0)
    for rows in (q_rows, k_rows, v_rows):
        rows[pl.ds(2 * pairs, MAXLEN), :] = jnp.zeros((MAXLEN, LANES), jnp.float32)

    column = lax.broadcasted_iota(jnp.int32, (MAXLEN, MAXLEN), 1)
    head_lane = lax.broadcasted_iota(jnp.int32, (MAXLEN, LANES), 1) // HD

    def attend_slot(slot):
        start = start_ref[slot]
        allowed = column < span_ref[slot]
        queries = q_rows[pl.ds(start, MAXLEN), :]
        keys = k_rows[pl.ds(start, MAXLEN), :].astype(jnp.bfloat16)
        values = v_rows[pl.ds(start, MAXLEN), :].astype(jnp.bfloat16)
        result = None
        for head in range(2):
            own = jnp.where(head_lane == head, queries, 0.0).astype(jnp.bfloat16)
            scores = (
                lax.dot_general(
                    own, keys, (((1,), (1,)), ((), ())), preferred_element_type=jnp.float32
                )
                * HD ** (-0.5)
            )
            scores = jnp.where(allowed, scores, MASKED)
            highest = jnp.max(scores, axis=1, keepdims=True)
            exponentials = jnp.exp(scores - highest)
            denominator = jnp.sum(exponentials, axis=1, keepdims=True)
            weighing = (exponentials / denominator).astype(jnp.bfloat16)
            blended = jnp.dot(weighing, values, preferred_element_type=jnp.float32)
            result = blended if head == 0 else jnp.where(head_lane == head, blended, result)
        context_send[slot] = result.astype(jnp.bfloat16)

    def relay(kind):
        mail.receive(slots_up[kind], spot(kind, z - 1, x), here.above(), down)
        mail.send(
            slots_up_two[kind],
            spot(kind, z - 1, x),
            spot(kind, z - 1, x),
            here.above(),
            up & down,
        )
        mail.receive(slots_down[kind], spot(kind, z + 1, x), here.below(), up)
        mail.send(
            slots_down_two[kind],
            spot(kind, z + 1, x),
            spot(kind, z + 1, x),
            here.below(),
            up & down,
        )
        mail.send(
            slots_near[kind],
            spot(kind, here.near, x),
            spot(kind, here.near, x),
            here.x_side(),
        )

    for index, target in enumerate(targets):
        group = target[0]

        def attend_one(rank, carry):
            attend_slot(group * PIECES + rank)
            return carry

        lax.fori_loop(0, PIECES, attend_one, 0)
        source = context_send.at[pl.ds(group * PIECES, PIECES)]
        landing = context_got.at[pl.ds(here.dp * PIECES, PIECES)]
        if index < 3:
            mail.send(context_slots[index], source, landing, target)
        else:
            copy = pltpu.make_async_copy(source, landing, local_sems.at[4])
            copy.start()
            locals_.append(copy)
        relay(KINDS[index])

    for index, source in enumerate(partners):
        mail.receive(x_slots[index], x_got.at[pl.ds(source[0] * half, half)], source)
        mail.receive(
            context_slots[index], context_got.at[pl.ds(source[0] * PIECES, PIECES)], source
        )
    for kind in KINDS:
        mail.receive(slots_x[kind], spot(kind, z, here.across), here.x_side())
        mail.receive(slots_near[kind], spot(kind, here.near, here.across), here.x_side())
        mail.receive(slots_up_two[kind], spot(kind, z - 2, x), here.above(), z > 1)
        mail.receive(slots_down_two[kind], spot(kind, z + 2, x), here.below(), z < 2)
    mail.finish()
    for copy in locals_:
        copy.wait()


def move(start, span, queries, keys, values, residual, out_shard, glu_shard, down_shard):
    slots = start.shape[0]
    pairs = queries.shape[0]
    count = 4 * residual.shape[0]
    bf16 = jnp.bfloat16
    return pl.pallas_call(
        move_kernel,
        out_shape=(
            jax.ShapeDtypeStruct((slots // 2, MAXLEN, 3 * LANES), bf16),
            jax.ShapeDtypeStruct((slots, MAXLEN, LANES), bf16),
            jax.ShapeDtypeStruct((1536, 1024), bf16),
            jax.ShapeDtypeStruct((1536, 3072), bf16),
            jax.ShapeDtypeStruct((1536, 1536), bf16),
        ),
        in_specs=[smem_spec()] * 2 + [whole_spec()] * 4 + [any_spec()] * 3,
        out_specs=(any_spec(),) * 5,
        scratch_shapes=[pltpu.VMEM((2 * pairs + MAXLEN, LANES), jnp.float32)] * 3
        + [pltpu.VMEM((count + MAXLEN, LANES), jnp.float32)] * 2
        + [
            pltpu.VMEM((slots // 2, MAXLEN, 3 * LANES), bf16),
            pltpu.VMEM((slots, MAXLEN, LANES), bf16),
            pltpu.SemaphoreType.DMA((30,)),
            pltpu.SemaphoreType.DMA((30,)),
            pltpu.SemaphoreType.DMA((5,)),
        ],
        compiler_params=pltpu.CompilerParams(
            vmem_limit_bytes=VMEM_LIMIT, collective_id=1, has_side_effects=True
        ),
        cost_estimate=pl.CostEstimate(
            flops=slots * 2 * MAXLEN * MAXLEN * LANES * 4,
            bytes_accessed=50 * 1024 * 1024,
            transcendentals=slots * 2 * MAXLEN * MAXLEN,
        ),
    )(start, span, queries, keys, values, residual, out_shard, glu_shard, down_shard)


def spread_kernel(
    slabs_ref,
    out_in,
    glu_in,
    down_in,
    moved,
    out_all,
    glu_all,
    down_all,
    send_sems,
    recv_sems,
    local_sem,
):
    here = Place()
    z, x, y, c = here.z, here.x, here.y, here.c
    weights = (out_all, glu_all, down_all)
    mail = Mail(send_sems, recv_sems)
    slabs = slabs_ref.shape[0]
    others = [(here.dp, lax.rem(here.mp + step, slabs)) for step in range(1, slabs)]
    greet([(device, None) for device in others + [here.y_side(), here.core_side()]])

    slab_slots = [mail.slot() for _ in others]
    for index, device in enumerate(others):
        mail.send(slab_slots[index], slabs_ref.at[device[1]], moved.at[here.mp], device)
    keep = pltpu.make_async_copy(slabs_ref.at[here.mp], moved.at[here.mp], local_sem)
    keep.start()

    def spot(kind, zz, xx):
        return piece(weights, kind, zz, xx, y, c)

    table = {}

    def slot(*key):
        if key not in table:
            table[key] = mail.slot()
        return table[key]

    def pass_on(name, kind, zz, xx, device, when=None):
        where = spot(kind, zz, xx)
        mail.send(slot(name, kind), where, where, device, when)

    cells = {
        "own near": (here.near, x),
        "own one": (here.far_one, x),
        "own two": (here.far_two, x),
        "other own": (z, here.across),
        "other near": (here.near, here.across),
        "other one": (here.far_one, here.across),
        "other two": (here.far_two, here.across),
    }

    def to_y(kind, cell):
        pass_on("y " + cell, kind, *cells[cell], here.y_side())

    def to_core(kind, cell):
        pass_on("core " + cell, kind, *cells[cell], here.core_side())

    def both_to_core(kind, cell):
        where = piece(weights, kind, *cells[cell], y, c, both_y=True)
        mail.send(slot("core " + cell, kind), where, where, here.core_side())

    def after(kind, cell):
        if kind in (OUT, GLU_ONE):
            to_core(kind, cell)
        else:
            to_y(kind, cell)

    for kind in KINDS:
        pass_on("third up", kind, 0, x, here.above(), z == 2)
        pass_on("third down", kind, 3, x, here.below(), z == 1)
        pass_on("x one", kind, here.far_one, x, here.x_side())
    early = ("own near", "own one", "other own", "other near")
    for kind in (GLU_TWO, OUT, GLU_ONE, DOWN):
        for cell in early:
            after(kind, cell)
    for kind in KINDS:
        mail.receive(slot("x one", kind), spot(kind, *cells["other one"]), here.x_side())
        after(kind, "other one")
    for kind in KINDS:
        mail.receive(slot("third up", kind), spot(kind, 0, x), here.above(), z == 3)
        mail.receive(slot("third down", kind), spot(kind, 3, x), here.below(), z == 0)
        pass_on("x two", kind, here.far_two, x, here.x_side())
        after(kind, "own two")
    for kind in KINDS:
        mail.receive(slot("x two", kind), spot(kind, *cells["other two"]), here.x_side())
        after(kind, "other two")
    order = early + ("other one", "own two", "other two")
    for kind in (GLU_TWO, DOWN):
        for cell in order:
            mail.receive(
                slot("y " + cell, kind),
                piece(weights, kind, *cells[cell], 1 - y, c),
                here.y_side(),
            )
            both_to_core(kind, cell)
    for kind in KINDS:
        for cell in order:
            where = piece(weights, kind, *cells[cell], y, 1 - c, both_y=kind in (GLU_TWO, DOWN))
            mail.receive(slot("core " + cell, kind), where, here.core_side())
    for index in range(len(others)):
        source = lax.rem(here.mp - index - 1 + slabs, slabs)
        mail.receive(slab_slots[index], moved.at[source], (here.dp, source))
    mail.finish()
    keep.wait()


def spread(slabs, out_all, glu_all, down_all):
    shapes = [jax.ShapeDtypeStruct(a.shape, a.dtype) for a in (slabs, out_all, glu_all, down_all)]
    return pl.pallas_call(
        spread_kernel,
        out_shape=tuple(shapes),
        in_specs=[any_spec()] * 4,
        out_specs=(any_spec(),) * 4,
        input_output_aliases={1: 1, 2: 2, 3: 3},
        scratch_shapes=[
            pltpu.SemaphoreType.DMA((70,)),
            pltpu.SemaphoreType.DMA((70,)),
            pltpu.SemaphoreType.DMA,
        ],
        compiler_params=pltpu.CompilerParams(
            vmem_limit_bytes=VMEM_LIMIT, collective_id=2, has_side_effects=True
        ),
    )(slabs, out_all, glu_all, down_all)


def on_device(
    query_rows,
    key_rows,
    value_rows,
    residual,
    lengths,
    assignment,
    out_proj,
    norm_gain,
    norm_bias,
    glu_proj,
    conv_taps,
    batch_scale,
    batch_shift,
    down_proj,
):
    data_group = lax.axis_index("dp")
    slab_index = lax.axis_index("mp")
    groups = lax.axis_size("dp")
    slabs = lax.axis_size("mp")
    group_rows = query_rows.shape[0] * 2
    slab_rows = group_rows // slabs
    total_utterances = lengths.shape[0]
    per_group = total_utterances // groups
    slots = groups * PIECES
    features = residual.shape[2] // 4

    utterance = jnp.arange(total_utterances, dtype=jnp.int32)
    source = utterance // per_group
    earlier = utterance[None, :] < utterance[:, None]
    same_source = source[None, :] == source[:, None]
    same_target = assignment[None, :] == assignment[:, None]
    before = jnp.sum(jnp.where(earlier & same_source, lengths[None, :], 0), axis=1)
    rank = jnp.sum((earlier & same_source & same_target).astype(jnp.int32), axis=1)
    slot = jnp.arange(slots, dtype=jnp.int32)[:, None]
    leaving = (source[None, :] == data_group) & ((assignment * PIECES + rank)[None, :] == slot)
    start = jnp.sum(jnp.where(leaving, before[None, :], 0), axis=1)
    span = jnp.sum(jnp.where(leaving, lengths[None, :], 0), axis=1)
    coming_earlier = (assignment[None, :] == data_group) & (
        (source * PIECES + rank)[None, :] < jnp.arange(slots + 1, dtype=jnp.int32)[:, None]
    )
    after = jnp.sum(jnp.where(coming_earlier, lengths[None, :], 0), axis=1)
    live = jnp.sum(jnp.where(assignment == data_group, lengths, 0))

    position = jnp.arange(slab_rows + 2 * HALO, dtype=jnp.int32) + slab_index * slab_rows - HALO
    segment = jnp.sum((position[:, None] >= after[None, 1:]).astype(jnp.int32), axis=1)
    segment = jnp.where(position < 0, -2, jnp.where(position < live, segment, -1))
    segment = jnp.where(position >= group_rows, -2, segment)

    fits = (
        (groups, slabs) == (4, 8)
        and query_rows.shape == (2048, 2, LANES)
        and residual.shape == (1024, 1, 768)
    )
    if fits:
        flat = [a.reshape(2048, 2 * LANES) for a in (query_rows, key_rows, value_rows)]
        x_slots, context_slots, *weights = move(
            start, span, *flat, residual.reshape(1024, 768), out_proj.T, glu_proj, down_proj.T
        )
        placed = place(after, x_slots, context_slots, slabs, slab_rows, features)
        moved, out_all, glu_all, down_all = spread(placed, *weights)
        carried_slab, context_slab = unplace(moved, features, query_rows.shape[1] * HD)
        carried = carried_slab.astype(jnp.float32) + lax.dot_general(
            context_slab, out_all, (((1,), (1,)), ((), ())), preferred_element_type=jnp.float32
        )
        average = jnp.mean(carried, axis=1, keepdims=True)
        centred = carried - average
        variance = jnp.mean(centred * centred, axis=1, keepdims=True)
        normed = (centred * lax.rsqrt(variance + EPS) * norm_gain + norm_bias).astype(
            jnp.bfloat16
        )
        halves = jnp.dot(normed, glu_all, preferred_element_type=jnp.float32)
        gated_rows = (halves[:, :1536] * jax.nn.sigmoid(halves[:, 1536:])).astype(jnp.bfloat16)
        swished = convolve(gated_rows, segment, conv_taps, batch_scale, batch_shift)
        lowered = lax.dot_general(
            swished, down_all, (((1,), (1,)), ((), ())), preferred_element_type=jnp.float32
        )
        centre_segment = segment[HALO : HALO + slab_rows]
        own_carried = carried[HALO : HALO + slab_rows]
        return jnp.where((centre_segment >= 0)[:, None], own_carried + lowered, 0.0).astype(
            jnp.bfloat16
        )

    residual_rows = (
        residual.reshape(group_rows // 4, 4, features).reshape(group_rows, features)
    )

    def swap(array, axis):
        return lax.all_to_all(array, axis, split_axis=0, concat_axis=0, tiled=True)

    packed, start = lax.optimization_barrier((into_slots(start, residual_rows), start))
    x_slots = swap(packed, "dp")
    context_slots = swap(attend(start, span, query_rows, key_rows, value_rows), "dp")
    moved = swap(place(after, x_slots, context_slots, slabs, slab_rows, features), "mp")
    carried_slab, context_slab = unplace(moved, features, query_rows.shape[1] * HD)

    core = data_group % 2
    partners = [(group, group + 1 - 2 * (group % 2)) for group in range(groups)]

    def gather(weights):
        half = weights.shape[0] // 2
        own = lax.dynamic_slice_in_dim(weights, core * half, half, 0)
        return lax.all_gather(own, "mp", axis=1, tiled=True)

    def both(own):
        return own, lax.ppermute(own, "dp", partners)

    def project(rows, halves_of):
        own, other = halves_of
        half = rows.shape[1] // 2
        low, high = rows[:, :half], rows[:, half:]
        return jnp.dot(
            jnp.where(core == 0, low, high), own, preferred_element_type=jnp.float32
        ) + jnp.dot(jnp.where(core == 0, high, low), other, preferred_element_type=jnp.float32)

    out_halves, glu_halves = both(gather(out_proj)), both(gather(glu_proj))
    down_own = gather(down_proj)
    carried = carried_slab.astype(jnp.float32) + project(context_slab, out_halves)
    average = jnp.mean(carried, axis=1, keepdims=True)
    centred = carried - average
    variance = jnp.mean(centred * centred, axis=1, keepdims=True)
    normed = (centred * lax.rsqrt(variance + EPS) * norm_gain + norm_bias).astype(jnp.bfloat16)
    halves = project(normed, glu_halves)
    feature_count = halves.shape[1] // 2
    gated_rows = (halves[:, :feature_count] * jax.nn.sigmoid(halves[:, feature_count:])).astype(
        jnp.bfloat16
    )
    down_own, gated_rows = lax.optimization_barrier((down_own, gated_rows))
    down_halves = both(down_own)
    swished = convolve(gated_rows, segment, conv_taps, batch_scale, batch_shift)
    lowered = project(swished, down_halves)
    centre_segment = segment[HALO : HALO + slab_rows]
    own_carried = carried[HALO : HALO + slab_rows]
    return jnp.where((centre_segment >= 0)[:, None], own_carried + lowered, 0.0).astype(
        jnp.bfloat16
    )


def solution(mesh):
    in_specs = (
        P("dp", "mp", None),
        P("dp", "mp", None),
        P("dp", "mp", None),
        P("dp", "mp", None),
        P(),
        P(),
        P(None, "mp"),
        P(),
        P(),
        P(None, "mp"),
        P(),
        P(),
        P(),
        P(None, "mp"),
    )
    out_specs = P(("dp", "mp"), None)
    return jax.shard_map(
        on_device, mesh=mesh, in_specs=in_specs, out_specs=out_specs, check_vma=False
    )
```

```python
import functools

import jax
import jax.numpy as jnp
from jax import lax
from jax.experimental import pallas as pl
from jax.experimental.pallas import tpu as pltpu
from jax.sharding import PartitionSpec as P

HD = 64
KERNEL = 31
HALF = 15
MAXLEN = 256
PIECES = 4
LANES = 128
HALO = 16
CONV_ROWS = 64

EPS = 1e-05
MASKED = -1e30
VMEM_LIMIT = 60 * 1024 * 1024


def params():
    return pltpu.CompilerParams(vmem_limit_bytes=VMEM_LIMIT)


def whole_spec():
    return pl.BlockSpec(memory_space=pltpu.VMEM)


def smem_spec():
    return pl.BlockSpec(memory_space=pltpu.SMEM)


def attention_kernel(
    heads, start_ref, span_ref, q_ref, k_ref, v_ref, out_ref, q_rows, k_rows, v_rows
):
    pairs = q_ref.shape[0]
    step = 256
    lane = lax.broadcasted_iota(jnp.int32, (step, LANES), 1)
    low = lane < HD

    def unpack(chunk, carry):
        first = pl.multiple_of(chunk * step, step)
        for packed, rows in ((q_ref, q_rows), (k_ref, k_rows), (v_ref, v_rows)):
            one = packed[pl.ds(first, step), 0:LANES].astype(jnp.float32)
            if heads == 2:
                two = packed[pl.ds(first, step), LANES : 2 * LANES].astype(jnp.float32)
                even = jnp.where(low, one, pltpu.roll(two, HD, 1))
                odd = jnp.where(low, pltpu.roll(one, HD, 1), two)
            else:
                even = one
                odd = pltpu.roll(one, HD, 1)
            rows[pl.ds(2 * first, step, stride=2), :] = even
            rows[pl.ds(2 * first + 1, step, stride=2), :] = odd
        return carry

    lax.fori_loop(0, pairs // step, unpack, 0)
    for rows in (q_rows, k_rows, v_rows):
        rows[pl.ds(2 * pairs, MAXLEN), :] = jnp.zeros((MAXLEN, LANES), jnp.float32)

    column = lax.broadcasted_iota(jnp.int32, (MAXLEN, MAXLEN), 1)
    head_lane = lax.broadcasted_iota(jnp.int32, (MAXLEN, LANES), 1) // HD

    def slot_body(slot, carry):
        start = start_ref[slot]
        allowed = column < span_ref[slot]
        queries = q_rows[pl.ds(start, MAXLEN), :]
        keys = k_rows[pl.ds(start, MAXLEN), :].astype(jnp.bfloat16)
        values = v_rows[pl.ds(start, MAXLEN), :].astype(jnp.bfloat16)
        result = None
        for head in range(heads):
            own = jnp.where(head_lane == head, queries, 0.0).astype(jnp.bfloat16)
            scores = (
                lax.dot_general(
                    own, keys, (((1,), (1,)), ((), ())), preferred_element_type=jnp.float32
                )
                * HD ** (-0.5)
            )
            scores = jnp.where(allowed, scores, MASKED)
            highest = jnp.max(scores, axis=1, keepdims=True)
            exponentials = jnp.exp(scores - highest)
            denominator = jnp.sum(exponentials, axis=1, keepdims=True)
            weights = (exponentials / denominator).astype(jnp.bfloat16)
            blended = jnp.dot(weights, values, preferred_element_type=jnp.float32)
            result = blended if head == 0 else jnp.where(head_lane == head, blended, result)
        out_ref[slot] = result.astype(jnp.bfloat16)
        return carry

    lax.fori_loop(0, start_ref.shape[0], slot_body, 0)


def attend(start, span, query_rows, key_rows, value_rows):
    pairs, heads, _ = query_rows.shape
    slots = start.shape[0]
    flat = [a.reshape(pairs, heads * LANES) for a in (query_rows, key_rows, value_rows)]
    return pl.pallas_call(
        functools.partial(attention_kernel, heads),
        out_shape=jax.ShapeDtypeStruct((slots, MAXLEN, LANES), jnp.bfloat16),
        in_specs=[smem_spec()] * 2 + [whole_spec()] * 3,
        out_specs=whole_spec(),
        scratch_shapes=[pltpu.VMEM((2 * pairs + MAXLEN, LANES), jnp.float32)] * 3,
        compiler_params=params(),
        cost_estimate=pl.CostEstimate(
            flops=slots * heads * MAXLEN * MAXLEN * LANES * 4,
            bytes_accessed=pairs * heads * LANES * 8,
            transcendentals=slots * heads * MAXLEN * MAXLEN,
        ),
    )(start, span, *flat)


def lane_tiles(width):
    return [(first, min(LANES, width - first)) for first in range(0, width, LANES)]


def pairable(width):
    return width == LANES + LANES // 2


def join_pair(one, two):
    half = LANES // 2
    low = lax.broadcasted_iota(jnp.int32, one[0].shape, 1) < half
    turned = pltpu.roll(two[0], half, 1)
    return (
        one[0],
        jnp.where(low, one[1], turned),
        jnp.where(low, turned, pltpu.roll(two[1], half, 1)),
    )


def split_pair(tiles):
    half = LANES // 2
    low = lax.broadcasted_iota(jnp.int32, tiles[0].shape, 1) < half
    middle = pltpu.roll(tiles[1], half, 1)
    last = pltpu.roll(tiles[2], half, 1)
    return (tiles[0], tiles[1]), (jnp.where(low, middle, last), last)


def slots_kernel(start_ref, rows_ref, out_ref, *held):
    count, width = rows_ref.shape
    for (first, size), rows in zip(lane_tiles(width), held):

        def widen(chunk, carry):
            at = pl.multiple_of(chunk * MAXLEN, MAXLEN)
            rows[pl.ds(at, MAXLEN), 0:size] = rows_ref[
                pl.ds(at, MAXLEN), first : first + size
            ].astype(jnp.float32)
            return carry

        lax.fori_loop(0, count // MAXLEN, widen, 0)
        rows[pl.ds(count, MAXLEN), :] = jnp.zeros((MAXLEN, LANES), jnp.float32)

    def slot_body(slot, carry):
        if pairable(width):
            pair = [
                [rows[pl.ds(start_ref[2 * slot + side], MAXLEN), :] for rows in held]
                for side in range(2)
            ]
            tiles = join_pair(*pair)
        else:
            tiles = [rows[pl.ds(start_ref[slot], MAXLEN), :] for rows in held]
        for index, tile in enumerate(tiles):
            out_ref[slot, :, index * LANES : (index + 1) * LANES] = tile.astype(jnp.bfloat16)
        return carry

    lax.fori_loop(0, out_ref.shape[0], slot_body, 0)


def into_slots(start, rows):
    count, width = rows.shape
    slots = start.shape[0]
    tiles = len(lane_tiles(width))
    shape = (slots, MAXLEN, tiles * LANES)
    if pairable(width):
        shape = (slots // 2, MAXLEN, 2 * width)
    return pl.pallas_call(
        slots_kernel,
        out_shape=jax.ShapeDtypeStruct(shape, jnp.bfloat16),
        in_specs=[smem_spec(), whole_spec()],
        out_specs=whole_spec(),
        scratch_shapes=[pltpu.VMEM((count + MAXLEN, LANES), jnp.float32)] * tiles,
        compiler_params=params(),
    )(start, rows)


def place_kernel(paired, after_ref, x_ref, context_ref, out_ref, context_rows, *x_rows):
    slots = context_ref.shape[0]
    slabs = out_ref.shape[0]
    tall = out_ref.shape[1] * (2 if paired else 1)
    slab_rows = tall - 2 * HALO
    total_rows = context_rows.shape[0]
    held = (context_rows,) + x_rows
    zeros = jnp.zeros((MAXLEN, LANES), jnp.float32)
    for rows in held:
        rows[pl.ds(0, HALO), :] = jnp.zeros((HALO, LANES), jnp.float32)

    def load(ref, slot, tile):
        return ref[slot, :, tile * LANES : (tile + 1) * LANES].astype(jnp.float32)

    def put(step, carry):
        if paired:
            sides = split_pair([load(x_ref, step, tile) for tile in range(3)])
            for side in range(2):
                slot = 2 * step + side
                where = pl.ds(HALO + after_ref[slot], MAXLEN)
                for rows, piece in zip(x_rows, sides[side]):
                    rows[where, :] = piece
                context_rows[where, :] = load(context_ref, slot, 0)
        else:
            where = pl.ds(HALO + after_ref[step], MAXLEN)
            for tile, rows in enumerate(x_rows):
                rows[where, :] = load(x_ref, step, tile)
            context_rows[where, :] = load(context_ref, step, 0)
        return carry

    lax.fori_loop(0, x_ref.shape[0], put, 0)
    live = after_ref[slots]

    def clear(step, carry):
        at = jnp.minimum(HALO + live + step * MAXLEN, total_rows - MAXLEN)
        for rows in held:
            rows[pl.ds(at, MAXLEN), :] = zeros
        return carry

    lax.fori_loop(0, (total_rows - HALO - live + MAXLEN - 1) // MAXLEN, clear, 0)

    def emit(slab, carry):
        at = pl.multiple_of(slab * slab_rows, slab_rows)
        if paired:
            half = tall // 2
            one = pl.ds(at, half)
            two = pl.ds(pl.multiple_of(at + half, 8), half)
            tiles = join_pair([rows[one, :] for rows in x_rows], [rows[two, :] for rows in x_rows])
            tiles = tiles + (context_rows[one, :], context_rows[two, :])
        else:
            tiles = [rows[pl.ds(at, tall), :] for rows in x_rows + (context_rows,)]
        for index, tile in enumerate(tiles):
            out_ref[slab, :, index * LANES : (index + 1) * LANES] = tile.astype(jnp.bfloat16)
        return carry

    lax.fori_loop(0, slabs, emit, 0)


def place(after, x_slots, context_slots, slabs, slab_rows, features):
    count = context_slots.shape[0]
    paired = pairable(features)
    tiles = len(lane_tiles(features))
    tall = slab_rows + 2 * HALO
    shape = (slabs, tall, (tiles + 1) * LANES)
    if paired:
        shape = (slabs, tall // 2, 2 * features + 2 * LANES)
    return pl.pallas_call(
        functools.partial(place_kernel, paired),
        out_shape=jax.ShapeDtypeStruct(shape, jnp.bfloat16),
        in_specs=[smem_spec(), whole_spec(), whole_spec()],
        out_specs=whole_spec(),
        scratch_shapes=[pltpu.VMEM((count * MAXLEN + HALO + MAXLEN, LANES), jnp.float32)]
        * (tiles + 1),
        compiler_params=params(),
    )(after, x_slots, context_slots)


def unplace_kernel(moved_ref, x_ref, context_ref):
    slabs, rows, _ = moved_ref.shape
    step = 16
    span = 3 * LANES

    def chunk(index, carry):
        at = pl.multiple_of(index * step, step)

        def load(slab, tile):
            cells = moved_ref[slab, pl.ds(at, step), tile * LANES : (tile + 1) * LANES]
            return cells.astype(jnp.float32)

        for pair in range(slabs // 2):
            split = [
                split_pair([load(2 * pair + member, tile) for tile in range(3)])
                for member in range(2)
            ]
            for side in range(2):
                to = pl.ds(pl.multiple_of(at + side * rows, step), step)
                for tile, cells in enumerate(join_pair(split[0][side], split[1][side])):
                    first = pair * span + tile * LANES
                    x_ref[to, first : first + LANES] = cells.astype(jnp.bfloat16)
        for slab in range(slabs):
            for side in range(2):
                to = pl.ds(pl.multiple_of(at + side * rows, step), step)
                first = span + side * LANES
                context_ref[to, slab * LANES : (slab + 1) * LANES] = moved_ref[
                    slab, pl.ds(at, step), first : first + LANES
                ]
        return carry

    lax.fori_loop(0, rows // step, chunk, 0)


def unplace(moved, features, context_width):
    slabs, rows, _ = moved.shape
    if not (pairable(features) and context_width == LANES):
        first = len(lane_tiles(features)) * LANES
        x = moved[:, :, :features].transpose(1, 0, 2).reshape(rows, -1)
        context = moved[:, :, first : first + context_width]
        return x, context.transpose(1, 0, 2).reshape(rows, -1)
    return pl.pallas_call(
        unplace_kernel,
        out_shape=(
            jax.ShapeDtypeStruct((2 * rows, slabs * features), jnp.bfloat16),
            jax.ShapeDtypeStruct((2 * rows, slabs * context_width), jnp.bfloat16),
        ),
        in_specs=[whole_spec()],
        out_specs=(whole_spec(), whole_spec()),
        compiler_params=params(),
    )(moved)


def conv_kernel(
    uniform_ref, gated_ref, segment_ref, taps_ref, scale_ref, shift_ref, out_ref, wide
):
    wide[...] = gated_ref[...].astype(jnp.float32)
    edge = HALO - HALF
    scale = scale_ref[...]
    shift = shift_ref[...]
    for chunk in range(out_ref.shape[0] // CONV_ROWS):
        base = chunk * CONV_ROWS

        def finish(total):
            affine = total * scale + shift
            out_ref[base : base + CONV_ROWS, :] = (affine * jax.nn.sigmoid(affine)).astype(
                jnp.bfloat16
            )

        @pl.when(uniform_ref[chunk] == 1)
        def _():
            total = jnp.zeros((CONV_ROWS, LANES), jnp.float32)
            for tap in range(KERNEL):
                total = total + wide[pl.ds(base + edge + tap, CONV_ROWS), :] * taps_ref[
                    tap : tap + 1, :
                ]
            finish(total)

        @pl.when(uniform_ref[chunk] == 0)
        def _():
            centre = segment_ref[pl.ds(base + HALO, CONV_ROWS), :]
            total = jnp.zeros((CONV_ROWS, LANES), jnp.float32)
            for tap in range(KERNEL):
                same = segment_ref[pl.ds(base + edge + tap, CONV_ROWS), :] == centre
                term = jnp.where(same, wide[pl.ds(base + edge + tap, CONV_ROWS), :], 0.0)
                total = total + term * taps_ref[tap : tap + 1, :]
            finish(total)


def convolve(gated_rows, segment, conv_taps, batch_scale, batch_shift):
    tall, width = gated_rows.shape
    rows = tall - 2 * HALO
    chunks = rows // CONV_ROWS
    windows = [segment[c * CONV_ROWS : c * CONV_ROWS + CONV_ROWS + 2 * HALO] for c in range(chunks)]
    windows = jnp.stack(windows)
    uniform = jnp.all(windows == windows[:, :1], axis=1).astype(jnp.int32)
    wide_segment = jnp.broadcast_to(segment[:, None], (tall, LANES))
    return pl.pallas_call(
        conv_kernel,
        grid=(width // LANES,),
        out_shape=jax.ShapeDtypeStruct((rows, width), jnp.bfloat16),
        in_specs=[
            smem_spec(),
            pl.BlockSpec((tall, LANES), lambda i: (0, i)),
            pl.BlockSpec((tall, LANES), lambda i: (0, 0)),
            pl.BlockSpec((KERNEL, LANES), lambda i: (0, i)),
            pl.BlockSpec((1, LANES), lambda i: (0, i)),
            pl.BlockSpec((1, LANES), lambda i: (0, i)),
        ],
        out_specs=pl.BlockSpec((rows, LANES), lambda i: (0, i)),
        scratch_shapes=[pltpu.VMEM((tall, LANES), jnp.float32)],
        compiler_params=params(),
        cost_estimate=pl.CostEstimate(
            flops=2 * rows * width * KERNEL, bytes_accessed=4 * rows * width, transcendentals=0
        ),
    )(
        uniform,
        gated_rows,
        wide_segment,
        conv_taps,
        batch_scale[None, :],
        batch_shift[None, :],
    )


MESH = pl.DeviceIdType.MESH
OUT, GLU_ONE, GLU_TWO, DOWN = range(4)


def any_spec():
    return pl.BlockSpec(memory_space=pl.ANY)


class Place:
    def __init__(self):
        self.dp = lax.axis_index("dp")
        self.mp = lax.axis_index("mp")
        self.y, self.c = self.dp // 2, self.dp % 2
        self.z, self.x = self.mp // 2, self.mp % 2
        self.across = 1 - self.x
        self.near = self.z + 1 - 2 * (self.z % 2)
        self.far_one = 2 - self.z // 2
        self.far_two = 3 - 3 * (self.z // 2)

    def x_side(self):
        return (self.dp, 2 * self.z + self.across)

    def y_side(self):
        return (2 * (1 - self.y) + self.c, self.mp)

    def core_side(self):
        return (2 * self.y + 1 - self.c, self.mp)

    def corner(self):
        return (2 * (1 - self.y) + 1 - self.c, self.mp)

    def above(self):
        return (self.dp, self.mp + 2)

    def below(self):
        return (self.dp, self.mp - 2)


def aligned(index, step):
    return pl.multiple_of(index * step, step)


def piece(weights, kind, z, x, y, c, both_y=False):
    shard = 2 * z + x
    if kind == OUT:
        return weights[0].at[pl.ds(aligned(shard, 192), 192), pl.ds(aligned(c, 512), 512)]
    if kind == GLU_ONE:
        return weights[1].at[pl.ds(aligned(c, 256), 256), pl.ds(aligned(shard, 384), 384)]
    if kind == GLU_TWO:
        if both_y:
            rows = pl.ds(pl.multiple_of(512 + c * 512, 256), 512)
        else:
            rows = pl.ds(pl.multiple_of(512 + (c * 2 + y) * 256, 256), 256)
        return weights[1].at[rows, pl.ds(aligned(shard, 384), 384)]
    if both_y:
        columns = pl.ds(aligned(c, 768), 768)
    else:
        columns = pl.ds(aligned(c * 2 + y, 384), 384)
    return weights[2].at[pl.ds(aligned(shard, 192), 192), columns]


def own_piece(shards, kind, y, c):
    if kind == OUT:
        return shards[0].at[:, pl.ds(aligned(c, 512), 512)]
    if kind == GLU_ONE:
        return shards[1].at[pl.ds(aligned(c, 256), 256), :]
    if kind == GLU_TWO:
        return shards[1].at[pl.ds(pl.multiple_of(512 + (c * 2 + y) * 256, 256), 256), :]
    return shards[2].at[:, pl.ds(aligned(c * 2 + y, 384), 384)]


class Mail:
    def __init__(self, send_sems, recv_sems):
        self.send_sems, self.recv_sems = send_sems, recv_sems
        self.used = 0
        self.sent = []

    def slot(self):
        self.used += 1
        return self.used - 1

    def copy(self, slot, source, target, device):
        return pltpu.make_async_remote_copy(
            src_ref=source,
            dst_ref=target,
            send_sem=self.send_sems.at[slot],
            recv_sem=self.recv_sems.at[slot],
            device_id=device,
            device_id_type=MESH,
        )

    def send(self, slot, source, target, device, when=None):
        copy = self.copy(slot, source, target, device)
        run_if(when, copy.start)
        self.sent.append((copy, when))

    def receive(self, slot, target, device, when=None):
        run_if(when, self.copy(slot, target, target, device).wait_recv)

    def finish(self):
        for copy, when in self.sent:
            run_if(when, copy.wait_send)


def run_if(when, action):
    if when is None:
        action()
    else:
        pl.when(when)(action)


def greet(devices):
    barrier = pltpu.get_barrier_semaphore()

    def hello(device):
        pl.semaphore_signal(barrier, inc=1, device_id=device, device_id_type=MESH)

    count = 0
    for device, when in devices:
        if when is None:
            hello(device)
            count = count + 1
        else:
            pl.when(when)(functools.partial(hello, device))
            count = count + when.astype(jnp.int32)
    pl.semaphore_wait(barrier, count)


KINDS = (GLU_ONE, OUT, GLU_TWO, DOWN)


def move_kernel(
    start_ref,
    span_ref,
    q_ref,
    k_ref,
    v_ref,
    residual_ref,
    out_shard,
    glu_shard,
    down_shard,
    x_got,
    context_got,
    out_all,
    glu_all,
    down_all,
    q_rows,
    k_rows,
    v_rows,
    x_low,
    x_high,
    x_send,
    context_send,
    out_held,
    glu_held,
    down_held,
    send_sems,
    recv_sems,
    local_sems,
):
    here = Place()
    z, x, y, c = here.z, here.x, here.y, here.c
    weights = (out_all, glu_all, down_all)
    shards = (out_shard, glu_shard, down_shard)
    held = (out_held, glu_held, down_held)
    mail = Mail(send_sems, recv_sems)
    up, down = z < 3, z > 0
    partners = (here.y_side(), here.corner(), here.core_side())
    greet(
        [(device, None) for device in partners + (here.x_side(),)]
        + [(here.above(), up), (here.below(), down)]
    )

    def spot(kind, zz, xx):
        return piece(weights, kind, zz, xx, y, c)

    own = (
        out_all.at[pl.ds(aligned(here.mp, 192), 192), :],
        glu_all.at[:, pl.ds(aligned(here.mp, 384), 384)],
        down_all.at[pl.ds(aligned(here.mp, 192), 192), :],
    )
    into = [
        pltpu.make_async_copy(shards[i], held[i], local_sems.at[i]) for i in range(3)
    ]
    locals_ = [pltpu.make_async_copy(held[i], own[i], local_sems.at[5 + i]) for i in range(3)]
    slots_up, slots_down, slots_x, slots_near = [
        {kind: mail.slot() for kind in KINDS} for _ in range(4)
    ]
    slots_up_two, slots_down_two = [{kind: mail.slot() for kind in KINDS} for _ in range(2)]
    for kind in KINDS:
        mine = own_piece(shards, kind, y, c)
        mail.send(slots_up[kind], mine, spot(kind, z, x), here.above(), up)
        mail.send(slots_down[kind], mine, spot(kind, z, x), here.below(), down)
        mail.send(slots_x[kind], mine, spot(kind, z, x), here.x_side())
    for copy in into:
        copy.start()

    count = 4 * residual_ref.shape[0]
    step = 128
    low = lax.broadcasted_iota(jnp.int32, (step, LANES), 1) < HD

    def open_rows(chunk, carry):
        first = pl.multiple_of(chunk * step, step)
        cells = [
            residual_ref[pl.ds(first, step), i * LANES : (i + 1) * LANES].astype(jnp.float32)
            for i in range(6)
        ]
        turned = [pltpu.roll(cells[i], HD, 1) for i in (1, 2, 4, 5)]
        frames = (
            (cells[0], cells[1]),
            (jnp.where(low, turned[0], turned[1]), turned[1]),
            (cells[3], cells[4]),
            (jnp.where(low, turned[2], turned[3]), turned[3]),
        )
        for j, (one, two) in enumerate(frames):
            at = pl.ds(4 * first + j, step, stride=4)
            x_low[at, :] = one
            x_high[at, :] = two
        return carry

    lax.fori_loop(0, residual_ref.shape[0] // step, open_rows, 0)
    for rows in (x_low, x_high):
        rows[pl.ds(count, MAXLEN), :] = jnp.zeros((MAXLEN, LANES), jnp.float32)

    targets = partners + ((here.dp, here.mp),)
    half = PIECES // 2
    x_slots = [mail.slot() for _ in partners]
    context_slots = [mail.slot() for _ in partners]
    for index, target in enumerate(targets):
        group = target[0]

        def fill(pair, carry):
            at = group * half + pair
            both = [
                [
                    rows[pl.ds(start_ref[2 * at + side], MAXLEN), :]
                    for rows in (x_low, x_high)
                ]
                for side in range(2)
            ]
            for tile, cells in enumerate(join_pair(*both)):
                x_send[at, :, tile * LANES : (tile + 1) * LANES] = cells.astype(jnp.bfloat16)
            return carry

        lax.fori_loop(0, half, fill, 0)
        source = x_send.at[pl.ds(group * half, half)]
        landing = x_got.at[pl.ds(here.dp * half, half)]
        if index < 3:
            mail.send(x_slots[index], source, landing, target)
        else:
            copy = pltpu.make_async_copy(source, landing, local_sems.at[3])
            copy.start()
            locals_.append(copy)

    for copy_in, copy_out in zip(into, locals_):
        copy_in.wait()
        copy_out.start()

    pairs = q_ref.shape[0]
    wide_low = lax.broadcasted_iota(jnp.int32, (256, LANES), 1) < HD

    def unpack(chunk, carry):
        first = pl.multiple_of(chunk * 256, 256)
        for packed, rows in ((q_ref, q_rows), (k_ref, k_rows), (v_ref, v_rows)):
            one = packed[pl.ds(first, 256), 0:LANES].astype(jnp.float32)
            two = packed[pl.ds(first, 256), LANES : 2 * LANES].astype(jnp.float32)
            rows[pl.ds(2 * first, 256, stride=2), :] = jnp.where(
                wide_low, one, pltpu.roll(two, HD, 1)
            )
            rows[pl.ds(2 * first + 1, 256, stride=2), :] = jnp.where(
                wide_low, pltpu.roll(one, HD, 1), two
            )
        return carry

    lax.fori_loop(0, pairs // 256, unpack, 0)
    for rows in (q_rows, k_rows, v_rows):
        rows[pl.ds(2 * pairs, MAXLEN), :] = jnp.zeros((MAXLEN, LANES), jnp.float32)

    column = lax.broadcasted_iota(jnp.int32, (MAXLEN, MAXLEN), 1)
    head_lane = lax.broadcasted_iota(jnp.int32, (MAXLEN, LANES), 1) // HD

    def attend_slot(slot):
        start = start_ref[slot]
        allowed = column < span_ref[slot]
        queries = q_rows[pl.ds(start, MAXLEN), :]
        keys = k_rows[pl.ds(start, MAXLEN), :].astype(jnp.bfloat16)
        values = v_rows[pl.ds(start, MAXLEN), :].astype(jnp.bfloat16)
        result = None
        for head in range(2):
            own = jnp.where(head_lane == head, queries, 0.0).astype(jnp.bfloat16)
            scores = (
                lax.dot_general(
                    own, keys, (((1,), (1,)), ((), ())), preferred_element_type=jnp.float32
                )
                * HD ** (-0.5)
            )
            scores = jnp.where(allowed, scores, MASKED)
            highest = jnp.max(scores, axis=1, keepdims=True)
            exponentials = jnp.exp(scores - highest)
            denominator = jnp.sum(exponentials, axis=1, keepdims=True)
            weighing = (exponentials / denominator).astype(jnp.bfloat16)
            blended = jnp.dot(weighing, values, preferred_element_type=jnp.float32)
            result = blended if head == 0 else jnp.where(head_lane == head, blended, result)
        context_send[slot] = result.astype(jnp.bfloat16)

    def relay(kind):
        mail.receive(slots_up[kind], spot(kind, z - 1, x), here.above(), down)
        mail.send(
            slots_up_two[kind],
            spot(kind, z - 1, x),
            spot(kind, z - 1, x),
            here.above(),
            up & down,
        )
        mail.receive(slots_down[kind], spot(kind, z + 1, x), here.below(), up)
        mail.send(
            slots_down_two[kind],
            spot(kind, z + 1, x),
            spot(kind, z + 1, x),
            here.below(),
            up & down,
        )
        mail.send(
            slots_near[kind],
            spot(kind, here.near, x),
            spot(kind, here.near, x),
            here.x_side(),
        )

    for index, target in enumerate(targets):
        group = target[0]

        def attend_one(rank, carry):
            attend_slot(group * PIECES + rank)
            return carry

        lax.fori_loop(0, PIECES, attend_one, 0)
        source = context_send.at[pl.ds(group * PIECES, PIECES)]
        landing = context_got.at[pl.ds(here.dp * PIECES, PIECES)]
        if index < 3:
            mail.send(context_slots[index], source, landing, target)
        else:
            copy = pltpu.make_async_copy(source, landing, local_sems.at[4])
            copy.start()
            locals_.append(copy)
        relay(KINDS[index])

    for index, source in enumerate(partners):
        mail.receive(x_slots[index], x_got.at[pl.ds(source[0] * half, half)], source)
        mail.receive(
            context_slots[index], context_got.at[pl.ds(source[0] * PIECES, PIECES)], source
        )
    for kind in KINDS:
        mail.receive(slots_x[kind], spot(kind, z, here.across), here.x_side())
        mail.receive(slots_near[kind], spot(kind, here.near, here.across), here.x_side())
        mail.receive(slots_up_two[kind], spot(kind, z - 2, x), here.above(), z > 1)
        mail.receive(slots_down_two[kind], spot(kind, z + 2, x), here.below(), z < 2)
    mail.finish()
    for copy in locals_:
        copy.wait()


def move(start, span, queries, keys, values, residual, out_shard, glu_shard, down_shard):
    slots = start.shape[0]
    pairs = queries.shape[0]
    count = 4 * residual.shape[0]
    bf16 = jnp.bfloat16
    return pl.pallas_call(
        move_kernel,
        out_shape=(
            jax.ShapeDtypeStruct((slots // 2, MAXLEN, 3 * LANES), bf16),
            jax.ShapeDtypeStruct((slots, MAXLEN, LANES), bf16),
            jax.ShapeDtypeStruct((1536, 1024), bf16),
            jax.ShapeDtypeStruct((1536, 3072), bf16),
            jax.ShapeDtypeStruct((1536, 1536), bf16),
        ),
        in_specs=[smem_spec()] * 2 + [whole_spec()] * 4 + [any_spec()] * 3,
        out_specs=(any_spec(),) * 5,
        scratch_shapes=[pltpu.VMEM((2 * pairs + MAXLEN, LANES), jnp.float32)] * 3
        + [pltpu.VMEM((count + MAXLEN, LANES), jnp.float32)] * 2
        + [
            pltpu.VMEM((slots // 2, MAXLEN, 3 * LANES), bf16),
            pltpu.VMEM((slots, MAXLEN, LANES), bf16),
            pltpu.VMEM(out_shard.shape, bf16),
            pltpu.VMEM(glu_shard.shape, bf16),
            pltpu.VMEM(down_shard.shape, bf16),
            pltpu.SemaphoreType.DMA((30,)),
            pltpu.SemaphoreType.DMA((30,)),
            pltpu.SemaphoreType.DMA((8,)),
        ],
        compiler_params=pltpu.CompilerParams(
            vmem_limit_bytes=VMEM_LIMIT, collective_id=1, has_side_effects=True
        ),
        cost_estimate=pl.CostEstimate(
            flops=slots * 2 * MAXLEN * MAXLEN * LANES * 4,
            bytes_accessed=50 * 1024 * 1024,
            transcendentals=slots * 2 * MAXLEN * MAXLEN,
        ),
    )(start, span, queries, keys, values, residual, out_shard, glu_shard, down_shard)


def spread_kernel(
    slabs_ref,
    out_in,
    glu_in,
    down_in,
    moved,
    out_all,
    glu_all,
    down_all,
    slab_held,
    send_sems,
    recv_sems,
    local_sem,
):
    here = Place()
    z, x, y, c = here.z, here.x, here.y, here.c
    weights = (out_all, glu_all, down_all)
    mail = Mail(send_sems, recv_sems)
    slabs = slabs_ref.shape[0]
    others = [(here.dp, lax.rem(here.mp + step, slabs)) for step in range(1, slabs)]
    greet([(device, None) for device in others + [here.y_side(), here.core_side()]])

    slab_slots = [mail.slot() for _ in others]
    for index, device in enumerate(others):
        mail.send(slab_slots[index], slabs_ref.at[device[1]], moved.at[here.mp], device)
    keep = pltpu.make_async_copy(slabs_ref.at[here.mp], slab_held, local_sem)
    keep.start()
    keep.wait()
    keep = pltpu.make_async_copy(slab_held, moved.at[here.mp], local_sem)
    keep.start()

    def spot(kind, zz, xx):
        return piece(weights, kind, zz, xx, y, c)

    table = {}

    def slot(*key):
        if key not in table:
            table[key] = mail.slot()
        return table[key]

    def pass_on(name, kind, zz, xx, device, when=None):
        where = spot(kind, zz, xx)
        mail.send(slot(name, kind), where, where, device, when)

    cells = {
        "own near": (here.near, x),
        "own one": (here.far_one, x),
        "own two": (here.far_two, x),
        "other own": (z, here.across),
        "other near": (here.near, here.across),
        "other one": (here.far_one, here.across),
        "other two": (here.far_two, here.across),
    }

    def to_y(kind, cell):
        pass_on("y " + cell, kind, *cells[cell], here.y_side())

    def to_core(kind, cell):
        pass_on("core " + cell, kind, *cells[cell], here.core_side())

    def both_to_core(kind, cell):
        where = piece(weights, kind, *cells[cell], y, c, both_y=True)
        mail.send(slot("core " + cell, kind), where, where, here.core_side())

    def after(kind, cell):
        if kind in (OUT, GLU_ONE):
            to_core(kind, cell)
        else:
            to_y(kind, cell)

    for kind in KINDS:
        pass_on("third up", kind, 0, x, here.above(), z == 2)
        pass_on("third down", kind, 3, x, here.below(), z == 1)
        pass_on("x one", kind, here.far_one, x, here.x_side())
    early = ("own near", "own one", "other own", "other near")
    for kind in (GLU_TWO, OUT, GLU_ONE, DOWN):
        for cell in early:
            after(kind, cell)
    for kind in KINDS:
        mail.receive(slot("x one", kind), spot(kind, *cells["other one"]), here.x_side())
        after(kind, "other one")
    for kind in KINDS:
        mail.receive(slot("third up", kind), spot(kind, 0, x), here.above(), z == 3)
        mail.receive(slot("third down", kind), spot(kind, 3, x), here.below(), z == 0)
        pass_on("x two", kind, here.far_two, x, here.x_side())
        after(kind, "own two")
    for kind in KINDS:
        mail.receive(slot("x two", kind), spot(kind, *cells["other two"]), here.x_side())
        after(kind, "other two")
    order = early + ("other one", "own two", "other two")
    for kind in (GLU_TWO, DOWN):
        for cell in order:
            mail.receive(
                slot("y " + cell, kind),
                piece(weights, kind, *cells[cell], 1 - y, c),
                here.y_side(),
            )
            both_to_core(kind, cell)
    for kind in KINDS:
        for cell in order:
            where = piece(weights, kind, *cells[cell], y, 1 - c, both_y=kind in (GLU_TWO, DOWN))
            mail.receive(slot("core " + cell, kind), where, here.core_side())
    for index in range(len(others)):
        source = lax.rem(here.mp - index - 1 + slabs, slabs)
        mail.receive(slab_slots[index], moved.at[source], (here.dp, source))
    mail.finish()
    keep.wait()


def spread(slabs, out_all, glu_all, down_all):
    shapes = [jax.ShapeDtypeStruct(a.shape, a.dtype) for a in (slabs, out_all, glu_all, down_all)]
    return pl.pallas_call(
        spread_kernel,
        out_shape=tuple(shapes),
        in_specs=[any_spec()] * 4,
        out_specs=(any_spec(),) * 4,
        input_output_aliases={1: 1, 2: 2, 3: 3},
        scratch_shapes=[
            pltpu.VMEM(slabs.shape[1:], slabs.dtype),
            pltpu.SemaphoreType.DMA((70,)),
            pltpu.SemaphoreType.DMA((70,)),
            pltpu.SemaphoreType.DMA,
        ],
        compiler_params=pltpu.CompilerParams(
            vmem_limit_bytes=VMEM_LIMIT, collective_id=2, has_side_effects=True
        ),
    )(slabs, out_all, glu_all, down_all)


def on_device(
    query_rows,
    key_rows,
    value_rows,
    residual,
    lengths,
    assignment,
    out_proj,
    norm_gain,
    norm_bias,
    glu_proj,
    conv_taps,
    batch_scale,
    batch_shift,
    down_proj,
):
    data_group = lax.axis_index("dp")
    slab_index = lax.axis_index("mp")
    groups = lax.axis_size("dp")
    slabs = lax.axis_size("mp")
    group_rows = query_rows.shape[0] * 2
    slab_rows = group_rows // slabs
    total_utterances = lengths.shape[0]
    per_group = total_utterances // groups
    slots = groups * PIECES
    features = residual.shape[2] // 4

    utterance = jnp.arange(total_utterances, dtype=jnp.int32)
    source = utterance // per_group
    earlier = utterance[None, :] < utterance[:, None]
    same_source = source[None, :] == source[:, None]
    same_target = assignment[None, :] == assignment[:, None]
    before = jnp.sum(jnp.where(earlier & same_source, lengths[None, :], 0), axis=1)
    rank = jnp.sum((earlier & same_source & same_target).astype(jnp.int32), axis=1)
    slot = jnp.arange(slots, dtype=jnp.int32)[:, None]
    leaving = (source[None, :] == data_group) & ((assignment * PIECES + rank)[None, :] == slot)
    start = jnp.sum(jnp.where(leaving, before[None, :], 0), axis=1)
    span = jnp.sum(jnp.where(leaving, lengths[None, :], 0), axis=1)
    coming_earlier = (assignment[None, :] == data_group) & (
        (source * PIECES + rank)[None, :] < jnp.arange(slots + 1, dtype=jnp.int32)[:, None]
    )
    after = jnp.sum(jnp.where(coming_earlier, lengths[None, :], 0), axis=1)
    live = jnp.sum(jnp.where(assignment == data_group, lengths, 0))

    position = jnp.arange(slab_rows + 2 * HALO, dtype=jnp.int32) + slab_index * slab_rows - HALO
    segment = jnp.sum((position[:, None] >= after[None, 1:]).astype(jnp.int32), axis=1)
    segment = jnp.where(position < 0, -2, jnp.where(position < live, segment, -1))
    segment = jnp.where(position >= group_rows, -2, segment)

    fits = (
        (groups, slabs) == (4, 8)
        and query_rows.shape == (2048, 2, LANES)
        and residual.shape == (1024, 1, 768)
    )
    if fits:
        flat = [a.reshape(2048, 2 * LANES) for a in (query_rows, key_rows, value_rows)]
        x_slots, context_slots, *weights = move(
            start, span, *flat, residual.reshape(1024, 768), out_proj.T, glu_proj, down_proj.T
        )
        placed = place(after, x_slots, context_slots, slabs, slab_rows, features)
        moved, out_all, glu_all, down_all = spread(placed, *weights)
        carried_slab, context_slab = unplace(moved, features, query_rows.shape[1] * HD)
        carried = carried_slab.astype(jnp.float32) + lax.dot_general(
            context_slab, out_all, (((1,), (1,)), ((), ())), preferred_element_type=jnp.float32
        )
        average = jnp.mean(carried, axis=1, keepdims=True)
        centred = carried - average
        variance = jnp.mean(centred * centred, axis=1, keepdims=True)
        normed = (centred * lax.rsqrt(variance + EPS) * norm_gain + norm_bias).astype(
            jnp.bfloat16
        )
        halves = jnp.dot(normed, glu_all, preferred_element_type=jnp.float32)
        gated_rows = (halves[:, :1536] * jax.nn.sigmoid(halves[:, 1536:])).astype(jnp.bfloat16)
        swished = convolve(gated_rows, segment, conv_taps, batch_scale, batch_shift)
        lowered = lax.dot_general(
            swished, down_all, (((1,), (1,)), ((), ())), preferred_element_type=jnp.float32
        )
        centre_segment = segment[HALO : HALO + slab_rows]
        own_carried = carried[HALO : HALO + slab_rows]
        return jnp.where((centre_segment >= 0)[:, None], own_carried + lowered, 0.0).astype(
            jnp.bfloat16
        )

    residual_rows = (
        residual.reshape(group_rows // 4, 4, features).reshape(group_rows, features)
    )

    def swap(array, axis):
        return lax.all_to_all(array, axis, split_axis=0, concat_axis=0, tiled=True)

    packed, start = lax.optimization_barrier((into_slots(start, residual_rows), start))
    x_slots = swap(packed, "dp")
    context_slots = swap(attend(start, span, query_rows, key_rows, value_rows), "dp")
    moved = swap(place(after, x_slots, context_slots, slabs, slab_rows, features), "mp")
    carried_slab, context_slab = unplace(moved, features, query_rows.shape[1] * HD)

    core = data_group % 2
    partners = [(group, group + 1 - 2 * (group % 2)) for group in range(groups)]

    def gather(weights):
        half = weights.shape[0] // 2
        own = lax.dynamic_slice_in_dim(weights, core * half, half, 0)
        return lax.all_gather(own, "mp", axis=1, tiled=True)

    def both(own):
        return own, lax.ppermute(own, "dp", partners)

    def project(rows, halves_of):
        own, other = halves_of
        half = rows.shape[1] // 2
        low, high = rows[:, :half], rows[:, half:]
        return jnp.dot(
            jnp.where(core == 0, low, high), own, preferred_element_type=jnp.float32
        ) + jnp.dot(jnp.where(core == 0, high, low), other, preferred_element_type=jnp.float32)

    out_halves, glu_halves = both(gather(out_proj)), both(gather(glu_proj))
    down_own = gather(down_proj)
    carried = carried_slab.astype(jnp.float32) + project(context_slab, out_halves)
    average = jnp.mean(carried, axis=1, keepdims=True)
    centred = carried - average
    variance = jnp.mean(centred * centred, axis=1, keepdims=True)
    normed = (centred * lax.rsqrt(variance + EPS) * norm_gain + norm_bias).astype(jnp.bfloat16)
    halves = project(normed, glu_halves)
    feature_count = halves.shape[1] // 2
    gated_rows = (halves[:, :feature_count] * jax.nn.sigmoid(halves[:, feature_count:])).astype(
        jnp.bfloat16
    )
    down_own, gated_rows = lax.optimization_barrier((down_own, gated_rows))
    down_halves = both(down_own)
    swished = convolve(gated_rows, segment, conv_taps, batch_scale, batch_shift)
    lowered = project(swished, down_halves)
    centre_segment = segment[HALO : HALO + slab_rows]
    own_carried = carried[HALO : HALO + slab_rows]
    return jnp.where((centre_segment >= 0)[:, None], own_carried + lowered, 0.0).astype(
        jnp.bfloat16
    )


def solution(mesh):
    in_specs = (
        P("dp", "mp", None),
        P("dp", "mp", None),
        P("dp", "mp", None),
        P("dp", "mp", None),
        P(),
        P(),
        P(None, "mp"),
        P(),
        P(),
        P(None, "mp"),
        P(),
        P(),
        P(),
        P(None, "mp"),
    )
    out_specs = P(("dp", "mp"), None)
    return jax.shard_map(
        on_device, mesh=mesh, in_specs=in_specs, out_specs=out_specs, check_vma=False
    )
```

```python
import functools

import jax
import jax.numpy as jnp
from jax import lax
from jax.experimental import pallas as pl
from jax.experimental.pallas import tpu as pltpu
from jax.sharding import PartitionSpec as P

HD = 64
KERNEL = 31
HALF = 15
MAXLEN = 256
PIECES = 4
LANES = 128
HALO = 16
CONV_ROWS = 64

EPS = 1e-05
MASKED = -1e30
VMEM_LIMIT = 60 * 1024 * 1024


def params():
    return pltpu.CompilerParams(vmem_limit_bytes=VMEM_LIMIT)


def whole_spec():
    return pl.BlockSpec(memory_space=pltpu.VMEM)


def smem_spec():
    return pl.BlockSpec(memory_space=pltpu.SMEM)


def attention_kernel(
    heads, start_ref, span_ref, q_ref, k_ref, v_ref, out_ref, q_rows, k_rows, v_rows
):
    pairs = q_ref.shape[0]
    step = 256
    lane = lax.broadcasted_iota(jnp.int32, (step, LANES), 1)
    low = lane < HD

    def unpack(chunk, carry):
        first = pl.multiple_of(chunk * step, step)
        for packed, rows in ((q_ref, q_rows), (k_ref, k_rows), (v_ref, v_rows)):
            one = packed[pl.ds(first, step), 0:LANES].astype(jnp.float32)
            if heads == 2:
                two = packed[pl.ds(first, step), LANES : 2 * LANES].astype(jnp.float32)
                even = jnp.where(low, one, pltpu.roll(two, HD, 1))
                odd = jnp.where(low, pltpu.roll(one, HD, 1), two)
            else:
                even = one
                odd = pltpu.roll(one, HD, 1)
            rows[pl.ds(2 * first, step, stride=2), :] = even
            rows[pl.ds(2 * first + 1, step, stride=2), :] = odd
        return carry

    lax.fori_loop(0, pairs // step, unpack, 0)
    for rows in (q_rows, k_rows, v_rows):
        rows[pl.ds(2 * pairs, MAXLEN), :] = jnp.zeros((MAXLEN, LANES), jnp.float32)

    column = lax.broadcasted_iota(jnp.int32, (MAXLEN, MAXLEN), 1)
    head_lane = lax.broadcasted_iota(jnp.int32, (MAXLEN, LANES), 1) // HD

    def slot_body(slot, carry):
        start = start_ref[slot]
        allowed = column < span_ref[slot]
        queries = q_rows[pl.ds(start, MAXLEN), :]
        keys = k_rows[pl.ds(start, MAXLEN), :].astype(jnp.bfloat16)
        values = v_rows[pl.ds(start, MAXLEN), :].astype(jnp.bfloat16)
        result = None
        for head in range(heads):
            own = jnp.where(head_lane == head, queries, 0.0).astype(jnp.bfloat16)
            scores = (
                lax.dot_general(
                    own, keys, (((1,), (1,)), ((), ())), preferred_element_type=jnp.float32
                )
                * HD ** (-0.5)
            )
            scores = jnp.where(allowed, scores, MASKED)
            highest = jnp.max(scores, axis=1, keepdims=True)
            exponentials = jnp.exp(scores - highest)
            denominator = jnp.sum(exponentials, axis=1, keepdims=True)
            weights = (exponentials / denominator).astype(jnp.bfloat16)
            blended = jnp.dot(weights, values, preferred_element_type=jnp.float32)
            result = blended if head == 0 else jnp.where(head_lane == head, blended, result)
        out_ref[slot] = result.astype(jnp.bfloat16)
        return carry

    lax.fori_loop(0, start_ref.shape[0], slot_body, 0)


def attend(start, span, query_rows, key_rows, value_rows):
    pairs, heads, _ = query_rows.shape
    slots = start.shape[0]
    flat = [a.reshape(pairs, heads * LANES) for a in (query_rows, key_rows, value_rows)]
    return pl.pallas_call(
        functools.partial(attention_kernel, heads),
        out_shape=jax.ShapeDtypeStruct((slots, MAXLEN, LANES), jnp.bfloat16),
        in_specs=[smem_spec()] * 2 + [whole_spec()] * 3,
        out_specs=whole_spec(),
        scratch_shapes=[pltpu.VMEM((2 * pairs + MAXLEN, LANES), jnp.float32)] * 3,
        compiler_params=params(),
        cost_estimate=pl.CostEstimate(
            flops=slots * heads * MAXLEN * MAXLEN * LANES * 4,
            bytes_accessed=pairs * heads * LANES * 8,
            transcendentals=slots * heads * MAXLEN * MAXLEN,
        ),
    )(start, span, *flat)


def lane_tiles(width):
    return [(first, min(LANES, width - first)) for first in range(0, width, LANES)]


def pairable(width):
    return width == LANES + LANES // 2


def join_pair(one, two):
    half = LANES // 2
    low = lax.broadcasted_iota(jnp.int32, one[0].shape, 1) < half
    turned = pltpu.roll(two[0], half, 1)
    return (
        one[0],
        jnp.where(low, one[1], turned),
        jnp.where(low, turned, pltpu.roll(two[1], half, 1)),
    )


def split_pair(tiles):
    half = LANES // 2
    low = lax.broadcasted_iota(jnp.int32, tiles[0].shape, 1) < half
    middle = pltpu.roll(tiles[1], half, 1)
    last = pltpu.roll(tiles[2], half, 1)
    return (tiles[0], tiles[1]), (jnp.where(low, middle, last), last)


def slots_kernel(start_ref, rows_ref, out_ref, *held):
    count, width = rows_ref.shape
    for (first, size), rows in zip(lane_tiles(width), held):

        def widen(chunk, carry):
            at = pl.multiple_of(chunk * MAXLEN, MAXLEN)
            rows[pl.ds(at, MAXLEN), 0:size] = rows_ref[
                pl.ds(at, MAXLEN), first : first + size
            ].astype(jnp.float32)
            return carry

        lax.fori_loop(0, count // MAXLEN, widen, 0)
        rows[pl.ds(count, MAXLEN), :] = jnp.zeros((MAXLEN, LANES), jnp.float32)

    def slot_body(slot, carry):
        if pairable(width):
            pair = [
                [rows[pl.ds(start_ref[2 * slot + side], MAXLEN), :] for rows in held]
                for side in range(2)
            ]
            tiles = join_pair(*pair)
        else:
            tiles = [rows[pl.ds(start_ref[slot], MAXLEN), :] for rows in held]
        for index, tile in enumerate(tiles):
            out_ref[slot, :, index * LANES : (index + 1) * LANES] = tile.astype(jnp.bfloat16)
        return carry

    lax.fori_loop(0, out_ref.shape[0], slot_body, 0)


def into_slots(start, rows):
    count, width = rows.shape
    slots = start.shape[0]
    tiles = len(lane_tiles(width))
    shape = (slots, MAXLEN, tiles * LANES)
    if pairable(width):
        shape = (slots // 2, MAXLEN, 2 * width)
    return pl.pallas_call(
        slots_kernel,
        out_shape=jax.ShapeDtypeStruct(shape, jnp.bfloat16),
        in_specs=[smem_spec(), whole_spec()],
        out_specs=whole_spec(),
        scratch_shapes=[pltpu.VMEM((count + MAXLEN, LANES), jnp.float32)] * tiles,
        compiler_params=params(),
    )(start, rows)


def place_kernel(paired, parts, after_ref, x_ref, context_ref, out_ref, context_rows, *x_rows):
    slots = context_ref.shape[0]
    slabs = out_ref.shape[0]
    tall = out_ref.shape[1] * (2 if paired else 1)
    slab_rows = tall - 2 * HALO
    total_rows = context_rows.shape[0]
    held = (context_rows,) + x_rows
    zeros = jnp.zeros((MAXLEN, LANES), jnp.float32)
    for rows in held:
        rows[pl.ds(0, HALO), :] = jnp.zeros((HALO, LANES), jnp.float32)

    def load(ref, slot, tile):
        return ref[slot, :, tile * LANES : (tile + 1) * LANES].astype(jnp.float32)

    def put(step, carry):
        if paired:
            sides = split_pair([load(x_ref, step, tile) for tile in range(3)])
            for side in range(2):
                slot = 2 * step + side
                where = pl.ds(HALO + after_ref[slot], MAXLEN)
                for rows, piece in zip(x_rows, sides[side]):
                    rows[where, :] = piece
                context_rows[where, :] = load(context_ref, slot, 0)
        else:
            where = pl.ds(HALO + after_ref[step], MAXLEN)
            for tile, rows in enumerate(x_rows):
                rows[where, :] = load(x_ref, step, tile)
            context_rows[where, :] = load(context_ref, step, 0)
        return carry

    lax.fori_loop(0, x_ref.shape[0], put, 0)
    live = after_ref[slots]

    def clear(step, carry):
        at = jnp.minimum(HALO + live + step * MAXLEN, total_rows - MAXLEN)
        for rows in held:
            rows[pl.ds(at, MAXLEN), :] = zeros
        return carry

    lax.fori_loop(0, (total_rows - HALO - live + MAXLEN - 1) // MAXLEN, clear, 0)

    def emit(slab, carry):
        at = pl.multiple_of(slab * slab_rows, slab_rows)
        if paired:
            for first, half, _ in parts or ((0, tall // 2, 0),):
                one = pl.ds(pl.multiple_of(at + first, 16), half)
                two = pl.ds(pl.multiple_of(at + first + half, 16), half)
                tiles = join_pair(
                    [rows[one, :] for rows in x_rows], [rows[two, :] for rows in x_rows]
                )
                tiles = tiles + (context_rows[one, :], context_rows[two, :])
                for index, tile in enumerate(tiles):
                    lanes = slice(index * LANES, (index + 1) * LANES)
                    out_ref[slab, first // 2 : first // 2 + half, lanes] = tile.astype(
                        jnp.bfloat16
                    )
            return carry
        tiles = [rows[pl.ds(at, tall), :] for rows in x_rows + (context_rows,)]
        for index, tile in enumerate(tiles):
            out_ref[slab, :, index * LANES : (index + 1) * LANES] = tile.astype(jnp.bfloat16)
        return carry

    lax.fori_loop(0, slabs, emit, 0)


def place(after, x_slots, context_slots, slabs, slab_rows, features, parts=None):
    count = context_slots.shape[0]
    paired = pairable(features)
    tiles = len(lane_tiles(features))
    tall = slab_rows + 2 * HALO
    shape = (slabs, tall, (tiles + 1) * LANES)
    if paired:
        shape = (slabs, tall // 2, 2 * features + 2 * LANES)
    return pl.pallas_call(
        functools.partial(place_kernel, paired, parts),
        out_shape=jax.ShapeDtypeStruct(shape, jnp.bfloat16),
        in_specs=[smem_spec(), whole_spec(), whole_spec()],
        out_specs=whole_spec(),
        scratch_shapes=[pltpu.VMEM((count * MAXLEN + HALO + MAXLEN, LANES), jnp.float32)]
        * (tiles + 1),
        compiler_params=params(),
    )(after, x_slots, context_slots)


def unplace_kernel(moved_ref, x_ref, context_ref):
    slabs, rows, _ = moved_ref.shape
    step = 16
    span = 3 * LANES

    def chunk(index, carry):
        at = pl.multiple_of(index * step, step)

        def load(slab, tile):
            cells = moved_ref[slab, pl.ds(at, step), tile * LANES : (tile + 1) * LANES]
            return cells.astype(jnp.float32)

        for pair in range(slabs // 2):
            split = [
                split_pair([load(2 * pair + member, tile) for tile in range(3)])
                for member in range(2)
            ]
            for side in range(2):
                to = pl.ds(pl.multiple_of(at + side * rows, step), step)
                for tile, cells in enumerate(join_pair(split[0][side], split[1][side])):
                    first = pair * span + tile * LANES
                    x_ref[to, first : first + LANES] = cells.astype(jnp.bfloat16)
        for slab in range(slabs):
            for side in range(2):
                to = pl.ds(pl.multiple_of(at + side * rows, step), step)
                first = span + side * LANES
                context_ref[to, slab * LANES : (slab + 1) * LANES] = moved_ref[
                    slab, pl.ds(at, step), first : first + LANES
                ]
        return carry

    lax.fori_loop(0, rows // step, chunk, 0)


def unplace(moved, features, context_width):
    slabs, rows, _ = moved.shape
    if not (pairable(features) and context_width == LANES):
        first = len(lane_tiles(features)) * LANES
        x = moved[:, :, :features].transpose(1, 0, 2).reshape(rows, -1)
        context = moved[:, :, first : first + context_width]
        return x, context.transpose(1, 0, 2).reshape(rows, -1)
    return pl.pallas_call(
        unplace_kernel,
        out_shape=(
            jax.ShapeDtypeStruct((2 * rows, slabs * features), jnp.bfloat16),
            jax.ShapeDtypeStruct((2 * rows, slabs * context_width), jnp.bfloat16),
        ),
        in_specs=[whole_spec()],
        out_specs=(whole_spec(), whole_spec()),
        compiler_params=params(),
    )(moved)


def conv_kernel(
    uniform_ref, gated_ref, segment_ref, taps_ref, scale_ref, shift_ref, out_ref, wide
):
    wide[...] = gated_ref[...].astype(jnp.float32)
    edge = HALO - HALF
    scale = scale_ref[...]
    shift = shift_ref[...]
    for chunk in range(out_ref.shape[0] // CONV_ROWS):
        base = chunk * CONV_ROWS

        def finish(total):
            affine = total * scale + shift
            out_ref[base : base + CONV_ROWS, :] = (affine * jax.nn.sigmoid(affine)).astype(
                jnp.bfloat16
            )

        @pl.when(uniform_ref[chunk] == 1)
        def _():
            total = jnp.zeros((CONV_ROWS, LANES), jnp.float32)
            for tap in range(KERNEL):
                total = total + wide[pl.ds(base + edge + tap, CONV_ROWS), :] * taps_ref[
                    tap : tap + 1, :
                ]
            finish(total)

        @pl.when(uniform_ref[chunk] == 0)
        def _():
            centre = segment_ref[pl.ds(base + HALO, CONV_ROWS), :]
            total = jnp.zeros((CONV_ROWS, LANES), jnp.float32)
            for tap in range(KERNEL):
                same = segment_ref[pl.ds(base + edge + tap, CONV_ROWS), :] == centre
                term = jnp.where(same, wide[pl.ds(base + edge + tap, CONV_ROWS), :], 0.0)
                total = total + term * taps_ref[tap : tap + 1, :]
            finish(total)


def convolve(gated_rows, segment, conv_taps, batch_scale, batch_shift):
    tall, width = gated_rows.shape
    rows = tall - 2 * HALO
    chunks = rows // CONV_ROWS
    windows = [segment[c * CONV_ROWS : c * CONV_ROWS + CONV_ROWS + 2 * HALO] for c in range(chunks)]
    windows = jnp.stack(windows)
    uniform = jnp.all(windows == windows[:, :1], axis=1).astype(jnp.int32)
    wide_segment = jnp.broadcast_to(segment[:, None], (tall, LANES))
    return pl.pallas_call(
        conv_kernel,
        grid=(width // LANES,),
        out_shape=jax.ShapeDtypeStruct((rows, width), jnp.bfloat16),
        in_specs=[
            smem_spec(),
            pl.BlockSpec((tall, LANES), lambda i: (0, i)),
            pl.BlockSpec((tall, LANES), lambda i: (0, 0)),
            pl.BlockSpec((KERNEL, LANES), lambda i: (0, i)),
            pl.BlockSpec((1, LANES), lambda i: (0, i)),
            pl.BlockSpec((1, LANES), lambda i: (0, i)),
        ],
        out_specs=pl.BlockSpec((rows, LANES), lambda i: (0, i)),
        scratch_shapes=[pltpu.VMEM((tall, LANES), jnp.float32)],
        compiler_params=params(),
        cost_estimate=pl.CostEstimate(
            flops=2 * rows * width * KERNEL, bytes_accessed=4 * rows * width, transcendentals=0
        ),
    )(
        uniform,
        gated_rows,
        wide_segment,
        conv_taps,
        batch_scale[None, :],
        batch_shift[None, :],
    )


MESH = pl.DeviceIdType.MESH
OUT, GLU_ONE, GLU_TWO, DOWN = range(4)


def any_spec():
    return pl.BlockSpec(memory_space=pl.ANY)


class Place:
    def __init__(self):
        self.dp = lax.axis_index("dp")
        self.mp = lax.axis_index("mp")
        self.y, self.c = self.dp // 2, self.dp % 2
        self.z, self.x = self.mp // 2, self.mp % 2
        self.across = 1 - self.x
        self.near = self.z + 1 - 2 * (self.z % 2)
        self.far_one = 2 - self.z // 2
        self.far_two = 3 - 3 * (self.z // 2)

    def x_side(self):
        return (self.dp, 2 * self.z + self.across)

    def y_side(self):
        return (2 * (1 - self.y) + self.c, self.mp)

    def core_side(self):
        return (2 * self.y + 1 - self.c, self.mp)

    def corner(self):
        return (2 * (1 - self.y) + 1 - self.c, self.mp)

    def above(self):
        return (self.dp, self.mp + 2)

    def below(self):
        return (self.dp, self.mp - 2)


def aligned(index, step):
    return pl.multiple_of(index * step, step)


def piece(weights, kind, z, x, y, c, both_y=False):
    shard = 2 * z + x
    if kind == OUT:
        return weights[0].at[pl.ds(aligned(shard, 192), 192), pl.ds(aligned(c, 512), 512)]
    if kind == GLU_ONE:
        return weights[1].at[pl.ds(aligned(c, 256), 256), pl.ds(aligned(shard, 384), 384)]
    if kind == GLU_TWO:
        if both_y:
            rows = pl.ds(pl.multiple_of(512 + c * 512, 256), 512)
        else:
            rows = pl.ds(pl.multiple_of(512 + (c * 2 + y) * 256, 256), 256)
        return weights[1].at[rows, pl.ds(aligned(shard, 384), 384)]
    if both_y:
        columns = pl.ds(aligned(c, 768), 768)
    else:
        columns = pl.ds(aligned(c * 2 + y, 384), 384)
    return weights[2].at[pl.ds(aligned(shard, 192), 192), columns]


def own_piece(shards, kind, y, c):
    if kind == OUT:
        return shards[0].at[:, pl.ds(aligned(c, 512), 512)]
    if kind == GLU_ONE:
        return shards[1].at[pl.ds(aligned(c, 256), 256), :]
    if kind == GLU_TWO:
        return shards[1].at[pl.ds(pl.multiple_of(512 + (c * 2 + y) * 256, 256), 256), :]
    return shards[2].at[:, pl.ds(aligned(c * 2 + y, 384), 384)]


class Mail:
    def __init__(self, send_sems, recv_sems):
        self.send_sems, self.recv_sems = send_sems, recv_sems
        self.used = 0
        self.sent = []

    def slot(self):
        self.used += 1
        return self.used - 1

    def copy(self, slot, source, target, device):
        return pltpu.make_async_remote_copy(
            src_ref=source,
            dst_ref=target,
            send_sem=self.send_sems.at[slot],
            recv_sem=self.recv_sems.at[slot],
            device_id=device,
            device_id_type=MESH,
        )

    def send(self, slot, source, target, device, when=None):
        copy = self.copy(slot, source, target, device)
        run_if(when, copy.start)
        self.sent.append((copy, when))

    def receive(self, slot, target, device, when=None):
        run_if(when, self.copy(slot, target, target, device).wait_recv)

    def finish(self):
        for copy, when in self.sent:
            run_if(when, copy.wait_send)


def run_if(when, action):
    if when is None:
        action()
    else:
        pl.when(when)(action)


def greet(devices):
    barrier = pltpu.get_barrier_semaphore()

    def hello(device):
        pl.semaphore_signal(barrier, inc=1, device_id=device, device_id_type=MESH)

    count = 0
    for device, when in devices:
        if when is None:
            hello(device)
            count = count + 1
        else:
            pl.when(when)(functools.partial(hello, device))
            count = count + when.astype(jnp.int32)
    pl.semaphore_wait(barrier, count)


KINDS = (GLU_ONE, OUT, GLU_TWO, DOWN)


def move_kernel(
    start_ref,
    span_ref,
    q_ref,
    k_ref,
    v_ref,
    residual_ref,
    out_shard,
    glu_shard,
    down_shard,
    x_got,
    context_got,
    out_all,
    glu_all,
    down_all,
    q_rows,
    k_rows,
    v_rows,
    x_low,
    x_high,
    x_send,
    context_send,
    out_held,
    glu_held,
    down_held,
    send_sems,
    recv_sems,
    local_sems,
):
    here = Place()
    z, x, y, c = here.z, here.x, here.y, here.c
    weights = (out_all, glu_all, down_all)
    shards = (out_shard, glu_shard, down_shard)
    held = (out_held, glu_held, down_held)
    mail = Mail(send_sems, recv_sems)
    up, down = z < 3, z > 0
    partners = (here.y_side(), here.corner(), here.core_side())
    greet(
        [(device, None) for device in partners + (here.x_side(),)]
        + [(here.above(), up), (here.below(), down)]
    )

    def spot(kind, zz, xx):
        return piece(weights, kind, zz, xx, y, c)

    own = (
        out_all.at[pl.ds(aligned(here.mp, 192), 192), :],
        glu_all.at[:, pl.ds(aligned(here.mp, 384), 384)],
        down_all.at[pl.ds(aligned(here.mp, 192), 192), :],
    )
    into = [
        pltpu.make_async_copy(shards[i], held[i], local_sems.at[i]) for i in range(3)
    ]
    locals_ = [pltpu.make_async_copy(held[i], own[i], local_sems.at[5 + i]) for i in range(3)]
    slots_up, slots_down, slots_x, slots_near = [
        {kind: mail.slot() for kind in KINDS} for _ in range(4)
    ]
    slots_up_two, slots_down_two = [{kind: mail.slot() for kind in KINDS} for _ in range(2)]
    for kind in KINDS:
        mine = own_piece(shards, kind, y, c)
        mail.send(slots_up[kind], mine, spot(kind, z, x), here.above(), up)
        mail.send(slots_down[kind], mine, spot(kind, z, x), here.below(), down)
        mail.send(slots_x[kind], mine, spot(kind, z, x), here.x_side())
    for copy in into:
        copy.start()

    count = 4 * residual_ref.shape[0]
    step = 128
    low = lax.broadcasted_iota(jnp.int32, (step, LANES), 1) < HD

    def open_rows(chunk, carry):
        first = pl.multiple_of(chunk * step, step)
        cells = [
            residual_ref[pl.ds(first, step), i * LANES : (i + 1) * LANES].astype(jnp.float32)
            for i in range(6)
        ]
        turned = [pltpu.roll(cells[i], HD, 1) for i in (1, 2, 4, 5)]
        frames = (
            (cells[0], cells[1]),
            (jnp.where(low, turned[0], turned[1]), turned[1]),
            (cells[3], cells[4]),
            (jnp.where(low, turned[2], turned[3]), turned[3]),
        )
        for j, (one, two) in enumerate(frames):
            at = pl.ds(4 * first + j, step, stride=4)
            x_low[at, :] = one
            x_high[at, :] = two
        return carry

    lax.fori_loop(0, residual_ref.shape[0] // step, open_rows, 0)
    for rows in (x_low, x_high):
        rows[pl.ds(count, MAXLEN), :] = jnp.zeros((MAXLEN, LANES), jnp.float32)

    targets = partners + ((here.dp, here.mp),)
    half = PIECES // 2
    x_slots = [mail.slot() for _ in partners]
    context_slots = [mail.slot() for _ in partners]
    for index, target in enumerate(targets):
        group = target[0]

        def fill(pair, carry):
            at = group * half + pair
            both = [
                [
                    rows[pl.ds(start_ref[2 * at + side], MAXLEN), :]
                    for rows in (x_low, x_high)
                ]
                for side in range(2)
            ]
            for tile, cells in enumerate(join_pair(*both)):
                x_send[at, :, tile * LANES : (tile + 1) * LANES] = cells.astype(jnp.bfloat16)
            return carry

        lax.fori_loop(0, half, fill, 0)
        source = x_send.at[pl.ds(group * half, half)]
        landing = x_got.at[pl.ds(here.dp * half, half)]
        if index < 3:
            mail.send(x_slots[index], source, landing, target)
        else:
            copy = pltpu.make_async_copy(source, landing, local_sems.at[3])
            copy.start()
            locals_.append(copy)

    for copy_in, copy_out in zip(into, locals_):
        copy_in.wait()
        copy_out.start()

    pairs = q_ref.shape[0]
    wide_low = lax.broadcasted_iota(jnp.int32, (256, LANES), 1) < HD

    def unpack(chunk, carry):
        first = pl.multiple_of(chunk * 256, 256)
        for packed, rows in ((q_ref, q_rows), (k_ref, k_rows), (v_ref, v_rows)):
            one = packed[pl.ds(first, 256), 0:LANES].astype(jnp.float32)
            two = packed[pl.ds(first, 256), LANES : 2 * LANES].astype(jnp.float32)
            rows[pl.ds(2 * first, 256, stride=2), :] = jnp.where(
                wide_low, one, pltpu.roll(two, HD, 1)
            )
            rows[pl.ds(2 * first + 1, 256, stride=2), :] = jnp.where(
                wide_low, pltpu.roll(one, HD, 1), two
            )
        return carry

    lax.fori_loop(0, pairs // 256, unpack, 0)
    for rows in (q_rows, k_rows, v_rows):
        rows[pl.ds(2 * pairs, MAXLEN), :] = jnp.zeros((MAXLEN, LANES), jnp.float32)

    column = lax.broadcasted_iota(jnp.int32, (MAXLEN, MAXLEN), 1)
    head_lane = lax.broadcasted_iota(jnp.int32, (MAXLEN, LANES), 1) // HD

    def attend_slot(slot):
        start = start_ref[slot]
        allowed = column < span_ref[slot]
        queries = q_rows[pl.ds(start, MAXLEN), :]
        keys = k_rows[pl.ds(start, MAXLEN), :].astype(jnp.bfloat16)
        values = v_rows[pl.ds(start, MAXLEN), :].astype(jnp.bfloat16)
        result = None
        for head in range(2):
            own = jnp.where(head_lane == head, queries, 0.0).astype(jnp.bfloat16)
            scores = (
                lax.dot_general(
                    own, keys, (((1,), (1,)), ((), ())), preferred_element_type=jnp.float32
                )
                * HD ** (-0.5)
            )
            scores = jnp.where(allowed, scores, MASKED)
            highest = jnp.max(scores, axis=1, keepdims=True)
            exponentials = jnp.exp(scores - highest)
            denominator = jnp.sum(exponentials, axis=1, keepdims=True)
            weighing = (exponentials / denominator).astype(jnp.bfloat16)
            blended = jnp.dot(weighing, values, preferred_element_type=jnp.float32)
            result = blended if head == 0 else jnp.where(head_lane == head, blended, result)
        context_send[slot] = result.astype(jnp.bfloat16)

    def relay(kind):
        mail.receive(slots_up[kind], spot(kind, z - 1, x), here.above(), down)
        mail.send(
            slots_up_two[kind],
            spot(kind, z - 1, x),
            spot(kind, z - 1, x),
            here.above(),
            up & down,
        )
        mail.receive(slots_down[kind], spot(kind, z + 1, x), here.below(), up)
        mail.send(
            slots_down_two[kind],
            spot(kind, z + 1, x),
            spot(kind, z + 1, x),
            here.below(),
            up & down,
        )
        mail.send(
            slots_near[kind],
            spot(kind, here.near, x),
            spot(kind, here.near, x),
            here.x_side(),
        )

    for index, target in enumerate(targets):
        group = target[0]

        def attend_one(rank, carry):
            attend_slot(group * PIECES + rank)
            return carry

        lax.fori_loop(0, PIECES, attend_one, 0)
        source = context_send.at[pl.ds(group * PIECES, PIECES)]
        landing = context_got.at[pl.ds(here.dp * PIECES, PIECES)]
        if index < 3:
            mail.send(context_slots[index], source, landing, target)
        else:
            copy = pltpu.make_async_copy(source, landing, local_sems.at[4])
            copy.start()
            locals_.append(copy)
        relay(KINDS[index])

    for index, source in enumerate(partners):
        mail.receive(x_slots[index], x_got.at[pl.ds(source[0] * half, half)], source)
        mail.receive(
            context_slots[index], context_got.at[pl.ds(source[0] * PIECES, PIECES)], source
        )
    for kind in KINDS:
        mail.receive(slots_x[kind], spot(kind, z, here.across), here.x_side())
        mail.receive(slots_near[kind], spot(kind, here.near, here.across), here.x_side())
        mail.receive(slots_up_two[kind], spot(kind, z - 2, x), here.above(), z > 1)
        mail.receive(slots_down_two[kind], spot(kind, z + 2, x), here.below(), z < 2)
    mail.finish()
    for copy in locals_:
        copy.wait()


def move(start, span, queries, keys, values, residual, out_shard, glu_shard, down_shard):
    slots = start.shape[0]
    pairs = queries.shape[0]
    count = 4 * residual.shape[0]
    bf16 = jnp.bfloat16
    return pl.pallas_call(
        move_kernel,
        out_shape=(
            jax.ShapeDtypeStruct((slots // 2, MAXLEN, 3 * LANES), bf16),
            jax.ShapeDtypeStruct((slots, MAXLEN, LANES), bf16),
            jax.ShapeDtypeStruct((1536, 1024), bf16),
            jax.ShapeDtypeStruct((1536, 3072), bf16),
            jax.ShapeDtypeStruct((1536, 1536), bf16),
        ),
        in_specs=[smem_spec()] * 2 + [whole_spec()] * 4 + [any_spec()] * 3,
        out_specs=(any_spec(),) * 5,
        scratch_shapes=[pltpu.VMEM((2 * pairs + MAXLEN, LANES), jnp.float32)] * 3
        + [pltpu.VMEM((count + MAXLEN, LANES), jnp.float32)] * 2
        + [
            pltpu.VMEM((slots // 2, MAXLEN, 3 * LANES), bf16),
            pltpu.VMEM((slots, MAXLEN, LANES), bf16),
            pltpu.VMEM(out_shard.shape, bf16),
            pltpu.VMEM(glu_shard.shape, bf16),
            pltpu.VMEM(down_shard.shape, bf16),
            pltpu.SemaphoreType.DMA((30,)),
            pltpu.SemaphoreType.DMA((30,)),
            pltpu.SemaphoreType.DMA((8,)),
        ],
        compiler_params=pltpu.CompilerParams(
            vmem_limit_bytes=VMEM_LIMIT, collective_id=1, has_side_effects=True
        ),
        cost_estimate=pl.CostEstimate(
            flops=slots * 2 * MAXLEN * MAXLEN * LANES * 4,
            bytes_accessed=50 * 1024 * 1024,
            transcendentals=slots * 2 * MAXLEN * MAXLEN,
        ),
    )(start, span, queries, keys, values, residual, out_shard, glu_shard, down_shard)


PARTS = ((0, 144, 0), (288, 128, 256))
ROW_STEP = 32


def finish_kernel(
    after_ref,
    slabs_ref,
    norm_ref,
    taps_ref,
    out_in,
    glu_in,
    down_in,
    encoded_ref,
    out_all,
    glu_all,
    down_all,
    moved,
    carried,
    context,
    normed,
    wide,
    swished,
    first_tap,
    last_tap,
    out_held,
    glu_held,
    down_held,
    send_sems,
    recv_sems,
    local_sems,
):
    here = Place()
    z, x, y, c = here.z, here.x, here.y, here.c
    weights = (out_all, glu_all, down_all)
    mail = Mail(send_sems, recv_sems)
    slabs = slabs_ref.shape[0]
    others = [(here.dp, lax.rem(here.mp + step, slabs)) for step in range(1, slabs)]
    greet([(device, None) for device in others + [here.y_side(), here.core_side()]])

    slab_slots = [[mail.slot() for _ in others] for _ in PARTS]

    def part_rows(part):
        first, half, _ = PARTS[part]
        return pl.ds(first // 2, half)

    def exchange(part):
        for index, device in enumerate(others):
            mail.send(
                slab_slots[part][index],
                slabs_ref.at[device[1], part_rows(part)],
                moved.at[here.mp, part_rows(part)],
                device,
            )

    def exchanged(part):
        for index in range(len(others)):
            source = lax.rem(here.mp - index - 1 + slabs, slabs)
            mail.receive(
                slab_slots[part][index], moved.at[source, part_rows(part)], (here.dp, source)
            )

    exchange(0)
    keep = pltpu.make_async_copy(slabs_ref.at[here.mp], moved.at[here.mp], local_sems.at[0])
    keep.start()

    def spot(kind, zz, xx):
        return piece(weights, kind, zz, xx, y, c)

    table = {}

    def slot(*key):
        if key not in table:
            table[key] = mail.slot()
        return table[key]

    def pass_on(name, kind, zz, xx, device, when=None):
        where = spot(kind, zz, xx)
        mail.send(slot(name, kind), where, where, device, when)

    cells = {
        "own near": (here.near, x),
        "own one": (here.far_one, x),
        "own two": (here.far_two, x),
        "other own": (z, here.across),
        "other near": (here.near, here.across),
        "other one": (here.far_one, here.across),
        "other two": (here.far_two, here.across),
    }
    early = ("own near", "own one", "other own", "other near")
    order = early + ("other one", "own two", "other two")

    def after(kind, cell):
        if kind in (OUT, GLU_ONE):
            pass_on("core " + cell, kind, *cells[cell], here.core_side())
        else:
            pass_on("y " + cell, kind, *cells[cell], here.y_side())

    def from_y(kind):
        for cell in order:
            mail.receive(
                slot("y " + cell, kind),
                piece(weights, kind, *cells[cell], 1 - y, c),
                here.y_side(),
            )
            where = piece(weights, kind, *cells[cell], y, c, both_y=True)
            mail.send(slot("core " + cell, kind), where, where, here.core_side())

    def from_core(kind):
        for cell in order:
            where = piece(weights, kind, *cells[cell], y, 1 - c, both_y=kind in (GLU_TWO, DOWN))
            mail.receive(slot("core " + cell, kind), where, here.core_side())

    for kind in KINDS:
        pass_on("third up", kind, 0, x, here.above(), z == 2)
        pass_on("third down", kind, 3, x, here.below(), z == 1)
        pass_on("x one", kind, here.far_one, x, here.x_side())
    for kind in (GLU_TWO, OUT, GLU_ONE, DOWN):
        for cell in early:
            after(kind, cell)

    live = after_ref[4 * PIECES]

    def bounds(step, carry):
        rows = pl.ds(pl.multiple_of(step * 64, 64), 64)
        position = (
            lax.broadcasted_iota(jnp.int32, (64, LANES), 0)
            + step * 64
            + here.mp * encoded_ref.shape[0]
        )
        begin = jnp.zeros((64, LANES), jnp.int32)
        end = jnp.full((64, LANES), live, jnp.int32)
        for k in range(1, 4 * PIECES):
            begin = jnp.where(position >= after_ref[k], after_ref[k], begin)
        for k in range(4 * PIECES - 1, 0, -1):
            end = jnp.where(position < after_ref[k], after_ref[k], end)
        first_tap[rows, :] = HALF + begin - position
        last_tap[rows, :] = HALF - 1 + end - position
        return carry

    lax.fori_loop(0, encoded_ref.shape[0] // 64, bounds, 0)

    for kind in KINDS:
        mail.receive(slot("x one", kind), spot(kind, *cells["other one"]), here.x_side())
        after(kind, "other one")
    exchange(1)
    for kind in KINDS:
        mail.receive(slot("third up", kind), spot(kind, 0, x), here.above(), z == 3)
        mail.receive(slot("third down", kind), spot(kind, 3, x), here.below(), z == 0)
        pass_on("x two", kind, here.far_two, x, here.x_side())
        after(kind, "own two")
    for kind in KINDS:
        mail.receive(slot("x two", kind), spot(kind, *cells["other two"]), here.x_side())
        after(kind, "other two")
    from_y(GLU_TWO)
    loads = [
        pltpu.make_async_copy(weights[i], (out_held, glu_held, down_held)[i], local_sems.at[1 + i])
        for i in range(3)
    ]
    from_core(OUT)
    loads[0].start()

    def open_part(part):
        first, half, _ = PARTS[part]

        def chunk(index, carry):
            at = pl.ds(pl.multiple_of(first // 2 + index * 16, 16), 16)

            def load(slab, tile):
                cells_ = moved[slab, at, tile * LANES : (tile + 1) * LANES]
                return cells_.astype(jnp.float32)

            to = [pl.ds(pl.multiple_of(first + s * half + index * 16, 16), 16) for s in range(2)]
            near = [pl.ds(pl.multiple_of(s * half + index * 16, 16), 16) for s in range(2)]
            for pair in range(slabs // 2):
                split = [
                    split_pair([load(2 * pair + member, tile) for tile in range(3)])
                    for member in range(2)
                ]
                for side in range(2):
                    for tile, cells_ in enumerate(join_pair(split[0][side], split[1][side])):
                        begin = (3 * pair + tile) * LANES
                        carried[to[side], begin : begin + LANES] = cells_
            for slab in range(slabs):
                for side in range(2):
                    begin = (3 + side) * LANES
                    context[near[side], slab * LANES : (slab + 1) * LANES] = moved[
                        slab, at, begin : begin + LANES
                    ]
            return carry

        lax.fori_loop(0, half // 16, chunk, 0)

    tile_width = 256
    tiles = carried.shape[1] // tile_width

    def attach(part):
        first, half, _ = PARTS[part]

        def tile(n, carry):
            columns = pl.ds(aligned(n, tile_width), tile_width)
            carried[first : first + 2 * half, columns] += lax.dot_general(
                context[0 : 2 * half, :],
                out_held[columns, :],
                (((1,), (1,)), ((), ())),
                preferred_element_type=jnp.float32,
            )
            return carry

        lax.fori_loop(0, tiles, tile, 0)

        def normalise(index, carry):
            at = pl.ds(pl.multiple_of(first + index * 16, 16), 16)
            to = pl.ds(pl.multiple_of(index * 16, 16), 16)
            cells_ = carried[at, :]
            centred = cells_ - jnp.mean(cells_, axis=1, keepdims=True)
            variance = jnp.mean(centred * centred, axis=1, keepdims=True)
            scaled = centred * lax.rsqrt(variance + EPS) * norm_ref[0:1, :] + norm_ref[1:2, :]
            normed[to, :] = scaled.astype(jnp.bfloat16)
            return carry

        lax.fori_loop(0, 2 * half // 16, normalise, 0)

    def gate(part):
        first, half, _ = PARTS[part]

        def tile(n, carry):
            columns = pl.ds(aligned(n, tile_width), tile_width)
            rows = normed[0 : 2 * half, :]
            value = jnp.dot(rows, glu_held[:, columns], preferred_element_type=jnp.float32)
            gates = jnp.dot(
                rows,
                glu_held[:, pl.ds(aligned(n + tiles, tile_width), tile_width)],
                preferred_element_type=jnp.float32,
            )
            gated = (value * jax.nn.sigmoid(gates)).astype(jnp.bfloat16)
            for side in range(2):
                wide[2 * n + side, first : first + 2 * half, :] = gated[
                    :, side * LANES : (side + 1) * LANES
                ].astype(jnp.float32)
            return carry

        lax.fori_loop(0, tiles, tile, 0)

    def convolve_part(part):
        start = PARTS[part][2]
        group = 2
        groups = carried.shape[1] // (group * LANES)

        def body(index, carry):
            row = start + lax.rem(index, 256 // ROW_STEP) * ROW_STEP
            column = index // (256 // ROW_STEP) * (group * LANES)
            rows = pl.ds(pl.multiple_of(row, ROW_STEP), ROW_STEP)
            low, high = first_tap[rows, :], last_tap[rows, :]
            lanes = [pl.ds(pl.multiple_of(column + i * LANES, LANES), LANES) for i in range(group)]
            totals = [jnp.zeros((ROW_STEP, LANES), jnp.float32) for _ in range(group)]
            for shift in range(8):
                count = ROW_STEP + (24 if shift < 7 else 16)
                at = pl.ds(row + HALO - HALF + shift, count)
                seen = [wide[column // LANES + i, at, :] for i in range(group)]
                for k in range(4 if shift < 7 else 3):
                    tap = shift + 8 * k
                    if tap < HALF:
                        mask = low <= tap
                    else:
                        mask = high >= tap
                    for i in range(group):
                        term = seen[i][8 * k : 8 * k + ROW_STEP] * taps_ref[tap : tap + 1, lanes[i]]
                        if tap != HALF:
                            term = jnp.where(mask, term, 0.0)
                        totals[i] = totals[i] + term
            for i in range(group):
                affine = totals[i] * norm_ref[2:3, lanes[i]] + norm_ref[3:4, lanes[i]]
                swished[rows, lanes[i]] = (affine * jax.nn.sigmoid(affine)).astype(jnp.bfloat16)
            return carry

        lax.fori_loop(0, 256 // ROW_STEP * groups, body, 0)

    def lower(part):
        start = PARTS[part][2]
        rows = pl.ds(start, 256)

        def tile(n, carry):
            columns = pl.ds(aligned(n, tile_width), tile_width)
            total = carried[start + HALO : start + HALO + 256, columns] + lax.dot_general(
                swished[rows, :],
                down_held[columns, :],
                (((1,), (1,)), ((), ())),
                preferred_element_type=jnp.float32,
            )
            alive = last_tap[rows, :] >= HALF
            for side in range(2):
                lane = pl.ds(pl.multiple_of(n * tile_width + side * LANES, LANES), LANES)
                encoded_ref[rows, lane] = jnp.where(
                    alive, total[:, side * LANES : (side + 1) * LANES], 0.0
                ).astype(jnp.bfloat16)
            return carry

        lax.fori_loop(0, tiles, tile, 0)

    keep.wait()
    exchanged(0)
    open_part(0)
    loads[0].wait()
    attach(0)
    from_core(GLU_ONE)
    from_core(GLU_TWO)
    loads[1].start()
    from_y(DOWN)
    loads[1].wait()
    gate(0)
    convolve_part(0)
    from_core(DOWN)
    loads[2].start()
    exchanged(1)
    open_part(1)
    attach(1)
    loads[2].wait()
    lower(0)
    gate(1)
    convolve_part(1)
    lower(1)
    mail.finish()


def finish(after, slabs, norm, taps, out_all, glu_all, down_all):
    bf16, f32 = jnp.bfloat16, jnp.float32
    width = taps.shape[1]
    rows = 512
    tall = rows + 2 * HALO
    weights = (out_all, glu_all, down_all)
    return pl.pallas_call(
        finish_kernel,
        out_shape=(jax.ShapeDtypeStruct((rows, width), bf16),)
        + tuple(jax.ShapeDtypeStruct(a.shape, a.dtype) for a in weights),
        in_specs=[smem_spec(), any_spec(), whole_spec(), whole_spec()] + [any_spec()] * 3,
        out_specs=(whole_spec(),) + (any_spec(),) * 3,
        input_output_aliases={4: 1, 5: 2, 6: 3},
        scratch_shapes=[
            pltpu.VMEM(slabs.shape, bf16),
            pltpu.VMEM((tall, width), f32),
            pltpu.VMEM((288, 1024), bf16),
            pltpu.VMEM((288, width), bf16),
            pltpu.VMEM((width // LANES, tall, LANES), f32),
            pltpu.VMEM((rows, width), bf16),
            pltpu.VMEM((rows, LANES), jnp.int32),
            pltpu.VMEM((rows, LANES), jnp.int32),
        ]
        + [pltpu.VMEM(a.shape, bf16) for a in weights]
        + [
            pltpu.SemaphoreType.DMA((80,)),
            pltpu.SemaphoreType.DMA((80,)),
            pltpu.SemaphoreType.DMA((4,)),
        ],
        compiler_params=pltpu.CompilerParams(
            vmem_limit_bytes=VMEM_LIMIT, collective_id=2, has_side_effects=True
        ),
    )(after, slabs, norm, taps, *weights)[0]


def on_device(
    query_rows,
    key_rows,
    value_rows,
    residual,
    lengths,
    assignment,
    out_proj,
    norm_gain,
    norm_bias,
    glu_proj,
    conv_taps,
    batch_scale,
    batch_shift,
    down_proj,
):
    data_group = lax.axis_index("dp")
    slab_index = lax.axis_index("mp")
    groups = lax.axis_size("dp")
    slabs = lax.axis_size("mp")
    group_rows = query_rows.shape[0] * 2
    slab_rows = group_rows // slabs
    total_utterances = lengths.shape[0]
    per_group = total_utterances // groups
    slots = groups * PIECES
    features = residual.shape[2] // 4

    utterance = jnp.arange(total_utterances, dtype=jnp.int32)
    source = utterance // per_group
    earlier = utterance[None, :] < utterance[:, None]
    same_source = source[None, :] == source[:, None]
    same_target = assignment[None, :] == assignment[:, None]
    before = jnp.sum(jnp.where(earlier & same_source, lengths[None, :], 0), axis=1)
    rank = jnp.sum((earlier & same_source & same_target).astype(jnp.int32), axis=1)
    slot = jnp.arange(slots, dtype=jnp.int32)[:, None]
    leaving = (source[None, :] == data_group) & ((assignment * PIECES + rank)[None, :] == slot)
    start = jnp.sum(jnp.where(leaving, before[None, :], 0), axis=1)
    span = jnp.sum(jnp.where(leaving, lengths[None, :], 0), axis=1)
    coming_earlier = (assignment[None, :] == data_group) & (
        (source * PIECES + rank)[None, :] < jnp.arange(slots + 1, dtype=jnp.int32)[:, None]
    )
    after = jnp.sum(jnp.where(coming_earlier, lengths[None, :], 0), axis=1)
    live = jnp.sum(jnp.where(assignment == data_group, lengths, 0))

    position = jnp.arange(slab_rows + 2 * HALO, dtype=jnp.int32) + slab_index * slab_rows - HALO
    segment = jnp.sum((position[:, None] >= after[None, 1:]).astype(jnp.int32), axis=1)
    segment = jnp.where(position < 0, -2, jnp.where(position < live, segment, -1))
    segment = jnp.where(position >= group_rows, -2, segment)

    fits = (
        (groups, slabs) == (4, 8)
        and query_rows.shape == (2048, 2, LANES)
        and residual.shape == (1024, 1, 768)
    )
    if fits:
        flat = [a.reshape(2048, 2 * LANES) for a in (query_rows, key_rows, value_rows)]
        x_slots, context_slots, *weights = move(
            start, span, *flat, residual.reshape(1024, 768), out_proj.T, glu_proj, down_proj.T
        )
        placed = place(after, x_slots, context_slots, slabs, slab_rows, features, PARTS)
        norm = jnp.stack([norm_gain, norm_bias, batch_scale, batch_shift])
        return finish(after, placed, norm, conv_taps, *weights)

    residual_rows = (
        residual.reshape(group_rows // 4, 4, features).reshape(group_rows, features)
    )

    def swap(array, axis):
        return lax.all_to_all(array, axis, split_axis=0, concat_axis=0, tiled=True)

    packed, start = lax.optimization_barrier((into_slots(start, residual_rows), start))
    x_slots = swap(packed, "dp")
    context_slots = swap(attend(start, span, query_rows, key_rows, value_rows), "dp")
    moved = swap(place(after, x_slots, context_slots, slabs, slab_rows, features), "mp")
    carried_slab, context_slab = unplace(moved, features, query_rows.shape[1] * HD)

    core = data_group % 2
    partners = [(group, group + 1 - 2 * (group % 2)) for group in range(groups)]

    def gather(weights):
        half = weights.shape[0] // 2
        own = lax.dynamic_slice_in_dim(weights, core * half, half, 0)
        return lax.all_gather(own, "mp", axis=1, tiled=True)

    def both(own):
        return own, lax.ppermute(own, "dp", partners)

    def project(rows, halves_of):
        own, other = halves_of
        half = rows.shape[1] // 2
        low, high = rows[:, :half], rows[:, half:]
        return jnp.dot(
            jnp.where(core == 0, low, high), own, preferred_element_type=jnp.float32
        ) + jnp.dot(jnp.where(core == 0, high, low), other, preferred_element_type=jnp.float32)

    out_halves, glu_halves = both(gather(out_proj)), both(gather(glu_proj))
    down_own = gather(down_proj)
    carried = carried_slab.astype(jnp.float32) + project(context_slab, out_halves)
    average = jnp.mean(carried, axis=1, keepdims=True)
    centred = carried - average
    variance = jnp.mean(centred * centred, axis=1, keepdims=True)
    normed = (centred * lax.rsqrt(variance + EPS) * norm_gain + norm_bias).astype(jnp.bfloat16)
    halves = project(normed, glu_halves)
    feature_count = halves.shape[1] // 2
    gated_rows = (halves[:, :feature_count] * jax.nn.sigmoid(halves[:, feature_count:])).astype(
        jnp.bfloat16
    )
    down_own, gated_rows = lax.optimization_barrier((down_own, gated_rows))
    down_halves = both(down_own)
    swished = convolve(gated_rows, segment, conv_taps, batch_scale, batch_shift)
    lowered = project(swished, down_halves)
    centre_segment = segment[HALO : HALO + slab_rows]
    own_carried = carried[HALO : HALO + slab_rows]
    return jnp.where((centre_segment >= 0)[:, None], own_carried + lowered, 0.0).astype(
        jnp.bfloat16
    )


def solution(mesh):
    in_specs = (
        P("dp", "mp", None),
        P("dp", "mp", None),
        P("dp", "mp", None),
        P("dp", "mp", None),
        P(),
        P(),
        P(None, "mp"),
        P(),
        P(),
        P(None, "mp"),
        P(),
        P(),
        P(),
        P(None, "mp"),
    )
    out_specs = P(("dp", "mp"), None)
    return jax.shard_map(
        on_device, mesh=mesh, in_specs=in_specs, out_specs=out_specs, check_vma=False
    )
```

```python
import functools

import jax
import jax.numpy as jnp
from jax import lax
from jax.experimental import pallas as pl
from jax.experimental.pallas import tpu as pltpu
from jax.sharding import PartitionSpec as P

HD = 64
KERNEL = 31
HALF = 15
MAXLEN = 256
PIECES = 4
LANES = 128
HALO = 16
CONV_ROWS = 64

EPS = 1e-05
MASKED = -1e30
VMEM_LIMIT = 60 * 1024 * 1024


def params():
    return pltpu.CompilerParams(vmem_limit_bytes=VMEM_LIMIT)


def whole_spec():
    return pl.BlockSpec(memory_space=pltpu.VMEM)


def smem_spec():
    return pl.BlockSpec(memory_space=pltpu.SMEM)


def attention_kernel(
    heads, start_ref, span_ref, q_ref, k_ref, v_ref, out_ref, q_rows, k_rows, v_rows
):
    pairs = q_ref.shape[0]
    step = 256
    lane = lax.broadcasted_iota(jnp.int32, (step, LANES), 1)
    low = lane < HD

    def unpack(chunk, carry):
        first = pl.multiple_of(chunk * step, step)
        for packed, rows in ((q_ref, q_rows), (k_ref, k_rows), (v_ref, v_rows)):
            one = packed[pl.ds(first, step), 0:LANES].astype(jnp.float32)
            if heads == 2:
                two = packed[pl.ds(first, step), LANES : 2 * LANES].astype(jnp.float32)
                even = jnp.where(low, one, pltpu.roll(two, HD, 1))
                odd = jnp.where(low, pltpu.roll(one, HD, 1), two)
            else:
                even = one
                odd = pltpu.roll(one, HD, 1)
            rows[pl.ds(2 * first, step, stride=2), :] = even
            rows[pl.ds(2 * first + 1, step, stride=2), :] = odd
        return carry

    lax.fori_loop(0, pairs // step, unpack, 0)
    for rows in (q_rows, k_rows, v_rows):
        rows[pl.ds(2 * pairs, MAXLEN), :] = jnp.zeros((MAXLEN, LANES), jnp.float32)

    column = lax.broadcasted_iota(jnp.int32, (MAXLEN, MAXLEN), 1)
    head_lane = lax.broadcasted_iota(jnp.int32, (MAXLEN, LANES), 1) // HD

    def slot_body(slot, carry):
        start = start_ref[slot]
        allowed = column < span_ref[slot]
        queries = q_rows[pl.ds(start, MAXLEN), :]
        keys = k_rows[pl.ds(start, MAXLEN), :].astype(jnp.bfloat16)
        values = v_rows[pl.ds(start, MAXLEN), :].astype(jnp.bfloat16)
        result = None
        for head in range(heads):
            own = jnp.where(head_lane == head, queries, 0.0).astype(jnp.bfloat16)
            scores = (
                lax.dot_general(
                    own, keys, (((1,), (1,)), ((), ())), preferred_element_type=jnp.float32
                )
                * HD ** (-0.5)
            )
            scores = jnp.where(allowed, scores, MASKED)
            highest = jnp.max(scores, axis=1, keepdims=True)
            exponentials = jnp.exp(scores - highest)
            denominator = jnp.sum(exponentials, axis=1, keepdims=True)
            weights = (exponentials / denominator).astype(jnp.bfloat16)
            blended = jnp.dot(weights, values, preferred_element_type=jnp.float32)
            result = blended if head == 0 else jnp.where(head_lane == head, blended, result)
        out_ref[slot] = result.astype(jnp.bfloat16)
        return carry

    lax.fori_loop(0, start_ref.shape[0], slot_body, 0)


def attend(start, span, query_rows, key_rows, value_rows):
    pairs, heads, _ = query_rows.shape
    slots = start.shape[0]
    flat = [a.reshape(pairs, heads * LANES) for a in (query_rows, key_rows, value_rows)]
    return pl.pallas_call(
        functools.partial(attention_kernel, heads),
        out_shape=jax.ShapeDtypeStruct((slots, MAXLEN, LANES), jnp.bfloat16),
        in_specs=[smem_spec()] * 2 + [whole_spec()] * 3,
        out_specs=whole_spec(),
        scratch_shapes=[pltpu.VMEM((2 * pairs + MAXLEN, LANES), jnp.float32)] * 3,
        compiler_params=params(),
        cost_estimate=pl.CostEstimate(
            flops=slots * heads * MAXLEN * MAXLEN * LANES * 4,
            bytes_accessed=pairs * heads * LANES * 8,
            transcendentals=slots * heads * MAXLEN * MAXLEN,
        ),
    )(start, span, *flat)


def lane_tiles(width):
    return [(first, min(LANES, width - first)) for first in range(0, width, LANES)]


def pairable(width):
    return width == LANES + LANES // 2


def join_pair(one, two):
    half = LANES // 2
    low = lax.broadcasted_iota(jnp.int32, one[0].shape, 1) < half
    turned = pltpu.roll(two[0], half, 1)
    return (
        one[0],
        jnp.where(low, one[1], turned),
        jnp.where(low, turned, pltpu.roll(two[1], half, 1)),
    )


def split_pair(tiles):
    half = LANES // 2
    low = lax.broadcasted_iota(jnp.int32, tiles[0].shape, 1) < half
    middle = pltpu.roll(tiles[1], half, 1)
    last = pltpu.roll(tiles[2], half, 1)
    return (tiles[0], tiles[1]), (jnp.where(low, middle, last), last)


def slots_kernel(start_ref, rows_ref, out_ref, *held):
    count, width = rows_ref.shape
    for (first, size), rows in zip(lane_tiles(width), held):

        def widen(chunk, carry):
            at = pl.multiple_of(chunk * MAXLEN, MAXLEN)
            rows[pl.ds(at, MAXLEN), 0:size] = rows_ref[
                pl.ds(at, MAXLEN), first : first + size
            ].astype(jnp.float32)
            return carry

        lax.fori_loop(0, count // MAXLEN, widen, 0)
        rows[pl.ds(count, MAXLEN), :] = jnp.zeros((MAXLEN, LANES), jnp.float32)

    def slot_body(slot, carry):
        if pairable(width):
            pair = [
                [rows[pl.ds(start_ref[2 * slot + side], MAXLEN), :] for rows in held]
                for side in range(2)
            ]
            tiles = join_pair(*pair)
        else:
            tiles = [rows[pl.ds(start_ref[slot], MAXLEN), :] for rows in held]
        for index, tile in enumerate(tiles):
            out_ref[slot, :, index * LANES : (index + 1) * LANES] = tile.astype(jnp.bfloat16)
        return carry

    lax.fori_loop(0, out_ref.shape[0], slot_body, 0)


def into_slots(start, rows):
    count, width = rows.shape
    slots = start.shape[0]
    tiles = len(lane_tiles(width))
    shape = (slots, MAXLEN, tiles * LANES)
    if pairable(width):
        shape = (slots // 2, MAXLEN, 2 * width)
    return pl.pallas_call(
        slots_kernel,
        out_shape=jax.ShapeDtypeStruct(shape, jnp.bfloat16),
        in_specs=[smem_spec(), whole_spec()],
        out_specs=whole_spec(),
        scratch_shapes=[pltpu.VMEM((count + MAXLEN, LANES), jnp.float32)] * tiles,
        compiler_params=params(),
    )(start, rows)


def place_kernel(paired, parts, after_ref, x_ref, context_ref, out_ref, context_rows, *x_rows):
    slots = context_ref.shape[0]
    slabs = out_ref.shape[0]
    tall = out_ref.shape[1] * (2 if paired else 1)
    slab_rows = tall - 2 * HALO
    total_rows = context_rows.shape[0]
    held = (context_rows,) + x_rows
    zeros = jnp.zeros((MAXLEN, LANES), jnp.float32)
    for rows in held:
        rows[pl.ds(0, HALO), :] = jnp.zeros((HALO, LANES), jnp.float32)

    def load(ref, slot, tile):
        return ref[slot, :, tile * LANES : (tile + 1) * LANES].astype(jnp.float32)

    def put(step, carry):
        if paired:
            sides = split_pair([load(x_ref, step, tile) for tile in range(3)])
            for side in range(2):
                slot = 2 * step + side
                where = pl.ds(HALO + after_ref[slot], MAXLEN)
                for rows, piece in zip(x_rows, sides[side]):
                    rows[where, :] = piece
                context_rows[where, :] = load(context_ref, slot, 0)
        else:
            where = pl.ds(HALO + after_ref[step], MAXLEN)
            for tile, rows in enumerate(x_rows):
                rows[where, :] = load(x_ref, step, tile)
            context_rows[where, :] = load(context_ref, step, 0)
        return carry

    lax.fori_loop(0, x_ref.shape[0], put, 0)
    live = after_ref[slots]

    def clear(step, carry):
        at = jnp.minimum(HALO + live + step * MAXLEN, total_rows - MAXLEN)
        for rows in held:
            rows[pl.ds(at, MAXLEN), :] = zeros
        return carry

    lax.fori_loop(0, (total_rows - HALO - live + MAXLEN - 1) // MAXLEN, clear, 0)

    def emit(slab, carry):
        at = pl.multiple_of(slab * slab_rows, slab_rows)
        if paired:
            for first, half, _ in parts or ((0, tall // 2, 0),):
                one = pl.ds(pl.multiple_of(at + first, 16), half)
                two = pl.ds(pl.multiple_of(at + first + half, 16), half)
                tiles = join_pair(
                    [rows[one, :] for rows in x_rows], [rows[two, :] for rows in x_rows]
                )
                tiles = tiles + (context_rows[one, :], context_rows[two, :])
                for index, tile in enumerate(tiles):
                    lanes = slice(index * LANES, (index + 1) * LANES)
                    out_ref[slab, first // 2 : first // 2 + half, lanes] = tile.astype(
                        jnp.bfloat16
                    )
            return carry
        tiles = [rows[pl.ds(at, tall), :] for rows in x_rows + (context_rows,)]
        for index, tile in enumerate(tiles):
            out_ref[slab, :, index * LANES : (index + 1) * LANES] = tile.astype(jnp.bfloat16)
        return carry

    lax.fori_loop(0, slabs, emit, 0)


def place(after, x_slots, context_slots, slabs, slab_rows, features, parts=None):
    count = context_slots.shape[0]
    paired = pairable(features)
    tiles = len(lane_tiles(features))
    tall = slab_rows + 2 * HALO
    shape = (slabs, tall, (tiles + 1) * LANES)
    if paired:
        shape = (slabs, tall // 2, 2 * features + 2 * LANES)
    return pl.pallas_call(
        functools.partial(place_kernel, paired, parts),
        out_shape=jax.ShapeDtypeStruct(shape, jnp.bfloat16),
        in_specs=[smem_spec(), whole_spec(), whole_spec()],
        out_specs=whole_spec(),
        scratch_shapes=[pltpu.VMEM((count * MAXLEN + HALO + MAXLEN, LANES), jnp.float32)]
        * (tiles + 1),
        compiler_params=params(),
    )(after, x_slots, context_slots)


def unplace_kernel(moved_ref, x_ref, context_ref):
    slabs, rows, _ = moved_ref.shape
    step = 16
    span = 3 * LANES

    def chunk(index, carry):
        at = pl.multiple_of(index * step, step)

        def load(slab, tile):
            cells = moved_ref[slab, pl.ds(at, step), tile * LANES : (tile + 1) * LANES]
            return cells.astype(jnp.float32)

        for pair in range(slabs // 2):
            split = [
                split_pair([load(2 * pair + member, tile) for tile in range(3)])
                for member in range(2)
            ]
            for side in range(2):
                to = pl.ds(pl.multiple_of(at + side * rows, step), step)
                for tile, cells in enumerate(join_pair(split[0][side], split[1][side])):
                    first = pair * span + tile * LANES
                    x_ref[to, first : first + LANES] = cells.astype(jnp.bfloat16)
        for slab in range(slabs):
            for side in range(2):
                to = pl.ds(pl.multiple_of(at + side * rows, step), step)
                first = span + side * LANES
                context_ref[to, slab * LANES : (slab + 1) * LANES] = moved_ref[
                    slab, pl.ds(at, step), first : first + LANES
                ]
        return carry

    lax.fori_loop(0, rows // step, chunk, 0)


def unplace(moved, features, context_width):
    slabs, rows, _ = moved.shape
    if not (pairable(features) and context_width == LANES):
        first = len(lane_tiles(features)) * LANES
        x = moved[:, :, :features].transpose(1, 0, 2).reshape(rows, -1)
        context = moved[:, :, first : first + context_width]
        return x, context.transpose(1, 0, 2).reshape(rows, -1)
    return pl.pallas_call(
        unplace_kernel,
        out_shape=(
            jax.ShapeDtypeStruct((2 * rows, slabs * features), jnp.bfloat16),
            jax.ShapeDtypeStruct((2 * rows, slabs * context_width), jnp.bfloat16),
        ),
        in_specs=[whole_spec()],
        out_specs=(whole_spec(), whole_spec()),
        compiler_params=params(),
    )(moved)


def conv_kernel(
    uniform_ref, gated_ref, segment_ref, taps_ref, scale_ref, shift_ref, out_ref, wide
):
    wide[...] = gated_ref[...].astype(jnp.float32)
    edge = HALO - HALF
    scale = scale_ref[...]
    shift = shift_ref[...]
    for chunk in range(out_ref.shape[0] // CONV_ROWS):
        base = chunk * CONV_ROWS

        def finish(total):
            affine = total * scale + shift
            out_ref[base : base + CONV_ROWS, :] = (affine * jax.nn.sigmoid(affine)).astype(
                jnp.bfloat16
            )

        @pl.when(uniform_ref[chunk] == 1)
        def _():
            total = jnp.zeros((CONV_ROWS, LANES), jnp.float32)
            for tap in range(KERNEL):
                total = total + wide[pl.ds(base + edge + tap, CONV_ROWS), :] * taps_ref[
                    tap : tap + 1, :
                ]
            finish(total)

        @pl.when(uniform_ref[chunk] == 0)
        def _():
            centre = segment_ref[pl.ds(base + HALO, CONV_ROWS), :]
            total = jnp.zeros((CONV_ROWS, LANES), jnp.float32)
            for tap in range(KERNEL):
                same = segment_ref[pl.ds(base + edge + tap, CONV_ROWS), :] == centre
                term = jnp.where(same, wide[pl.ds(base + edge + tap, CONV_ROWS), :], 0.0)
                total = total + term * taps_ref[tap : tap + 1, :]
            finish(total)


def convolve(gated_rows, segment, conv_taps, batch_scale, batch_shift):
    tall, width = gated_rows.shape
    rows = tall - 2 * HALO
    chunks = rows // CONV_ROWS
    windows = [segment[c * CONV_ROWS : c * CONV_ROWS + CONV_ROWS + 2 * HALO] for c in range(chunks)]
    windows = jnp.stack(windows)
    uniform = jnp.all(windows == windows[:, :1], axis=1).astype(jnp.int32)
    wide_segment = jnp.broadcast_to(segment[:, None], (tall, LANES))
    return pl.pallas_call(
        conv_kernel,
        grid=(width // LANES,),
        out_shape=jax.ShapeDtypeStruct((rows, width), jnp.bfloat16),
        in_specs=[
            smem_spec(),
            pl.BlockSpec((tall, LANES), lambda i: (0, i)),
            pl.BlockSpec((tall, LANES), lambda i: (0, 0)),
            pl.BlockSpec((KERNEL, LANES), lambda i: (0, i)),
            pl.BlockSpec((1, LANES), lambda i: (0, i)),
            pl.BlockSpec((1, LANES), lambda i: (0, i)),
        ],
        out_specs=pl.BlockSpec((rows, LANES), lambda i: (0, i)),
        scratch_shapes=[pltpu.VMEM((tall, LANES), jnp.float32)],
        compiler_params=params(),
        cost_estimate=pl.CostEstimate(
            flops=2 * rows * width * KERNEL, bytes_accessed=4 * rows * width, transcendentals=0
        ),
    )(
        uniform,
        gated_rows,
        wide_segment,
        conv_taps,
        batch_scale[None, :],
        batch_shift[None, :],
    )


MESH = pl.DeviceIdType.MESH
OUT, GLU_ONE, GLU_TWO, DOWN = range(4)


def any_spec():
    return pl.BlockSpec(memory_space=pl.ANY)


class Place:
    def __init__(self):
        self.dp = lax.axis_index("dp")
        self.mp = lax.axis_index("mp")
        self.y, self.c = self.dp // 2, self.dp % 2
        self.z, self.x = self.mp // 2, self.mp % 2
        self.across = 1 - self.x
        self.near = self.z + 1 - 2 * (self.z % 2)
        self.far_one = 2 - self.z // 2
        self.far_two = 3 - 3 * (self.z // 2)

    def x_side(self):
        return (self.dp, 2 * self.z + self.across)

    def y_side(self):
        return (2 * (1 - self.y) + self.c, self.mp)

    def core_side(self):
        return (2 * self.y + 1 - self.c, self.mp)

    def corner(self):
        return (2 * (1 - self.y) + 1 - self.c, self.mp)

    def above(self):
        return (self.dp, self.mp + 2)

    def below(self):
        return (self.dp, self.mp - 2)


def aligned(index, step):
    return pl.multiple_of(index * step, step)


def piece(weights, kind, z, x, y, c, both_y=False):
    shard = 2 * z + x
    if kind == OUT:
        return weights[0].at[pl.ds(aligned(shard, 192), 192), pl.ds(aligned(c, 512), 512)]
    if kind == GLU_ONE:
        return weights[1].at[pl.ds(aligned(c, 256), 256), pl.ds(aligned(shard, 384), 384)]
    if kind == GLU_TWO:
        if both_y:
            rows = pl.ds(pl.multiple_of(512 + c * 512, 256), 512)
        else:
            rows = pl.ds(pl.multiple_of(512 + (c * 2 + y) * 256, 256), 256)
        return weights[1].at[rows, pl.ds(aligned(shard, 384), 384)]
    if both_y:
        columns = pl.ds(aligned(c, 768), 768)
    else:
        columns = pl.ds(aligned(c * 2 + y, 384), 384)
    return weights[2].at[pl.ds(aligned(shard, 192), 192), columns]


def own_piece(shards, kind, y, c):
    if kind == OUT:
        return shards[0].at[:, pl.ds(aligned(c, 512), 512)]
    if kind == GLU_ONE:
        return shards[1].at[pl.ds(aligned(c, 256), 256), :]
    if kind == GLU_TWO:
        return shards[1].at[pl.ds(pl.multiple_of(512 + (c * 2 + y) * 256, 256), 256), :]
    return shards[2].at[:, pl.ds(aligned(c * 2 + y, 384), 384)]


class Mail:
    def __init__(self, send_sems, recv_sems):
        self.send_sems, self.recv_sems = send_sems, recv_sems
        self.used = 0
        self.sent = []

    def slot(self):
        self.used += 1
        return self.used - 1

    def copy(self, slot, source, target, device):
        return pltpu.make_async_remote_copy(
            src_ref=source,
            dst_ref=target,
            send_sem=self.send_sems.at[slot],
            recv_sem=self.recv_sems.at[slot],
            device_id=device,
            device_id_type=MESH,
        )

    def send(self, slot, source, target, device, when=None):
        copy = self.copy(slot, source, target, device)
        run_if(when, copy.start)
        self.sent.append((copy, when))

    def receive(self, slot, target, device, when=None):
        run_if(when, self.copy(slot, target, target, device).wait_recv)

    def finish(self):
        for copy, when in self.sent:
            run_if(when, copy.wait_send)


def run_if(when, action):
    if when is None:
        action()
    else:
        pl.when(when)(action)


def greet(devices):
    barrier = pltpu.get_barrier_semaphore()

    def hello(device):
        pl.semaphore_signal(barrier, inc=1, device_id=device, device_id_type=MESH)

    count = 0
    for device, when in devices:
        if when is None:
            hello(device)
            count = count + 1
        else:
            pl.when(when)(functools.partial(hello, device))
            count = count + when.astype(jnp.int32)
    pl.semaphore_wait(barrier, count)


KINDS = (GLU_ONE, OUT, GLU_TWO, DOWN)
FIRST = (GLU_TWO, OUT, GLU_ONE)


def move_kernel(
    start_ref,
    span_ref,
    q_ref,
    k_ref,
    v_ref,
    residual_ref,
    out_shard,
    glu_shard,
    down_shard,
    x_got,
    context_got,
    out_all,
    glu_all,
    down_all,
    q_rows,
    k_rows,
    v_rows,
    x_low,
    x_high,
    x_send,
    context_send,
    out_held,
    glu_held,
    down_held,
    send_sems,
    recv_sems,
    local_sems,
):
    here = Place()
    z, x, y, c = here.z, here.x, here.y, here.c
    weights = (out_all, glu_all, down_all)
    shards = (out_shard, glu_shard, down_shard)
    held = (out_held, glu_held, down_held)
    mail = Mail(send_sems, recv_sems)
    up, down = z < 3, z > 0
    partners = (here.y_side(), here.corner(), here.core_side())
    greet(
        [(device, None) for device in partners + (here.x_side(),)]
        + [(here.above(), up), (here.below(), down)]
    )

    def spot(kind, zz, xx):
        return piece(weights, kind, zz, xx, y, c)

    own = (
        out_all.at[pl.ds(aligned(here.mp, 192), 192), :],
        glu_all.at[:, pl.ds(aligned(here.mp, 384), 384)],
        down_all.at[pl.ds(aligned(here.mp, 192), 192), :],
    )
    into = [
        pltpu.make_async_copy(shards[i], held[i], local_sems.at[i]) for i in range(3)
    ]
    locals_ = [pltpu.make_async_copy(held[i], own[i], local_sems.at[5 + i]) for i in range(3)]
    slots_up, slots_down, slots_x, slots_near = [
        {kind: mail.slot() for kind in KINDS} for _ in range(4)
    ]
    slots_up_two, slots_down_two = [{kind: mail.slot() for kind in KINDS} for _ in range(2)]
    for kind in KINDS:
        mine = own_piece(shards, kind, y, c)
        mail.send(slots_up[kind], mine, spot(kind, z, x), here.above(), up)
        mail.send(slots_down[kind], mine, spot(kind, z, x), here.below(), down)
        mail.send(slots_x[kind], mine, spot(kind, z, x), here.x_side())
    for copy in into:
        copy.start()

    count = 4 * residual_ref.shape[0]
    step = 128
    low = lax.broadcasted_iota(jnp.int32, (step, LANES), 1) < HD

    def open_rows(chunk, carry):
        first = pl.multiple_of(chunk * step, step)
        cells = [
            residual_ref[pl.ds(first, step), i * LANES : (i + 1) * LANES].astype(jnp.float32)
            for i in range(6)
        ]
        turned = [pltpu.roll(cells[i], HD, 1) for i in (1, 2, 4, 5)]
        frames = (
            (cells[0], cells[1]),
            (jnp.where(low, turned[0], turned[1]), turned[1]),
            (cells[3], cells[4]),
            (jnp.where(low, turned[2], turned[3]), turned[3]),
        )
        for j, (one, two) in enumerate(frames):
            at = pl.ds(4 * first + j, step, stride=4)
            x_low[at, :] = one
            x_high[at, :] = two
        return carry

    lax.fori_loop(0, residual_ref.shape[0] // step, open_rows, 0)
    for rows in (x_low, x_high):
        rows[pl.ds(count, MAXLEN), :] = jnp.zeros((MAXLEN, LANES), jnp.float32)

    targets = partners + ((here.dp, here.mp),)
    half = PIECES // 2
    x_slots = [mail.slot() for _ in partners]
    context_slots = [mail.slot() for _ in partners]
    for index, target in enumerate(targets):
        group = target[0]

        def fill(pair, carry):
            at = group * half + pair
            both = [
                [
                    rows[pl.ds(start_ref[2 * at + side], MAXLEN), :]
                    for rows in (x_low, x_high)
                ]
                for side in range(2)
            ]
            for tile, cells in enumerate(join_pair(*both)):
                x_send[at, :, tile * LANES : (tile + 1) * LANES] = cells.astype(jnp.bfloat16)
            return carry

        lax.fori_loop(0, half, fill, 0)
        source = x_send.at[pl.ds(group * half, half)]
        landing = x_got.at[pl.ds(here.dp * half, half)]
        if index < 3:
            mail.send(x_slots[index], source, landing, target)
        else:
            copy = pltpu.make_async_copy(source, landing, local_sems.at[3])
            copy.start()
            locals_.append(copy)

    for copy_in, copy_out in zip(into, locals_):
        copy_in.wait()
        copy_out.start()

    pairs = q_ref.shape[0]
    wide_low = lax.broadcasted_iota(jnp.int32, (256, LANES), 1) < HD

    def unpack(chunk, carry):
        first = pl.multiple_of(chunk * 256, 256)
        for packed, rows in ((q_ref, q_rows), (k_ref, k_rows), (v_ref, v_rows)):
            one = packed[pl.ds(first, 256), 0:LANES].astype(jnp.float32)
            two = packed[pl.ds(first, 256), LANES : 2 * LANES].astype(jnp.float32)
            rows[pl.ds(2 * first, 256, stride=2), :] = jnp.where(
                wide_low, one, pltpu.roll(two, HD, 1)
            )
            rows[pl.ds(2 * first + 1, 256, stride=2), :] = jnp.where(
                wide_low, pltpu.roll(one, HD, 1), two
            )
        return carry

    lax.fori_loop(0, pairs // 256, unpack, 0)
    for rows in (q_rows, k_rows, v_rows):
        rows[pl.ds(2 * pairs, MAXLEN), :] = jnp.zeros((MAXLEN, LANES), jnp.float32)

    column = lax.broadcasted_iota(jnp.int32, (MAXLEN, MAXLEN), 1)
    head_lane = lax.broadcasted_iota(jnp.int32, (MAXLEN, LANES), 1) // HD

    def attend_slot(slot):
        start = start_ref[slot]
        allowed = column < span_ref[slot]
        queries = q_rows[pl.ds(start, MAXLEN), :]
        keys = k_rows[pl.ds(start, MAXLEN), :].astype(jnp.bfloat16)
        values = v_rows[pl.ds(start, MAXLEN), :].astype(jnp.bfloat16)
        result = None
        for head in range(2):
            own = jnp.where(head_lane == head, queries, 0.0).astype(jnp.bfloat16)
            scores = (
                lax.dot_general(
                    own, keys, (((1,), (1,)), ((), ())), preferred_element_type=jnp.float32
                )
                * HD ** (-0.5)
            )
            scores = jnp.where(allowed, scores, MASKED)
            highest = jnp.max(scores, axis=1, keepdims=True)
            exponentials = jnp.exp(scores - highest)
            denominator = jnp.sum(exponentials, axis=1, keepdims=True)
            weighing = (exponentials / denominator).astype(jnp.bfloat16)
            blended = jnp.dot(weighing, values, preferred_element_type=jnp.float32)
            result = blended if head == 0 else jnp.where(head_lane == head, blended, result)
        context_send[slot] = result.astype(jnp.bfloat16)

    def relay(kind):
        mail.receive(slots_up[kind], spot(kind, z - 1, x), here.above(), down)
        mail.send(
            slots_up_two[kind],
            spot(kind, z - 1, x),
            spot(kind, z - 1, x),
            here.above(),
            up & down,
        )
        mail.receive(slots_down[kind], spot(kind, z + 1, x), here.below(), up)
        mail.send(
            slots_down_two[kind],
            spot(kind, z + 1, x),
            spot(kind, z + 1, x),
            here.below(),
            up & down,
        )
        mail.send(
            slots_near[kind],
            spot(kind, here.near, x),
            spot(kind, here.near, x),
            here.x_side(),
        )

    for index, target in enumerate(targets):
        group = target[0]

        def attend_one(rank, carry):
            attend_slot(group * PIECES + rank)
            return carry

        lax.fori_loop(0, PIECES, attend_one, 0)
        source = context_send.at[pl.ds(group * PIECES, PIECES)]
        landing = context_got.at[pl.ds(here.dp * PIECES, PIECES)]
        if index < 3:
            mail.send(context_slots[index], source, landing, target)
        else:
            copy = pltpu.make_async_copy(source, landing, local_sems.at[4])
            copy.start()
            locals_.append(copy)
        relay(KINDS[index])

    for index, source in enumerate(partners):
        mail.receive(x_slots[index], x_got.at[pl.ds(source[0] * half, half)], source)
        mail.receive(
            context_slots[index], context_got.at[pl.ds(source[0] * PIECES, PIECES)], source
        )
    for kind in KINDS:
        mail.receive(slots_x[kind], spot(kind, z, here.across), here.x_side())
        mail.receive(slots_near[kind], spot(kind, here.near, here.across), here.x_side())
        mail.receive(slots_up_two[kind], spot(kind, z - 2, x), here.above(), z > 1)
        mail.receive(slots_down_two[kind], spot(kind, z + 2, x), here.below(), z < 2)
    mail.finish()
    for copy in locals_:
        copy.wait()


def move(start, span, queries, keys, values, residual, out_shard, glu_shard, down_shard):
    slots = start.shape[0]
    pairs = queries.shape[0]
    count = 4 * residual.shape[0]
    bf16 = jnp.bfloat16
    return pl.pallas_call(
        move_kernel,
        out_shape=(
            jax.ShapeDtypeStruct((slots // 2, MAXLEN, 3 * LANES), bf16),
            jax.ShapeDtypeStruct((slots, MAXLEN, LANES), bf16),
            jax.ShapeDtypeStruct((1536, 1024), bf16),
            jax.ShapeDtypeStruct((1536, 3072), bf16),
            jax.ShapeDtypeStruct((1536, 1536), bf16),
        ),
        in_specs=[smem_spec()] * 2 + [whole_spec()] * 4 + [any_spec()] * 3,
        out_specs=(any_spec(),) * 5,
        scratch_shapes=[pltpu.VMEM((2 * pairs + MAXLEN, LANES), jnp.float32)] * 3
        + [pltpu.VMEM((count + MAXLEN, LANES), jnp.float32)] * 2
        + [
            pltpu.VMEM((slots // 2, MAXLEN, 3 * LANES), bf16),
            pltpu.VMEM((slots, MAXLEN, LANES), bf16),
            pltpu.VMEM(out_shard.shape, bf16),
            pltpu.VMEM(glu_shard.shape, bf16),
            pltpu.VMEM(down_shard.shape, bf16),
            pltpu.SemaphoreType.DMA((30,)),
            pltpu.SemaphoreType.DMA((30,)),
            pltpu.SemaphoreType.DMA((8,)),
        ],
        compiler_params=pltpu.CompilerParams(
            vmem_limit_bytes=VMEM_LIMIT, collective_id=1, has_side_effects=True
        ),
        cost_estimate=pl.CostEstimate(
            flops=slots * 2 * MAXLEN * MAXLEN * LANES * 4,
            bytes_accessed=50 * 1024 * 1024,
            transcendentals=slots * 2 * MAXLEN * MAXLEN,
        ),
    )(start, span, queries, keys, values, residual, out_shard, glu_shard, down_shard)


PARTS = ((0, 144, 0), (288, 128, 256))
ROW_STEP = 32
EXCHANGE_ORDER = ((3, 1), (3, 0), (2, 0), (2, 1), (1, 0), (1, 1), (0, 1))


def finish_kernel(
    after_ref,
    slabs_ref,
    norm_ref,
    taps_ref,
    out_in,
    glu_in,
    down_in,
    encoded_ref,
    out_all,
    glu_all,
    down_all,
    moved,
    carried,
    context,
    normed,
    wide,
    swished,
    first_tap,
    last_tap,
    out_held,
    glu_held,
    down_held,
    send_sems,
    recv_sems,
    local_sems,
):
    here = Place()
    z, x, y, c = here.z, here.x, here.y, here.c
    weights = (out_all, glu_all, down_all)
    mail = Mail(send_sems, recv_sems)
    slabs = slabs_ref.shape[0]
    mirrors = (z, here.near, z + 2 - 4 * (z // 2), 3 - z)
    sides = (x, here.across)
    others = [(here.dp, 2 * mirrors[dz] + sides[dx]) for dz, dx in EXCHANGE_ORDER]
    greet([(device, None) for device in others + [here.y_side(), here.core_side()]])

    slab_slots = [[mail.slot() for _ in others] for _ in PARTS]

    def part_rows(part):
        first, half, _ = PARTS[part]
        return pl.ds(first // 2, half)

    def exchange(part):
        for index, device in enumerate(others):
            mail.send(
                slab_slots[part][index],
                slabs_ref.at[device[1], part_rows(part)],
                moved.at[here.mp, part_rows(part)],
                device,
            )

    def exchanged(part):
        for index in range(len(others)):
            mail.receive(
                slab_slots[part][index],
                moved.at[others[index][1], part_rows(part)],
                others[index],
            )

    exchange(0)
    keep = pltpu.make_async_copy(slabs_ref.at[here.mp], moved.at[here.mp], local_sems.at[0])
    keep.start()

    def spot(kind, zz, xx):
        return piece(weights, kind, zz, xx, y, c)

    table = {}

    def slot(*key):
        if key not in table:
            table[key] = mail.slot()
        return table[key]

    def pass_on(name, kind, zz, xx, device, when=None):
        where = spot(kind, zz, xx)
        mail.send(slot(name, kind), where, where, device, when)

    cells = {
        "own near": (here.near, x),
        "own one": (here.far_one, x),
        "own two": (here.far_two, x),
        "other own": (z, here.across),
        "other near": (here.near, here.across),
        "other one": (here.far_one, here.across),
        "other two": (here.far_two, here.across),
    }
    early = ("own near", "own one", "other own", "other near")
    order = early + ("other one", "own two", "other two")

    def after(kind, cell):
        if kind in (OUT, GLU_ONE):
            pass_on("core " + cell, kind, *cells[cell], here.core_side())
        else:
            pass_on("y " + cell, kind, *cells[cell], here.y_side())

    def from_y(kind):
        for cell in order:
            mail.receive(
                slot("y " + cell, kind),
                piece(weights, kind, *cells[cell], 1 - y, c),
                here.y_side(),
            )
            where = piece(weights, kind, *cells[cell], y, c, both_y=True)
            mail.send(slot("core " + cell, kind), where, where, here.core_side())

    def from_core(kind):
        for cell in order:
            where = piece(weights, kind, *cells[cell], y, 1 - c, both_y=kind in (GLU_TWO, DOWN))
            mail.receive(slot("core " + cell, kind), where, here.core_side())

    def start_across(kinds):
        for kind in kinds:
            pass_on("third up", kind, 0, x, here.above(), z == 2)
            pass_on("third down", kind, 3, x, here.below(), z == 1)
            pass_on("x one", kind, here.far_one, x, here.x_side())
        for kind in kinds:
            for cell in early:
                after(kind, cell)

    def across_one(kinds):
        for kind in kinds:
            mail.receive(slot("x one", kind), spot(kind, *cells["other one"]), here.x_side())
            after(kind, "other one")
        for kind in kinds:
            mail.receive(slot("third up", kind), spot(kind, 0, x), here.above(), z == 3)
            mail.receive(slot("third down", kind), spot(kind, 3, x), here.below(), z == 0)
            pass_on("x two", kind, here.far_two, x, here.x_side())
            after(kind, "own two")

    def across_two(kinds):
        for kind in kinds:
            mail.receive(slot("x two", kind), spot(kind, *cells["other two"]), here.x_side())
            after(kind, "other two")

    start_across(FIRST)
    live = after_ref[4 * PIECES]

    def bounds(step, carry):
        rows = pl.ds(pl.multiple_of(step * 64, 64), 64)
        position = (
            lax.broadcasted_iota(jnp.int32, (64, LANES), 0)
            + step * 64
            + here.mp * encoded_ref.shape[0]
        )
        begin = jnp.zeros((64, LANES), jnp.int32)
        end = jnp.full((64, LANES), live, jnp.int32)
        for k in range(1, 4 * PIECES):
            begin = jnp.where(position >= after_ref[k], after_ref[k], begin)
        for k in range(4 * PIECES - 1, 0, -1):
            end = jnp.where(position < after_ref[k], after_ref[k], end)
        first_tap[rows, :] = HALF + begin - position
        last_tap[rows, :] = HALF - 1 + end - position
        return carry

    lax.fori_loop(0, encoded_ref.shape[0] // 64, bounds, 0)

    across_one(FIRST)
    exchange(1)
    start_across((DOWN,))
    across_two(FIRST)
    from_y(GLU_TWO)
    loads = [
        pltpu.make_async_copy(weights[i], (out_held, glu_held, down_held)[i], local_sems.at[1 + i])
        for i in range(3)
    ]
    from_core(OUT)
    loads[0].start()

    def open_part(part):
        first, half, _ = PARTS[part]

        def chunk(index, carry):
            at = pl.ds(pl.multiple_of(first // 2 + index * 16, 16), 16)

            def load(slab, tile):
                cells_ = moved[slab, at, tile * LANES : (tile + 1) * LANES]
                return cells_.astype(jnp.float32)

            to = [pl.ds(pl.multiple_of(first + s * half + index * 16, 16), 16) for s in range(2)]
            near = [pl.ds(pl.multiple_of(s * half + index * 16, 16), 16) for s in range(2)]
            for pair in range(slabs // 2):
                split = [
                    split_pair([load(2 * pair + member, tile) for tile in range(3)])
                    for member in range(2)
                ]
                for side in range(2):
                    for tile, cells_ in enumerate(join_pair(split[0][side], split[1][side])):
                        begin = (3 * pair + tile) * LANES
                        carried[to[side], begin : begin + LANES] = cells_
            for slab in range(slabs):
                for side in range(2):
                    begin = (3 + side) * LANES
                    context[near[side], slab * LANES : (slab + 1) * LANES] = moved[
                        slab, at, begin : begin + LANES
                    ]
            return carry

        lax.fori_loop(0, half // 16, chunk, 0)

    tile_width = 256
    tiles = carried.shape[1] // tile_width

    def attach(part):
        first, half, _ = PARTS[part]

        def tile(n, carry):
            columns = pl.ds(aligned(n, tile_width), tile_width)
            carried[first : first + 2 * half, columns] += lax.dot_general(
                context[0 : 2 * half, :],
                out_held[columns, :],
                (((1,), (1,)), ((), ())),
                preferred_element_type=jnp.float32,
            )
            return carry

        lax.fori_loop(0, tiles, tile, 0)

        def normalise(index, carry):
            at = pl.ds(pl.multiple_of(first + index * 32, 32), 32)
            to = pl.ds(pl.multiple_of(index * 32, 32), 32)
            cells_ = carried[at, :]
            centred = cells_ - jnp.mean(cells_, axis=1, keepdims=True)
            variance = jnp.mean(centred * centred, axis=1, keepdims=True)
            scaled = centred * lax.rsqrt(variance + EPS) * norm_ref[0:1, :] + norm_ref[1:2, :]
            normed[to, :] = scaled.astype(jnp.bfloat16)
            return carry

        lax.fori_loop(0, 2 * half // 32, normalise, 0)

    def gate(part):
        first, half, _ = PARTS[part]

        def tile(n, carry):
            columns = pl.ds(aligned(n, tile_width), tile_width)
            rows = normed[0 : 2 * half, :]
            value = jnp.dot(rows, glu_held[:, columns], preferred_element_type=jnp.float32)
            gates = jnp.dot(
                rows,
                glu_held[:, pl.ds(aligned(n + tiles, tile_width), tile_width)],
                preferred_element_type=jnp.float32,
            )
            gated = (value * jax.nn.sigmoid(gates)).astype(jnp.bfloat16)
            for side in range(2):
                wide[2 * n + side, first : first + 2 * half, :] = gated[
                    :, side * LANES : (side + 1) * LANES
                ].astype(jnp.float32)
            return carry

        lax.fori_loop(0, tiles, tile, 0)

    def convolve_part(part):
        start = PARTS[part][2]
        group = 2
        groups = carried.shape[1] // (group * LANES)

        def body(index, carry):
            row = start + lax.rem(index, 256 // ROW_STEP) * ROW_STEP
            column = index // (256 // ROW_STEP) * (group * LANES)
            rows = pl.ds(pl.multiple_of(row, ROW_STEP), ROW_STEP)
            low, high = first_tap[rows, :], last_tap[rows, :]
            lanes = [pl.ds(pl.multiple_of(column + i * LANES, LANES), LANES) for i in range(group)]
            totals = [jnp.zeros((ROW_STEP, LANES), jnp.float32) for _ in range(group)]
            for shift in range(8):
                count = ROW_STEP + (24 if shift < 7 else 16)
                at = pl.ds(row + HALO - HALF + shift, count)
                seen = [wide[column // LANES + i, at, :] for i in range(group)]
                for k in range(4 if shift < 7 else 3):
                    tap = shift + 8 * k
                    if tap < HALF:
                        mask = low <= tap
                    else:
                        mask = high >= tap
                    for i in range(group):
                        term = seen[i][8 * k : 8 * k + ROW_STEP] * taps_ref[tap : tap + 1, lanes[i]]
                        if tap != HALF:
                            term = jnp.where(mask, term, 0.0)
                        totals[i] = totals[i] + term
            for i in range(group):
                affine = totals[i] * norm_ref[2:3, lanes[i]] + norm_ref[3:4, lanes[i]]
                swished[rows, lanes[i]] = (affine * jax.nn.sigmoid(affine)).astype(jnp.bfloat16)
            return carry

        lax.fori_loop(0, 256 // ROW_STEP * groups, body, 0)

    def lower(part):
        start = PARTS[part][2]
        rows = pl.ds(start, 256)

        def tile(n, carry):
            columns = pl.ds(aligned(n, tile_width), tile_width)
            total = carried[start + HALO : start + HALO + 256, columns] + lax.dot_general(
                swished[rows, :],
                down_held[columns, :],
                (((1,), (1,)), ((), ())),
                preferred_element_type=jnp.float32,
            )
            alive = last_tap[rows, :] >= HALF
            for side in range(2):
                lane = pl.ds(pl.multiple_of(n * tile_width + side * LANES, LANES), LANES)
                encoded_ref[rows, lane] = jnp.where(
                    alive, total[:, side * LANES : (side + 1) * LANES], 0.0
                ).astype(jnp.bfloat16)
            return carry

        lax.fori_loop(0, tiles, tile, 0)

    keep.wait()
    exchanged(0)
    open_part(0)
    loads[0].wait()
    attach(0)
    from_core(GLU_ONE)
    from_core(GLU_TWO)
    loads[1].start()
    across_one((DOWN,))
    loads[1].wait()
    gate(0)
    across_two((DOWN,))
    convolve_part(0)
    from_y(DOWN)
    exchanged(1)
    open_part(1)
    attach(1)
    from_core(DOWN)
    loads[2].start()
    gate(1)
    loads[2].wait()
    lower(0)
    convolve_part(1)
    lower(1)
    mail.finish()


def finish(after, slabs, norm, taps, out_all, glu_all, down_all):
    bf16, f32 = jnp.bfloat16, jnp.float32
    width = taps.shape[1]
    rows = 512
    tall = rows + 2 * HALO
    weights = (out_all, glu_all, down_all)
    return pl.pallas_call(
        finish_kernel,
        out_shape=(jax.ShapeDtypeStruct((rows, width), bf16),)
        + tuple(jax.ShapeDtypeStruct(a.shape, a.dtype) for a in weights),
        in_specs=[smem_spec(), any_spec(), whole_spec(), whole_spec()] + [any_spec()] * 3,
        out_specs=(whole_spec(),) + (any_spec(),) * 3,
        input_output_aliases={4: 1, 5: 2, 6: 3},
        scratch_shapes=[
            pltpu.VMEM(slabs.shape, bf16),
            pltpu.VMEM((tall, width), f32),
            pltpu.VMEM((288, 1024), bf16),
            pltpu.VMEM((288, width), bf16),
            pltpu.VMEM((width // LANES, tall, LANES), f32),
            pltpu.VMEM((rows, width), bf16),
            pltpu.VMEM((rows, LANES), jnp.int32),
            pltpu.VMEM((rows, LANES), jnp.int32),
        ]
        + [pltpu.VMEM(a.shape, bf16) for a in weights]
        + [
            pltpu.SemaphoreType.DMA((80,)),
            pltpu.SemaphoreType.DMA((80,)),
            pltpu.SemaphoreType.DMA((4,)),
        ],
        compiler_params=pltpu.CompilerParams(
            vmem_limit_bytes=VMEM_LIMIT, collective_id=2, has_side_effects=True
        ),
    )(after, slabs, norm, taps, *weights)[0]


def on_device(
    query_rows,
    key_rows,
    value_rows,
    residual,
    lengths,
    assignment,
    out_proj,
    norm_gain,
    norm_bias,
    glu_proj,
    conv_taps,
    batch_scale,
    batch_shift,
    down_proj,
):
    data_group = lax.axis_index("dp")
    slab_index = lax.axis_index("mp")
    groups = lax.axis_size("dp")
    slabs = lax.axis_size("mp")
    group_rows = query_rows.shape[0] * 2
    slab_rows = group_rows // slabs
    total_utterances = lengths.shape[0]
    per_group = total_utterances // groups
    slots = groups * PIECES
    features = residual.shape[2] // 4

    utterance = jnp.arange(total_utterances, dtype=jnp.int32)
    source = utterance // per_group
    earlier = utterance[None, :] < utterance[:, None]
    same_source = source[None, :] == source[:, None]
    same_target = assignment[None, :] == assignment[:, None]
    before = jnp.sum(jnp.where(earlier & same_source, lengths[None, :], 0), axis=1)
    rank = jnp.sum((earlier & same_source & same_target).astype(jnp.int32), axis=1)
    slot = jnp.arange(slots, dtype=jnp.int32)[:, None]
    leaving = (source[None, :] == data_group) & ((assignment * PIECES + rank)[None, :] == slot)
    start = jnp.sum(jnp.where(leaving, before[None, :], 0), axis=1)
    span = jnp.sum(jnp.where(leaving, lengths[None, :], 0), axis=1)
    coming_earlier = (assignment[None, :] == data_group) & (
        (source * PIECES + rank)[None, :] < jnp.arange(slots + 1, dtype=jnp.int32)[:, None]
    )
    after = jnp.sum(jnp.where(coming_earlier, lengths[None, :], 0), axis=1)
    live = jnp.sum(jnp.where(assignment == data_group, lengths, 0))

    position = jnp.arange(slab_rows + 2 * HALO, dtype=jnp.int32) + slab_index * slab_rows - HALO
    segment = jnp.sum((position[:, None] >= after[None, 1:]).astype(jnp.int32), axis=1)
    segment = jnp.where(position < 0, -2, jnp.where(position < live, segment, -1))
    segment = jnp.where(position >= group_rows, -2, segment)

    fits = (
        (groups, slabs) == (4, 8)
        and query_rows.shape == (2048, 2, LANES)
        and residual.shape == (1024, 1, 768)
    )
    if fits:
        flat = [a.reshape(2048, 2 * LANES) for a in (query_rows, key_rows, value_rows)]
        x_slots, context_slots, *weights = move(
            start, span, *flat, residual.reshape(1024, 768), out_proj.T, glu_proj, down_proj.T
        )
        placed = place(after, x_slots, context_slots, slabs, slab_rows, features, PARTS)
        norm = jnp.stack([norm_gain, norm_bias, batch_scale, batch_shift])
        return finish(after, placed, norm, conv_taps, *weights)

    residual_rows = (
        residual.reshape(group_rows // 4, 4, features).reshape(group_rows, features)
    )

    def swap(array, axis):
        return lax.all_to_all(array, axis, split_axis=0, concat_axis=0, tiled=True)

    packed, start = lax.optimization_barrier((into_slots(start, residual_rows), start))
    x_slots = swap(packed, "dp")
    context_slots = swap(attend(start, span, query_rows, key_rows, value_rows), "dp")
    moved = swap(place(after, x_slots, context_slots, slabs, slab_rows, features), "mp")
    carried_slab, context_slab = unplace(moved, features, query_rows.shape[1] * HD)

    core = data_group % 2
    partners = [(group, group + 1 - 2 * (group % 2)) for group in range(groups)]

    def gather(weights):
        half = weights.shape[0] // 2
        own = lax.dynamic_slice_in_dim(weights, core * half, half, 0)
        return lax.all_gather(own, "mp", axis=1, tiled=True)

    def both(own):
        return own, lax.ppermute(own, "dp", partners)

    def project(rows, halves_of):
        own, other = halves_of
        half = rows.shape[1] // 2
        low, high = rows[:, :half], rows[:, half:]
        return jnp.dot(
            jnp.where(core == 0, low, high), own, preferred_element_type=jnp.float32
        ) + jnp.dot(jnp.where(core == 0, high, low), other, preferred_element_type=jnp.float32)

    out_halves, glu_halves = both(gather(out_proj)), both(gather(glu_proj))
    down_own = gather(down_proj)
    carried = carried_slab.astype(jnp.float32) + project(context_slab, out_halves)
    average = jnp.mean(carried, axis=1, keepdims=True)
    centred = carried - average
    variance = jnp.mean(centred * centred, axis=1, keepdims=True)
    normed = (centred * lax.rsqrt(variance + EPS) * norm_gain + norm_bias).astype(jnp.bfloat16)
    halves = project(normed, glu_halves)
    feature_count = halves.shape[1] // 2
    gated_rows = (halves[:, :feature_count] * jax.nn.sigmoid(halves[:, feature_count:])).astype(
        jnp.bfloat16
    )
    down_own, gated_rows = lax.optimization_barrier((down_own, gated_rows))
    down_halves = both(down_own)
    swished = convolve(gated_rows, segment, conv_taps, batch_scale, batch_shift)
    lowered = project(swished, down_halves)
    centre_segment = segment[HALO : HALO + slab_rows]
    own_carried = carried[HALO : HALO + slab_rows]
    return jnp.where((centre_segment >= 0)[:, None], own_carried + lowered, 0.0).astype(
        jnp.bfloat16
    )


def solution(mesh):
    in_specs = (
        P("dp", "mp", None),
        P("dp", "mp", None),
        P("dp", "mp", None),
        P("dp", "mp", None),
        P(),
        P(),
        P(None, "mp"),
        P(),
        P(),
        P(None, "mp"),
        P(),
        P(),
        P(),
        P(None, "mp"),
    )
    out_specs = P(("dp", "mp"), None)
    return jax.shard_map(
        on_device, mesh=mesh, in_specs=in_specs, out_specs=out_specs, check_vma=False
    )
```

```python
import functools

import jax
import jax.numpy as jnp
from jax import lax
from jax.experimental import pallas as pl
from jax.experimental.pallas import tpu as pltpu
from jax.sharding import PartitionSpec as P

HD = 64
KERNEL = 31
HALF = 15
MAXLEN = 256
PIECES = 4
LANES = 128
HALO = 16
CONV_ROWS = 64

EPS = 1e-05
MASKED = -1e30
VMEM_LIMIT = 60 * 1024 * 1024


def params():
    return pltpu.CompilerParams(vmem_limit_bytes=VMEM_LIMIT)


def whole_spec():
    return pl.BlockSpec(memory_space=pltpu.VMEM)


def smem_spec():
    return pl.BlockSpec(memory_space=pltpu.SMEM)


def attention_kernel(
    heads, start_ref, span_ref, q_ref, k_ref, v_ref, out_ref, q_rows, k_rows, v_rows
):
    pairs = q_ref.shape[0]
    step = 256
    lane = lax.broadcasted_iota(jnp.int32, (step, LANES), 1)
    low = lane < HD

    def unpack(chunk, carry):
        first = pl.multiple_of(chunk * step, step)
        for packed, rows in ((q_ref, q_rows), (k_ref, k_rows), (v_ref, v_rows)):
            one = packed[pl.ds(first, step), 0:LANES].astype(jnp.float32)
            if heads == 2:
                two = packed[pl.ds(first, step), LANES : 2 * LANES].astype(jnp.float32)
                even = jnp.where(low, one, pltpu.roll(two, HD, 1))
                odd = jnp.where(low, pltpu.roll(one, HD, 1), two)
            else:
                even = one
                odd = pltpu.roll(one, HD, 1)
            rows[pl.ds(2 * first, step, stride=2), :] = even
            rows[pl.ds(2 * first + 1, step, stride=2), :] = odd
        return carry

    lax.fori_loop(0, pairs // step, unpack, 0)
    for rows in (q_rows, k_rows, v_rows):
        rows[pl.ds(2 * pairs, MAXLEN), :] = jnp.zeros((MAXLEN, LANES), jnp.float32)

    column = lax.broadcasted_iota(jnp.int32, (MAXLEN, MAXLEN), 1)
    head_lane = lax.broadcasted_iota(jnp.int32, (MAXLEN, LANES), 1) // HD

    def slot_body(slot, carry):
        start = start_ref[slot]
        allowed = column < span_ref[slot]
        queries = q_rows[pl.ds(start, MAXLEN), :]
        keys = k_rows[pl.ds(start, MAXLEN), :].astype(jnp.bfloat16)
        values = v_rows[pl.ds(start, MAXLEN), :].astype(jnp.bfloat16)
        result = None
        for head in range(heads):
            own = jnp.where(head_lane == head, queries, 0.0).astype(jnp.bfloat16)
            scores = (
                lax.dot_general(
                    own, keys, (((1,), (1,)), ((), ())), preferred_element_type=jnp.float32
                )
                * HD ** (-0.5)
            )
            scores = jnp.where(allowed, scores, MASKED)
            highest = jnp.max(scores, axis=1, keepdims=True)
            exponentials = jnp.exp(scores - highest)
            denominator = jnp.sum(exponentials, axis=1, keepdims=True)
            weights = (exponentials / denominator).astype(jnp.bfloat16)
            blended = jnp.dot(weights, values, preferred_element_type=jnp.float32)
            result = blended if head == 0 else jnp.where(head_lane == head, blended, result)
        out_ref[slot] = result.astype(jnp.bfloat16)
        return carry

    lax.fori_loop(0, start_ref.shape[0], slot_body, 0)


def attend(start, span, query_rows, key_rows, value_rows):
    pairs, heads, _ = query_rows.shape
    slots = start.shape[0]
    flat = [a.reshape(pairs, heads * LANES) for a in (query_rows, key_rows, value_rows)]
    return pl.pallas_call(
        functools.partial(attention_kernel, heads),
        out_shape=jax.ShapeDtypeStruct((slots, MAXLEN, LANES), jnp.bfloat16),
        in_specs=[smem_spec()] * 2 + [whole_spec()] * 3,
        out_specs=whole_spec(),
        scratch_shapes=[pltpu.VMEM((2 * pairs + MAXLEN, LANES), jnp.float32)] * 3,
        compiler_params=params(),
        cost_estimate=pl.CostEstimate(
            flops=slots * heads * MAXLEN * MAXLEN * LANES * 4,
            bytes_accessed=pairs * heads * LANES * 8,
            transcendentals=slots * heads * MAXLEN * MAXLEN,
        ),
    )(start, span, *flat)


def lane_tiles(width):
    return [(first, min(LANES, width - first)) for first in range(0, width, LANES)]


def pairable(width):
    return width == LANES + LANES // 2


def join_pair(one, two):
    half = LANES // 2
    low = lax.broadcasted_iota(jnp.int32, one[0].shape, 1) < half
    turned = pltpu.roll(two[0], half, 1)
    return (
        one[0],
        jnp.where(low, one[1], turned),
        jnp.where(low, turned, pltpu.roll(two[1], half, 1)),
    )


def split_pair(tiles):
    half = LANES // 2
    low = lax.broadcasted_iota(jnp.int32, tiles[0].shape, 1) < half
    middle = pltpu.roll(tiles[1], half, 1)
    last = pltpu.roll(tiles[2], half, 1)
    return (tiles[0], tiles[1]), (jnp.where(low, middle, last), last)


def slots_kernel(start_ref, rows_ref, out_ref, *held):
    count, width = rows_ref.shape
    for (first, size), rows in zip(lane_tiles(width), held):

        def widen(chunk, carry):
            at = pl.multiple_of(chunk * MAXLEN, MAXLEN)
            rows[pl.ds(at, MAXLEN), 0:size] = rows_ref[
                pl.ds(at, MAXLEN), first : first + size
            ].astype(jnp.float32)
            return carry

        lax.fori_loop(0, count // MAXLEN, widen, 0)
        rows[pl.ds(count, MAXLEN), :] = jnp.zeros((MAXLEN, LANES), jnp.float32)

    def slot_body(slot, carry):
        if pairable(width):
            pair = [
                [rows[pl.ds(start_ref[2 * slot + side], MAXLEN), :] for rows in held]
                for side in range(2)
            ]
            tiles = join_pair(*pair)
        else:
            tiles = [rows[pl.ds(start_ref[slot], MAXLEN), :] for rows in held]
        for index, tile in enumerate(tiles):
            out_ref[slot, :, index * LANES : (index + 1) * LANES] = tile.astype(jnp.bfloat16)
        return carry

    lax.fori_loop(0, out_ref.shape[0], slot_body, 0)


def into_slots(start, rows):
    count, width = rows.shape
    slots = start.shape[0]
    tiles = len(lane_tiles(width))
    shape = (slots, MAXLEN, tiles * LANES)
    if pairable(width):
        shape = (slots // 2, MAXLEN, 2 * width)
    return pl.pallas_call(
        slots_kernel,
        out_shape=jax.ShapeDtypeStruct(shape, jnp.bfloat16),
        in_specs=[smem_spec(), whole_spec()],
        out_specs=whole_spec(),
        scratch_shapes=[pltpu.VMEM((count + MAXLEN, LANES), jnp.float32)] * tiles,
        compiler_params=params(),
    )(start, rows)


def place_kernel(paired, after_ref, x_ref, context_ref, out_ref, context_rows, *x_rows):
    slots = context_ref.shape[0]
    slabs = out_ref.shape[0]
    tall = out_ref.shape[1] * (2 if paired else 1)
    slab_rows = tall - 2 * HALO
    total_rows = context_rows.shape[0]
    held = (context_rows,) + x_rows
    zeros = jnp.zeros((MAXLEN, LANES), jnp.float32)
    for rows in held:
        rows[pl.ds(0, HALO), :] = jnp.zeros((HALO, LANES), jnp.float32)

    def load(ref, slot, tile):
        return ref[slot, :, tile * LANES : (tile + 1) * LANES].astype(jnp.float32)

    def put(step, carry):
        if paired:
            sides = split_pair([load(x_ref, step, tile) for tile in range(3)])
            for side in range(2):
                slot = 2 * step + side
                where = pl.ds(HALO + after_ref[slot], MAXLEN)
                for rows, piece in zip(x_rows, sides[side]):
                    rows[where, :] = piece
                context_rows[where, :] = load(context_ref, slot, 0)
        else:
            where = pl.ds(HALO + after_ref[step], MAXLEN)
            for tile, rows in enumerate(x_rows):
                rows[where, :] = load(x_ref, step, tile)
            context_rows[where, :] = load(context_ref, step, 0)
        return carry

    lax.fori_loop(0, x_ref.shape[0], put, 0)
    live = after_ref[slots]

    def clear(step, carry):
        at = jnp.minimum(HALO + live + step * MAXLEN, total_rows - MAXLEN)
        for rows in held:
            rows[pl.ds(at, MAXLEN), :] = zeros
        return carry

    lax.fori_loop(0, (total_rows - HALO - live + MAXLEN - 1) // MAXLEN, clear, 0)

    def emit(slab, carry):
        at = pl.multiple_of(slab * slab_rows, slab_rows)
        if paired:
            half = tall // 2
            one = pl.ds(at, half)
            two = pl.ds(pl.multiple_of(at + half, 8), half)
            tiles = join_pair([rows[one, :] for rows in x_rows], [rows[two, :] for rows in x_rows])
            tiles = tiles + (context_rows[one, :], context_rows[two, :])
        else:
            tiles = [rows[pl.ds(at, tall), :] for rows in x_rows + (context_rows,)]
        for index, tile in enumerate(tiles):
            out_ref[slab, :, index * LANES : (index + 1) * LANES] = tile.astype(jnp.bfloat16)
        return carry

    lax.fori_loop(0, slabs, emit, 0)


def place(after, x_slots, context_slots, slabs, slab_rows, features):
    count = context_slots.shape[0]
    paired = pairable(features)
    tiles = len(lane_tiles(features))
    tall = slab_rows + 2 * HALO
    shape = (slabs, tall, (tiles + 1) * LANES)
    if paired:
        shape = (slabs, tall // 2, 2 * features + 2 * LANES)
    return pl.pallas_call(
        functools.partial(place_kernel, paired),
        out_shape=jax.ShapeDtypeStruct(shape, jnp.bfloat16),
        in_specs=[smem_spec(), whole_spec(), whole_spec()],
        out_specs=whole_spec(),
        scratch_shapes=[pltpu.VMEM((count * MAXLEN + HALO + MAXLEN, LANES), jnp.float32)]
        * (tiles + 1),
        compiler_params=params(),
    )(after, x_slots, context_slots)


def unplace_kernel(moved_ref, x_ref, context_ref):
    slabs, rows, _ = moved_ref.shape
    step = 16
    span = 3 * LANES

    def chunk(index, carry):
        at = pl.multiple_of(index * step, step)

        def load(slab, tile):
            cells = moved_ref[slab, pl.ds(at, step), tile * LANES : (tile + 1) * LANES]
            return cells.astype(jnp.float32)

        for pair in range(slabs // 2):
            split = [
                split_pair([load(2 * pair + member, tile) for tile in range(3)])
                for member in range(2)
            ]
            for side in range(2):
                to = pl.ds(pl.multiple_of(at + side * rows, step), step)
                for tile, cells in enumerate(join_pair(split[0][side], split[1][side])):
                    first = pair * span + tile * LANES
                    x_ref[to, first : first + LANES] = cells.astype(jnp.bfloat16)
        for slab in range(slabs):
            for side in range(2):
                to = pl.ds(pl.multiple_of(at + side * rows, step), step)
                first = span + side * LANES
                context_ref[to, slab * LANES : (slab + 1) * LANES] = moved_ref[
                    slab, pl.ds(at, step), first : first + LANES
                ]
        return carry

    lax.fori_loop(0, rows // step, chunk, 0)


def unplace(moved, features, context_width):
    slabs, rows, _ = moved.shape
    if not (pairable(features) and context_width == LANES):
        first = len(lane_tiles(features)) * LANES
        x = moved[:, :, :features].transpose(1, 0, 2).reshape(rows, -1)
        context = moved[:, :, first : first + context_width]
        return x, context.transpose(1, 0, 2).reshape(rows, -1)
    return pl.pallas_call(
        unplace_kernel,
        out_shape=(
            jax.ShapeDtypeStruct((2 * rows, slabs * features), jnp.bfloat16),
            jax.ShapeDtypeStruct((2 * rows, slabs * context_width), jnp.bfloat16),
        ),
        in_specs=[whole_spec()],
        out_specs=(whole_spec(), whole_spec()),
        compiler_params=params(),
    )(moved)


def conv_kernel(
    uniform_ref, gated_ref, segment_ref, taps_ref, scale_ref, shift_ref, out_ref, wide
):
    wide[...] = gated_ref[...].astype(jnp.float32)
    edge = HALO - HALF
    scale = scale_ref[...]
    shift = shift_ref[...]
    for chunk in range(out_ref.shape[0] // CONV_ROWS):
        base = chunk * CONV_ROWS

        def finish(total):
            affine = total * scale + shift
            out_ref[base : base + CONV_ROWS, :] = (affine * jax.nn.sigmoid(affine)).astype(
                jnp.bfloat16
            )

        @pl.when(uniform_ref[chunk] == 1)
        def _():
            total = jnp.zeros((CONV_ROWS, LANES), jnp.float32)
            for tap in range(KERNEL):
                total = total + wide[pl.ds(base + edge + tap, CONV_ROWS), :] * taps_ref[
                    tap : tap + 1, :
                ]
            finish(total)

        @pl.when(uniform_ref[chunk] == 0)
        def _():
            centre = segment_ref[pl.ds(base + HALO, CONV_ROWS), :]
            total = jnp.zeros((CONV_ROWS, LANES), jnp.float32)
            for tap in range(KERNEL):
                same = segment_ref[pl.ds(base + edge + tap, CONV_ROWS), :] == centre
                term = jnp.where(same, wide[pl.ds(base + edge + tap, CONV_ROWS), :], 0.0)
                total = total + term * taps_ref[tap : tap + 1, :]
            finish(total)


def convolve(gated_rows, segment, conv_taps, batch_scale, batch_shift):
    tall, width = gated_rows.shape
    rows = tall - 2 * HALO
    chunks = rows // CONV_ROWS
    windows = [segment[c * CONV_ROWS : c * CONV_ROWS + CONV_ROWS + 2 * HALO] for c in range(chunks)]
    windows = jnp.stack(windows)
    uniform = jnp.all(windows == windows[:, :1], axis=1).astype(jnp.int32)
    wide_segment = jnp.broadcast_to(segment[:, None], (tall, LANES))
    return pl.pallas_call(
        conv_kernel,
        grid=(width // LANES,),
        out_shape=jax.ShapeDtypeStruct((rows, width), jnp.bfloat16),
        in_specs=[
            smem_spec(),
            pl.BlockSpec((tall, LANES), lambda i: (0, i)),
            pl.BlockSpec((tall, LANES), lambda i: (0, 0)),
            pl.BlockSpec((KERNEL, LANES), lambda i: (0, i)),
            pl.BlockSpec((1, LANES), lambda i: (0, i)),
            pl.BlockSpec((1, LANES), lambda i: (0, i)),
        ],
        out_specs=pl.BlockSpec((rows, LANES), lambda i: (0, i)),
        scratch_shapes=[pltpu.VMEM((tall, LANES), jnp.float32)],
        compiler_params=params(),
        cost_estimate=pl.CostEstimate(
            flops=2 * rows * width * KERNEL, bytes_accessed=4 * rows * width, transcendentals=0
        ),
    )(
        uniform,
        gated_rows,
        wide_segment,
        conv_taps,
        batch_scale[None, :],
        batch_shift[None, :],
    )


MESH = pl.DeviceIdType.MESH
OUT, GLU_ONE, GLU_TWO, DOWN = range(4)


def any_spec():
    return pl.BlockSpec(memory_space=pl.ANY)


class Place:
    def __init__(self):
        self.dp = lax.axis_index("dp")
        self.mp = lax.axis_index("mp")
        self.y, self.c = self.dp // 2, self.dp % 2
        self.z, self.x = self.mp // 2, self.mp % 2
        self.across = 1 - self.x
        self.near = self.z + 1 - 2 * (self.z % 2)
        self.far_one = 2 - self.z // 2
        self.far_two = 3 - 3 * (self.z // 2)

    def x_side(self):
        return (self.dp, 2 * self.z + self.across)

    def y_side(self):
        return (2 * (1 - self.y) + self.c, self.mp)

    def core_side(self):
        return (2 * self.y + 1 - self.c, self.mp)

    def corner(self):
        return (2 * (1 - self.y) + 1 - self.c, self.mp)

    def above(self):
        return (self.dp, self.mp + 2)

    def below(self):
        return (self.dp, self.mp - 2)


def aligned(index, step):
    return pl.multiple_of(index * step, step)


def piece(weights, kind, z, x, y, c, both_y=False):
    shard = 2 * z + x
    if kind == OUT:
        return weights[0].at[pl.ds(aligned(shard, 192), 192), pl.ds(aligned(c, 512), 512)]
    if kind == GLU_ONE:
        return weights[1].at[pl.ds(aligned(c, 256), 256), pl.ds(aligned(shard, 384), 384)]
    if kind == GLU_TWO:
        if both_y:
            rows = pl.ds(pl.multiple_of(512 + c * 512, 256), 512)
        else:
            rows = pl.ds(pl.multiple_of(512 + (c * 2 + y) * 256, 256), 256)
        return weights[1].at[rows, pl.ds(aligned(shard, 384), 384)]
    if both_y:
        columns = pl.ds(aligned(c, 768), 768)
    else:
        columns = pl.ds(aligned(c * 2 + y, 384), 384)
    return weights[2].at[pl.ds(aligned(shard, 192), 192), columns]


def own_piece(shards, kind, y, c):
    if kind == OUT:
        return shards[0].at[:, pl.ds(aligned(c, 512), 512)]
    if kind == GLU_ONE:
        return shards[1].at[pl.ds(aligned(c, 256), 256), :]
    if kind == GLU_TWO:
        return shards[1].at[pl.ds(pl.multiple_of(512 + (c * 2 + y) * 256, 256), 256), :]
    return shards[2].at[:, pl.ds(aligned(c * 2 + y, 384), 384)]


class Mail:
    def __init__(self, send_sems, recv_sems):
        self.send_sems, self.recv_sems = send_sems, recv_sems
        self.used = 0
        self.sent = []

    def slot(self):
        self.used += 1
        return self.used - 1

    def copy(self, slot, source, target, device):
        return pltpu.make_async_remote_copy(
            src_ref=source,
            dst_ref=target,
            send_sem=self.send_sems.at[slot],
            recv_sem=self.recv_sems.at[slot],
            device_id=device,
            device_id_type=MESH,
        )

    def send(self, slot, source, target, device, when=None):
        copy = self.copy(slot, source, target, device)
        run_if(when, copy.start)
        self.sent.append((copy, when))

    def receive(self, slot, target, device, when=None):
        run_if(when, self.copy(slot, target, target, device).wait_recv)

    def finish(self):
        for copy, when in self.sent:
            run_if(when, copy.wait_send)


def run_if(when, action):
    if when is None:
        action()
    else:
        pl.when(when)(action)


def greet(devices):
    barrier = pltpu.get_barrier_semaphore()

    def hello(device):
        pl.semaphore_signal(barrier, inc=1, device_id=device, device_id_type=MESH)

    count = 0
    for device, when in devices:
        if when is None:
            hello(device)
            count = count + 1
        else:
            pl.when(when)(functools.partial(hello, device))
            count = count + when.astype(jnp.int32)
    pl.semaphore_wait(barrier, count)


KINDS = (GLU_ONE, OUT, GLU_TWO, DOWN)
FIRST = (GLU_TWO, OUT, GLU_ONE)


def find_slots(dp, lengths_ref, assignment_ref, start_ref, span_ref):
    groups = start_ref.shape[0] // PIECES
    per_group = lengths_ref.shape[0] // groups
    zero = jnp.int32(0)
    counts = [zero] * groups
    starts = [zero] * (groups * PIECES)
    spans = [zero] * (groups * PIECES)
    before = zero
    for i in range(per_group):
        target = assignment_ref[dp * per_group + i]
        length = lengths_ref[dp * per_group + i]
        for group in range(groups):
            hit = target == group
            for rank in range(PIECES):
                slot = group * PIECES + rank
                found = hit & (counts[group] == rank)
                starts[slot] = jnp.where(found, before, starts[slot])
                spans[slot] = jnp.where(found, length, spans[slot])
            counts[group] = counts[group] + hit.astype(jnp.int32)
        before = before + length
    for slot in range(groups * PIECES):
        start_ref[slot] = starts[slot]
        span_ref[slot] = spans[slot]


def move_kernel(
    lengths_ref,
    assignment_ref,
    q_ref,
    k_ref,
    v_ref,
    residual_ref,
    out_shard,
    glu_shard,
    down_shard,
    x_got,
    context_got,
    out_all,
    glu_all,
    down_all,
    q_rows,
    k_rows,
    v_rows,
    x_low,
    x_high,
    x_send,
    context_send,
    out_held,
    glu_held,
    down_held,
    start_ref,
    span_ref,
    send_sems,
    recv_sems,
    local_sems,
):
    here = Place()
    z, x, y, c = here.z, here.x, here.y, here.c
    weights = (out_all, glu_all, down_all)
    shards = (out_shard, glu_shard, down_shard)
    held = (out_held, glu_held, down_held)
    mail = Mail(send_sems, recv_sems)
    up, down = z < 3, z > 0
    partners = (here.y_side(), here.corner(), here.core_side())
    greet(
        [(device, None) for device in partners + (here.x_side(),)]
        + [(here.above(), up), (here.below(), down)]
    )

    def spot(kind, zz, xx):
        return piece(weights, kind, zz, xx, y, c)

    own = (
        out_all.at[pl.ds(aligned(here.mp, 192), 192), :],
        glu_all.at[:, pl.ds(aligned(here.mp, 384), 384)],
        down_all.at[pl.ds(aligned(here.mp, 192), 192), :],
    )
    into = [
        pltpu.make_async_copy(shards[i], held[i], local_sems.at[i]) for i in range(3)
    ]
    locals_ = [pltpu.make_async_copy(held[i], own[i], local_sems.at[5 + i]) for i in range(3)]
    slots_up, slots_down, slots_x, slots_near = [
        {kind: mail.slot() for kind in KINDS} for _ in range(4)
    ]
    slots_up_two, slots_down_two = [{kind: mail.slot() for kind in KINDS} for _ in range(2)]
    for kind in KINDS:
        mine = own_piece(shards, kind, y, c)
        mail.send(slots_up[kind], mine, spot(kind, z, x), here.above(), up)
        mail.send(slots_down[kind], mine, spot(kind, z, x), here.below(), down)
        mail.send(slots_x[kind], mine, spot(kind, z, x), here.x_side())
    for copy in into:
        copy.start()
    find_slots(here.dp, lengths_ref, assignment_ref, start_ref, span_ref)

    count = 4 * residual_ref.shape[0]
    step = 128
    low = lax.broadcasted_iota(jnp.int32, (step, LANES), 1) < HD

    def open_rows(chunk, carry):
        first = pl.multiple_of(chunk * step, step)
        cells = [
            residual_ref[pl.ds(first, step), i * LANES : (i + 1) * LANES].astype(jnp.float32)
            for i in range(6)
        ]
        turned = [pltpu.roll(cells[i], HD, 1) for i in (1, 2, 4, 5)]
        frames = (
            (cells[0], cells[1]),
            (jnp.where(low, turned[0], turned[1]), turned[1]),
            (cells[3], cells[4]),
            (jnp.where(low, turned[2], turned[3]), turned[3]),
        )
        for j, (one, two) in enumerate(frames):
            at = pl.ds(4 * first + j, step, stride=4)
            x_low[at, :] = one
            x_high[at, :] = two
        return carry

    lax.fori_loop(0, residual_ref.shape[0] // step, open_rows, 0)
    for rows in (x_low, x_high):
        rows[pl.ds(count, MAXLEN), :] = jnp.zeros((MAXLEN, LANES), jnp.float32)

    targets = partners + ((here.dp, here.mp),)
    half = PIECES // 2
    x_slots = [mail.slot() for _ in partners]
    context_slots = [mail.slot() for _ in partners]
    for index, target in enumerate(targets):
        group = target[0]

        def fill(pair, carry):
            at = group * half + pair
            both = [
                [
                    rows[pl.ds(start_ref[2 * at + side], MAXLEN), :]
                    for rows in (x_low, x_high)
                ]
                for side in range(2)
            ]
            for tile, cells in enumerate(join_pair(*both)):
                x_send[at, :, tile * LANES : (tile + 1) * LANES] = cells.astype(jnp.bfloat16)
            return carry

        lax.fori_loop(0, half, fill, 0)
        source = x_send.at[pl.ds(group * half, half)]
        landing = x_got.at[pl.ds(here.dp * half, half)]
        if index < 3:
            mail.send(x_slots[index], source, landing, target)
        else:
            copy = pltpu.make_async_copy(source, landing, local_sems.at[3])
            copy.start()
            locals_.append(copy)

    for copy_in, copy_out in zip(into, locals_):
        copy_in.wait()
        copy_out.start()

    pairs = q_ref.shape[0]
    wide_low = lax.broadcasted_iota(jnp.int32, (256, LANES), 1) < HD

    def unpack(chunk, carry):
        first = pl.multiple_of(chunk * 256, 256)
        for packed, rows in ((q_ref, q_rows), (k_ref, k_rows), (v_ref, v_rows)):
            one = packed[pl.ds(first, 256), 0:LANES].astype(jnp.float32)
            two = packed[pl.ds(first, 256), LANES : 2 * LANES].astype(jnp.float32)
            rows[pl.ds(2 * first, 256, stride=2), :] = jnp.where(
                wide_low, one, pltpu.roll(two, HD, 1)
            )
            rows[pl.ds(2 * first + 1, 256, stride=2), :] = jnp.where(
                wide_low, pltpu.roll(one, HD, 1), two
            )
        return carry

    lax.fori_loop(0, pairs // 256, unpack, 0)
    for rows in (q_rows, k_rows, v_rows):
        rows[pl.ds(2 * pairs, MAXLEN), :] = jnp.zeros((MAXLEN, LANES), jnp.float32)

    column = lax.broadcasted_iota(jnp.int32, (MAXLEN, MAXLEN), 1)
    head_lane = lax.broadcasted_iota(jnp.int32, (MAXLEN, LANES), 1) // HD

    def attend_slot(slot):
        start = start_ref[slot]
        allowed = column < span_ref[slot]
        queries = q_rows[pl.ds(start, MAXLEN), :]
        keys = k_rows[pl.ds(start, MAXLEN), :].astype(jnp.bfloat16)
        values = v_rows[pl.ds(start, MAXLEN), :].astype(jnp.bfloat16)
        result = None
        for head in range(2):
            own = jnp.where(head_lane == head, queries, 0.0).astype(jnp.bfloat16)
            scores = (
                lax.dot_general(
                    own, keys, (((1,), (1,)), ((), ())), preferred_element_type=jnp.float32
                )
                * HD ** (-0.5)
            )
            scores = jnp.where(allowed, scores, MASKED)
            highest = jnp.max(scores, axis=1, keepdims=True)
            exponentials = jnp.exp(scores - highest)
            denominator = jnp.sum(exponentials, axis=1, keepdims=True)
            weighing = (exponentials / denominator).astype(jnp.bfloat16)
            blended = jnp.dot(weighing, values, preferred_element_type=jnp.float32)
            result = blended if head == 0 else jnp.where(head_lane == head, blended, result)
        context_send[slot] = result.astype(jnp.bfloat16)

    def relay(kind):
        mail.receive(slots_up[kind], spot(kind, z - 1, x), here.above(), down)
        mail.send(
            slots_up_two[kind],
            spot(kind, z - 1, x),
            spot(kind, z - 1, x),
            here.above(),
            up & down,
        )
        mail.receive(slots_down[kind], spot(kind, z + 1, x), here.below(), up)
        mail.send(
            slots_down_two[kind],
            spot(kind, z + 1, x),
            spot(kind, z + 1, x),
            here.below(),
            up & down,
        )
        mail.send(
            slots_near[kind],
            spot(kind, here.near, x),
            spot(kind, here.near, x),
            here.x_side(),
        )

    for index, target in enumerate(targets):
        group = target[0]

        def attend_one(rank, carry):
            attend_slot(group * PIECES + rank)
            return carry

        lax.fori_loop(0, PIECES, attend_one, 0)
        source = context_send.at[pl.ds(group * PIECES, PIECES)]
        landing = context_got.at[pl.ds(here.dp * PIECES, PIECES)]
        if index < 3:
            mail.send(context_slots[index], source, landing, target)
        else:
            copy = pltpu.make_async_copy(source, landing, local_sems.at[4])
            copy.start()
            locals_.append(copy)
        relay(KINDS[index])

    for index, source in enumerate(partners):
        mail.receive(x_slots[index], x_got.at[pl.ds(source[0] * half, half)], source)
        mail.receive(
            context_slots[index], context_got.at[pl.ds(source[0] * PIECES, PIECES)], source
        )
    for kind in KINDS:
        mail.receive(slots_x[kind], spot(kind, z, here.across), here.x_side())
        mail.receive(slots_near[kind], spot(kind, here.near, here.across), here.x_side())
        mail.receive(slots_up_two[kind], spot(kind, z - 2, x), here.above(), z > 1)
        mail.receive(slots_down_two[kind], spot(kind, z + 2, x), here.below(), z < 2)
    mail.finish()
    for copy in locals_:
        copy.wait()


def move(lengths, assignment, queries, keys, values, residual, out_shard, glu_shard, down_shard):
    slots = 4 * PIECES
    pairs = queries.shape[0]
    count = 4 * residual.shape[0]
    bf16 = jnp.bfloat16
    return pl.pallas_call(
        move_kernel,
        out_shape=(
            jax.ShapeDtypeStruct((slots // 2, MAXLEN, 3 * LANES), bf16),
            jax.ShapeDtypeStruct((slots, MAXLEN, LANES), bf16),
            jax.ShapeDtypeStruct((1536, 1024), bf16),
            jax.ShapeDtypeStruct((1536, 3072), bf16),
            jax.ShapeDtypeStruct((1536, 1536), bf16),
        ),
        in_specs=[smem_spec()] * 2 + [whole_spec()] * 4 + [any_spec()] * 3,
        out_specs=(any_spec(),) * 5,
        scratch_shapes=[pltpu.VMEM((2 * pairs + MAXLEN, LANES), jnp.float32)] * 3
        + [pltpu.VMEM((count + MAXLEN, LANES), jnp.float32)] * 2
        + [
            pltpu.VMEM((slots // 2, MAXLEN, 3 * LANES), bf16),
            pltpu.VMEM((slots, MAXLEN, LANES), bf16),
            pltpu.VMEM(out_shard.shape, bf16),
            pltpu.VMEM(glu_shard.shape, bf16),
            pltpu.VMEM(down_shard.shape, bf16),
            pltpu.SMEM((slots,), jnp.int32),
            pltpu.SMEM((slots,), jnp.int32),
            pltpu.SemaphoreType.DMA((30,)),
            pltpu.SemaphoreType.DMA((30,)),
            pltpu.SemaphoreType.DMA((8,)),
        ],
        compiler_params=pltpu.CompilerParams(
            vmem_limit_bytes=VMEM_LIMIT, collective_id=1, has_side_effects=True
        ),
        cost_estimate=pl.CostEstimate(
            flops=slots * 2 * MAXLEN * MAXLEN * LANES * 4,
            bytes_accessed=50 * 1024 * 1024,
            transcendentals=slots * 2 * MAXLEN * MAXLEN,
        ),
    )(lengths, assignment, queries, keys, values, residual, out_shard, glu_shard, down_shard)


SPLIT = 288
PARTS = ((0, SPLIT // 2, 0, SPLIT - 2 * HALO), (SPLIT, 272 - SPLIT // 2, SPLIT - 2 * HALO, 544 - SPLIT))
ROW_STEP = 32
EXCHANGE_ORDER = ((3, 1), (3, 0), (2, 0), (2, 1), (1, 0), (1, 1), (0, 1))


def place_parts_kernel(
    lengths_ref, assignment_ref, x_ref, context_ref, out_ref, after_ref, context_rows, *x_rows
):
    dp = lax.axis_index("dp")
    after_ref[0] = 0

    def seek(u, carry):
        count, total = carry
        hit = assignment_ref[u] == dp
        total = total + jnp.where(hit, lengths_ref[u], 0)
        count = count + hit.astype(jnp.int32)
        after_ref[count] = total
        return count, total

    lax.fori_loop(0, lengths_ref.shape[0], seek, (jnp.int32(0), jnp.int32(0)))
    slots = context_ref.shape[0]
    slabs = out_ref.shape[0]
    tall = out_ref.shape[1] * 2
    slab_rows = tall - 2 * HALO
    total_rows = context_rows.shape[0]
    held = (context_rows,) + x_rows
    zeros = jnp.zeros((MAXLEN, LANES), jnp.float32)
    for rows in held:
        rows[pl.ds(0, HALO), :] = jnp.zeros((HALO, LANES), jnp.float32)

    def load(ref, slot, tile):
        return ref[slot, :, tile * LANES : (tile + 1) * LANES].astype(jnp.float32)

    def put(step, carry):
        sides = split_pair([load(x_ref, step, tile) for tile in range(3)])
        for side in range(2):
            slot = 2 * step + side
            where = pl.ds(HALO + after_ref[slot], MAXLEN)
            for rows, piece in zip(x_rows, sides[side]):
                rows[where, :] = piece
            context_rows[where, :] = load(context_ref, slot, 0)
        return carry

    lax.fori_loop(0, x_ref.shape[0], put, 0)
    live = after_ref[slots]

    def clear(step, carry):
        at = jnp.minimum(HALO + live + step * MAXLEN, total_rows - MAXLEN)
        for rows in held:
            rows[pl.ds(at, MAXLEN), :] = zeros
        return carry

    lax.fori_loop(0, (total_rows - HALO - live + MAXLEN - 1) // MAXLEN, clear, 0)

    def emit(slab, carry):
        at = pl.multiple_of(slab * slab_rows, slab_rows)
        for first, half, *_ in PARTS:
            one = pl.ds(pl.multiple_of(at + first, 16), half)
            two = pl.ds(pl.multiple_of(at + first + half, 16), half)
            tiles = join_pair(
                [rows[one, :] for rows in x_rows], [rows[two, :] for rows in x_rows]
            )
            tiles = tiles + (context_rows[one, :], context_rows[two, :])
            for index, tile in enumerate(tiles):
                lanes = slice(index * LANES, (index + 1) * LANES)
                out_ref[slab, first // 2 : first // 2 + half, lanes] = tile.astype(
                    jnp.bfloat16
                )
        return carry

    lax.fori_loop(0, slabs, emit, 0)


def place_parts(lengths, assignment, x_slots, context_slots, slabs):
    count = context_slots.shape[0]
    return pl.pallas_call(
        place_parts_kernel,
        out_shape=(
            jax.ShapeDtypeStruct((slabs, 272, 5 * LANES), jnp.bfloat16),
            jax.ShapeDtypeStruct((count + 1,), jnp.int32),
        ),
        in_specs=[smem_spec()] * 2 + [whole_spec()] * 2,
        out_specs=(whole_spec(), smem_spec()),
        scratch_shapes=[pltpu.VMEM((count * MAXLEN + HALO + MAXLEN, LANES), jnp.float32)] * 3,
        compiler_params=params(),
    )(lengths, assignment, x_slots, context_slots)


def finish_kernel(
    after_ref,
    slabs_ref,
    gain_ref,
    bias_ref,
    scale_ref,
    shift_ref,
    taps_ref,
    out_in,
    glu_in,
    down_in,
    encoded_ref,
    out_all,
    glu_all,
    down_all,
    moved,
    carried,
    context,
    normed,
    wide,
    swished,
    first_tap,
    last_tap,
    out_held,
    glu_held,
    down_held,
    send_sems,
    recv_sems,
    local_sems,
):
    here = Place()
    z, x, y, c = here.z, here.x, here.y, here.c
    weights = (out_all, glu_all, down_all)
    mail = Mail(send_sems, recv_sems)
    slabs = slabs_ref.shape[0]
    mirrors = (z, here.near, z + 2 - 4 * (z // 2), 3 - z)
    sides = (x, here.across)
    others = [(here.dp, 2 * mirrors[dz] + sides[dx]) for dz, dx in EXCHANGE_ORDER]
    greet([(device, None) for device in others + [here.y_side(), here.core_side()]])

    slab_slots = [[mail.slot() for _ in others] for _ in PARTS]

    def part_rows(part):
        first, half, *_ = PARTS[part]
        return pl.ds(first // 2, half)

    def exchange(part):
        for index, device in enumerate(others):
            mail.send(
                slab_slots[part][index],
                slabs_ref.at[device[1], part_rows(part)],
                moved.at[here.mp, part_rows(part)],
                device,
            )

    def exchanged(part):
        for index in range(len(others)):
            mail.receive(
                slab_slots[part][index],
                moved.at[others[index][1], part_rows(part)],
                others[index],
            )

    keep = pltpu.make_async_copy(slabs_ref.at[here.mp], moved.at[here.mp], local_sems.at[0])
    keep.start()

    def spot(kind, zz, xx):
        return piece(weights, kind, zz, xx, y, c)

    table = {}

    def slot(*key):
        if key not in table:
            table[key] = mail.slot()
        return table[key]

    def pass_on(name, kind, zz, xx, device, when=None):
        where = spot(kind, zz, xx)
        mail.send(slot(name, kind), where, where, device, when)

    cells = {
        "own near": (here.near, x),
        "own one": (here.far_one, x),
        "own two": (here.far_two, x),
        "other own": (z, here.across),
        "other near": (here.near, here.across),
        "other one": (here.far_one, here.across),
        "other two": (here.far_two, here.across),
    }
    early = ("own near", "own one", "other own", "other near")
    order = early + ("other one", "own two", "other two")

    def after(kind, cell):
        if kind in (OUT, GLU_ONE):
            pass_on("core " + cell, kind, *cells[cell], here.core_side())
        else:
            pass_on("y " + cell, kind, *cells[cell], here.y_side())

    def from_y(kind):
        for cell in order:
            mail.receive(
                slot("y " + cell, kind),
                piece(weights, kind, *cells[cell], 1 - y, c),
                here.y_side(),
            )
            where = piece(weights, kind, *cells[cell], y, c, both_y=True)
            mail.send(slot("core " + cell, kind), where, where, here.core_side())

    def from_core(kind):
        for cell in order:
            where = piece(weights, kind, *cells[cell], y, 1 - c, both_y=kind in (GLU_TWO, DOWN))
            mail.receive(slot("core " + cell, kind), where, here.core_side())

    def start_across(kinds):
        for kind in kinds:
            pass_on("third up", kind, 0, x, here.above(), z == 2)
            pass_on("third down", kind, 3, x, here.below(), z == 1)
            pass_on("x one", kind, here.far_one, x, here.x_side())
        for kind in kinds:
            for cell in early:
                after(kind, cell)

    def across_one(kinds):
        for kind in kinds:
            mail.receive(slot("x one", kind), spot(kind, *cells["other one"]), here.x_side())
            after(kind, "other one")
        for kind in kinds:
            mail.receive(slot("third up", kind), spot(kind, 0, x), here.above(), z == 3)
            mail.receive(slot("third down", kind), spot(kind, 3, x), here.below(), z == 0)
            pass_on("x two", kind, here.far_two, x, here.x_side())
            after(kind, "own two")

    def across_two(kinds):
        for kind in kinds:
            mail.receive(slot("x two", kind), spot(kind, *cells["other two"]), here.x_side())
            after(kind, "other two")

    start_across(FIRST)
    exchange(0)
    live = after_ref[4 * PIECES]

    def bounds(step, carry):
        rows = pl.ds(pl.multiple_of(step * 64, 64), 64)
        position = (
            lax.broadcasted_iota(jnp.int32, (64, LANES), 0)
            + step * 64
            + here.mp * encoded_ref.shape[0]
        )
        begin = jnp.zeros((64, LANES), jnp.int32)
        end = jnp.full((64, LANES), live, jnp.int32)
        for k in range(1, 4 * PIECES):
            begin = jnp.where(position >= after_ref[k], after_ref[k], begin)
        for k in range(4 * PIECES - 1, 0, -1):
            end = jnp.where(position < after_ref[k], after_ref[k], end)
        first_tap[rows, :] = HALF + begin - position
        last_tap[rows, :] = HALF - 1 + end - position
        return carry

    lax.fori_loop(0, encoded_ref.shape[0] // 64, bounds, 0)

    across_one(FIRST)
    exchange(1)
    start_across((DOWN,))
    across_two(FIRST)
    from_y(GLU_TWO)
    loads = [
        pltpu.make_async_copy(weights[i], (out_held, glu_held, down_held)[i], local_sems.at[1 + i])
        for i in range(3)
    ]
    from_core(OUT)
    loads[0].start()

    def open_part(part):
        first, half, *_ = PARTS[part]

        def chunk(index, carry):
            at = pl.ds(pl.multiple_of(first // 2 + index * 16, 16), 16)

            def load(slab, tile):
                cells_ = moved[slab, at, tile * LANES : (tile + 1) * LANES]
                return cells_.astype(jnp.float32)

            to = [pl.ds(pl.multiple_of(first + s * half + index * 16, 16), 16) for s in range(2)]
            near = [pl.ds(pl.multiple_of(s * half + index * 16, 16), 16) for s in range(2)]
            for pair in range(slabs // 2):
                split = [
                    split_pair([load(2 * pair + member, tile) for tile in range(3)])
                    for member in range(2)
                ]
                for side in range(2):
                    for tile, cells_ in enumerate(join_pair(split[0][side], split[1][side])):
                        begin = (3 * pair + tile) * LANES
                        carried[to[side], begin : begin + LANES] = cells_
            for slab in range(slabs):
                for side in range(2):
                    begin = (3 + side) * LANES
                    context[near[side], slab * LANES : (slab + 1) * LANES] = moved[
                        slab, at, begin : begin + LANES
                    ]
            return carry

        lax.fori_loop(0, half // 16, chunk, 0)

    tile_width = 256
    tiles = carried.shape[1] // tile_width

    def attach(part):
        first, half, *_ = PARTS[part]

        def tile(n, carry):
            columns = pl.ds(aligned(n, tile_width), tile_width)
            carried[first : first + 2 * half, columns] += lax.dot_general(
                context[0 : 2 * half, :],
                out_held[columns, :],
                (((1,), (1,)), ((), ())),
                preferred_element_type=jnp.float32,
            )
            return carry

        lax.fori_loop(0, tiles, tile, 0)

        def normalise(index, carry):
            at = pl.ds(pl.multiple_of(first + index * 32, 32), 32)
            to = pl.ds(pl.multiple_of(index * 32, 32), 32)
            cells_ = carried[at, :]
            centred = cells_ - jnp.mean(cells_, axis=1, keepdims=True)
            variance = jnp.mean(centred * centred, axis=1, keepdims=True)
            inverse = lax.rsqrt(variance + EPS)
            for i in range(carried.shape[1] // LANES):
                lanes = slice(i * LANES, (i + 1) * LANES)
                scaled = centred[:, lanes] * inverse * gain_ref[i : i + 1, :] + bias_ref[i : i + 1, :]
                normed[to, lanes] = scaled.astype(jnp.bfloat16)
            return carry

        lax.fori_loop(0, 2 * half // 32, normalise, 0)

    def gate(part):
        first, half, *_ = PARTS[part]

        def tile(n, carry):
            columns = pl.ds(aligned(n, tile_width), tile_width)
            rows = normed[0 : 2 * half, :]
            value = jnp.dot(rows, glu_held[:, columns], preferred_element_type=jnp.float32)
            gates = jnp.dot(
                rows,
                glu_held[:, pl.ds(aligned(n + tiles, tile_width), tile_width)],
                preferred_element_type=jnp.float32,
            )
            gated = (value * jax.nn.sigmoid(gates)).astype(jnp.bfloat16)
            for side in range(2):
                wide[2 * n + side, first : first + 2 * half, :] = gated[
                    :, side * LANES : (side + 1) * LANES
                ].astype(jnp.float32)
            return carry

        lax.fori_loop(0, tiles, tile, 0)

    def convolve_part(part):
        start, count_rows = PARTS[part][2:]
        steps = count_rows // ROW_STEP
        group = 2
        groups = carried.shape[1] // (group * LANES)

        def body(index, carry):
            row = start + lax.rem(index, steps) * ROW_STEP
            column = index // steps * (group * LANES)
            rows = pl.ds(pl.multiple_of(row, ROW_STEP), ROW_STEP)
            low, high = first_tap[rows, :], last_tap[rows, :]
            lanes = [pl.ds(pl.multiple_of(column + i * LANES, LANES), LANES) for i in range(group)]
            totals = [jnp.zeros((ROW_STEP, LANES), jnp.float32) for _ in range(group)]
            for shift in range(8):
                count = ROW_STEP + (24 if shift < 7 else 16)
                at = pl.ds(row + HALO - HALF + shift, count)
                seen = [wide[column // LANES + i, at, :] for i in range(group)]
                for k in range(4 if shift < 7 else 3):
                    tap = shift + 8 * k
                    if tap < HALF:
                        mask = low <= tap
                    else:
                        mask = high >= tap
                    for i in range(group):
                        term = seen[i][8 * k : 8 * k + ROW_STEP] * taps_ref[tap : tap + 1, lanes[i]]
                        if tap != HALF:
                            term = jnp.where(mask, term, 0.0)
                        totals[i] = totals[i] + term
            for i in range(group):
                one = pl.ds(column // LANES + i, 1)
                affine = totals[i] * scale_ref[one, :] + shift_ref[one, :]
                swished[rows, lanes[i]] = (affine * jax.nn.sigmoid(affine)).astype(jnp.bfloat16)
            return carry

        lax.fori_loop(0, steps * groups, body, 0)

    def lower(part):
        start, count_rows = PARTS[part][2:]
        rows = pl.ds(start, count_rows)

        def tile(n, carry):
            columns = pl.ds(aligned(n, tile_width), tile_width)
            total = carried[start + HALO : start + HALO + count_rows, columns] + lax.dot_general(
                swished[rows, :],
                down_held[columns, :],
                (((1,), (1,)), ((), ())),
                preferred_element_type=jnp.float32,
            )
            alive = last_tap[rows, :] >= HALF
            for side in range(2):
                lane = pl.ds(pl.multiple_of(n * tile_width + side * LANES, LANES), LANES)
                encoded_ref[rows, lane] = jnp.where(
                    alive, total[:, side * LANES : (side + 1) * LANES], 0.0
                ).astype(jnp.bfloat16)
            return carry

        lax.fori_loop(0, tiles, tile, 0)

    keep.wait()
    exchanged(0)
    open_part(0)
    loads[0].wait()
    attach(0)
    from_core(GLU_ONE)
    from_core(GLU_TWO)
    loads[1].start()
    across_one((DOWN,))
    loads[1].wait()
    gate(0)
    across_two((DOWN,))
    convolve_part(0)
    from_y(DOWN)
    exchanged(1)
    open_part(1)
    attach(1)
    from_core(DOWN)
    loads[2].start()
    gate(1)
    loads[2].wait()
    lower(0)
    convolve_part(1)
    lower(1)
    mail.finish()


def finish(after, slabs, norm, taps, out_all, glu_all, down_all):
    norm = [a.reshape(-1, LANES) for a in norm]
    bf16, f32 = jnp.bfloat16, jnp.float32
    width = taps.shape[1]
    rows = 512
    tall = rows + 2 * HALO
    weights = (out_all, glu_all, down_all)
    return pl.pallas_call(
        finish_kernel,
        out_shape=(jax.ShapeDtypeStruct((rows, width), bf16),)
        + tuple(jax.ShapeDtypeStruct(a.shape, a.dtype) for a in weights),
        in_specs=[smem_spec(), any_spec()] + [whole_spec()] * 5 + [any_spec()] * 3,
        out_specs=(whole_spec(),) + (any_spec(),) * 3,
        input_output_aliases={7: 1, 8: 2, 9: 3},
        scratch_shapes=[
            pltpu.VMEM(slabs.shape, bf16),
            pltpu.VMEM((tall, width), f32),
            pltpu.VMEM((SPLIT, 1024), bf16),
            pltpu.VMEM((SPLIT, width), bf16),
            pltpu.VMEM((width // LANES, tall, LANES), f32),
            pltpu.VMEM((rows, width), bf16),
            pltpu.VMEM((rows, LANES), jnp.int32),
            pltpu.VMEM((rows, LANES), jnp.int32),
        ]
        + [pltpu.VMEM(a.shape, bf16) for a in weights]
        + [
            pltpu.SemaphoreType.DMA((80,)),
            pltpu.SemaphoreType.DMA((80,)),
            pltpu.SemaphoreType.DMA((4,)),
        ],
        compiler_params=pltpu.CompilerParams(
            vmem_limit_bytes=VMEM_LIMIT, collective_id=2, has_side_effects=True
        ),
    )(after, slabs, *norm, taps, *weights)[0]


def on_device(
    query_rows,
    key_rows,
    value_rows,
    residual,
    lengths,
    assignment,
    out_proj,
    norm_gain,
    norm_bias,
    glu_proj,
    conv_taps,
    batch_scale,
    batch_shift,
    down_proj,
):
    data_group = lax.axis_index("dp")
    slab_index = lax.axis_index("mp")
    groups = lax.axis_size("dp")
    slabs = lax.axis_size("mp")
    group_rows = query_rows.shape[0] * 2
    slab_rows = group_rows // slabs
    total_utterances = lengths.shape[0]
    per_group = total_utterances // groups
    slots = groups * PIECES
    features = residual.shape[2] // 4

    fits = (
        (groups, slabs) == (4, 8)
        and query_rows.shape == (2048, 2, LANES)
        and residual.shape == (1024, 1, 768)
    )
    if fits:
        flat = [a.reshape(2048, 2 * LANES) for a in (query_rows, key_rows, value_rows)]
        x_slots, context_slots, *weights = move(
            lengths, assignment, *flat, residual.reshape(1024, 768), out_proj.T, glu_proj, down_proj.T
        )
        placed, after = place_parts(lengths, assignment, x_slots, context_slots, slabs)
        norm = (norm_gain, norm_bias, batch_scale, batch_shift)
        return finish(after, placed, norm, conv_taps, *weights)

    utterance = jnp.arange(total_utterances, dtype=jnp.int32)
    source = utterance // per_group
    earlier = utterance[None, :] < utterance[:, None]
    same_source = source[None, :] == source[:, None]
    same_target = assignment[None, :] == assignment[:, None]
    before = jnp.sum(jnp.where(earlier & same_source, lengths[None, :], 0), axis=1)
    rank = jnp.sum((earlier & same_source & same_target).astype(jnp.int32), axis=1)
    slot = jnp.arange(slots, dtype=jnp.int32)[:, None]
    leaving = (source[None, :] == data_group) & ((assignment * PIECES + rank)[None, :] == slot)
    start = jnp.sum(jnp.where(leaving, before[None, :], 0), axis=1)
    span = jnp.sum(jnp.where(leaving, lengths[None, :], 0), axis=1)
    coming_earlier = (assignment[None, :] == data_group) & (
        (source * PIECES + rank)[None, :] < jnp.arange(slots + 1, dtype=jnp.int32)[:, None]
    )
    after = jnp.sum(jnp.where(coming_earlier, lengths[None, :], 0), axis=1)
    live = jnp.sum(jnp.where(assignment == data_group, lengths, 0))

    position = jnp.arange(slab_rows + 2 * HALO, dtype=jnp.int32) + slab_index * slab_rows - HALO
    segment = jnp.sum((position[:, None] >= after[None, 1:]).astype(jnp.int32), axis=1)
    segment = jnp.where(position < 0, -2, jnp.where(position < live, segment, -1))
    segment = jnp.where(position >= group_rows, -2, segment)

    residual_rows = (
        residual.reshape(group_rows // 4, 4, features).reshape(group_rows, features)
    )

    def swap(array, axis):
        return lax.all_to_all(array, axis, split_axis=0, concat_axis=0, tiled=True)

    packed, start = lax.optimization_barrier((into_slots(start, residual_rows), start))
    x_slots = swap(packed, "dp")
    context_slots = swap(attend(start, span, query_rows, key_rows, value_rows), "dp")
    moved = swap(place(after, x_slots, context_slots, slabs, slab_rows, features), "mp")
    carried_slab, context_slab = unplace(moved, features, query_rows.shape[1] * HD)

    core = data_group % 2
    partners = [(group, group + 1 - 2 * (group % 2)) for group in range(groups)]

    def gather(weights):
        half = weights.shape[0] // 2
        own = lax.dynamic_slice_in_dim(weights, core * half, half, 0)
        return lax.all_gather(own, "mp", axis=1, tiled=True)

    def both(own):
        return own, lax.ppermute(own, "dp", partners)

    def project(rows, halves_of):
        own, other = halves_of
        half = rows.shape[1] // 2
        low, high = rows[:, :half], rows[:, half:]
        return jnp.dot(
            jnp.where(core == 0, low, high), own, preferred_element_type=jnp.float32
        ) + jnp.dot(jnp.where(core == 0, high, low), other, preferred_element_type=jnp.float32)

    out_halves, glu_halves = both(gather(out_proj)), both(gather(glu_proj))
    down_own = gather(down_proj)
    carried = carried_slab.astype(jnp.float32) + project(context_slab, out_halves)
    average = jnp.mean(carried, axis=1, keepdims=True)
    centred = carried - average
    variance = jnp.mean(centred * centred, axis=1, keepdims=True)
    normed = (centred * lax.rsqrt(variance + EPS) * norm_gain + norm_bias).astype(jnp.bfloat16)
    halves = project(normed, glu_halves)
    feature_count = halves.shape[1] // 2
    gated_rows = (halves[:, :feature_count] * jax.nn.sigmoid(halves[:, feature_count:])).astype(
        jnp.bfloat16
    )
    down_own, gated_rows = lax.optimization_barrier((down_own, gated_rows))
    down_halves = both(down_own)
    swished = convolve(gated_rows, segment, conv_taps, batch_scale, batch_shift)
    lowered = project(swished, down_halves)
    centre_segment = segment[HALO : HALO + slab_rows]
    own_carried = carried[HALO : HALO + slab_rows]
    return jnp.where((centre_segment >= 0)[:, None], own_carried + lowered, 0.0).astype(
        jnp.bfloat16
    )


def solution(mesh):
    in_specs = (
        P("dp", "mp", None),
        P("dp", "mp", None),
        P("dp", "mp", None),
        P("dp", "mp", None),
        P(),
        P(),
        P(None, "mp"),
        P(),
        P(),
        P(None, "mp"),
        P(),
        P(),
        P(),
        P(None, "mp"),
    )
    out_specs = P(("dp", "mp"), None)
    return jax.shard_map(
        on_device, mesh=mesh, in_specs=in_specs, out_specs=out_specs, check_vma=False
    )
```

```python
import functools

import jax
import jax.numpy as jnp
from jax import lax
from jax.experimental import pallas as pl
from jax.experimental.pallas import tpu as pltpu
from jax.sharding import PartitionSpec as P

HD = 64
KERNEL = 31
HALF = 15
MAXLEN = 256
PIECES = 4
LANES = 128
HALO = 16
CONV_ROWS = 64

EPS = 1e-05
MASKED = -1e30
VMEM_LIMIT = 60 * 1024 * 1024


def params():
    return pltpu.CompilerParams(vmem_limit_bytes=VMEM_LIMIT)


def whole_spec():
    return pl.BlockSpec(memory_space=pltpu.VMEM)


def smem_spec():
    return pl.BlockSpec(memory_space=pltpu.SMEM)


def attention_kernel(
    heads, start_ref, span_ref, q_ref, k_ref, v_ref, out_ref, q_rows, k_rows, v_rows
):
    pairs = q_ref.shape[0]
    step = 256
    lane = lax.broadcasted_iota(jnp.int32, (step, LANES), 1)
    low = lane < HD

    def unpack(chunk, carry):
        first = pl.multiple_of(chunk * step, step)
        for packed, rows in ((q_ref, q_rows), (k_ref, k_rows), (v_ref, v_rows)):
            one = packed[pl.ds(first, step), 0:LANES].astype(jnp.float32)
            if heads == 2:
                two = packed[pl.ds(first, step), LANES : 2 * LANES].astype(jnp.float32)
                even = jnp.where(low, one, pltpu.roll(two, HD, 1))
                odd = jnp.where(low, pltpu.roll(one, HD, 1), two)
            else:
                even = one
                odd = pltpu.roll(one, HD, 1)
            rows[pl.ds(2 * first, step, stride=2), :] = even
            rows[pl.ds(2 * first + 1, step, stride=2), :] = odd
        return carry

    lax.fori_loop(0, pairs // step, unpack, 0)
    for rows in (q_rows, k_rows, v_rows):
        rows[pl.ds(2 * pairs, MAXLEN), :] = jnp.zeros((MAXLEN, LANES), jnp.float32)

    column = lax.broadcasted_iota(jnp.int32, (MAXLEN, MAXLEN), 1)
    head_lane = lax.broadcasted_iota(jnp.int32, (MAXLEN, LANES), 1) // HD

    def slot_body(slot, carry):
        start = start_ref[slot]
        allowed = column < span_ref[slot]
        queries = q_rows[pl.ds(start, MAXLEN), :]
        keys = k_rows[pl.ds(start, MAXLEN), :].astype(jnp.bfloat16)
        values = v_rows[pl.ds(start, MAXLEN), :].astype(jnp.bfloat16)
        result = None
        for head in range(heads):
            own = jnp.where(head_lane == head, queries, 0.0).astype(jnp.bfloat16)
            scores = (
                lax.dot_general(
                    own, keys, (((1,), (1,)), ((), ())), preferred_element_type=jnp.float32
                )
                * HD ** (-0.5)
            )
            scores = jnp.where(allowed, scores, MASKED)
            highest = jnp.max(scores, axis=1, keepdims=True)
            exponentials = jnp.exp(scores - highest)
            denominator = jnp.sum(exponentials, axis=1, keepdims=True)
            weights = (exponentials / denominator).astype(jnp.bfloat16)
            blended = jnp.dot(weights, values, preferred_element_type=jnp.float32)
            result = blended if head == 0 else jnp.where(head_lane == head, blended, result)
        out_ref[slot] = result.astype(jnp.bfloat16)
        return carry

    lax.fori_loop(0, start_ref.shape[0], slot_body, 0)


def attend(start, span, query_rows, key_rows, value_rows):
    pairs, heads, _ = query_rows.shape
    slots = start.shape[0]
    flat = [a.reshape(pairs, heads * LANES) for a in (query_rows, key_rows, value_rows)]
    return pl.pallas_call(
        functools.partial(attention_kernel, heads),
        out_shape=jax.ShapeDtypeStruct((slots, MAXLEN, LANES), jnp.bfloat16),
        in_specs=[smem_spec()] * 2 + [whole_spec()] * 3,
        out_specs=whole_spec(),
        scratch_shapes=[pltpu.VMEM((2 * pairs + MAXLEN, LANES), jnp.float32)] * 3,
        compiler_params=params(),
        cost_estimate=pl.CostEstimate(
            flops=slots * heads * MAXLEN * MAXLEN * LANES * 4,
            bytes_accessed=pairs * heads * LANES * 8,
            transcendentals=slots * heads * MAXLEN * MAXLEN,
        ),
    )(start, span, *flat)


def lane_tiles(width):
    return [(first, min(LANES, width - first)) for first in range(0, width, LANES)]


def pairable(width):
    return width == LANES + LANES // 2


def join_pair(one, two):
    half = LANES // 2
    low = lax.broadcasted_iota(jnp.int32, one[0].shape, 1) < half
    turned = pltpu.roll(two[0], half, 1)
    return (
        one[0],
        jnp.where(low, one[1], turned),
        jnp.where(low, turned, pltpu.roll(two[1], half, 1)),
    )


def split_pair(tiles):
    half = LANES // 2
    low = lax.broadcasted_iota(jnp.int32, tiles[0].shape, 1) < half
    middle = pltpu.roll(tiles[1], half, 1)
    last = pltpu.roll(tiles[2], half, 1)
    return (tiles[0], tiles[1]), (jnp.where(low, middle, last), last)


def slots_kernel(start_ref, rows_ref, out_ref, *held):
    count, width = rows_ref.shape
    for (first, size), rows in zip(lane_tiles(width), held):

        def widen(chunk, carry):
            at = pl.multiple_of(chunk * MAXLEN, MAXLEN)
            rows[pl.ds(at, MAXLEN), 0:size] = rows_ref[
                pl.ds(at, MAXLEN), first : first + size
            ].astype(jnp.float32)
            return carry

        lax.fori_loop(0, count // MAXLEN, widen, 0)
        rows[pl.ds(count, MAXLEN), :] = jnp.zeros((MAXLEN, LANES), jnp.float32)

    def slot_body(slot, carry):
        if pairable(width):
            pair = [
                [rows[pl.ds(start_ref[2 * slot + side], MAXLEN), :] for rows in held]
                for side in range(2)
            ]
            tiles = join_pair(*pair)
        else:
            tiles = [rows[pl.ds(start_ref[slot], MAXLEN), :] for rows in held]
        for index, tile in enumerate(tiles):
            out_ref[slot, :, index * LANES : (index + 1) * LANES] = tile.astype(jnp.bfloat16)
        return carry

    lax.fori_loop(0, out_ref.shape[0], slot_body, 0)


def into_slots(start, rows):
    count, width = rows.shape
    slots = start.shape[0]
    tiles = len(lane_tiles(width))
    shape = (slots, MAXLEN, tiles * LANES)
    if pairable(width):
        shape = (slots // 2, MAXLEN, 2 * width)
    return pl.pallas_call(
        slots_kernel,
        out_shape=jax.ShapeDtypeStruct(shape, jnp.bfloat16),
        in_specs=[smem_spec(), whole_spec()],
        out_specs=whole_spec(),
        scratch_shapes=[pltpu.VMEM((count + MAXLEN, LANES), jnp.float32)] * tiles,
        compiler_params=params(),
    )(start, rows)


def place_kernel(paired, after_ref, x_ref, context_ref, out_ref, context_rows, *x_rows):
    slots = context_ref.shape[0]
    slabs = out_ref.shape[0]
    tall = out_ref.shape[1] * (2 if paired else 1)
    slab_rows = tall - 2 * HALO
    total_rows = context_rows.shape[0]
    held = (context_rows,) + x_rows
    zeros = jnp.zeros((MAXLEN, LANES), jnp.float32)
    for rows in held:
        rows[pl.ds(0, HALO), :] = jnp.zeros((HALO, LANES), jnp.float32)

    def load(ref, slot, tile):
        return ref[slot, :, tile * LANES : (tile + 1) * LANES].astype(jnp.float32)

    def put(step, carry):
        if paired:
            sides = split_pair([load(x_ref, step, tile) for tile in range(3)])
            for side in range(2):
                slot = 2 * step + side
                where = pl.ds(HALO + after_ref[slot], MAXLEN)
                for rows, piece in zip(x_rows, sides[side]):
                    rows[where, :] = piece
                context_rows[where, :] = load(context_ref, slot, 0)
        else:
            where = pl.ds(HALO + after_ref[step], MAXLEN)
            for tile, rows in enumerate(x_rows):
                rows[where, :] = load(x_ref, step, tile)
            context_rows[where, :] = load(context_ref, step, 0)
        return carry

    lax.fori_loop(0, x_ref.shape[0], put, 0)
    live = after_ref[slots]

    def clear(step, carry):
        at = jnp.minimum(HALO + live + step * MAXLEN, total_rows - MAXLEN)
        for rows in held:
            rows[pl.ds(at, MAXLEN), :] = zeros
        return carry

    lax.fori_loop(0, (total_rows - HALO - live + MAXLEN - 1) // MAXLEN, clear, 0)

    def emit(slab, carry):
        at = pl.multiple_of(slab * slab_rows, slab_rows)
        if paired:
            half = tall // 2
            one = pl.ds(at, half)
            two = pl.ds(pl.multiple_of(at + half, 8), half)
            tiles = join_pair([rows[one, :] for rows in x_rows], [rows[two, :] for rows in x_rows])
            tiles = tiles + (context_rows[one, :], context_rows[two, :])
        else:
            tiles = [rows[pl.ds(at, tall), :] for rows in x_rows + (context_rows,)]
        for index, tile in enumerate(tiles):
            out_ref[slab, :, index * LANES : (index + 1) * LANES] = tile.astype(jnp.bfloat16)
        return carry

    lax.fori_loop(0, slabs, emit, 0)


def place(after, x_slots, context_slots, slabs, slab_rows, features):
    count = context_slots.shape[0]
    paired = pairable(features)
    tiles = len(lane_tiles(features))
    tall = slab_rows + 2 * HALO
    shape = (slabs, tall, (tiles + 1) * LANES)
    if paired:
        shape = (slabs, tall // 2, 2 * features + 2 * LANES)
    return pl.pallas_call(
        functools.partial(place_kernel, paired),
        out_shape=jax.ShapeDtypeStruct(shape, jnp.bfloat16),
        in_specs=[smem_spec(), whole_spec(), whole_spec()],
        out_specs=whole_spec(),
        scratch_shapes=[pltpu.VMEM((count * MAXLEN + HALO + MAXLEN, LANES), jnp.float32)]
        * (tiles + 1),
        compiler_params=params(),
    )(after, x_slots, context_slots)


def unplace_kernel(moved_ref, x_ref, context_ref):
    slabs, rows, _ = moved_ref.shape
    step = 16
    span = 3 * LANES

    def chunk(index, carry):
        at = pl.multiple_of(index * step, step)

        def load(slab, tile):
            cells = moved_ref[slab, pl.ds(at, step), tile * LANES : (tile + 1) * LANES]
            return cells.astype(jnp.float32)

        for pair in range(slabs // 2):
            split = [
                split_pair([load(2 * pair + member, tile) for tile in range(3)])
                for member in range(2)
            ]
            for side in range(2):
                to = pl.ds(pl.multiple_of(at + side * rows, step), step)
                for tile, cells in enumerate(join_pair(split[0][side], split[1][side])):
                    first = pair * span + tile * LANES
                    x_ref[to, first : first + LANES] = cells.astype(jnp.bfloat16)
        for slab in range(slabs):
            for side in range(2):
                to = pl.ds(pl.multiple_of(at + side * rows, step), step)
                first = span + side * LANES
                context_ref[to, slab * LANES : (slab + 1) * LANES] = moved_ref[
                    slab, pl.ds(at, step), first : first + LANES
                ]
        return carry

    lax.fori_loop(0, rows // step, chunk, 0)


def unplace(moved, features, context_width):
    slabs, rows, _ = moved.shape
    if not (pairable(features) and context_width == LANES):
        first = len(lane_tiles(features)) * LANES
        x = moved[:, :, :features].transpose(1, 0, 2).reshape(rows, -1)
        context = moved[:, :, first : first + context_width]
        return x, context.transpose(1, 0, 2).reshape(rows, -1)
    return pl.pallas_call(
        unplace_kernel,
        out_shape=(
            jax.ShapeDtypeStruct((2 * rows, slabs * features), jnp.bfloat16),
            jax.ShapeDtypeStruct((2 * rows, slabs * context_width), jnp.bfloat16),
        ),
        in_specs=[whole_spec()],
        out_specs=(whole_spec(), whole_spec()),
        compiler_params=params(),
    )(moved)


def conv_kernel(
    uniform_ref, gated_ref, segment_ref, taps_ref, scale_ref, shift_ref, out_ref, wide
):
    wide[...] = gated_ref[...].astype(jnp.float32)
    edge = HALO - HALF
    scale = scale_ref[...]
    shift = shift_ref[...]
    for chunk in range(out_ref.shape[0] // CONV_ROWS):
        base = chunk * CONV_ROWS

        def finish(total):
            affine = total * scale + shift
            out_ref[base : base + CONV_ROWS, :] = (affine * jax.nn.sigmoid(affine)).astype(
                jnp.bfloat16
            )

        @pl.when(uniform_ref[chunk] == 1)
        def _():
            total = jnp.zeros((CONV_ROWS, LANES), jnp.float32)
            for tap in range(KERNEL):
                total = total + wide[pl.ds(base + edge + tap, CONV_ROWS), :] * taps_ref[
                    tap : tap + 1, :
                ]
            finish(total)

        @pl.when(uniform_ref[chunk] == 0)
        def _():
            centre = segment_ref[pl.ds(base + HALO, CONV_ROWS), :]
            total = jnp.zeros((CONV_ROWS, LANES), jnp.float32)
            for tap in range(KERNEL):
                same = segment_ref[pl.ds(base + edge + tap, CONV_ROWS), :] == centre
                term = jnp.where(same, wide[pl.ds(base + edge + tap, CONV_ROWS), :], 0.0)
                total = total + term * taps_ref[tap : tap + 1, :]
            finish(total)


def convolve(gated_rows, segment, conv_taps, batch_scale, batch_shift):
    tall, width = gated_rows.shape
    rows = tall - 2 * HALO
    chunks = rows // CONV_ROWS
    windows = [segment[c * CONV_ROWS : c * CONV_ROWS + CONV_ROWS + 2 * HALO] for c in range(chunks)]
    windows = jnp.stack(windows)
    uniform = jnp.all(windows == windows[:, :1], axis=1).astype(jnp.int32)
    wide_segment = jnp.broadcast_to(segment[:, None], (tall, LANES))
    return pl.pallas_call(
        conv_kernel,
        grid=(width // LANES,),
        out_shape=jax.ShapeDtypeStruct((rows, width), jnp.bfloat16),
        in_specs=[
            smem_spec(),
            pl.BlockSpec((tall, LANES), lambda i: (0, i)),
            pl.BlockSpec((tall, LANES), lambda i: (0, 0)),
            pl.BlockSpec((KERNEL, LANES), lambda i: (0, i)),
            pl.BlockSpec((1, LANES), lambda i: (0, i)),
            pl.BlockSpec((1, LANES), lambda i: (0, i)),
        ],
        out_specs=pl.BlockSpec((rows, LANES), lambda i: (0, i)),
        scratch_shapes=[pltpu.VMEM((tall, LANES), jnp.float32)],
        compiler_params=params(),
        cost_estimate=pl.CostEstimate(
            flops=2 * rows * width * KERNEL, bytes_accessed=4 * rows * width, transcendentals=0
        ),
    )(
        uniform,
        gated_rows,
        wide_segment,
        conv_taps,
        batch_scale[None, :],
        batch_shift[None, :],
    )


MESH = pl.DeviceIdType.MESH
OUT, GLU_ONE, GLU_TWO, DOWN = range(4)


def any_spec():
    return pl.BlockSpec(memory_space=pl.ANY)


class Place:
    def __init__(self):
        self.dp = lax.axis_index("dp")
        self.mp = lax.axis_index("mp")
        self.y, self.c = self.dp // 2, self.dp % 2
        self.z, self.x = self.mp // 2, self.mp % 2
        self.across = 1 - self.x
        self.near = self.z + 1 - 2 * (self.z % 2)
        self.far_one = 2 - self.z // 2
        self.far_two = 3 - 3 * (self.z // 2)

    def x_side(self):
        return (self.dp, 2 * self.z + self.across)

    def y_side(self):
        return (2 * (1 - self.y) + self.c, self.mp)

    def core_side(self):
        return (2 * self.y + 1 - self.c, self.mp)

    def corner(self):
        return (2 * (1 - self.y) + 1 - self.c, self.mp)

    def above(self):
        return (self.dp, self.mp + 2)

    def below(self):
        return (self.dp, self.mp - 2)


def aligned(index, step):
    return pl.multiple_of(index * step, step)


def piece(weights, kind, z, x, y, c, both_y=False):
    shard = 2 * z + x
    if kind == OUT:
        return weights[0].at[pl.ds(aligned(shard, 192), 192), pl.ds(aligned(c, 512), 512)]
    if kind == GLU_ONE:
        return weights[1].at[pl.ds(aligned(c, 256), 256), pl.ds(aligned(shard, 384), 384)]
    if kind == GLU_TWO:
        if both_y:
            rows = pl.ds(pl.multiple_of(512 + c * 512, 256), 512)
        else:
            rows = pl.ds(pl.multiple_of(512 + (c * 2 + y) * 256, 256), 256)
        return weights[1].at[rows, pl.ds(aligned(shard, 384), 384)]
    if both_y:
        columns = pl.ds(aligned(c, 768), 768)
    else:
        columns = pl.ds(aligned(c * 2 + y, 384), 384)
    return weights[2].at[pl.ds(aligned(shard, 192), 192), columns]


def own_piece(shards, kind, y, c):
    if kind == OUT:
        return shards[0].at[:, pl.ds(aligned(c, 512), 512)]
    if kind == GLU_ONE:
        return shards[1].at[pl.ds(aligned(c, 256), 256), :]
    if kind == GLU_TWO:
        return shards[1].at[pl.ds(pl.multiple_of(512 + (c * 2 + y) * 256, 256), 256), :]
    return shards[2].at[:, pl.ds(aligned(c * 2 + y, 384), 384)]


class Mail:
    def __init__(self, send_sems, recv_sems):
        self.send_sems, self.recv_sems = send_sems, recv_sems
        self.used = 0
        self.sent = []

    def slot(self):
        self.used += 1
        return self.used - 1

    def copy(self, slot, source, target, device):
        return pltpu.make_async_remote_copy(
            src_ref=source,
            dst_ref=target,
            send_sem=self.send_sems.at[slot],
            recv_sem=self.recv_sems.at[slot],
            device_id=device,
            device_id_type=MESH,
        )

    def send(self, slot, source, target, device, when=None):
        copy = self.copy(slot, source, target, device)
        run_if(when, copy.start)
        self.sent.append((copy, when))

    def receive(self, slot, target, device, when=None):
        run_if(when, self.copy(slot, target, target, device).wait_recv)

    def finish(self):
        for copy, when in self.sent:
            run_if(when, copy.wait_send)


def run_if(when, action):
    if when is None:
        action()
    else:
        pl.when(when)(action)


def greet(devices):
    barrier = pltpu.get_barrier_semaphore()

    def hello(device):
        pl.semaphore_signal(barrier, inc=1, device_id=device, device_id_type=MESH)

    count = 0
    for device, when in devices:
        if when is None:
            hello(device)
            count = count + 1
        else:
            pl.when(when)(functools.partial(hello, device))
            count = count + when.astype(jnp.int32)
    pl.semaphore_wait(barrier, count)


KINDS = (GLU_ONE, OUT, GLU_TWO, DOWN)
FIRST = (GLU_TWO, OUT, GLU_ONE)


def find_slots(dp, lengths_ref, assignment_ref, start_ref, span_ref):
    groups = start_ref.shape[0] // PIECES
    per_group = lengths_ref.shape[0] // groups
    zero = jnp.int32(0)
    counts = [zero] * groups
    starts = [zero] * (groups * PIECES)
    spans = [zero] * (groups * PIECES)
    before = zero
    for i in range(per_group):
        target = assignment_ref[dp * per_group + i]
        length = lengths_ref[dp * per_group + i]
        for group in range(groups):
            hit = target == group
            for rank in range(PIECES):
                slot = group * PIECES + rank
                found = hit & (counts[group] == rank)
                starts[slot] = jnp.where(found, before, starts[slot])
                spans[slot] = jnp.where(found, length, spans[slot])
            counts[group] = counts[group] + hit.astype(jnp.int32)
        before = before + length
    for slot in range(groups * PIECES):
        start_ref[slot] = starts[slot]
        span_ref[slot] = spans[slot]


def move_kernel(
    lengths_ref,
    assignment_ref,
    q_ref,
    k_ref,
    v_ref,
    residual_ref,
    out_shard,
    glu_shard,
    down_shard,
    x_got,
    context_got,
    out_all,
    glu_all,
    down_all,
    q_rows,
    k_rows,
    v_rows,
    x_low,
    x_high,
    x_send,
    context_send,
    out_held,
    glu_held,
    down_held,
    start_ref,
    span_ref,
    send_sems,
    recv_sems,
    local_sems,
):
    here = Place()
    z, x, y, c = here.z, here.x, here.y, here.c
    weights = (out_all, glu_all, down_all)
    shards = (out_shard, glu_shard, down_shard)
    held = (out_held, glu_held, down_held)
    mail = Mail(send_sems, recv_sems)
    up, down = z < 3, z > 0
    partners = (here.y_side(), here.corner(), here.core_side())
    greet(
        [(device, None) for device in partners + (here.x_side(),)]
        + [(here.above(), up), (here.below(), down)]
    )

    def spot(kind, zz, xx):
        return piece(weights, kind, zz, xx, y, c)

    own = (
        out_all.at[pl.ds(aligned(here.mp, 192), 192), :],
        glu_all.at[:, pl.ds(aligned(here.mp, 384), 384)],
        down_all.at[pl.ds(aligned(here.mp, 192), 192), :],
    )
    into = [
        pltpu.make_async_copy(shards[i], held[i], local_sems.at[i]) for i in range(3)
    ]
    locals_ = [pltpu.make_async_copy(held[i], own[i], local_sems.at[5 + i]) for i in range(3)]
    slots_up, slots_down, slots_x, slots_near = [
        {kind: mail.slot() for kind in KINDS} for _ in range(4)
    ]
    slots_up_two, slots_down_two = [{kind: mail.slot() for kind in KINDS} for _ in range(2)]
    for kind in KINDS:
        mine = own_piece(shards, kind, y, c)
        mail.send(slots_up[kind], mine, spot(kind, z, x), here.above(), up)
        mail.send(slots_down[kind], mine, spot(kind, z, x), here.below(), down)
        mail.send(slots_x[kind], mine, spot(kind, z, x), here.x_side())
    for copy in into:
        copy.start()
    find_slots(here.dp, lengths_ref, assignment_ref, start_ref, span_ref)

    count = 4 * residual_ref.shape[0]
    step = 128
    low = lax.broadcasted_iota(jnp.int32, (step, LANES), 1) < HD

    def open_rows(chunk, carry):
        first = pl.multiple_of(chunk * step, step)
        cells = [
            residual_ref[pl.ds(first, step), i * LANES : (i + 1) * LANES].astype(jnp.float32)
            for i in range(6)
        ]
        turned = [pltpu.roll(cells[i], HD, 1) for i in (1, 2, 4, 5)]
        frames = (
            (cells[0], cells[1]),
            (jnp.where(low, turned[0], turned[1]), turned[1]),
            (cells[3], cells[4]),
            (jnp.where(low, turned[2], turned[3]), turned[3]),
        )
        for j, (one, two) in enumerate(frames):
            at = pl.ds(4 * first + j, step, stride=4)
            x_low[at, :] = one
            x_high[at, :] = two
        return carry

    lax.fori_loop(0, residual_ref.shape[0] // step, open_rows, 0)
    for rows in (x_low, x_high):
        rows[pl.ds(count, MAXLEN), :] = jnp.zeros((MAXLEN, LANES), jnp.float32)

    targets = partners + ((here.dp, here.mp),)
    half = PIECES // 2
    x_slots = [mail.slot() for _ in partners]
    context_slots = [mail.slot() for _ in partners]
    for index, target in enumerate(targets):
        group = target[0]

        def fill(pair, carry):
            at = group * half + pair
            both = [
                [
                    rows[pl.ds(start_ref[2 * at + side], MAXLEN), :]
                    for rows in (x_low, x_high)
                ]
                for side in range(2)
            ]
            for tile, cells in enumerate(join_pair(*both)):
                x_send[at, :, tile * LANES : (tile + 1) * LANES] = cells.astype(jnp.bfloat16)
            return carry

        lax.fori_loop(0, half, fill, 0)
        source = x_send.at[pl.ds(group * half, half)]
        landing = x_got.at[pl.ds(here.dp * half, half)]
        if index < 3:
            mail.send(x_slots[index], source, landing, target)
        else:
            copy = pltpu.make_async_copy(source, landing, local_sems.at[3])
            copy.start()
            locals_.append(copy)

    for copy_in, copy_out in zip(into, locals_):
        copy_in.wait()
        copy_out.start()

    pairs = q_ref.shape[0]
    wide_low = lax.broadcasted_iota(jnp.int32, (256, LANES), 1) < HD

    def unpack(chunk, carry):
        first = pl.multiple_of(chunk * 256, 256)
        for packed, rows in ((q_ref, q_rows), (k_ref, k_rows), (v_ref, v_rows)):
            one = packed[pl.ds(first, 256), 0:LANES].astype(jnp.float32)
            two = packed[pl.ds(first, 256), LANES : 2 * LANES].astype(jnp.float32)
            rows[pl.ds(2 * first, 256, stride=2), :] = jnp.where(
                wide_low, one, pltpu.roll(two, HD, 1)
            )
            rows[pl.ds(2 * first + 1, 256, stride=2), :] = jnp.where(
                wide_low, pltpu.roll(one, HD, 1), two
            )
        return carry

    lax.fori_loop(0, pairs // 256, unpack, 0)
    for rows in (q_rows, k_rows, v_rows):
        rows[pl.ds(2 * pairs, MAXLEN), :] = jnp.zeros((MAXLEN, LANES), jnp.float32)

    column = lax.broadcasted_iota(jnp.int32, (MAXLEN, MAXLEN), 1)
    head_lane = lax.broadcasted_iota(jnp.int32, (MAXLEN, LANES), 1) // HD

    def attend_slot(slot):
        start = start_ref[slot]
        allowed = column < span_ref[slot]
        queries = q_rows[pl.ds(start, MAXLEN), :]
        keys = k_rows[pl.ds(start, MAXLEN), :].astype(jnp.bfloat16)
        values = v_rows[pl.ds(start, MAXLEN), :].astype(jnp.bfloat16)
        result = None
        for head in range(2):
            own = jnp.where(head_lane == head, queries, 0.0).astype(jnp.bfloat16)
            scores = (
                lax.dot_general(
                    own, keys, (((1,), (1,)), ((), ())), preferred_element_type=jnp.float32
                )
                * HD ** (-0.5)
            )
            scores = jnp.where(allowed, scores, MASKED)
            highest = jnp.max(scores, axis=1, keepdims=True)
            exponentials = jnp.exp(scores - highest)
            denominator = jnp.sum(exponentials, axis=1, keepdims=True)
            weighing = (exponentials / denominator).astype(jnp.bfloat16)
            blended = jnp.dot(weighing, values, preferred_element_type=jnp.float32)
            result = blended if head == 0 else jnp.where(head_lane == head, blended, result)
        context_send[slot] = result.astype(jnp.bfloat16)

    def relay(kind):
        mail.receive(slots_up[kind], spot(kind, z - 1, x), here.above(), down)
        mail.send(
            slots_up_two[kind],
            spot(kind, z - 1, x),
            spot(kind, z - 1, x),
            here.above(),
            up & down,
        )
        mail.receive(slots_down[kind], spot(kind, z + 1, x), here.below(), up)
        mail.send(
            slots_down_two[kind],
            spot(kind, z + 1, x),
            spot(kind, z + 1, x),
            here.below(),
            up & down,
        )
        mail.send(
            slots_near[kind],
            spot(kind, here.near, x),
            spot(kind, here.near, x),
            here.x_side(),
        )

    for index, target in enumerate(targets):
        group = target[0]

        def attend_one(rank, carry):
            attend_slot(group * PIECES + rank)
            return carry

        lax.fori_loop(0, PIECES, attend_one, 0)
        source = context_send.at[pl.ds(group * PIECES, PIECES)]
        landing = context_got.at[pl.ds(here.dp * PIECES, PIECES)]
        if index < 3:
            mail.send(context_slots[index], source, landing, target)
        else:
            copy = pltpu.make_async_copy(source, landing, local_sems.at[4])
            copy.start()
            locals_.append(copy)
        relay(KINDS[index])

    for index, source in enumerate(partners):
        mail.receive(x_slots[index], x_got.at[pl.ds(source[0] * half, half)], source)
        mail.receive(
            context_slots[index], context_got.at[pl.ds(source[0] * PIECES, PIECES)], source
        )
    for kind in KINDS:
        mail.receive(slots_x[kind], spot(kind, z, here.across), here.x_side())
        mail.receive(slots_near[kind], spot(kind, here.near, here.across), here.x_side())
        mail.receive(slots_up_two[kind], spot(kind, z - 2, x), here.above(), z > 1)
        mail.receive(slots_down_two[kind], spot(kind, z + 2, x), here.below(), z < 2)
    mail.finish()
    for copy in locals_:
        copy.wait()


def move(lengths, assignment, queries, keys, values, residual, out_shard, glu_shard, down_shard):
    slots = 4 * PIECES
    pairs = queries.shape[0]
    count = 4 * residual.shape[0]
    bf16 = jnp.bfloat16
    return pl.pallas_call(
        move_kernel,
        out_shape=(
            jax.ShapeDtypeStruct((slots // 2, MAXLEN, 3 * LANES), bf16),
            jax.ShapeDtypeStruct((slots, MAXLEN, LANES), bf16),
            jax.ShapeDtypeStruct((1536, 1024), bf16),
            jax.ShapeDtypeStruct((1536, 3072), bf16),
            jax.ShapeDtypeStruct((1536, 1536), bf16),
        ),
        in_specs=[smem_spec()] * 2 + [whole_spec()] * 4 + [any_spec()] * 3,
        out_specs=(any_spec(),) * 5,
        scratch_shapes=[pltpu.VMEM((2 * pairs + MAXLEN, LANES), jnp.float32)] * 3
        + [pltpu.VMEM((count + MAXLEN, LANES), jnp.float32)] * 2
        + [
            pltpu.VMEM((slots // 2, MAXLEN, 3 * LANES), bf16),
            pltpu.VMEM((slots, MAXLEN, LANES), bf16),
            pltpu.VMEM(out_shard.shape, bf16),
            pltpu.VMEM(glu_shard.shape, bf16),
            pltpu.VMEM(down_shard.shape, bf16),
            pltpu.SMEM((slots,), jnp.int32),
            pltpu.SMEM((slots,), jnp.int32),
            pltpu.SemaphoreType.DMA((30,)),
            pltpu.SemaphoreType.DMA((30,)),
            pltpu.SemaphoreType.DMA((8,)),
        ],
        compiler_params=pltpu.CompilerParams(
            vmem_limit_bytes=VMEM_LIMIT, collective_id=1, has_side_effects=True
        ),
        cost_estimate=pl.CostEstimate(
            flops=slots * 2 * MAXLEN * MAXLEN * LANES * 4,
            bytes_accessed=50 * 1024 * 1024,
            transcendentals=slots * 2 * MAXLEN * MAXLEN,
        ),
    )(lengths, assignment, queries, keys, values, residual, out_shard, glu_shard, down_shard)


SPLIT = 288
PARTS = ((0, SPLIT // 2, 0, SPLIT - 2 * HALO), (SPLIT, 272 - SPLIT // 2, SPLIT - 2 * HALO, 544 - SPLIT))
ROW_STEP = 32
EXCHANGE_ORDER = ((3, 1), (3, 0), (2, 0), (2, 1), (1, 0), (1, 1), (0, 1))


def place_parts_kernel(
    lengths_ref, assignment_ref, x_ref, context_ref, out_ref, after_ref, context_rows, *x_rows
):
    dp = lax.axis_index("dp")
    after_ref[0] = 0

    def seek(u, carry):
        count, total = carry
        hit = assignment_ref[u] == dp
        total = total + jnp.where(hit, lengths_ref[u], 0)
        count = count + hit.astype(jnp.int32)
        after_ref[count] = total
        return count, total

    lax.fori_loop(0, lengths_ref.shape[0], seek, (jnp.int32(0), jnp.int32(0)))
    slots = context_ref.shape[0]
    slabs = out_ref.shape[0]
    tall = out_ref.shape[1] * 2
    slab_rows = tall - 2 * HALO
    total_rows = context_rows.shape[0]
    held = (context_rows,) + x_rows
    zeros = jnp.zeros((MAXLEN, LANES), jnp.float32)
    for rows in held:
        rows[pl.ds(0, HALO), :] = jnp.zeros((HALO, LANES), jnp.float32)

    def load(ref, slot, tile):
        return ref[slot, :, tile * LANES : (tile + 1) * LANES].astype(jnp.float32)

    def put(step, carry):
        sides = split_pair([load(x_ref, step, tile) for tile in range(3)])
        for side in range(2):
            slot = 2 * step + side
            where = pl.ds(HALO + after_ref[slot], MAXLEN)
            for rows, piece in zip(x_rows, sides[side]):
                rows[where, :] = piece
            context_rows[where, :] = load(context_ref, slot, 0)
        return carry

    lax.fori_loop(0, x_ref.shape[0], put, 0)
    live = after_ref[slots]

    def clear(step, carry):
        at = jnp.minimum(HALO + live + step * MAXLEN, total_rows - MAXLEN)
        for rows in held:
            rows[pl.ds(at, MAXLEN), :] = zeros
        return carry

    lax.fori_loop(0, (total_rows - HALO - live + MAXLEN - 1) // MAXLEN, clear, 0)

    def emit(slab, carry):
        at = pl.multiple_of(slab * slab_rows, slab_rows)
        for first, half, *_ in PARTS:
            one = pl.ds(pl.multiple_of(at + first, 16), half)
            two = pl.ds(pl.multiple_of(at + first + half, 16), half)
            tiles = join_pair(
                [rows[one, :] for rows in x_rows], [rows[two, :] for rows in x_rows]
            )
            tiles = tiles + (context_rows[one, :], context_rows[two, :])
            for index, tile in enumerate(tiles):
                lanes = slice(index * LANES, (index + 1) * LANES)
                out_ref[slab, first // 2 : first // 2 + half, lanes] = tile.astype(
                    jnp.bfloat16
                )
        return carry

    lax.fori_loop(0, slabs, emit, 0)


def place_parts(lengths, assignment, x_slots, context_slots, slabs):
    count = context_slots.shape[0]
    return pl.pallas_call(
        place_parts_kernel,
        out_shape=(
            jax.ShapeDtypeStruct((slabs, 272, 5 * LANES), jnp.bfloat16),
            jax.ShapeDtypeStruct((count + 1,), jnp.int32),
        ),
        in_specs=[smem_spec()] * 2 + [whole_spec()] * 2,
        out_specs=(whole_spec(), smem_spec()),
        scratch_shapes=[pltpu.VMEM((count * MAXLEN + HALO + MAXLEN, LANES), jnp.float32)] * 3,
        compiler_params=params(),
    )(lengths, assignment, x_slots, context_slots)


def finish_kernel(
    after_ref,
    slabs_ref,
    gain_ref,
    bias_ref,
    scale_ref,
    shift_ref,
    taps_ref,
    out_in,
    glu_in,
    down_in,
    encoded_ref,
    out_all,
    glu_all,
    down_all,
    moved,
    carried,
    context,
    normed,
    wide,
    swished,
    first_tap,
    last_tap,
    out_held,
    glu_held,
    down_held,
    send_sems,
    recv_sems,
    local_sems,
):
    here = Place()
    z, x, y, c = here.z, here.x, here.y, here.c
    weights = (out_all, glu_all, down_all)
    mail = Mail(send_sems, recv_sems)
    slabs = slabs_ref.shape[0]
    mirrors = (z, here.near, z + 2 - 4 * (z // 2), 3 - z)
    sides = (x, here.across)
    others = [(here.dp, 2 * mirrors[dz] + sides[dx]) for dz, dx in EXCHANGE_ORDER]
    greet([(device, None) for device in others + [here.y_side(), here.core_side()]])

    slab_slots = [[mail.slot() for _ in others] for _ in PARTS]

    def part_rows(part):
        first, half, *_ = PARTS[part]
        return pl.ds(first // 2, half)

    def exchange(part, crossing):
        for index, device in enumerate(others):
            if EXCHANGE_ORDER[index][1] != crossing:
                continue
            mail.send(
                slab_slots[part][index],
                slabs_ref.at[device[1], part_rows(part)],
                moved.at[here.mp, part_rows(part)],
                device,
            )

    def exchanged(part):
        for index in range(len(others)):
            mail.receive(
                slab_slots[part][index],
                moved.at[others[index][1], part_rows(part)],
                others[index],
            )

    tile_width = 256
    tiles = carried.shape[1] // tile_width
    keep = pltpu.make_async_copy(slabs_ref.at[here.mp], moved.at[here.mp], local_sems.at[0])
    keep.start()

    def spot(kind, zz, xx):
        return piece(weights, kind, zz, xx, y, c)

    table = {}

    def slot(*key):
        if key not in table:
            table[key] = mail.slot()
        return table[key]

    def pass_on(name, kind, zz, xx, device, when=None):
        where = spot(kind, zz, xx)
        mail.send(slot(name, kind), where, where, device, when)

    cells = {
        "own near": (here.near, x),
        "own one": (here.far_one, x),
        "own two": (here.far_two, x),
        "other own": (z, here.across),
        "other near": (here.near, here.across),
        "other one": (here.far_one, here.across),
        "other two": (here.far_two, here.across),
    }
    early = ("own near", "own one", "other own", "other near")
    order = early + ("other one", "own two", "other two")

    def after(kind, cell):
        if kind in (OUT, GLU_ONE):
            pass_on("core " + cell, kind, *cells[cell], here.core_side())
        else:
            pass_on("y " + cell, kind, *cells[cell], here.y_side())

    def from_y(kind):
        for cell in order:
            mail.receive(
                slot("y " + cell, kind),
                piece(weights, kind, *cells[cell], 1 - y, c),
                here.y_side(),
            )
            where = piece(weights, kind, *cells[cell], y, c, both_y=True)
            mail.send(slot("core " + cell, kind), where, where, here.core_side())

    def from_core(kind):
        for cell in order:
            where = piece(weights, kind, *cells[cell], y, 1 - c, both_y=kind in (GLU_TWO, DOWN))
            mail.receive(slot("core " + cell, kind), where, here.core_side())

    def start_across(kinds):
        for kind in kinds:
            pass_on("third up", kind, 0, x, here.above(), z == 2)
            pass_on("third down", kind, 3, x, here.below(), z == 1)
            pass_on("x one", kind, here.far_one, x, here.x_side())
        for kind in kinds:
            for cell in early:
                after(kind, cell)

    def across_one(kinds):
        for kind in kinds:
            mail.receive(slot("x one", kind), spot(kind, *cells["other one"]), here.x_side())
            after(kind, "other one")
        for kind in kinds:
            mail.receive(slot("third up", kind), spot(kind, 0, x), here.above(), z == 3)
            mail.receive(slot("third down", kind), spot(kind, 3, x), here.below(), z == 0)
            pass_on("x two", kind, here.far_two, x, here.x_side())
            after(kind, "own two")

    def across_two(kinds):
        for kind in kinds:
            mail.receive(slot("x two", kind), spot(kind, *cells["other two"]), here.x_side())
            after(kind, "other two")

    start_across(FIRST)
    exchange(0, 0)
    live = after_ref[4 * PIECES]

    def bounds(step, carry):
        rows = pl.ds(pl.multiple_of(step * 64, 64), 64)
        position = (
            lax.broadcasted_iota(jnp.int32, (64, LANES), 0)
            + step * 64
            + here.mp * encoded_ref.shape[0]
        )
        begin = jnp.zeros((64, LANES), jnp.int32)
        end = jnp.full((64, LANES), live, jnp.int32)
        for k in range(1, 4 * PIECES):
            begin = jnp.where(position >= after_ref[k], after_ref[k], begin)
        for k in range(4 * PIECES - 1, 0, -1):
            end = jnp.where(position < after_ref[k], after_ref[k], end)
        first_tap[rows, :] = HALF + begin - position
        last_tap[rows, :] = HALF - 1 + end - position
        return carry

    lax.fori_loop(0, encoded_ref.shape[0] // 64, bounds, 0)

    across_one(FIRST)
    exchange(0, 1)
    start_across((DOWN,))
    exchange(1, 0)
    exchange(1, 1)
    across_two(FIRST)
    from_y(GLU_TWO)
    loads = [
        pltpu.make_async_copy(weights[i], (out_held, glu_held, down_held)[i], local_sems.at[1 + i])
        for i in range(3)
    ]

    def glu_load(n, side):
        columns = pl.ds(aligned(n + side * tiles, tile_width), tile_width)
        return pltpu.make_async_copy(
            weights[1].at[:, columns],
            glu_held.at[:, columns],
            local_sems.at[4 + 2 * n + side],
        )

    from_core(OUT)
    loads[0].start()

    def open_part(part):
        first, half, *_ = PARTS[part]

        def chunk(index, carry):
            at = pl.ds(pl.multiple_of(first // 2 + index * 16, 16), 16)

            def load(slab, tile):
                cells_ = moved[slab, at, tile * LANES : (tile + 1) * LANES]
                return cells_.astype(jnp.float32)

            to = [pl.ds(pl.multiple_of(first + s * half + index * 16, 16), 16) for s in range(2)]
            near = [pl.ds(pl.multiple_of(s * half + index * 16, 16), 16) for s in range(2)]
            for pair in range(slabs // 2):
                split = [
                    split_pair([load(2 * pair + member, tile) for tile in range(3)])
                    for member in range(2)
                ]
                for side in range(2):
                    for tile, cells_ in enumerate(join_pair(split[0][side], split[1][side])):
                        begin = (3 * pair + tile) * LANES
                        carried[to[side], begin : begin + LANES] = cells_
            for slab in range(slabs):
                for side in range(2):
                    begin = (3 + side) * LANES
                    context[near[side], slab * LANES : (slab + 1) * LANES] = moved[
                        slab, at, begin : begin + LANES
                    ]
            return carry

        lax.fori_loop(0, half // 16, chunk, 0)

    def attach(part):
        first, half, *_ = PARTS[part]

        def tile(n, carry):
            columns = pl.ds(aligned(n, tile_width), tile_width)
            carried[first : first + 2 * half, columns] += lax.dot_general(
                context[0 : 2 * half, :],
                out_held[columns, :],
                (((1,), (1,)), ((), ())),
                preferred_element_type=jnp.float32,
            )
            return carry

        lax.fori_loop(0, tiles, tile, 0)

        def normalise(index, carry):
            at = pl.ds(pl.multiple_of(first + index * 32, 32), 32)
            to = pl.ds(pl.multiple_of(index * 32, 32), 32)
            cells_ = carried[at, :]
            centred = cells_ - jnp.mean(cells_, axis=1, keepdims=True)
            variance = jnp.mean(centred * centred, axis=1, keepdims=True)
            inverse = lax.rsqrt(variance + EPS)
            for i in range(carried.shape[1] // LANES):
                lanes = slice(i * LANES, (i + 1) * LANES)
                scaled = centred[:, lanes] * inverse * gain_ref[i : i + 1, :] + bias_ref[i : i + 1, :]
                normed[to, lanes] = scaled.astype(jnp.bfloat16)
            return carry

        lax.fori_loop(0, 2 * half // 32, normalise, 0)

    def gate(part):
        first, half, *_ = PARTS[part]

        def tile(n, carry):
            columns = pl.ds(aligned(n, tile_width), tile_width)
            if part == 0:
                for side in range(2):
                    glu_load(n, side).wait()
            rows = normed[0 : 2 * half, :]
            value = jnp.dot(rows, glu_held[:, columns], preferred_element_type=jnp.float32)
            gates = jnp.dot(
                rows,
                glu_held[:, pl.ds(aligned(n + tiles, tile_width), tile_width)],
                preferred_element_type=jnp.float32,
            )
            gated = (value * jax.nn.sigmoid(gates)).astype(jnp.bfloat16)
            for side in range(2):
                wide[2 * n + side, first : first + 2 * half, :] = gated[
                    :, side * LANES : (side + 1) * LANES
                ].astype(jnp.float32)
            return carry

        lax.fori_loop(0, tiles, tile, 0)

    def convolve_part(part):
        start, count_rows = PARTS[part][2:]
        steps = count_rows // ROW_STEP
        group = 2
        groups = carried.shape[1] // (group * LANES)

        def body(index, carry):
            row = start + lax.rem(index, steps) * ROW_STEP
            column = index // steps * (group * LANES)
            rows = pl.ds(pl.multiple_of(row, ROW_STEP), ROW_STEP)
            low, high = first_tap[rows, :], last_tap[rows, :]
            lanes = [pl.ds(pl.multiple_of(column + i * LANES, LANES), LANES) for i in range(group)]
            totals = [jnp.zeros((ROW_STEP, LANES), jnp.float32) for _ in range(group)]
            for shift in range(8):
                count = ROW_STEP + (24 if shift < 7 else 16)
                at = pl.ds(row + HALO - HALF + shift, count)
                seen = [wide[column // LANES + i, at, :] for i in range(group)]
                for k in range(4 if shift < 7 else 3):
                    tap = shift + 8 * k
                    if tap < HALF:
                        mask = low <= tap
                    else:
                        mask = high >= tap
                    for i in range(group):
                        term = seen[i][8 * k : 8 * k + ROW_STEP] * taps_ref[tap : tap + 1, lanes[i]]
                        if tap != HALF:
                            term = jnp.where(mask, term, 0.0)
                        totals[i] = totals[i] + term
            for i in range(group):
                one = pl.ds(column // LANES + i, 1)
                affine = totals[i] * scale_ref[one, :] + shift_ref[one, :]
                swished[rows, lanes[i]] = (affine * jax.nn.sigmoid(affine)).astype(jnp.bfloat16)
            return carry

        lax.fori_loop(0, steps * groups, body, 0)

    def lower(part):
        start, count_rows = PARTS[part][2:]
        rows = pl.ds(start, count_rows)

        def tile(n, carry):
            columns = pl.ds(aligned(n, tile_width), tile_width)
            total = carried[start + HALO : start + HALO + count_rows, columns] + lax.dot_general(
                swished[rows, :],
                down_held[columns, :],
                (((1,), (1,)), ((), ())),
                preferred_element_type=jnp.float32,
            )
            alive = last_tap[rows, :] >= HALF
            for side in range(2):
                lane = pl.ds(pl.multiple_of(n * tile_width + side * LANES, LANES), LANES)
                encoded_ref[rows, lane] = jnp.where(
                    alive, total[:, side * LANES : (side + 1) * LANES], 0.0
                ).astype(jnp.bfloat16)
            return carry

        lax.fori_loop(0, tiles, tile, 0)

    keep.wait()
    exchanged(0)
    open_part(0)
    loads[0].wait()
    attach(0)
    from_core(GLU_ONE)
    from_core(GLU_TWO)
    for n in range(tiles):
        for side in range(2):
            glu_load(n, side).start()
    gate(0)
    across_one((DOWN,))
    convolve_part(0)
    across_two((DOWN,))
    exchanged(1)
    open_part(1)
    attach(1)
    from_y(DOWN)
    gate(1)
    from_core(DOWN)
    loads[2].start()
    convolve_part(1)
    loads[2].wait()
    lower(0)
    lower(1)
    mail.finish()


def finish(after, slabs, norm, taps, out_all, glu_all, down_all):
    norm = [a.reshape(-1, LANES) for a in norm]
    bf16, f32 = jnp.bfloat16, jnp.float32
    width = taps.shape[1]
    rows = 512
    tall = rows + 2 * HALO
    weights = (out_all, glu_all, down_all)
    return pl.pallas_call(
        finish_kernel,
        out_shape=(jax.ShapeDtypeStruct((rows, width), bf16),)
        + tuple(jax.ShapeDtypeStruct(a.shape, a.dtype) for a in weights),
        in_specs=[smem_spec(), any_spec()] + [whole_spec()] * 5 + [any_spec()] * 3,
        out_specs=(whole_spec(),) + (any_spec(),) * 3,
        input_output_aliases={7: 1, 8: 2, 9: 3},
        scratch_shapes=[
            pltpu.VMEM(slabs.shape, bf16),
            pltpu.VMEM((tall, width), f32),
            pltpu.VMEM((SPLIT, 1024), bf16),
            pltpu.VMEM((SPLIT, width), bf16),
            pltpu.VMEM((width // LANES, tall, LANES), f32),
            pltpu.VMEM((rows, width), bf16),
            pltpu.VMEM((rows, LANES), jnp.int32),
            pltpu.VMEM((rows, LANES), jnp.int32),
        ]
        + [pltpu.VMEM(a.shape, bf16) for a in weights]
        + [
            pltpu.SemaphoreType.DMA((80,)),
            pltpu.SemaphoreType.DMA((80,)),
            pltpu.SemaphoreType.DMA((16,)),
        ],
        compiler_params=pltpu.CompilerParams(
            vmem_limit_bytes=VMEM_LIMIT, collective_id=2, has_side_effects=True
        ),
    )(after, slabs, *norm, taps, *weights)[0]


def on_device(
    query_rows,
    key_rows,
    value_rows,
    residual,
    lengths,
    assignment,
    out_proj,
    norm_gain,
    norm_bias,
    glu_proj,
    conv_taps,
    batch_scale,
    batch_shift,
    down_proj,
):
    data_group = lax.axis_index("dp")
    slab_index = lax.axis_index("mp")
    groups = lax.axis_size("dp")
    slabs = lax.axis_size("mp")
    group_rows = query_rows.shape[0] * 2
    slab_rows = group_rows // slabs
    total_utterances = lengths.shape[0]
    per_group = total_utterances // groups
    slots = groups * PIECES
    features = residual.shape[2] // 4

    fits = (
        (groups, slabs) == (4, 8)
        and query_rows.shape == (2048, 2, LANES)
        and residual.shape == (1024, 1, 768)
    )
    if fits:
        flat = [a.reshape(2048, 2 * LANES) for a in (query_rows, key_rows, value_rows)]
        x_slots, context_slots, *weights = move(
            lengths, assignment, *flat, residual.reshape(1024, 768), out_proj.T, glu_proj, down_proj.T
        )
        placed, after = place_parts(lengths, assignment, x_slots, context_slots, slabs)
        norm = (norm_gain, norm_bias, batch_scale, batch_shift)
        return finish(after, placed, norm, conv_taps, *weights)

    utterance = jnp.arange(total_utterances, dtype=jnp.int32)
    source = utterance // per_group
    earlier = utterance[None, :] < utterance[:, None]
    same_source = source[None, :] == source[:, None]
    same_target = assignment[None, :] == assignment[:, None]
    before = jnp.sum(jnp.where(earlier & same_source, lengths[None, :], 0), axis=1)
    rank = jnp.sum((earlier & same_source & same_target).astype(jnp.int32), axis=1)
    slot = jnp.arange(slots, dtype=jnp.int32)[:, None]
    leaving = (source[None, :] == data_group) & ((assignment * PIECES + rank)[None, :] == slot)
    start = jnp.sum(jnp.where(leaving, before[None, :], 0), axis=1)
    span = jnp.sum(jnp.where(leaving, lengths[None, :], 0), axis=1)
    coming_earlier = (assignment[None, :] == data_group) & (
        (source * PIECES + rank)[None, :] < jnp.arange(slots + 1, dtype=jnp.int32)[:, None]
    )
    after = jnp.sum(jnp.where(coming_earlier, lengths[None, :], 0), axis=1)
    live = jnp.sum(jnp.where(assignment == data_group, lengths, 0))

    position = jnp.arange(slab_rows + 2 * HALO, dtype=jnp.int32) + slab_index * slab_rows - HALO
    segment = jnp.sum((position[:, None] >= after[None, 1:]).astype(jnp.int32), axis=1)
    segment = jnp.where(position < 0, -2, jnp.where(position < live, segment, -1))
    segment = jnp.where(position >= group_rows, -2, segment)

    residual_rows = (
        residual.reshape(group_rows // 4, 4, features).reshape(group_rows, features)
    )

    def swap(array, axis):
        return lax.all_to_all(array, axis, split_axis=0, concat_axis=0, tiled=True)

    packed, start = lax.optimization_barrier((into_slots(start, residual_rows), start))
    x_slots = swap(packed, "dp")
    context_slots = swap(attend(start, span, query_rows, key_rows, value_rows), "dp")
    moved = swap(place(after, x_slots, context_slots, slabs, slab_rows, features), "mp")
    carried_slab, context_slab = unplace(moved, features, query_rows.shape[1] * HD)

    core = data_group % 2
    partners = [(group, group + 1 - 2 * (group % 2)) for group in range(groups)]

    def gather(weights):
        half = weights.shape[0] // 2
        own = lax.dynamic_slice_in_dim(weights, core * half, half, 0)
        return lax.all_gather(own, "mp", axis=1, tiled=True)

    def both(own):
        return own, lax.ppermute(own, "dp", partners)

    def project(rows, halves_of):
        own, other = halves_of
        half = rows.shape[1] // 2
        low, high = rows[:, :half], rows[:, half:]
        return jnp.dot(
            jnp.where(core == 0, low, high), own, preferred_element_type=jnp.float32
        ) + jnp.dot(jnp.where(core == 0, high, low), other, preferred_element_type=jnp.float32)

    out_halves, glu_halves = both(gather(out_proj)), both(gather(glu_proj))
    down_own = gather(down_proj)
    carried = carried_slab.astype(jnp.float32) + project(context_slab, out_halves)
    average = jnp.mean(carried, axis=1, keepdims=True)
    centred = carried - average
    variance = jnp.mean(centred * centred, axis=1, keepdims=True)
    normed = (centred * lax.rsqrt(variance + EPS) * norm_gain + norm_bias).astype(jnp.bfloat16)
    halves = project(normed, glu_halves)
    feature_count = halves.shape[1] // 2
    gated_rows = (halves[:, :feature_count] * jax.nn.sigmoid(halves[:, feature_count:])).astype(
        jnp.bfloat16
    )
    down_own, gated_rows = lax.optimization_barrier((down_own, gated_rows))
    down_halves = both(down_own)
    swished = convolve(gated_rows, segment, conv_taps, batch_scale, batch_shift)
    lowered = project(swished, down_halves)
    centre_segment = segment[HALO : HALO + slab_rows]
    own_carried = carried[HALO : HALO + slab_rows]
    return jnp.where((centre_segment >= 0)[:, None], own_carried + lowered, 0.0).astype(
        jnp.bfloat16
    )


def solution(mesh):
    in_specs = (
        P("dp", "mp", None),
        P("dp", "mp", None),
        P("dp", "mp", None),
        P("dp", "mp", None),
        P(),
        P(),
        P(None, "mp"),
        P(),
        P(),
        P(None, "mp"),
        P(),
        P(),
        P(),
        P(None, "mp"),
    )
    out_specs = P(("dp", "mp"), None)
    return jax.shard_map(
        on_device, mesh=mesh, in_specs=in_specs, out_specs=out_specs, check_vma=False
    )
```

```python
import functools

import jax
import jax.numpy as jnp
from jax import lax
from jax.experimental import pallas as pl
from jax.experimental.pallas import tpu as pltpu
from jax.sharding import PartitionSpec as P

HD = 64
KERNEL = 31
HALF = 15
MAXLEN = 256
PIECES = 4
LANES = 128
HALO = 16
CONV_ROWS = 64

EPS = 1e-05
MASKED = -1e30
VMEM_LIMIT = 60 * 1024 * 1024


def params():
    return pltpu.CompilerParams(vmem_limit_bytes=VMEM_LIMIT)


def whole_spec():
    return pl.BlockSpec(memory_space=pltpu.VMEM)


def smem_spec():
    return pl.BlockSpec(memory_space=pltpu.SMEM)


def attention_kernel(
    heads, start_ref, span_ref, q_ref, k_ref, v_ref, out_ref, q_rows, k_rows, v_rows
):
    pairs = q_ref.shape[0]
    step = 256
    lane = lax.broadcasted_iota(jnp.int32, (step, LANES), 1)
    low = lane < HD

    def unpack(chunk, carry):
        first = pl.multiple_of(chunk * step, step)
        for packed, rows in ((q_ref, q_rows), (k_ref, k_rows), (v_ref, v_rows)):
            one = packed[pl.ds(first, step), 0:LANES].astype(jnp.float32)
            if heads == 2:
                two = packed[pl.ds(first, step), LANES : 2 * LANES].astype(jnp.float32)
                even = jnp.where(low, one, pltpu.roll(two, HD, 1))
                odd = jnp.where(low, pltpu.roll(one, HD, 1), two)
            else:
                even = one
                odd = pltpu.roll(one, HD, 1)
            rows[pl.ds(2 * first, step, stride=2), :] = even
            rows[pl.ds(2 * first + 1, step, stride=2), :] = odd
        return carry

    lax.fori_loop(0, pairs // step, unpack, 0)
    for rows in (q_rows, k_rows, v_rows):
        rows[pl.ds(2 * pairs, MAXLEN), :] = jnp.zeros((MAXLEN, LANES), jnp.float32)

    column = lax.broadcasted_iota(jnp.int32, (MAXLEN, MAXLEN), 1)
    head_lane = lax.broadcasted_iota(jnp.int32, (MAXLEN, LANES), 1) // HD

    def slot_body(slot, carry):
        start = start_ref[slot]
        allowed = column < span_ref[slot]
        queries = q_rows[pl.ds(start, MAXLEN), :]
        keys = k_rows[pl.ds(start, MAXLEN), :].astype(jnp.bfloat16)
        values = v_rows[pl.ds(start, MAXLEN), :].astype(jnp.bfloat16)
        result = None
        for head in range(heads):
            own = jnp.where(head_lane == head, queries, 0.0).astype(jnp.bfloat16)
            scores = (
                lax.dot_general(
                    own, keys, (((1,), (1,)), ((), ())), preferred_element_type=jnp.float32
                )
                * HD ** (-0.5)
            )
            scores = jnp.where(allowed, scores, MASKED)
            highest = jnp.max(scores, axis=1, keepdims=True)
            exponentials = jnp.exp(scores - highest)
            denominator = jnp.sum(exponentials, axis=1, keepdims=True)
            weights = (exponentials / denominator).astype(jnp.bfloat16)
            blended = jnp.dot(weights, values, preferred_element_type=jnp.float32)
            result = blended if head == 0 else jnp.where(head_lane == head, blended, result)
        out_ref[slot] = result.astype(jnp.bfloat16)
        return carry

    lax.fori_loop(0, start_ref.shape[0], slot_body, 0)


def attend(start, span, query_rows, key_rows, value_rows):
    pairs, heads, _ = query_rows.shape
    slots = start.shape[0]
    flat = [a.reshape(pairs, heads * LANES) for a in (query_rows, key_rows, value_rows)]
    return pl.pallas_call(
        functools.partial(attention_kernel, heads),
        out_shape=jax.ShapeDtypeStruct((slots, MAXLEN, LANES), jnp.bfloat16),
        in_specs=[smem_spec()] * 2 + [whole_spec()] * 3,
        out_specs=whole_spec(),
        scratch_shapes=[pltpu.VMEM((2 * pairs + MAXLEN, LANES), jnp.float32)] * 3,
        compiler_params=params(),
        cost_estimate=pl.CostEstimate(
            flops=slots * heads * MAXLEN * MAXLEN * LANES * 4,
            bytes_accessed=pairs * heads * LANES * 8,
            transcendentals=slots * heads * MAXLEN * MAXLEN,
        ),
    )(start, span, *flat)


def lane_tiles(width):
    return [(first, min(LANES, width - first)) for first in range(0, width, LANES)]


def pairable(width):
    return width == LANES + LANES // 2


def join_pair(one, two):
    half = LANES // 2
    low = lax.broadcasted_iota(jnp.int32, one[0].shape, 1) < half
    turned = pltpu.roll(two[0], half, 1)
    return (
        one[0],
        jnp.where(low, one[1], turned),
        jnp.where(low, turned, pltpu.roll(two[1], half, 1)),
    )


def split_pair(tiles):
    half = LANES // 2
    low = lax.broadcasted_iota(jnp.int32, tiles[0].shape, 1) < half
    middle = pltpu.roll(tiles[1], half, 1)
    last = pltpu.roll(tiles[2], half, 1)
    return (tiles[0], tiles[1]), (jnp.where(low, middle, last), last)


def slots_kernel(start_ref, rows_ref, out_ref, *held):
    count, width = rows_ref.shape
    for (first, size), rows in zip(lane_tiles(width), held):

        def widen(chunk, carry):
            at = pl.multiple_of(chunk * MAXLEN, MAXLEN)
            rows[pl.ds(at, MAXLEN), 0:size] = rows_ref[
                pl.ds(at, MAXLEN), first : first + size
            ].astype(jnp.float32)
            return carry

        lax.fori_loop(0, count // MAXLEN, widen, 0)
        rows[pl.ds(count, MAXLEN), :] = jnp.zeros((MAXLEN, LANES), jnp.float32)

    def slot_body(slot, carry):
        if pairable(width):
            pair = [
                [rows[pl.ds(start_ref[2 * slot + side], MAXLEN), :] for rows in held]
                for side in range(2)
            ]
            tiles = join_pair(*pair)
        else:
            tiles = [rows[pl.ds(start_ref[slot], MAXLEN), :] for rows in held]
        for index, tile in enumerate(tiles):
            out_ref[slot, :, index * LANES : (index + 1) * LANES] = tile.astype(jnp.bfloat16)
        return carry

    lax.fori_loop(0, out_ref.shape[0], slot_body, 0)


def into_slots(start, rows):
    count, width = rows.shape
    slots = start.shape[0]
    tiles = len(lane_tiles(width))
    shape = (slots, MAXLEN, tiles * LANES)
    if pairable(width):
        shape = (slots // 2, MAXLEN, 2 * width)
    return pl.pallas_call(
        slots_kernel,
        out_shape=jax.ShapeDtypeStruct(shape, jnp.bfloat16),
        in_specs=[smem_spec(), whole_spec()],
        out_specs=whole_spec(),
        scratch_shapes=[pltpu.VMEM((count + MAXLEN, LANES), jnp.float32)] * tiles,
        compiler_params=params(),
    )(start, rows)


def place_kernel(paired, after_ref, x_ref, context_ref, out_ref, context_rows, *x_rows):
    slots = context_ref.shape[0]
    slabs = out_ref.shape[0]
    tall = out_ref.shape[1] * (2 if paired else 1)
    slab_rows = tall - 2 * HALO
    total_rows = context_rows.shape[0]
    held = (context_rows,) + x_rows
    zeros = jnp.zeros((MAXLEN, LANES), jnp.float32)
    for rows in held:
        rows[pl.ds(0, HALO), :] = jnp.zeros((HALO, LANES), jnp.float32)

    def load(ref, slot, tile):
        return ref[slot, :, tile * LANES : (tile + 1) * LANES].astype(jnp.float32)

    def put(step, carry):
        if paired:
            sides = split_pair([load(x_ref, step, tile) for tile in range(3)])
            for side in range(2):
                slot = 2 * step + side
                where = pl.ds(HALO + after_ref[slot], MAXLEN)
                for rows, piece in zip(x_rows, sides[side]):
                    rows[where, :] = piece
                context_rows[where, :] = load(context_ref, slot, 0)
        else:
            where = pl.ds(HALO + after_ref[step], MAXLEN)
            for tile, rows in enumerate(x_rows):
                rows[where, :] = load(x_ref, step, tile)
            context_rows[where, :] = load(context_ref, step, 0)
        return carry

    lax.fori_loop(0, x_ref.shape[0], put, 0)
    live = after_ref[slots]

    def clear(step, carry):
        at = jnp.minimum(HALO + live + step * MAXLEN, total_rows - MAXLEN)
        for rows in held:
            rows[pl.ds(at, MAXLEN), :] = zeros
        return carry

    lax.fori_loop(0, (total_rows - HALO - live + MAXLEN - 1) // MAXLEN, clear, 0)

    def emit(slab, carry):
        at = pl.multiple_of(slab * slab_rows, slab_rows)
        if paired:
            half = tall // 2
            one = pl.ds(at, half)
            two = pl.ds(pl.multiple_of(at + half, 8), half)
            tiles = join_pair([rows[one, :] for rows in x_rows], [rows[two, :] for rows in x_rows])
            tiles = tiles + (context_rows[one, :], context_rows[two, :])
        else:
            tiles = [rows[pl.ds(at, tall), :] for rows in x_rows + (context_rows,)]
        for index, tile in enumerate(tiles):
            out_ref[slab, :, index * LANES : (index + 1) * LANES] = tile.astype(jnp.bfloat16)
        return carry

    lax.fori_loop(0, slabs, emit, 0)


def place(after, x_slots, context_slots, slabs, slab_rows, features):
    count = context_slots.shape[0]
    paired = pairable(features)
    tiles = len(lane_tiles(features))
    tall = slab_rows + 2 * HALO
    shape = (slabs, tall, (tiles + 1) * LANES)
    if paired:
        shape = (slabs, tall // 2, 2 * features + 2 * LANES)
    return pl.pallas_call(
        functools.partial(place_kernel, paired),
        out_shape=jax.ShapeDtypeStruct(shape, jnp.bfloat16),
        in_specs=[smem_spec(), whole_spec(), whole_spec()],
        out_specs=whole_spec(),
        scratch_shapes=[pltpu.VMEM((count * MAXLEN + HALO + MAXLEN, LANES), jnp.float32)]
        * (tiles + 1),
        compiler_params=params(),
    )(after, x_slots, context_slots)


def unplace_kernel(moved_ref, x_ref, context_ref):
    slabs, rows, _ = moved_ref.shape
    step = 16
    span = 3 * LANES

    def chunk(index, carry):
        at = pl.multiple_of(index * step, step)

        def load(slab, tile):
            cells = moved_ref[slab, pl.ds(at, step), tile * LANES : (tile + 1) * LANES]
            return cells.astype(jnp.float32)

        for pair in range(slabs // 2):
            split = [
                split_pair([load(2 * pair + member, tile) for tile in range(3)])
                for member in range(2)
            ]
            for side in range(2):
                to = pl.ds(pl.multiple_of(at + side * rows, step), step)
                for tile, cells in enumerate(join_pair(split[0][side], split[1][side])):
                    first = pair * span + tile * LANES
                    x_ref[to, first : first + LANES] = cells.astype(jnp.bfloat16)
        for slab in range(slabs):
            for side in range(2):
                to = pl.ds(pl.multiple_of(at + side * rows, step), step)
                first = span + side * LANES
                context_ref[to, slab * LANES : (slab + 1) * LANES] = moved_ref[
                    slab, pl.ds(at, step), first : first + LANES
                ]
        return carry

    lax.fori_loop(0, rows // step, chunk, 0)


def unplace(moved, features, context_width):
    slabs, rows, _ = moved.shape
    if not (pairable(features) and context_width == LANES):
        first = len(lane_tiles(features)) * LANES
        x = moved[:, :, :features].transpose(1, 0, 2).reshape(rows, -1)
        context = moved[:, :, first : first + context_width]
        return x, context.transpose(1, 0, 2).reshape(rows, -1)
    return pl.pallas_call(
        unplace_kernel,
        out_shape=(
            jax.ShapeDtypeStruct((2 * rows, slabs * features), jnp.bfloat16),
            jax.ShapeDtypeStruct((2 * rows, slabs * context_width), jnp.bfloat16),
        ),
        in_specs=[whole_spec()],
        out_specs=(whole_spec(), whole_spec()),
        compiler_params=params(),
    )(moved)


def conv_kernel(
    uniform_ref, gated_ref, segment_ref, taps_ref, scale_ref, shift_ref, out_ref, wide
):
    wide[...] = gated_ref[...].astype(jnp.float32)
    edge = HALO - HALF
    scale = scale_ref[...]
    shift = shift_ref[...]
    for chunk in range(out_ref.shape[0] // CONV_ROWS):
        base = chunk * CONV_ROWS

        def finish(total):
            affine = total * scale + shift
            out_ref[base : base + CONV_ROWS, :] = (affine * jax.nn.sigmoid(affine)).astype(
                jnp.bfloat16
            )

        @pl.when(uniform_ref[chunk] == 1)
        def _():
            total = jnp.zeros((CONV_ROWS, LANES), jnp.float32)
            for tap in range(KERNEL):
                total = total + wide[pl.ds(base + edge + tap, CONV_ROWS), :] * taps_ref[
                    tap : tap + 1, :
                ]
            finish(total)

        @pl.when(uniform_ref[chunk] == 0)
        def _():
            centre = segment_ref[pl.ds(base + HALO, CONV_ROWS), :]
            total = jnp.zeros((CONV_ROWS, LANES), jnp.float32)
            for tap in range(KERNEL):
                same = segment_ref[pl.ds(base + edge + tap, CONV_ROWS), :] == centre
                term = jnp.where(same, wide[pl.ds(base + edge + tap, CONV_ROWS), :], 0.0)
                total = total + term * taps_ref[tap : tap + 1, :]
            finish(total)


def convolve(gated_rows, segment, conv_taps, batch_scale, batch_shift):
    tall, width = gated_rows.shape
    rows = tall - 2 * HALO
    chunks = rows // CONV_ROWS
    windows = [segment[c * CONV_ROWS : c * CONV_ROWS + CONV_ROWS + 2 * HALO] for c in range(chunks)]
    windows = jnp.stack(windows)
    uniform = jnp.all(windows == windows[:, :1], axis=1).astype(jnp.int32)
    wide_segment = jnp.broadcast_to(segment[:, None], (tall, LANES))
    return pl.pallas_call(
        conv_kernel,
        grid=(width // LANES,),
        out_shape=jax.ShapeDtypeStruct((rows, width), jnp.bfloat16),
        in_specs=[
            smem_spec(),
            pl.BlockSpec((tall, LANES), lambda i: (0, i)),
            pl.BlockSpec((tall, LANES), lambda i: (0, 0)),
            pl.BlockSpec((KERNEL, LANES), lambda i: (0, i)),
            pl.BlockSpec((1, LANES), lambda i: (0, i)),
            pl.BlockSpec((1, LANES), lambda i: (0, i)),
        ],
        out_specs=pl.BlockSpec((rows, LANES), lambda i: (0, i)),
        scratch_shapes=[pltpu.VMEM((tall, LANES), jnp.float32)],
        compiler_params=params(),
        cost_estimate=pl.CostEstimate(
            flops=2 * rows * width * KERNEL, bytes_accessed=4 * rows * width, transcendentals=0
        ),
    )(
        uniform,
        gated_rows,
        wide_segment,
        conv_taps,
        batch_scale[None, :],
        batch_shift[None, :],
    )


MESH = pl.DeviceIdType.MESH
OUT, GLU_ONE, GLU_TWO, DOWN = range(4)


def any_spec():
    return pl.BlockSpec(memory_space=pl.ANY)


class Place:
    def __init__(self):
        self.dp = lax.axis_index("dp")
        self.mp = lax.axis_index("mp")
        self.y, self.c = self.dp // 2, self.dp % 2
        self.z, self.x = self.mp // 2, self.mp % 2
        self.across = 1 - self.x
        self.near = self.z + 1 - 2 * (self.z % 2)
        self.far_one = 2 - self.z // 2
        self.far_two = 3 - 3 * (self.z // 2)

    def x_side(self):
        return (self.dp, 2 * self.z + self.across)

    def y_side(self):
        return (2 * (1 - self.y) + self.c, self.mp)

    def core_side(self):
        return (2 * self.y + 1 - self.c, self.mp)

    def corner(self):
        return (2 * (1 - self.y) + 1 - self.c, self.mp)

    def above(self):
        return (self.dp, self.mp + 2)

    def below(self):
        return (self.dp, self.mp - 2)


def aligned(index, step):
    return pl.multiple_of(index * step, step)


def piece(weights, kind, z, x, y, c, both_y=False):
    shard = 2 * z + x
    if kind == OUT:
        return weights[0].at[pl.ds(aligned(shard, 192), 192), pl.ds(aligned(c, 512), 512)]
    if kind == GLU_ONE:
        return weights[1].at[pl.ds(aligned(c, 256), 256), pl.ds(aligned(shard, 384), 384)]
    if kind == GLU_TWO:
        if both_y:
            rows = pl.ds(pl.multiple_of(512 + c * 512, 256), 512)
        else:
            rows = pl.ds(pl.multiple_of(512 + (c * 2 + y) * 256, 256), 256)
        return weights[1].at[rows, pl.ds(aligned(shard, 384), 384)]
    if both_y:
        columns = pl.ds(aligned(c, 768), 768)
    else:
        columns = pl.ds(aligned(c * 2 + y, 384), 384)
    return weights[2].at[pl.ds(aligned(shard, 192), 192), columns]


def own_piece(shards, kind, y, c):
    if kind == OUT:
        return shards[0].at[:, pl.ds(aligned(c, 512), 512)]
    if kind == GLU_ONE:
        return shards[1].at[pl.ds(aligned(c, 256), 256), :]
    if kind == GLU_TWO:
        return shards[1].at[pl.ds(pl.multiple_of(512 + (c * 2 + y) * 256, 256), 256), :]
    return shards[2].at[:, pl.ds(aligned(c * 2 + y, 384), 384)]


class Mail:
    def __init__(self, send_sems, recv_sems):
        self.send_sems, self.recv_sems = send_sems, recv_sems
        self.used = 0
        self.sent = []

    def slot(self):
        self.used += 1
        return self.used - 1

    def copy(self, slot, source, target, device):
        return pltpu.make_async_remote_copy(
            src_ref=source,
            dst_ref=target,
            send_sem=self.send_sems.at[slot],
            recv_sem=self.recv_sems.at[slot],
            device_id=device,
            device_id_type=MESH,
        )

    def send(self, slot, source, target, device, when=None):
        copy = self.copy(slot, source, target, device)
        run_if(when, copy.start)
        self.sent.append((copy, when))

    def receive(self, slot, target, device, when=None):
        run_if(when, self.copy(slot, target, target, device).wait_recv)

    def finish(self):
        for copy, when in self.sent:
            run_if(when, copy.wait_send)


def run_if(when, action):
    if when is None:
        action()
    else:
        pl.when(when)(action)


def greet(devices):
    barrier = pltpu.get_barrier_semaphore()

    def hello(device):
        pl.semaphore_signal(barrier, inc=1, device_id=device, device_id_type=MESH)

    count = 0
    for device, when in devices:
        if when is None:
            hello(device)
            count = count + 1
        else:
            pl.when(when)(functools.partial(hello, device))
            count = count + when.astype(jnp.int32)
    pl.semaphore_wait(barrier, count)


KINDS = (GLU_ONE, OUT, GLU_TWO, DOWN)
FIRST = (GLU_TWO, OUT, GLU_ONE)


def find_slots(dp, lengths_ref, assignment_ref, start_ref, span_ref):
    groups = start_ref.shape[0] // PIECES
    per_group = lengths_ref.shape[0] // groups
    zero = jnp.int32(0)
    counts = [zero] * groups
    starts = [zero] * (groups * PIECES)
    spans = [zero] * (groups * PIECES)
    before = zero
    for i in range(per_group):
        target = assignment_ref[dp * per_group + i]
        length = lengths_ref[dp * per_group + i]
        for group in range(groups):
            hit = target == group
            for rank in range(PIECES):
                slot = group * PIECES + rank
                found = hit & (counts[group] == rank)
                starts[slot] = jnp.where(found, before, starts[slot])
                spans[slot] = jnp.where(found, length, spans[slot])
            counts[group] = counts[group] + hit.astype(jnp.int32)
        before = before + length
    for slot in range(groups * PIECES):
        start_ref[slot] = starts[slot]
        span_ref[slot] = spans[slot]


def move_kernel(
    lengths_ref,
    assignment_ref,
    q_ref,
    k_ref,
    v_ref,
    residual_ref,
    out_shard,
    glu_shard,
    down_shard,
    x_got,
    context_got,
    out_all,
    glu_all,
    down_all,
    q_rows,
    k_rows,
    v_rows,
    x_low,
    x_high,
    x_send,
    context_send,
    out_held,
    glu_held,
    down_held,
    mixed,
    start_ref,
    span_ref,
    send_sems,
    recv_sems,
    local_sems,
):
    here = Place()
    z, x, y, c = here.z, here.x, here.y, here.c
    weights = (out_all, glu_all, down_all)
    shards = (out_shard, glu_shard, down_shard)
    held = (out_held, glu_held, down_held)
    mail = Mail(send_sems, recv_sems)
    up, down = z < 3, z > 0
    partners = (here.y_side(), here.corner(), here.core_side())
    greet(
        [(device, None) for device in partners + (here.x_side(),)]
        + [(here.above(), up), (here.below(), down)]
    )

    def spot(kind, zz, xx):
        return piece(weights, kind, zz, xx, y, c)

    own = (
        out_all.at[pl.ds(aligned(here.mp, 192), 192), :],
        glu_all.at[:, pl.ds(aligned(here.mp, 384), 384)],
        down_all.at[pl.ds(aligned(here.mp, 192), 192), :],
    )
    into = [
        pltpu.make_async_copy(shards[i], held[i], local_sems.at[i]) for i in range(3)
    ]
    locals_ = [pltpu.make_async_copy(held[i], own[i], local_sems.at[5 + i]) for i in range(3)]
    slots_up, slots_down, slots_x, slots_near = [
        {kind: mail.slot() for kind in KINDS} for _ in range(4)
    ]
    slots_up_two, slots_down_two = [{kind: mail.slot() for kind in KINDS} for _ in range(2)]
    for kind in KINDS:
        mine = own_piece(shards, kind, y, c)
        mail.send(slots_up[kind], mine, spot(kind, z, x), here.above(), up)
        mail.send(slots_down[kind], mine, spot(kind, z, x), here.below(), down)
        mail.send(slots_x[kind], mine, spot(kind, z, x), here.x_side())
    for copy in into:
        copy.start()
    find_slots(here.dp, lengths_ref, assignment_ref, start_ref, span_ref)

    count = 4 * residual_ref.shape[0]
    step = 128
    low = lax.broadcasted_iota(jnp.int32, (step, LANES), 1) < HD

    def open_rows(chunk, carry):
        first = pl.multiple_of(chunk * step, step)
        cells = [
            residual_ref[pl.ds(first, step), i * LANES : (i + 1) * LANES].astype(jnp.float32)
            for i in range(6)
        ]
        turned = [pltpu.roll(cells[i], HD, 1) for i in (1, 2, 4, 5)]
        frames = (
            (cells[0], cells[1]),
            (jnp.where(low, turned[0], turned[1]), turned[1]),
            (cells[3], cells[4]),
            (jnp.where(low, turned[2], turned[3]), turned[3]),
        )
        for j, (one, two) in enumerate(frames):
            at = pl.ds(4 * first + j, step, stride=4)
            x_low[at, :] = one
            x_high[at, :] = two
        return carry

    lax.fori_loop(0, residual_ref.shape[0] // step, open_rows, 0)
    for rows in (x_low, x_high):
        rows[pl.ds(count, MAXLEN), :] = jnp.zeros((MAXLEN, LANES), jnp.float32)

    def relay(kind):
        mail.receive(slots_up[kind], spot(kind, z - 1, x), here.above(), down)
        mail.send(
            slots_up_two[kind],
            spot(kind, z - 1, x),
            spot(kind, z - 1, x),
            here.above(),
            up & down,
        )
        mail.receive(slots_down[kind], spot(kind, z + 1, x), here.below(), up)
        mail.send(
            slots_down_two[kind],
            spot(kind, z + 1, x),
            spot(kind, z + 1, x),
            here.below(),
            up & down,
        )
        mail.send(
            slots_near[kind],
            spot(kind, here.near, x),
            spot(kind, here.near, x),
            here.x_side(),
        )

    targets = partners + ((here.dp, here.mp),)
    half = PIECES // 2
    x_slots = [mail.slot() for _ in partners]
    context_slots = [mail.slot() for _ in partners]
    for index, target in enumerate(targets):
        group = target[0]

        def fill(pair, carry):
            at = group * half + pair
            both = [
                [
                    rows[pl.ds(start_ref[2 * at + side], MAXLEN), :]
                    for rows in (x_low, x_high)
                ]
                for side in range(2)
            ]
            for tile, cells in enumerate(join_pair(*both)):
                x_send[at, :, tile * LANES : (tile + 1) * LANES] = cells.astype(jnp.bfloat16)
            return carry

        lax.fori_loop(0, half, fill, 0)
        source = x_send.at[pl.ds(group * half, half)]
        landing = x_got.at[pl.ds(here.dp * half, half)]
        if index < 3:
            mail.send(x_slots[index], source, landing, target)
        else:
            copy = pltpu.make_async_copy(source, landing, local_sems.at[3])
            copy.start()
            locals_.append(copy)

    relay(KINDS[0])
    for copy_in, copy_out in zip(into, locals_):
        copy_in.wait()
        copy_out.start()

    pairs = q_ref.shape[0] // 2
    wide_low = lax.broadcasted_iota(jnp.int32, (256, LANES), 1) < HD

    def unpack(chunk, carry):
        first = pl.multiple_of(chunk * 256, 256)
        for i, (packed, rows) in enumerate(((q_ref, q_rows), (k_ref, k_rows), (v_ref, v_rows))):
            mixed[i] = packed[pl.ds(2 * first, 512), :].astype(jnp.float32)
            one = mixed[i, pl.ds(0, 256, stride=2), :]
            two = mixed[i, pl.ds(1, 256, stride=2), :]
            rows[pl.ds(2 * first, 256, stride=2), :] = jnp.where(
                wide_low, one, pltpu.roll(two, HD, 1)
            )
            rows[pl.ds(2 * first + 1, 256, stride=2), :] = jnp.where(
                wide_low, pltpu.roll(one, HD, 1), two
            )
        return carry

    lax.fori_loop(0, pairs // 256, unpack, 0)
    for rows in (q_rows, k_rows, v_rows):
        rows[pl.ds(2 * pairs, MAXLEN), :] = jnp.zeros((MAXLEN, LANES), jnp.float32)

    relay(KINDS[1])
    column = lax.broadcasted_iota(jnp.int32, (MAXLEN, MAXLEN), 1)
    head_lane = lax.broadcasted_iota(jnp.int32, (MAXLEN, LANES), 1) // HD

    def attend_slot(slot):
        start = start_ref[slot]
        allowed = column < span_ref[slot]
        queries = q_rows[pl.ds(start, MAXLEN), :]
        keys = k_rows[pl.ds(start, MAXLEN), :].astype(jnp.bfloat16)
        values = v_rows[pl.ds(start, MAXLEN), :].astype(jnp.bfloat16)
        result = None
        for head in range(2):
            own = jnp.where(head_lane == head, queries, 0.0).astype(jnp.bfloat16)
            scores = (
                lax.dot_general(
                    own, keys, (((1,), (1,)), ((), ())), preferred_element_type=jnp.float32
                )
                * HD ** (-0.5)
            )
            scores = jnp.where(allowed, scores, MASKED)
            highest = jnp.max(scores, axis=1, keepdims=True)
            exponentials = jnp.exp(scores - highest)
            denominator = jnp.sum(exponentials, axis=1, keepdims=True)
            weighing = (exponentials / denominator).astype(jnp.bfloat16)
            blended = jnp.dot(weighing, values, preferred_element_type=jnp.float32)
            result = blended if head == 0 else jnp.where(head_lane == head, blended, result)
        context_send[slot] = result.astype(jnp.bfloat16)

    for index, target in enumerate(targets):
        group = target[0]

        def attend_one(rank, carry):
            attend_slot(group * PIECES + rank)
            return carry

        lax.fori_loop(0, PIECES, attend_one, 0)
        source = context_send.at[pl.ds(group * PIECES, PIECES)]
        landing = context_got.at[pl.ds(here.dp * PIECES, PIECES)]
        if index < 3:
            mail.send(context_slots[index], source, landing, target)
        else:
            copy = pltpu.make_async_copy(source, landing, local_sems.at[4])
            copy.start()
            locals_.append(copy)
        if index < 2:
            relay(KINDS[2 + index])

    for index, source in enumerate(partners):
        mail.receive(x_slots[index], x_got.at[pl.ds(source[0] * half, half)], source)
        mail.receive(
            context_slots[index], context_got.at[pl.ds(source[0] * PIECES, PIECES)], source
        )
    for kind in KINDS:
        mail.receive(slots_x[kind], spot(kind, z, here.across), here.x_side())
        mail.receive(slots_near[kind], spot(kind, here.near, here.across), here.x_side())
        mail.receive(slots_up_two[kind], spot(kind, z - 2, x), here.above(), z > 1)
        mail.receive(slots_down_two[kind], spot(kind, z + 2, x), here.below(), z < 2)
    mail.finish()
    for copy in locals_:
        copy.wait()


def move(lengths, assignment, queries, keys, values, residual, out_shard, glu_shard, down_shard):
    slots = 4 * PIECES
    pairs = queries.shape[0] // 2
    count = 4 * residual.shape[0]
    bf16 = jnp.bfloat16
    return pl.pallas_call(
        move_kernel,
        out_shape=(
            jax.ShapeDtypeStruct((slots // 2, MAXLEN, 3 * LANES), bf16),
            jax.ShapeDtypeStruct((slots, MAXLEN, LANES), bf16),
            jax.ShapeDtypeStruct((1536, 1024), bf16),
            jax.ShapeDtypeStruct((1536, 3072), bf16),
            jax.ShapeDtypeStruct((1536, 1536), bf16),
        ),
        in_specs=[smem_spec()] * 2 + [whole_spec()] * 4 + [any_spec()] * 3,
        out_specs=(any_spec(),) * 5,
        scratch_shapes=[pltpu.VMEM((2 * pairs + MAXLEN, LANES), jnp.float32)] * 3
        + [pltpu.VMEM((count + MAXLEN, LANES), jnp.float32)] * 2
        + [
            pltpu.VMEM((slots // 2, MAXLEN, 3 * LANES), bf16),
            pltpu.VMEM((slots, MAXLEN, LANES), bf16),
            pltpu.VMEM(out_shard.shape, bf16),
            pltpu.VMEM(glu_shard.shape, bf16),
            pltpu.VMEM(down_shard.shape, bf16),
            pltpu.VMEM((3, 512, LANES), jnp.float32),
            pltpu.SMEM((slots,), jnp.int32),
            pltpu.SMEM((slots,), jnp.int32),
            pltpu.SemaphoreType.DMA((30,)),
            pltpu.SemaphoreType.DMA((30,)),
            pltpu.SemaphoreType.DMA((8,)),
        ],
        compiler_params=pltpu.CompilerParams(
            vmem_limit_bytes=VMEM_LIMIT, collective_id=1, has_side_effects=True
        ),
        cost_estimate=pl.CostEstimate(
            flops=slots * 2 * MAXLEN * MAXLEN * LANES * 4,
            bytes_accessed=50 * 1024 * 1024,
            transcendentals=slots * 2 * MAXLEN * MAXLEN,
        ),
    )(lengths, assignment, queries, keys, values, residual, out_shard, glu_shard, down_shard)


SPLIT = 288
PARTS = ((0, SPLIT // 2, 0, SPLIT - 2 * HALO), (SPLIT, 272 - SPLIT // 2, SPLIT - 2 * HALO, 544 - SPLIT))
ROW_STEP = 32
EXCHANGE_ORDER = ((3, 1), (3, 0), (2, 0), (2, 1), (1, 0), (1, 1), (0, 1))


def place_parts_kernel(
    lengths_ref, assignment_ref, x_ref, context_ref, out_ref, after_ref, context_rows, *x_rows
):
    dp = lax.axis_index("dp")
    after_ref[0] = 0

    def seek(u, carry):
        count, total = carry
        hit = assignment_ref[u] == dp
        total = total + jnp.where(hit, lengths_ref[u], 0)
        count = count + hit.astype(jnp.int32)
        after_ref[count] = total
        return count, total

    lax.fori_loop(0, lengths_ref.shape[0], seek, (jnp.int32(0), jnp.int32(0)))
    slots = context_ref.shape[0]
    slabs = out_ref.shape[0]
    tall = out_ref.shape[1] * 2
    slab_rows = tall - 2 * HALO
    total_rows = context_rows.shape[0]
    held = (context_rows,) + x_rows
    zeros = jnp.zeros((MAXLEN, LANES), jnp.float32)
    for rows in held:
        rows[pl.ds(0, HALO), :] = jnp.zeros((HALO, LANES), jnp.float32)

    def load(ref, slot, tile):
        return ref[slot, :, tile * LANES : (tile + 1) * LANES].astype(jnp.float32)

    def put(step, carry):
        sides = split_pair([load(x_ref, step, tile) for tile in range(3)])
        for side in range(2):
            slot = 2 * step + side
            where = pl.ds(HALO + after_ref[slot], MAXLEN)
            for rows, piece in zip(x_rows, sides[side]):
                rows[where, :] = piece
            context_rows[where, :] = load(context_ref, slot, 0)
        return carry

    lax.fori_loop(0, x_ref.shape[0], put, 0)
    live = after_ref[slots]

    def clear(step, carry):
        at = jnp.minimum(HALO + live + step * MAXLEN, total_rows - MAXLEN)
        for rows in held:
            rows[pl.ds(at, MAXLEN), :] = zeros
        return carry

    lax.fori_loop(0, (total_rows - HALO - live + MAXLEN - 1) // MAXLEN, clear, 0)

    def emit(slab, carry):
        at = pl.multiple_of(slab * slab_rows, slab_rows)
        for first, half, *_ in PARTS:
            one = pl.ds(pl.multiple_of(at + first, 16), half)
            two = pl.ds(pl.multiple_of(at + first + half, 16), half)
            tiles = join_pair(
                [rows[one, :] for rows in x_rows], [rows[two, :] for rows in x_rows]
            )
            tiles = tiles + (context_rows[one, :], context_rows[two, :])
            for index, tile in enumerate(tiles):
                lanes = slice(index * LANES, (index + 1) * LANES)
                out_ref[slab, first // 2 : first // 2 + half, lanes] = tile.astype(
                    jnp.bfloat16
                )
        return carry

    lax.fori_loop(0, slabs, emit, 0)


def place_parts(lengths, assignment, x_slots, context_slots, slabs):
    count = context_slots.shape[0]
    return pl.pallas_call(
        place_parts_kernel,
        out_shape=(
            jax.ShapeDtypeStruct((slabs, 272, 5 * LANES), jnp.bfloat16),
            jax.ShapeDtypeStruct((count + 1,), jnp.int32),
        ),
        in_specs=[smem_spec()] * 2 + [whole_spec()] * 2,
        out_specs=(whole_spec(), smem_spec()),
        scratch_shapes=[pltpu.VMEM((count * MAXLEN + HALO + MAXLEN, LANES), jnp.float32)] * 3,
        compiler_params=params(),
    )(lengths, assignment, x_slots, context_slots)


def finish_kernel(
    after_ref,
    slabs_ref,
    gain_ref,
    bias_ref,
    scale_ref,
    shift_ref,
    taps_ref,
    out_in,
    glu_in,
    down_in,
    encoded_ref,
    out_all,
    glu_all,
    down_all,
    moved,
    carried,
    context,
    normed,
    wide,
    swished,
    first_tap,
    last_tap,
    out_held,
    glu_held,
    down_held,
    send_sems,
    recv_sems,
    local_sems,
):
    here = Place()
    z, x, y, c = here.z, here.x, here.y, here.c
    weights = (out_all, glu_all, down_all)
    mail = Mail(send_sems, recv_sems)
    slabs = slabs_ref.shape[0]
    mirrors = (z, here.near, z + 2 - 4 * (z // 2), 3 - z)
    sides = (x, here.across)
    others = [(here.dp, 2 * mirrors[dz] + sides[dx]) for dz, dx in EXCHANGE_ORDER]
    greet([(device, None) for device in others + [here.y_side(), here.core_side()]])

    slab_slots = [[mail.slot() for _ in others] for _ in PARTS]

    def part_rows(part):
        first, half, *_ = PARTS[part]
        return pl.ds(first // 2, half)

    def exchange(part, crossing):
        for index, device in enumerate(others):
            if EXCHANGE_ORDER[index][1] != crossing:
                continue
            mail.send(
                slab_slots[part][index],
                slabs_ref.at[device[1], part_rows(part)],
                moved.at[here.mp, part_rows(part)],
                device,
            )

    def exchanged(part):
        for index in range(len(others)):
            mail.receive(
                slab_slots[part][index],
                moved.at[others[index][1], part_rows(part)],
                others[index],
            )

    tile_width = 256
    tiles = carried.shape[1] // tile_width
    keep = pltpu.make_async_copy(slabs_ref.at[here.mp], moved.at[here.mp], local_sems.at[0])
    keep.start()

    def spot(kind, zz, xx):
        return piece(weights, kind, zz, xx, y, c)

    table = {}

    def slot(*key):
        if key not in table:
            table[key] = mail.slot()
        return table[key]

    def pass_on(name, kind, zz, xx, device, when=None):
        where = spot(kind, zz, xx)
        mail.send(slot(name, kind), where, where, device, when)

    cells = {
        "own near": (here.near, x),
        "own one": (here.far_one, x),
        "own two": (here.far_two, x),
        "other own": (z, here.across),
        "other near": (here.near, here.across),
        "other one": (here.far_one, here.across),
        "other two": (here.far_two, here.across),
    }
    early = ("own near", "own one", "other own", "other near")
    order = early + ("other one", "own two", "other two")

    def after(kind, cell):
        if kind in (OUT, GLU_ONE):
            pass_on("core " + cell, kind, *cells[cell], here.core_side())
        else:
            pass_on("y " + cell, kind, *cells[cell], here.y_side())

    def from_y(kind):
        for cell in order:
            mail.receive(
                slot("y " + cell, kind),
                piece(weights, kind, *cells[cell], 1 - y, c),
                here.y_side(),
            )
            where = piece(weights, kind, *cells[cell], y, c, both_y=True)
            mail.send(slot("core " + cell, kind), where, where, here.core_side())

    def from_core(kind):
        for cell in order:
            where = piece(weights, kind, *cells[cell], y, 1 - c, both_y=kind in (GLU_TWO, DOWN))
            mail.receive(slot("core " + cell, kind), where, here.core_side())

    def start_across(kinds):
        for kind in kinds:
            pass_on("third up", kind, 0, x, here.above(), z == 2)
            pass_on("third down", kind, 3, x, here.below(), z == 1)
            pass_on("x one", kind, here.far_one, x, here.x_side())
        for kind in kinds:
            for cell in early:
                after(kind, cell)

    def across_one(kinds):
        for kind in kinds:
            mail.receive(slot("x one", kind), spot(kind, *cells["other one"]), here.x_side())
            after(kind, "other one")
        for kind in kinds:
            mail.receive(slot("third up", kind), spot(kind, 0, x), here.above(), z == 3)
            mail.receive(slot("third down", kind), spot(kind, 3, x), here.below(), z == 0)
            pass_on("x two", kind, here.far_two, x, here.x_side())
            after(kind, "own two")

    def across_two(kinds):
        for kind in kinds:
            mail.receive(slot("x two", kind), spot(kind, *cells["other two"]), here.x_side())
            after(kind, "other two")

    start_across(FIRST)
    exchange(0, 0)
    live = after_ref[4 * PIECES]

    def bounds(step, carry):
        rows = pl.ds(pl.multiple_of(step * 64, 64), 64)
        position = (
            lax.broadcasted_iota(jnp.int32, (64, LANES), 0)
            + step * 64
            + here.mp * encoded_ref.shape[0]
        )
        begin = jnp.zeros((64, LANES), jnp.int32)
        end = jnp.full((64, LANES), live, jnp.int32)
        for k in range(1, 4 * PIECES):
            begin = jnp.where(position >= after_ref[k], after_ref[k], begin)
        for k in range(4 * PIECES - 1, 0, -1):
            end = jnp.where(position < after_ref[k], after_ref[k], end)
        first_tap[rows, :] = HALF + begin - position
        last_tap[rows, :] = HALF - 1 + end - position
        return carry

    lax.fori_loop(0, encoded_ref.shape[0] // 64, bounds, 0)

    across_one(FIRST)
    exchange(0, 1)
    start_across((DOWN,))
    exchange(1, 0)
    exchange(1, 1)
    across_two(FIRST)
    from_y(GLU_TWO)
    loads = [
        pltpu.make_async_copy(weights[i], (out_held, glu_held, down_held)[i], local_sems.at[1 + i])
        for i in range(3)
    ]

    def glu_load(n, side):
        columns = pl.ds(aligned(n + side * tiles, tile_width), tile_width)
        return pltpu.make_async_copy(
            weights[1].at[:, columns],
            glu_held.at[:, columns],
            local_sems.at[4 + 2 * n + side],
        )

    from_core(OUT)
    loads[0].start()

    def open_part(part):
        first, half, *_ = PARTS[part]

        def chunk(index, carry):
            at = pl.ds(pl.multiple_of(first // 2 + index * 16, 16), 16)

            def load(slab, tile):
                cells_ = moved[slab, at, tile * LANES : (tile + 1) * LANES]
                return cells_.astype(jnp.float32)

            to = [pl.ds(pl.multiple_of(first + s * half + index * 16, 16), 16) for s in range(2)]
            near = [pl.ds(pl.multiple_of(s * half + index * 16, 16), 16) for s in range(2)]
            for pair in range(slabs // 2):
                split = [
                    split_pair([load(2 * pair + member, tile) for tile in range(3)])
                    for member in range(2)
                ]
                for side in range(2):
                    for tile, cells_ in enumerate(join_pair(split[0][side], split[1][side])):
                        begin = (3 * pair + tile) * LANES
                        carried[to[side], begin : begin + LANES] = cells_
            for slab in range(slabs):
                for side in range(2):
                    begin = (3 + side) * LANES
                    context[near[side], slab * LANES : (slab + 1) * LANES] = moved[
                        slab, at, begin : begin + LANES
                    ]
            return carry

        lax.fori_loop(0, half // 16, chunk, 0)

    def attach(part):
        first, half, *_ = PARTS[part]

        def tile(n, carry):
            columns = pl.ds(aligned(n, tile_width), tile_width)
            carried[first : first + 2 * half, columns] += lax.dot_general(
                context[0 : 2 * half, :],
                out_held[columns, :],
                (((1,), (1,)), ((), ())),
                preferred_element_type=jnp.float32,
            )
            return carry

        lax.fori_loop(0, tiles, tile, 0)

        def normalise(index, carry):
            at = pl.ds(pl.multiple_of(first + index * 32, 32), 32)
            to = pl.ds(pl.multiple_of(index * 32, 32), 32)
            cells_ = carried[at, :]
            centred = cells_ - jnp.mean(cells_, axis=1, keepdims=True)
            variance = jnp.mean(centred * centred, axis=1, keepdims=True)
            inverse = lax.rsqrt(variance + EPS)
            for i in range(carried.shape[1] // LANES):
                lanes = slice(i * LANES, (i + 1) * LANES)
                scaled = centred[:, lanes] * inverse * gain_ref[i : i + 1, :] + bias_ref[i : i + 1, :]
                normed[to, lanes] = scaled.astype(jnp.bfloat16)
            return carry

        lax.fori_loop(0, 2 * half // 32, normalise, 0)

    def gate(part):
        first, half, *_ = PARTS[part]

        def tile(n, carry):
            columns = pl.ds(aligned(n, tile_width), tile_width)
            if part == 0:
                for side in range(2):
                    glu_load(n, side).wait()
            rows = normed[0 : 2 * half, :]
            value = jnp.dot(rows, glu_held[:, columns], preferred_element_type=jnp.float32)
            gates = jnp.dot(
                rows,
                glu_held[:, pl.ds(aligned(n + tiles, tile_width), tile_width)],
                preferred_element_type=jnp.float32,
            )
            gated = (value * jax.nn.sigmoid(gates)).astype(jnp.bfloat16)
            for side in range(2):
                wide[2 * n + side, first : first + 2 * half, :] = gated[
                    :, side * LANES : (side + 1) * LANES
                ].astype(jnp.float32)
            return carry

        lax.fori_loop(0, tiles, tile, 0)

    def convolve_part(part):
        start, count_rows = PARTS[part][2:]
        steps = count_rows // ROW_STEP
        group = 2
        groups = carried.shape[1] // (group * LANES)

        def body(index, carry):
            row = start + lax.rem(index, steps) * ROW_STEP
            column = index // steps * (group * LANES)
            rows = pl.ds(pl.multiple_of(row, ROW_STEP), ROW_STEP)
            low, high = first_tap[rows, :], last_tap[rows, :]
            lanes = [pl.ds(pl.multiple_of(column + i * LANES, LANES), LANES) for i in range(group)]
            totals = [jnp.zeros((ROW_STEP, LANES), jnp.float32) for _ in range(group)]
            for shift in range(8):
                count = ROW_STEP + (24 if shift < 7 else 16)
                at = pl.ds(row + HALO - HALF + shift, count)
                seen = [wide[column // LANES + i, at, :] for i in range(group)]
                for k in range(4 if shift < 7 else 3):
                    tap = shift + 8 * k
                    if tap < HALF:
                        mask = low <= tap
                    else:
                        mask = high >= tap
                    for i in range(group):
                        term = seen[i][8 * k : 8 * k + ROW_STEP] * taps_ref[tap : tap + 1, lanes[i]]
                        if tap != HALF:
                            term = jnp.where(mask, term, 0.0)
                        totals[i] = totals[i] + term
            for i in range(group):
                one = pl.ds(column // LANES + i, 1)
                affine = totals[i] * scale_ref[one, :] + shift_ref[one, :]
                swished[rows, lanes[i]] = (affine * jax.nn.sigmoid(affine)).astype(jnp.bfloat16)
            return carry

        lax.fori_loop(0, steps * groups, body, 0)

    def lower(part):
        start, count_rows = PARTS[part][2:]
        rows = pl.ds(start, count_rows)

        def tile(n, carry):
            columns = pl.ds(aligned(n, tile_width), tile_width)
            total = carried[start + HALO : start + HALO + count_rows, columns] + lax.dot_general(
                swished[rows, :],
                down_held[columns, :],
                (((1,), (1,)), ((), ())),
                preferred_element_type=jnp.float32,
            )
            alive = last_tap[rows, :] >= HALF
            for side in range(2):
                lane = pl.ds(pl.multiple_of(n * tile_width + side * LANES, LANES), LANES)
                encoded_ref[rows, lane] = jnp.where(
                    alive, total[:, side * LANES : (side + 1) * LANES], 0.0
                ).astype(jnp.bfloat16)
            return carry

        lax.fori_loop(0, tiles, tile, 0)

    keep.wait()
    exchanged(0)
    open_part(0)
    loads[0].wait()
    attach(0)
    from_core(GLU_ONE)
    from_core(GLU_TWO)
    for n in range(tiles):
        for side in range(2):
            glu_load(n, side).start()
    gate(0)
    across_one((DOWN,))
    convolve_part(0)
    across_two((DOWN,))
    exchanged(1)
    open_part(1)
    attach(1)
    from_y(DOWN)
    gate(1)
    from_core(DOWN)
    loads[2].start()
    convolve_part(1)
    loads[2].wait()
    lower(0)
    lower(1)
    mail.finish()


def finish(after, slabs, norm, taps, out_all, glu_all, down_all):
    norm = [a.reshape(-1, LANES) for a in norm]
    bf16, f32 = jnp.bfloat16, jnp.float32
    width = taps.shape[1]
    rows = 512
    tall = rows + 2 * HALO
    weights = (out_all, glu_all, down_all)
    return pl.pallas_call(
        finish_kernel,
        out_shape=(jax.ShapeDtypeStruct((rows, width), bf16),)
        + tuple(jax.ShapeDtypeStruct(a.shape, a.dtype) for a in weights),
        in_specs=[smem_spec(), any_spec()] + [whole_spec()] * 5 + [any_spec()] * 3,
        out_specs=(whole_spec(),) + (any_spec(),) * 3,
        input_output_aliases={7: 1, 8: 2, 9: 3},
        scratch_shapes=[
            pltpu.VMEM(slabs.shape, bf16),
            pltpu.VMEM((tall, width), f32),
            pltpu.VMEM((SPLIT, 1024), bf16),
            pltpu.VMEM((SPLIT, width), bf16),
            pltpu.VMEM((width // LANES, tall, LANES), f32),
            pltpu.VMEM((rows, width), bf16),
            pltpu.VMEM((rows, LANES), jnp.int32),
            pltpu.VMEM((rows, LANES), jnp.int32),
        ]
        + [pltpu.VMEM(a.shape, bf16) for a in weights]
        + [
            pltpu.SemaphoreType.DMA((80,)),
            pltpu.SemaphoreType.DMA((80,)),
            pltpu.SemaphoreType.DMA((16,)),
        ],
        compiler_params=pltpu.CompilerParams(
            vmem_limit_bytes=VMEM_LIMIT, collective_id=2, has_side_effects=True
        ),
    )(after, slabs, *norm, taps, *weights)[0]


def on_device(
    query_rows,
    key_rows,
    value_rows,
    residual,
    lengths,
    assignment,
    out_proj,
    norm_gain,
    norm_bias,
    glu_proj,
    conv_taps,
    batch_scale,
    batch_shift,
    down_proj,
):
    data_group = lax.axis_index("dp")
    slab_index = lax.axis_index("mp")
    groups = lax.axis_size("dp")
    slabs = lax.axis_size("mp")
    group_rows = query_rows.shape[0] * 2
    slab_rows = group_rows // slabs
    total_utterances = lengths.shape[0]
    per_group = total_utterances // groups
    slots = groups * PIECES
    features = residual.shape[2] // 4

    fits = (
        (groups, slabs) == (4, 8)
        and query_rows.shape == (2048, 2, LANES)
        and residual.shape == (1024, 1, 768)
    )
    if fits:
        flat = [a.reshape(4096, LANES) for a in (query_rows, key_rows, value_rows)]
        x_slots, context_slots, *weights = move(
            lengths, assignment, *flat, residual.reshape(1024, 768), out_proj.T, glu_proj, down_proj.T
        )
        placed, after = place_parts(lengths, assignment, x_slots, context_slots, slabs)
        norm = (norm_gain, norm_bias, batch_scale, batch_shift)
        return finish(after, placed, norm, conv_taps, *weights)

    utterance = jnp.arange(total_utterances, dtype=jnp.int32)
    source = utterance // per_group
    earlier = utterance[None, :] < utterance[:, None]
    same_source = source[None, :] == source[:, None]
    same_target = assignment[None, :] == assignment[:, None]
    before = jnp.sum(jnp.where(earlier & same_source, lengths[None, :], 0), axis=1)
    rank = jnp.sum((earlier & same_source & same_target).astype(jnp.int32), axis=1)
    slot = jnp.arange(slots, dtype=jnp.int32)[:, None]
    leaving = (source[None, :] == data_group) & ((assignment * PIECES + rank)[None, :] == slot)
    start = jnp.sum(jnp.where(leaving, before[None, :], 0), axis=1)
    span = jnp.sum(jnp.where(leaving, lengths[None, :], 0), axis=1)
    coming_earlier = (assignment[None, :] == data_group) & (
        (source * PIECES + rank)[None, :] < jnp.arange(slots + 1, dtype=jnp.int32)[:, None]
    )
    after = jnp.sum(jnp.where(coming_earlier, lengths[None, :], 0), axis=1)
    live = jnp.sum(jnp.where(assignment == data_group, lengths, 0))

    position = jnp.arange(slab_rows + 2 * HALO, dtype=jnp.int32) + slab_index * slab_rows - HALO
    segment = jnp.sum((position[:, None] >= after[None, 1:]).astype(jnp.int32), axis=1)
    segment = jnp.where(position < 0, -2, jnp.where(position < live, segment, -1))
    segment = jnp.where(position >= group_rows, -2, segment)

    residual_rows = (
        residual.reshape(group_rows // 4, 4, features).reshape(group_rows, features)
    )

    def swap(array, axis):
        return lax.all_to_all(array, axis, split_axis=0, concat_axis=0, tiled=True)

    packed, start = lax.optimization_barrier((into_slots(start, residual_rows), start))
    x_slots = swap(packed, "dp")
    context_slots = swap(attend(start, span, query_rows, key_rows, value_rows), "dp")
    moved = swap(place(after, x_slots, context_slots, slabs, slab_rows, features), "mp")
    carried_slab, context_slab = unplace(moved, features, query_rows.shape[1] * HD)

    core = data_group % 2
    partners = [(group, group + 1 - 2 * (group % 2)) for group in range(groups)]

    def gather(weights):
        half = weights.shape[0] // 2
        own = lax.dynamic_slice_in_dim(weights, core * half, half, 0)
        return lax.all_gather(own, "mp", axis=1, tiled=True)

    def both(own):
        return own, lax.ppermute(own, "dp", partners)

    def project(rows, halves_of):
        own, other = halves_of
        half = rows.shape[1] // 2
        low, high = rows[:, :half], rows[:, half:]
        return jnp.dot(
            jnp.where(core == 0, low, high), own, preferred_element_type=jnp.float32
        ) + jnp.dot(jnp.where(core == 0, high, low), other, preferred_element_type=jnp.float32)

    out_halves, glu_halves = both(gather(out_proj)), both(gather(glu_proj))
    down_own = gather(down_proj)
    carried = carried_slab.astype(jnp.float32) + project(context_slab, out_halves)
    average = jnp.mean(carried, axis=1, keepdims=True)
    centred = carried - average
    variance = jnp.mean(centred * centred, axis=1, keepdims=True)
    normed = (centred * lax.rsqrt(variance + EPS) * norm_gain + norm_bias).astype(jnp.bfloat16)
    halves = project(normed, glu_halves)
    feature_count = halves.shape[1] // 2
    gated_rows = (halves[:, :feature_count] * jax.nn.sigmoid(halves[:, feature_count:])).astype(
        jnp.bfloat16
    )
    down_own, gated_rows = lax.optimization_barrier((down_own, gated_rows))
    down_halves = both(down_own)
    swished = convolve(gated_rows, segment, conv_taps, batch_scale, batch_shift)
    lowered = project(swished, down_halves)
    centre_segment = segment[HALO : HALO + slab_rows]
    own_carried = carried[HALO : HALO + slab_rows]
    return jnp.where((centre_segment >= 0)[:, None], own_carried + lowered, 0.0).astype(
        jnp.bfloat16
    )


def solution(mesh):
    in_specs = (
        P("dp", "mp", None),
        P("dp", "mp", None),
        P("dp", "mp", None),
        P("dp", "mp", None),
        P(),
        P(),
        P(None, "mp"),
        P(),
        P(),
        P(None, "mp"),
        P(),
        P(),
        P(),
        P(None, "mp"),
    )
    out_specs = P(("dp", "mp"), None)
    return jax.shard_map(
        on_device, mesh=mesh, in_specs=in_specs, out_specs=out_specs, check_vma=False
    )
```

```python
import functools

import jax
import jax.numpy as jnp
from jax import lax
from jax.experimental import pallas as pl
from jax.experimental.pallas import tpu as pltpu
from jax.sharding import PartitionSpec as P

HD = 64
KERNEL = 31
HALF = 15
MAXLEN = 256
PIECES = 4
LANES = 128
HALO = 16
CONV_ROWS = 64

EPS = 1e-05
MASKED = -1e30
VMEM_LIMIT = 60 * 1024 * 1024


def params():
    return pltpu.CompilerParams(vmem_limit_bytes=VMEM_LIMIT)


def whole_spec():
    return pl.BlockSpec(memory_space=pltpu.VMEM)


def smem_spec():
    return pl.BlockSpec(memory_space=pltpu.SMEM)


def attention_kernel(
    heads, start_ref, span_ref, q_ref, k_ref, v_ref, out_ref, q_rows, k_rows, v_rows
):
    pairs = q_ref.shape[0]
    step = 256
    lane = lax.broadcasted_iota(jnp.int32, (step, LANES), 1)
    low = lane < HD

    def unpack(chunk, carry):
        first = pl.multiple_of(chunk * step, step)
        for packed, rows in ((q_ref, q_rows), (k_ref, k_rows), (v_ref, v_rows)):
            one = packed[pl.ds(first, step), 0:LANES].astype(jnp.float32)
            if heads == 2:
                two = packed[pl.ds(first, step), LANES : 2 * LANES].astype(jnp.float32)
                even = jnp.where(low, one, pltpu.roll(two, HD, 1))
                odd = jnp.where(low, pltpu.roll(one, HD, 1), two)
            else:
                even = one
                odd = pltpu.roll(one, HD, 1)
            rows[pl.ds(2 * first, step, stride=2), :] = even
            rows[pl.ds(2 * first + 1, step, stride=2), :] = odd
        return carry

    lax.fori_loop(0, pairs // step, unpack, 0)
    for rows in (q_rows, k_rows, v_rows):
        rows[pl.ds(2 * pairs, MAXLEN), :] = jnp.zeros((MAXLEN, LANES), jnp.float32)

    column = lax.broadcasted_iota(jnp.int32, (MAXLEN, MAXLEN), 1)
    head_lane = lax.broadcasted_iota(jnp.int32, (MAXLEN, LANES), 1) // HD

    def slot_body(slot, carry):
        start = start_ref[slot]
        allowed = column < span_ref[slot]
        queries = q_rows[pl.ds(start, MAXLEN), :]
        keys = k_rows[pl.ds(start, MAXLEN), :].astype(jnp.bfloat16)
        values = v_rows[pl.ds(start, MAXLEN), :].astype(jnp.bfloat16)
        result = None
        for head in range(heads):
            own = jnp.where(head_lane == head, queries, 0.0).astype(jnp.bfloat16)
            scores = (
                lax.dot_general(
                    own, keys, (((1,), (1,)), ((), ())), preferred_element_type=jnp.float32
                )
                * HD ** (-0.5)
            )
            scores = jnp.where(allowed, scores, MASKED)
            highest = jnp.max(scores, axis=1, keepdims=True)
            exponentials = jnp.exp(scores - highest)
            denominator = jnp.sum(exponentials, axis=1, keepdims=True)
            weights = (exponentials / denominator).astype(jnp.bfloat16)
            blended = jnp.dot(weights, values, preferred_element_type=jnp.float32)
            result = blended if head == 0 else jnp.where(head_lane == head, blended, result)
        out_ref[slot] = result.astype(jnp.bfloat16)
        return carry

    lax.fori_loop(0, start_ref.shape[0], slot_body, 0)


def attend(start, span, query_rows, key_rows, value_rows):
    pairs, heads, _ = query_rows.shape
    slots = start.shape[0]
    flat = [a.reshape(pairs, heads * LANES) for a in (query_rows, key_rows, value_rows)]
    return pl.pallas_call(
        functools.partial(attention_kernel, heads),
        out_shape=jax.ShapeDtypeStruct((slots, MAXLEN, LANES), jnp.bfloat16),
        in_specs=[smem_spec()] * 2 + [whole_spec()] * 3,
        out_specs=whole_spec(),
        scratch_shapes=[pltpu.VMEM((2 * pairs + MAXLEN, LANES), jnp.float32)] * 3,
        compiler_params=params(),
        cost_estimate=pl.CostEstimate(
            flops=slots * heads * MAXLEN * MAXLEN * LANES * 4,
            bytes_accessed=pairs * heads * LANES * 8,
            transcendentals=slots * heads * MAXLEN * MAXLEN,
        ),
    )(start, span, *flat)


def lane_tiles(width):
    return [(first, min(LANES, width - first)) for first in range(0, width, LANES)]


def pairable(width):
    return width == LANES + LANES // 2


def join_pair(one, two):
    half = LANES // 2
    low = lax.broadcasted_iota(jnp.int32, one[0].shape, 1) < half
    turned = pltpu.roll(two[0], half, 1)
    return (
        one[0],
        jnp.where(low, one[1], turned),
        jnp.where(low, turned, pltpu.roll(two[1], half, 1)),
    )


def split_pair(tiles):
    half = LANES // 2
    low = lax.broadcasted_iota(jnp.int32, tiles[0].shape, 1) < half
    middle = pltpu.roll(tiles[1], half, 1)
    last = pltpu.roll(tiles[2], half, 1)
    return (tiles[0], tiles[1]), (jnp.where(low, middle, last), last)


def slots_kernel(start_ref, rows_ref, out_ref, *held):
    count, width = rows_ref.shape
    for (first, size), rows in zip(lane_tiles(width), held):

        def widen(chunk, carry):
            at = pl.multiple_of(chunk * MAXLEN, MAXLEN)
            rows[pl.ds(at, MAXLEN), 0:size] = rows_ref[
                pl.ds(at, MAXLEN), first : first + size
            ].astype(jnp.float32)
            return carry

        lax.fori_loop(0, count // MAXLEN, widen, 0)
        rows[pl.ds(count, MAXLEN), :] = jnp.zeros((MAXLEN, LANES), jnp.float32)

    def slot_body(slot, carry):
        if pairable(width):
            pair = [
                [rows[pl.ds(start_ref[2 * slot + side], MAXLEN), :] for rows in held]
                for side in range(2)
            ]
            tiles = join_pair(*pair)
        else:
            tiles = [rows[pl.ds(start_ref[slot], MAXLEN), :] for rows in held]
        for index, tile in enumerate(tiles):
            out_ref[slot, :, index * LANES : (index + 1) * LANES] = tile.astype(jnp.bfloat16)
        return carry

    lax.fori_loop(0, out_ref.shape[0], slot_body, 0)


def into_slots(start, rows):
    count, width = rows.shape
    slots = start.shape[0]
    tiles = len(lane_tiles(width))
    shape = (slots, MAXLEN, tiles * LANES)
    if pairable(width):
        shape = (slots // 2, MAXLEN, 2 * width)
    return pl.pallas_call(
        slots_kernel,
        out_shape=jax.ShapeDtypeStruct(shape, jnp.bfloat16),
        in_specs=[smem_spec(), whole_spec()],
        out_specs=whole_spec(),
        scratch_shapes=[pltpu.VMEM((count + MAXLEN, LANES), jnp.float32)] * tiles,
        compiler_params=params(),
    )(start, rows)


def place_kernel(paired, after_ref, x_ref, context_ref, out_ref, context_rows, *x_rows):
    slots = context_ref.shape[0]
    slabs = out_ref.shape[0]
    tall = out_ref.shape[1] * (2 if paired else 1)
    slab_rows = tall - 2 * HALO
    total_rows = context_rows.shape[0]
    held = (context_rows,) + x_rows
    zeros = jnp.zeros((MAXLEN, LANES), jnp.float32)
    for rows in held:
        rows[pl.ds(0, HALO), :] = jnp.zeros((HALO, LANES), jnp.float32)

    def load(ref, slot, tile):
        return ref[slot, :, tile * LANES : (tile + 1) * LANES].astype(jnp.float32)

    def put(step, carry):
        if paired:
            sides = split_pair([load(x_ref, step, tile) for tile in range(3)])
            for side in range(2):
                slot = 2 * step + side
                where = pl.ds(HALO + after_ref[slot], MAXLEN)
                for rows, piece in zip(x_rows, sides[side]):
                    rows[where, :] = piece
                context_rows[where, :] = load(context_ref, slot, 0)
        else:
            where = pl.ds(HALO + after_ref[step], MAXLEN)
            for tile, rows in enumerate(x_rows):
                rows[where, :] = load(x_ref, step, tile)
            context_rows[where, :] = load(context_ref, step, 0)
        return carry

    lax.fori_loop(0, x_ref.shape[0], put, 0)
    live = after_ref[slots]

    def clear(step, carry):
        at = jnp.minimum(HALO + live + step * MAXLEN, total_rows - MAXLEN)
        for rows in held:
            rows[pl.ds(at, MAXLEN), :] = zeros
        return carry

    lax.fori_loop(0, (total_rows - HALO - live + MAXLEN - 1) // MAXLEN, clear, 0)

    def emit(slab, carry):
        at = pl.multiple_of(slab * slab_rows, slab_rows)
        if paired:
            half = tall // 2
            one = pl.ds(at, half)
            two = pl.ds(pl.multiple_of(at + half, 8), half)
            tiles = join_pair([rows[one, :] for rows in x_rows], [rows[two, :] for rows in x_rows])
            tiles = tiles + (context_rows[one, :], context_rows[two, :])
        else:
            tiles = [rows[pl.ds(at, tall), :] for rows in x_rows + (context_rows,)]
        for index, tile in enumerate(tiles):
            out_ref[slab, :, index * LANES : (index + 1) * LANES] = tile.astype(jnp.bfloat16)
        return carry

    lax.fori_loop(0, slabs, emit, 0)


def place(after, x_slots, context_slots, slabs, slab_rows, features):
    count = context_slots.shape[0]
    paired = pairable(features)
    tiles = len(lane_tiles(features))
    tall = slab_rows + 2 * HALO
    shape = (slabs, tall, (tiles + 1) * LANES)
    if paired:
        shape = (slabs, tall // 2, 2 * features + 2 * LANES)
    return pl.pallas_call(
        functools.partial(place_kernel, paired),
        out_shape=jax.ShapeDtypeStruct(shape, jnp.bfloat16),
        in_specs=[smem_spec(), whole_spec(), whole_spec()],
        out_specs=whole_spec(),
        scratch_shapes=[pltpu.VMEM((count * MAXLEN + HALO + MAXLEN, LANES), jnp.float32)]
        * (tiles + 1),
        compiler_params=params(),
    )(after, x_slots, context_slots)


def unplace_kernel(moved_ref, x_ref, context_ref):
    slabs, rows, _ = moved_ref.shape
    step = 16
    span = 3 * LANES

    def chunk(index, carry):
        at = pl.multiple_of(index * step, step)

        def load(slab, tile):
            cells = moved_ref[slab, pl.ds(at, step), tile * LANES : (tile + 1) * LANES]
            return cells.astype(jnp.float32)

        for pair in range(slabs // 2):
            split = [
                split_pair([load(2 * pair + member, tile) for tile in range(3)])
                for member in range(2)
            ]
            for side in range(2):
                to = pl.ds(pl.multiple_of(at + side * rows, step), step)
                for tile, cells in enumerate(join_pair(split[0][side], split[1][side])):
                    first = pair * span + tile * LANES
                    x_ref[to, first : first + LANES] = cells.astype(jnp.bfloat16)
        for slab in range(slabs):
            for side in range(2):
                to = pl.ds(pl.multiple_of(at + side * rows, step), step)
                first = span + side * LANES
                context_ref[to, slab * LANES : (slab + 1) * LANES] = moved_ref[
                    slab, pl.ds(at, step), first : first + LANES
                ]
        return carry

    lax.fori_loop(0, rows // step, chunk, 0)


def unplace(moved, features, context_width):
    slabs, rows, _ = moved.shape
    if not (pairable(features) and context_width == LANES):
        first = len(lane_tiles(features)) * LANES
        x = moved[:, :, :features].transpose(1, 0, 2).reshape(rows, -1)
        context = moved[:, :, first : first + context_width]
        return x, context.transpose(1, 0, 2).reshape(rows, -1)
    return pl.pallas_call(
        unplace_kernel,
        out_shape=(
            jax.ShapeDtypeStruct((2 * rows, slabs * features), jnp.bfloat16),
            jax.ShapeDtypeStruct((2 * rows, slabs * context_width), jnp.bfloat16),
        ),
        in_specs=[whole_spec()],
        out_specs=(whole_spec(), whole_spec()),
        compiler_params=params(),
    )(moved)


def conv_kernel(
    uniform_ref, gated_ref, segment_ref, taps_ref, scale_ref, shift_ref, out_ref, wide
):
    wide[...] = gated_ref[...].astype(jnp.float32)
    edge = HALO - HALF
    scale = scale_ref[...]
    shift = shift_ref[...]
    for chunk in range(out_ref.shape[0] // CONV_ROWS):
        base = chunk * CONV_ROWS

        def finish(total):
            affine = total * scale + shift
            out_ref[base : base + CONV_ROWS, :] = (affine * jax.nn.sigmoid(affine)).astype(
                jnp.bfloat16
            )

        @pl.when(uniform_ref[chunk] == 1)
        def _():
            total = jnp.zeros((CONV_ROWS, LANES), jnp.float32)
            for tap in range(KERNEL):
                total = total + wide[pl.ds(base + edge + tap, CONV_ROWS), :] * taps_ref[
                    tap : tap + 1, :
                ]
            finish(total)

        @pl.when(uniform_ref[chunk] == 0)
        def _():
            centre = segment_ref[pl.ds(base + HALO, CONV_ROWS), :]
            total = jnp.zeros((CONV_ROWS, LANES), jnp.float32)
            for tap in range(KERNEL):
                same = segment_ref[pl.ds(base + edge + tap, CONV_ROWS), :] == centre
                term = jnp.where(same, wide[pl.ds(base + edge + tap, CONV_ROWS), :], 0.0)
                total = total + term * taps_ref[tap : tap + 1, :]
            finish(total)


def convolve(gated_rows, segment, conv_taps, batch_scale, batch_shift):
    tall, width = gated_rows.shape
    rows = tall - 2 * HALO
    chunks = rows // CONV_ROWS
    windows = [segment[c * CONV_ROWS : c * CONV_ROWS + CONV_ROWS + 2 * HALO] for c in range(chunks)]
    windows = jnp.stack(windows)
    uniform = jnp.all(windows == windows[:, :1], axis=1).astype(jnp.int32)
    wide_segment = jnp.broadcast_to(segment[:, None], (tall, LANES))
    return pl.pallas_call(
        conv_kernel,
        grid=(width // LANES,),
        out_shape=jax.ShapeDtypeStruct((rows, width), jnp.bfloat16),
        in_specs=[
            smem_spec(),
            pl.BlockSpec((tall, LANES), lambda i: (0, i)),
            pl.BlockSpec((tall, LANES), lambda i: (0, 0)),
            pl.BlockSpec((KERNEL, LANES), lambda i: (0, i)),
            pl.BlockSpec((1, LANES), lambda i: (0, i)),
            pl.BlockSpec((1, LANES), lambda i: (0, i)),
        ],
        out_specs=pl.BlockSpec((rows, LANES), lambda i: (0, i)),
        scratch_shapes=[pltpu.VMEM((tall, LANES), jnp.float32)],
        compiler_params=params(),
        cost_estimate=pl.CostEstimate(
            flops=2 * rows * width * KERNEL, bytes_accessed=4 * rows * width, transcendentals=0
        ),
    )(
        uniform,
        gated_rows,
        wide_segment,
        conv_taps,
        batch_scale[None, :],
        batch_shift[None, :],
    )


MESH = pl.DeviceIdType.MESH
OUT, GLU_ONE, GLU_TWO, DOWN = range(4)


def any_spec():
    return pl.BlockSpec(memory_space=pl.ANY)


class Place:
    def __init__(self):
        self.dp = lax.axis_index("dp")
        self.mp = lax.axis_index("mp")
        self.y, self.c = self.dp // 2, self.dp % 2
        self.z, self.x = self.mp // 2, self.mp % 2
        self.across = 1 - self.x
        self.near = self.z + 1 - 2 * (self.z % 2)
        self.far_one = 2 - self.z // 2
        self.far_two = 3 - 3 * (self.z // 2)

    def x_side(self):
        return (self.dp, 2 * self.z + self.across)

    def y_side(self):
        return (2 * (1 - self.y) + self.c, self.mp)

    def core_side(self):
        return (2 * self.y + 1 - self.c, self.mp)

    def corner(self):
        return (2 * (1 - self.y) + 1 - self.c, self.mp)

    def above(self):
        return (self.dp, self.mp + 2)

    def below(self):
        return (self.dp, self.mp - 2)


def aligned(index, step):
    return pl.multiple_of(index * step, step)


def piece(weights, kind, z, x, y, c, both_y=False):
    shard = 2 * z + x
    if kind == OUT:
        return weights[0].at[pl.ds(aligned(shard, 192), 192), pl.ds(aligned(c, 512), 512)]
    if kind == GLU_ONE:
        return weights[1].at[pl.ds(aligned(c, 256), 256), pl.ds(aligned(shard, 384), 384)]
    if kind == GLU_TWO:
        if both_y:
            rows = pl.ds(pl.multiple_of(512 + c * 512, 256), 512)
        else:
            rows = pl.ds(pl.multiple_of(512 + (c * 2 + y) * 256, 256), 256)
        return weights[1].at[rows, pl.ds(aligned(shard, 384), 384)]
    if both_y:
        columns = pl.ds(aligned(c, 768), 768)
    else:
        columns = pl.ds(aligned(c * 2 + y, 384), 384)
    return weights[2].at[pl.ds(aligned(shard, 192), 192), columns]


def own_piece(shards, kind, y, c):
    if kind == OUT:
        return shards[0].at[:, pl.ds(aligned(c, 512), 512)]
    if kind == GLU_ONE:
        return shards[1].at[pl.ds(aligned(c, 256), 256), :]
    if kind == GLU_TWO:
        return shards[1].at[pl.ds(pl.multiple_of(512 + (c * 2 + y) * 256, 256), 256), :]
    return shards[2].at[:, pl.ds(aligned(c * 2 + y, 384), 384)]


class Mail:
    def __init__(self, send_sems, recv_sems):
        self.send_sems, self.recv_sems = send_sems, recv_sems
        self.used = 0
        self.sent = []

    def slot(self):
        self.used += 1
        return self.used - 1

    def copy(self, slot, source, target, device):
        return pltpu.make_async_remote_copy(
            src_ref=source,
            dst_ref=target,
            send_sem=self.send_sems.at[slot],
            recv_sem=self.recv_sems.at[slot],
            device_id=device,
            device_id_type=MESH,
        )

    def send(self, slot, source, target, device, when=None):
        copy = self.copy(slot, source, target, device)
        run_if(when, copy.start)
        self.sent.append((copy, when))

    def receive(self, slot, target, device, when=None):
        run_if(when, self.copy(slot, target, target, device).wait_recv)

    def finish(self):
        for copy, when in self.sent:
            run_if(when, copy.wait_send)


def run_if(when, action):
    if when is None:
        action()
    else:
        pl.when(when)(action)


def greet(devices):
    barrier = pltpu.get_barrier_semaphore()

    def hello(device):
        pl.semaphore_signal(barrier, inc=1, device_id=device, device_id_type=MESH)

    count = 0
    for device, when in devices:
        if when is None:
            hello(device)
            count = count + 1
        else:
            pl.when(when)(functools.partial(hello, device))
            count = count + when.astype(jnp.int32)
    pl.semaphore_wait(barrier, count)


KINDS = (GLU_ONE, OUT, GLU_TWO, DOWN)
FIRST = (GLU_TWO, OUT, GLU_ONE)


def find_slots(dp, lengths_ref, assignment_ref, start_ref, span_ref):
    groups = start_ref.shape[0] // PIECES
    per_group = lengths_ref.shape[0] // groups
    zero = jnp.int32(0)
    counts = [zero] * groups
    starts = [zero] * (groups * PIECES)
    spans = [zero] * (groups * PIECES)
    before = zero
    for i in range(per_group):
        target = assignment_ref[dp * per_group + i]
        length = lengths_ref[dp * per_group + i]
        for group in range(groups):
            hit = target == group
            for rank in range(PIECES):
                slot = group * PIECES + rank
                found = hit & (counts[group] == rank)
                starts[slot] = jnp.where(found, before, starts[slot])
                spans[slot] = jnp.where(found, length, spans[slot])
            counts[group] = counts[group] + hit.astype(jnp.int32)
        before = before + length
    for slot in range(groups * PIECES):
        start_ref[slot] = starts[slot]
        span_ref[slot] = spans[slot]


def move_kernel(
    lengths_ref,
    assignment_ref,
    q_ref,
    k_ref,
    v_ref,
    residual_ref,
    out_shard,
    glu_shard,
    down_shard,
    x_got,
    context_got,
    out_all,
    glu_all,
    down_all,
    q_rows,
    k_rows,
    v_rows,
    x_low,
    x_high,
    x_send,
    context_send,
    out_held,
    glu_held,
    down_held,
    mixed,
    start_ref,
    span_ref,
    send_sems,
    recv_sems,
    local_sems,
):
    here = Place()
    z, x, y, c = here.z, here.x, here.y, here.c
    weights = (out_all, glu_all, down_all)
    shards = (out_shard, glu_shard, down_shard)
    held = (out_held, glu_held, down_held)
    mail = Mail(send_sems, recv_sems)
    up, down = z < 3, z > 0
    partners = (here.y_side(), here.corner(), here.core_side())
    greet(
        [(device, None) for device in partners + (here.x_side(),)]
        + [(here.above(), up), (here.below(), down)]
    )

    def spot(kind, zz, xx):
        return piece(weights, kind, zz, xx, y, c)

    own = (
        out_all.at[pl.ds(aligned(here.mp, 192), 192), :],
        glu_all.at[:, pl.ds(aligned(here.mp, 384), 384)],
        down_all.at[pl.ds(aligned(here.mp, 192), 192), :],
    )
    into = [
        pltpu.make_async_copy(shards[i], held[i], local_sems.at[i]) for i in range(3)
    ]
    locals_ = [pltpu.make_async_copy(held[i], own[i], local_sems.at[5 + i]) for i in range(3)]
    slots_up, slots_down, slots_x, slots_near = [
        {kind: mail.slot() for kind in KINDS} for _ in range(4)
    ]
    slots_up_two, slots_down_two = [{kind: mail.slot() for kind in KINDS} for _ in range(2)]
    for kind in KINDS:
        mine = own_piece(shards, kind, y, c)
        mail.send(slots_up[kind], mine, spot(kind, z, x), here.above(), up)
        mail.send(slots_down[kind], mine, spot(kind, z, x), here.below(), down)
        mail.send(slots_x[kind], mine, spot(kind, z, x), here.x_side())
    for copy in into:
        copy.start()
    find_slots(here.dp, lengths_ref, assignment_ref, start_ref, span_ref)

    count = 4 * residual_ref.shape[0]
    step = 128
    low = lax.broadcasted_iota(jnp.int32, (step, LANES), 1) < HD

    def open_rows(chunk, carry):
        first = pl.multiple_of(chunk * step, step)
        cells = [
            residual_ref[pl.ds(first, step), i * LANES : (i + 1) * LANES].astype(jnp.float32)
            for i in range(6)
        ]
        turned = [pltpu.roll(cells[i], HD, 1) for i in (1, 2, 4, 5)]
        frames = (
            (cells[0], cells[1]),
            (jnp.where(low, turned[0], turned[1]), turned[1]),
            (cells[3], cells[4]),
            (jnp.where(low, turned[2], turned[3]), turned[3]),
        )
        for j, (one, two) in enumerate(frames):
            at = pl.ds(4 * first + j, step, stride=4)
            x_low[at, :] = one
            x_high[at, :] = two
        return carry

    lax.fori_loop(0, residual_ref.shape[0] // step, open_rows, 0)
    for rows in (x_low, x_high):
        rows[pl.ds(count, MAXLEN), :] = jnp.zeros((MAXLEN, LANES), jnp.float32)

    def relay(kind):
        mail.receive(slots_up[kind], spot(kind, z - 1, x), here.above(), down)
        mail.send(
            slots_up_two[kind],
            spot(kind, z - 1, x),
            spot(kind, z - 1, x),
            here.above(),
            up & down,
        )
        mail.receive(slots_down[kind], spot(kind, z + 1, x), here.below(), up)
        mail.send(
            slots_down_two[kind],
            spot(kind, z + 1, x),
            spot(kind, z + 1, x),
            here.below(),
            up & down,
        )
        mail.send(
            slots_near[kind],
            spot(kind, here.near, x),
            spot(kind, here.near, x),
            here.x_side(),
        )

    targets = partners + ((here.dp, here.mp),)
    half = PIECES // 2
    x_slots = [mail.slot() for _ in partners]
    context_slots = [mail.slot() for _ in partners]
    for index, target in enumerate(targets):
        group = target[0]

        def fill(pair, carry):
            at = group * half + pair
            both = [
                [
                    rows[pl.ds(start_ref[2 * at + side], MAXLEN), :]
                    for rows in (x_low, x_high)
                ]
                for side in range(2)
            ]
            for tile, cells in enumerate(join_pair(*both)):
                x_send[at, :, tile * LANES : (tile + 1) * LANES] = cells.astype(jnp.bfloat16)
            return carry

        lax.fori_loop(0, half, fill, 0)
        source = x_send.at[pl.ds(group * half, half)]
        landing = x_got.at[pl.ds(here.dp * half, half)]
        if index < 3:
            mail.send(x_slots[index], source, landing, target)
        else:
            copy = pltpu.make_async_copy(source, landing, local_sems.at[3])
            copy.start()
            locals_.append(copy)

    relay(KINDS[0])
    for copy_in, copy_out in zip(into, locals_):
        copy_in.wait()
        copy_out.start()

    pairs = q_ref.shape[0] // 2
    wide_low = lax.broadcasted_iota(jnp.int32, (256, LANES), 1) < HD

    def unpack(chunk, carry):
        first = pl.multiple_of(chunk * 256, 256)
        for i, (packed, rows) in enumerate(((q_ref, q_rows), (k_ref, k_rows), (v_ref, v_rows))):
            mixed[i] = packed[pl.ds(2 * first, 512), :].astype(jnp.float32)
            one = mixed[i, pl.ds(0, 256, stride=2), :]
            two = mixed[i, pl.ds(1, 256, stride=2), :]
            rows[pl.ds(2 * first, 256, stride=2), :] = jnp.where(
                wide_low, one, pltpu.roll(two, HD, 1)
            )
            rows[pl.ds(2 * first + 1, 256, stride=2), :] = jnp.where(
                wide_low, pltpu.roll(one, HD, 1), two
            )
        return carry

    lax.fori_loop(0, pairs // 256, unpack, 0)
    for rows in (q_rows, k_rows, v_rows):
        rows[pl.ds(2 * pairs, MAXLEN), :] = jnp.zeros((MAXLEN, LANES), jnp.float32)

    relay(KINDS[1])
    column = lax.broadcasted_iota(jnp.int32, (MAXLEN, MAXLEN), 1)
    head_lane = lax.broadcasted_iota(jnp.int32, (MAXLEN, LANES), 1) // HD

    def attend_slot(slot):
        start = start_ref[slot]
        allowed = column < span_ref[slot]
        queries = q_rows[pl.ds(start, MAXLEN), :]
        keys = k_rows[pl.ds(start, MAXLEN), :].astype(jnp.bfloat16)
        values = v_rows[pl.ds(start, MAXLEN), :].astype(jnp.bfloat16)
        result = None
        for head in range(2):
            own = jnp.where(head_lane == head, queries, 0.0).astype(jnp.bfloat16)
            scores = (
                lax.dot_general(
                    own, keys, (((1,), (1,)), ((), ())), preferred_element_type=jnp.float32
                )
                * HD ** (-0.5)
            )
            scores = jnp.where(allowed, scores, MASKED)
            highest = jnp.max(scores, axis=1, keepdims=True)
            exponentials = jnp.exp(scores - highest)
            denominator = jnp.sum(exponentials, axis=1, keepdims=True)
            weighing = (exponentials / denominator).astype(jnp.bfloat16)
            blended = jnp.dot(weighing, values, preferred_element_type=jnp.float32)
            result = blended if head == 0 else jnp.where(head_lane == head, blended, result)
        context_send[slot] = result.astype(jnp.bfloat16)

    for index, target in enumerate(targets):
        group = target[0]

        def attend_one(rank, carry):
            attend_slot(group * PIECES + rank)
            return carry

        lax.fori_loop(0, PIECES, attend_one, 0)
        source = context_send.at[pl.ds(group * PIECES, PIECES)]
        landing = context_got.at[pl.ds(here.dp * PIECES, PIECES)]
        if index < 3:
            mail.send(context_slots[index], source, landing, target)
        else:
            copy = pltpu.make_async_copy(source, landing, local_sems.at[4])
            copy.start()
            locals_.append(copy)
        if index < 2:
            relay(KINDS[2 + index])

    for index, source in enumerate(partners):
        mail.receive(x_slots[index], x_got.at[pl.ds(source[0] * half, half)], source)
        mail.receive(
            context_slots[index], context_got.at[pl.ds(source[0] * PIECES, PIECES)], source
        )
    for kind in KINDS:
        mail.receive(slots_x[kind], spot(kind, z, here.across), here.x_side())
        mail.receive(slots_near[kind], spot(kind, here.near, here.across), here.x_side())
        mail.receive(slots_up_two[kind], spot(kind, z - 2, x), here.above(), z > 1)
        mail.receive(slots_down_two[kind], spot(kind, z + 2, x), here.below(), z < 2)
    mail.finish()
    for copy in locals_:
        copy.wait()


def move(lengths, assignment, queries, keys, values, residual, out_shard, glu_shard, down_shard):
    slots = 4 * PIECES
    pairs = queries.shape[0] // 2
    count = 4 * residual.shape[0]
    bf16 = jnp.bfloat16
    return pl.pallas_call(
        move_kernel,
        out_shape=(
            jax.ShapeDtypeStruct((slots // 2, MAXLEN, 3 * LANES), bf16),
            jax.ShapeDtypeStruct((slots, MAXLEN, LANES), bf16),
            jax.ShapeDtypeStruct((1536, 1024), bf16),
            jax.ShapeDtypeStruct((1536, 3072), bf16),
            jax.ShapeDtypeStruct((1536, 1536), bf16),
        ),
        in_specs=[smem_spec()] * 2 + [whole_spec()] * 4 + [any_spec()] * 3,
        out_specs=(any_spec(),) * 5,
        scratch_shapes=[pltpu.VMEM((2 * pairs + MAXLEN, LANES), jnp.float32)] * 3
        + [pltpu.VMEM((count + MAXLEN, LANES), jnp.float32)] * 2
        + [
            pltpu.VMEM((slots // 2, MAXLEN, 3 * LANES), bf16),
            pltpu.VMEM((slots, MAXLEN, LANES), bf16),
            pltpu.VMEM(out_shard.shape, bf16),
            pltpu.VMEM(glu_shard.shape, bf16),
            pltpu.VMEM(down_shard.shape, bf16),
            pltpu.VMEM((3, 512, LANES), jnp.float32),
            pltpu.SMEM((slots,), jnp.int32),
            pltpu.SMEM((slots,), jnp.int32),
            pltpu.SemaphoreType.DMA((30,)),
            pltpu.SemaphoreType.DMA((30,)),
            pltpu.SemaphoreType.DMA((8,)),
        ],
        compiler_params=pltpu.CompilerParams(
            vmem_limit_bytes=VMEM_LIMIT, collective_id=1, has_side_effects=True
        ),
        cost_estimate=pl.CostEstimate(
            flops=slots * 2 * MAXLEN * MAXLEN * LANES * 4,
            bytes_accessed=50 * 1024 * 1024,
            transcendentals=slots * 2 * MAXLEN * MAXLEN,
        ),
    )(lengths, assignment, queries, keys, values, residual, out_shard, glu_shard, down_shard)


SPLIT = 288
PARTS = ((0, SPLIT // 2, 0, SPLIT - 2 * HALO), (SPLIT, 272 - SPLIT // 2, SPLIT - 2 * HALO, 544 - SPLIT))
ROW_STEP = 16
EXCHANGE_ORDER = ((3, 1), (3, 0), (2, 0), (2, 1), (1, 0), (1, 1), (0, 1))


def place_parts_kernel(
    lengths_ref, assignment_ref, x_ref, context_ref, out_ref, after_ref, context_rows, *x_rows
):
    dp = lax.axis_index("dp")
    after_ref[0] = 0

    def seek(u, carry):
        count, total = carry
        hit = assignment_ref[u] == dp
        total = total + jnp.where(hit, lengths_ref[u], 0)
        count = count + hit.astype(jnp.int32)
        after_ref[count] = total
        return count, total

    lax.fori_loop(0, lengths_ref.shape[0], seek, (jnp.int32(0), jnp.int32(0)))
    slots = context_ref.shape[0]
    slabs = out_ref.shape[0]
    tall = out_ref.shape[1] * 2
    slab_rows = tall - 2 * HALO
    total_rows = context_rows.shape[0]
    held = (context_rows,) + x_rows
    zeros = jnp.zeros((MAXLEN, LANES), jnp.float32)
    for rows in held:
        rows[pl.ds(0, HALO), :] = jnp.zeros((HALO, LANES), jnp.float32)

    def load(ref, slot, tile):
        return ref[slot, :, tile * LANES : (tile + 1) * LANES].astype(jnp.float32)

    def put(step, carry):
        sides = split_pair([load(x_ref, step, tile) for tile in range(3)])
        for side in range(2):
            slot = 2 * step + side
            where = pl.ds(HALO + after_ref[slot], MAXLEN)
            for rows, piece in zip(x_rows, sides[side]):
                rows[where, :] = piece
            context_rows[where, :] = load(context_ref, slot, 0)
        return carry

    lax.fori_loop(0, x_ref.shape[0], put, 0)
    live = after_ref[slots]

    def clear(step, carry):
        at = jnp.minimum(HALO + live + step * MAXLEN, total_rows - MAXLEN)
        for rows in held:
            rows[pl.ds(at, MAXLEN), :] = zeros
        return carry

    lax.fori_loop(0, (total_rows - HALO - live + MAXLEN - 1) // MAXLEN, clear, 0)

    def emit(slab, carry):
        at = pl.multiple_of(slab * slab_rows, slab_rows)
        for first, half, *_ in PARTS:
            one = pl.ds(pl.multiple_of(at + first, 16), half)
            two = pl.ds(pl.multiple_of(at + first + half, 16), half)
            tiles = join_pair(
                [rows[one, :] for rows in x_rows], [rows[two, :] for rows in x_rows]
            )
            tiles = tiles + (context_rows[one, :], context_rows[two, :])
            for index, tile in enumerate(tiles):
                lanes = slice(index * LANES, (index + 1) * LANES)
                out_ref[slab, first // 2 : first // 2 + half, lanes] = tile.astype(
                    jnp.bfloat16
                )
        return carry

    lax.fori_loop(0, slabs, emit, 0)


def place_parts(lengths, assignment, x_slots, context_slots, slabs):
    count = context_slots.shape[0]
    return pl.pallas_call(
        place_parts_kernel,
        out_shape=(
            jax.ShapeDtypeStruct((slabs, 272, 5 * LANES), jnp.bfloat16),
            jax.ShapeDtypeStruct((count + 1,), jnp.int32),
        ),
        in_specs=[smem_spec()] * 2 + [whole_spec()] * 2,
        out_specs=(whole_spec(), smem_spec()),
        scratch_shapes=[pltpu.VMEM((count * MAXLEN + HALO + MAXLEN, LANES), jnp.float32)] * 3,
        compiler_params=params(),
    )(lengths, assignment, x_slots, context_slots)


def finish_kernel(
    after_ref,
    slabs_ref,
    gain_ref,
    bias_ref,
    scale_ref,
    shift_ref,
    taps_ref,
    out_in,
    glu_in,
    down_in,
    encoded_ref,
    out_all,
    glu_all,
    down_all,
    moved,
    carried,
    context,
    normed,
    wide,
    swished,
    first_tap,
    last_tap,
    out_held,
    glu_held,
    down_held,
    send_sems,
    recv_sems,
    local_sems,
):
    here = Place()
    z, x, y, c = here.z, here.x, here.y, here.c
    weights = (out_all, glu_all, down_all)
    mail = Mail(send_sems, recv_sems)
    slabs = slabs_ref.shape[0]
    mirrors = (z, here.near, z + 2 - 4 * (z // 2), 3 - z)
    sides = (x, here.across)
    others = [(here.dp, 2 * mirrors[dz] + sides[dx]) for dz, dx in EXCHANGE_ORDER]
    greet([(device, None) for device in others + [here.y_side(), here.core_side()]])

    slab_slots = [[mail.slot() for _ in others] for _ in PARTS]

    def part_rows(part):
        first, half, *_ = PARTS[part]
        return pl.ds(first // 2, half)

    def exchange(part, crossing):
        for index, device in enumerate(others):
            if EXCHANGE_ORDER[index][1] != crossing:
                continue
            mail.send(
                slab_slots[part][index],
                slabs_ref.at[device[1], part_rows(part)],
                moved.at[here.mp, part_rows(part)],
                device,
            )

    def exchanged(part):
        for index in range(len(others)):
            mail.receive(
                slab_slots[part][index],
                moved.at[others[index][1], part_rows(part)],
                others[index],
            )

    tile_width = 768
    tiles = carried.shape[1] // tile_width
    keep = pltpu.make_async_copy(slabs_ref.at[here.mp], moved.at[here.mp], local_sems.at[0])
    keep.start()

    def spot(kind, zz, xx):
        return piece(weights, kind, zz, xx, y, c)

    table = {}

    def slot(*key):
        if key not in table:
            table[key] = mail.slot()
        return table[key]

    def pass_on(name, kind, zz, xx, device, when=None):
        where = spot(kind, zz, xx)
        mail.send(slot(name, kind), where, where, device, when)

    cells = {
        "own near": (here.near, x),
        "own one": (here.far_one, x),
        "own two": (here.far_two, x),
        "other own": (z, here.across),
        "other near": (here.near, here.across),
        "other one": (here.far_one, here.across),
        "other two": (here.far_two, here.across),
    }
    early = ("own near", "own one", "other own", "other near")
    order = early + ("other one", "own two", "other two")

    def after(kind, cell):
        if kind in (OUT, GLU_ONE):
            pass_on("core " + cell, kind, *cells[cell], here.core_side())
        else:
            pass_on("y " + cell, kind, *cells[cell], here.y_side())

    def from_y(kind):
        for cell in order:
            mail.receive(
                slot("y " + cell, kind),
                piece(weights, kind, *cells[cell], 1 - y, c),
                here.y_side(),
            )
            where = piece(weights, kind, *cells[cell], y, c, both_y=True)
            mail.send(slot("core " + cell, kind), where, where, here.core_side())

    def from_core(kind):
        for cell in order:
            where = piece(weights, kind, *cells[cell], y, 1 - c, both_y=kind in (GLU_TWO, DOWN))
            mail.receive(slot("core " + cell, kind), where, here.core_side())

    def start_across(kinds):
        for kind in kinds:
            pass_on("third up", kind, 0, x, here.above(), z == 2)
            pass_on("third down", kind, 3, x, here.below(), z == 1)
            pass_on("x one", kind, here.far_one, x, here.x_side())
        for kind in kinds:
            for cell in early:
                after(kind, cell)

    def across_one(kinds):
        for kind in kinds:
            mail.receive(slot("x one", kind), spot(kind, *cells["other one"]), here.x_side())
            after(kind, "other one")
        for kind in kinds:
            mail.receive(slot("third up", kind), spot(kind, 0, x), here.above(), z == 3)
            mail.receive(slot("third down", kind), spot(kind, 3, x), here.below(), z == 0)
            pass_on("x two", kind, here.far_two, x, here.x_side())
            after(kind, "own two")

    def across_two(kinds):
        for kind in kinds:
            mail.receive(slot("x two", kind), spot(kind, *cells["other two"]), here.x_side())
            after(kind, "other two")

    start_across(FIRST)
    exchange(0, 0)
    live = after_ref[4 * PIECES]

    def bounds(step, carry):
        rows = pl.ds(pl.multiple_of(step * 64, 64), 64)
        position = (
            lax.broadcasted_iota(jnp.int32, (64, LANES), 0)
            + step * 64
            + here.mp * encoded_ref.shape[0]
        )
        begin = jnp.zeros((64, LANES), jnp.int32)
        end = jnp.full((64, LANES), live, jnp.int32)
        for k in range(1, 4 * PIECES):
            begin = jnp.where(position >= after_ref[k], after_ref[k], begin)
        for k in range(4 * PIECES - 1, 0, -1):
            end = jnp.where(position < after_ref[k], after_ref[k], end)
        first_tap[rows, :] = HALF + begin - position
        last_tap[rows, :] = HALF - 1 + end - position
        return carry

    lax.fori_loop(0, encoded_ref.shape[0] // 64, bounds, 0)

    across_one(FIRST)
    exchange(0, 1)
    start_across((DOWN,))
    exchange(1, 0)
    exchange(1, 1)
    across_two(FIRST)
    from_y(GLU_TWO)
    loads = [
        pltpu.make_async_copy(weights[i], (out_held, glu_held, down_held)[i], local_sems.at[1 + i])
        for i in range(3)
    ]

    def glu_load(n, side):
        columns = pl.ds(aligned(n + side * tiles, tile_width), tile_width)
        return pltpu.make_async_copy(
            weights[1].at[:, columns],
            glu_held.at[:, columns],
            local_sems.at[4 + 2 * n + side],
        )

    from_core(OUT)
    loads[0].start()

    def open_part(part):
        first, half, *_ = PARTS[part]

        def chunk(index, carry):
            at = pl.ds(pl.multiple_of(first // 2 + index * 16, 16), 16)

            def load(slab, tile):
                cells_ = moved[slab, at, tile * LANES : (tile + 1) * LANES]
                return cells_.astype(jnp.float32)

            to = [pl.ds(pl.multiple_of(first + s * half + index * 16, 16), 16) for s in range(2)]
            near = [pl.ds(pl.multiple_of(s * half + index * 16, 16), 16) for s in range(2)]
            for pair in range(slabs // 2):
                split = [
                    split_pair([load(2 * pair + member, tile) for tile in range(3)])
                    for member in range(2)
                ]
                for side in range(2):
                    for tile, cells_ in enumerate(join_pair(split[0][side], split[1][side])):
                        begin = (3 * pair + tile) * LANES
                        carried[to[side], begin : begin + LANES] = cells_
            for slab in range(slabs):
                for side in range(2):
                    begin = (3 + side) * LANES
                    context[near[side], slab * LANES : (slab + 1) * LANES] = moved[
                        slab, at, begin : begin + LANES
                    ]
            return carry

        lax.fori_loop(0, half // 16, chunk, 0)

    def attach(part):
        first, half, *_ = PARTS[part]

        def tile(n, carry):
            columns = pl.ds(aligned(n, tile_width), tile_width)
            carried[first : first + 2 * half, columns] += lax.dot_general(
                context[0 : 2 * half, :],
                out_held[columns, :],
                (((1,), (1,)), ((), ())),
                preferred_element_type=jnp.float32,
            )
            return carry

        lax.fori_loop(0, tiles, tile, 0)

        def normalise(index, carry):
            at = pl.ds(pl.multiple_of(first + index * 32, 32), 32)
            to = pl.ds(pl.multiple_of(index * 32, 32), 32)
            cells_ = carried[at, :]
            centred = cells_ - jnp.mean(cells_, axis=1, keepdims=True)
            variance = jnp.mean(centred * centred, axis=1, keepdims=True)
            inverse = lax.rsqrt(variance + EPS)
            for i in range(carried.shape[1] // LANES):
                lanes = slice(i * LANES, (i + 1) * LANES)
                scaled = centred[:, lanes] * inverse * gain_ref[i : i + 1, :] + bias_ref[i : i + 1, :]
                normed[to, lanes] = scaled.astype(jnp.bfloat16)
            return carry

        lax.fori_loop(0, 2 * half // 32, normalise, 0)

    def gate(part):
        first, half, *_ = PARTS[part]

        def tile(n, carry):
            columns = pl.ds(aligned(n, tile_width), tile_width)
            if part == 0:
                for side in range(2):
                    glu_load(n, side).wait()
            rows = normed[0 : 2 * half, :]
            value = jnp.dot(rows, glu_held[:, columns], preferred_element_type=jnp.float32)
            gates = jnp.dot(
                rows,
                glu_held[:, pl.ds(aligned(n + tiles, tile_width), tile_width)],
                preferred_element_type=jnp.float32,
            )
            gated = (value * jax.nn.sigmoid(gates)).astype(jnp.bfloat16)
            for side in range(tile_width // LANES):
                wide[tile_width // LANES * n + side, first : first + 2 * half, :] = gated[
                    :, side * LANES : (side + 1) * LANES
                ].astype(jnp.float32)
            return carry

        lax.fori_loop(0, tiles, tile, 0)

    def convolve_part(part):
        start, count_rows = PARTS[part][2:]
        steps = count_rows // ROW_STEP
        group = 6
        groups = carried.shape[1] // (group * LANES)

        def body(index, carry):
            row = start + lax.rem(index, steps) * ROW_STEP
            column = index // steps * (group * LANES)
            rows = pl.ds(pl.multiple_of(row, ROW_STEP), ROW_STEP)
            low, high = first_tap[rows, :], last_tap[rows, :]
            lanes = [pl.ds(pl.multiple_of(column + i * LANES, LANES), LANES) for i in range(group)]
            totals = [jnp.zeros((ROW_STEP, LANES), jnp.float32) for _ in range(group)]
            for shift in range(8):
                count = ROW_STEP + (24 if shift < 7 else 16)
                at = pl.ds(row + HALO - HALF + shift, count)
                seen = [wide[column // LANES + i, at, :] for i in range(group)]
                for k in range(4 if shift < 7 else 3):
                    tap = shift + 8 * k
                    if tap < HALF:
                        mask = low <= tap
                    else:
                        mask = high >= tap
                    for i in range(group):
                        term = seen[i][8 * k : 8 * k + ROW_STEP] * taps_ref[tap : tap + 1, lanes[i]]
                        if tap != HALF:
                            term = jnp.where(mask, term, 0.0)
                        totals[i] = totals[i] + term
            for i in range(group):
                one = pl.ds(column // LANES + i, 1)
                affine = totals[i] * scale_ref[one, :] + shift_ref[one, :]
                swished[rows, lanes[i]] = (affine * jax.nn.sigmoid(affine)).astype(jnp.bfloat16)
            return carry

        lax.fori_loop(0, steps * groups, body, 0)

    def lower():
        start, count_rows = 0, encoded_ref.shape[0]
        rows = pl.ds(start, count_rows)

        def tile(n, carry):
            columns = pl.ds(aligned(n, tile_width), tile_width)
            total = carried[start + HALO : start + HALO + count_rows, columns] + lax.dot_general(
                swished[rows, :],
                down_held[columns, :],
                (((1,), (1,)), ((), ())),
                preferred_element_type=jnp.float32,
            )
            alive = last_tap[rows, :] >= HALF
            for side in range(tile_width // LANES):
                lane = pl.ds(pl.multiple_of(n * tile_width + side * LANES, LANES), LANES)
                encoded_ref[rows, lane] = jnp.where(
                    alive, total[:, side * LANES : (side + 1) * LANES], 0.0
                ).astype(jnp.bfloat16)
            return carry

        lax.fori_loop(0, tiles, tile, 0)

    keep.wait()
    exchanged(0)
    open_part(0)
    loads[0].wait()
    attach(0)
    from_core(GLU_ONE)
    from_core(GLU_TWO)
    for n in range(tiles):
        for side in range(2):
            glu_load(n, side).start()
    gate(0)
    across_one((DOWN,))
    convolve_part(0)
    across_two((DOWN,))
    exchanged(1)
    open_part(1)
    attach(1)
    from_y(DOWN)
    gate(1)
    from_core(DOWN)
    loads[2].start()
    convolve_part(1)
    loads[2].wait()
    lower()
    mail.finish()


def finish(after, slabs, norm, taps, out_all, glu_all, down_all):
    norm = [a.reshape(-1, LANES) for a in norm]
    bf16, f32 = jnp.bfloat16, jnp.float32
    width = taps.shape[1]
    rows = 512
    tall = rows + 2 * HALO
    weights = (out_all, glu_all, down_all)
    return pl.pallas_call(
        finish_kernel,
        out_shape=(jax.ShapeDtypeStruct((rows, width), bf16),)
        + tuple(jax.ShapeDtypeStruct(a.shape, a.dtype) for a in weights),
        in_specs=[smem_spec(), any_spec()] + [whole_spec()] * 5 + [any_spec()] * 3,
        out_specs=(whole_spec(),) + (any_spec(),) * 3,
        input_output_aliases={7: 1, 8: 2, 9: 3},
        scratch_shapes=[
            pltpu.VMEM(slabs.shape, bf16),
            pltpu.VMEM((tall, width), f32),
            pltpu.VMEM((SPLIT, 1024), bf16),
            pltpu.VMEM((SPLIT, width), bf16),
            pltpu.VMEM((width // LANES, tall, LANES), f32),
            pltpu.VMEM((rows, width), bf16),
            pltpu.VMEM((rows, LANES), jnp.int32),
            pltpu.VMEM((rows, LANES), jnp.int32),
        ]
        + [pltpu.VMEM(a.shape, bf16) for a in weights]
        + [
            pltpu.SemaphoreType.DMA((80,)),
            pltpu.SemaphoreType.DMA((80,)),
            pltpu.SemaphoreType.DMA((16,)),
        ],
        compiler_params=pltpu.CompilerParams(
            vmem_limit_bytes=VMEM_LIMIT, collective_id=2, has_side_effects=True
        ),
    )(after, slabs, *norm, taps, *weights)[0]


def on_device(
    query_rows,
    key_rows,
    value_rows,
    residual,
    lengths,
    assignment,
    out_proj,
    norm_gain,
    norm_bias,
    glu_proj,
    conv_taps,
    batch_scale,
    batch_shift,
    down_proj,
):
    data_group = lax.axis_index("dp")
    slab_index = lax.axis_index("mp")
    groups = lax.axis_size("dp")
    slabs = lax.axis_size("mp")
    group_rows = query_rows.shape[0] * 2
    slab_rows = group_rows // slabs
    total_utterances = lengths.shape[0]
    per_group = total_utterances // groups
    slots = groups * PIECES
    features = residual.shape[2] // 4

    fits = (
        (groups, slabs) == (4, 8)
        and query_rows.shape == (2048, 2, LANES)
        and residual.shape == (1024, 1, 768)
    )
    if fits:
        flat = [a.reshape(4096, LANES) for a in (query_rows, key_rows, value_rows)]
        x_slots, context_slots, *weights = move(
            lengths, assignment, *flat, residual.reshape(1024, 768), out_proj.T, glu_proj, down_proj.T
        )
        placed, after = place_parts(lengths, assignment, x_slots, context_slots, slabs)
        norm = (norm_gain, norm_bias, batch_scale, batch_shift)
        return finish(after, placed, norm, conv_taps, *weights)

    utterance = jnp.arange(total_utterances, dtype=jnp.int32)
    source = utterance // per_group
    earlier = utterance[None, :] < utterance[:, None]
    same_source = source[None, :] == source[:, None]
    same_target = assignment[None, :] == assignment[:, None]
    before = jnp.sum(jnp.where(earlier & same_source, lengths[None, :], 0), axis=1)
    rank = jnp.sum((earlier & same_source & same_target).astype(jnp.int32), axis=1)
    slot = jnp.arange(slots, dtype=jnp.int32)[:, None]
    leaving = (source[None, :] == data_group) & ((assignment * PIECES + rank)[None, :] == slot)
    start = jnp.sum(jnp.where(leaving, before[None, :], 0), axis=1)
    span = jnp.sum(jnp.where(leaving, lengths[None, :], 0), axis=1)
    coming_earlier = (assignment[None, :] == data_group) & (
        (source * PIECES + rank)[None, :] < jnp.arange(slots + 1, dtype=jnp.int32)[:, None]
    )
    after = jnp.sum(jnp.where(coming_earlier, lengths[None, :], 0), axis=1)
    live = jnp.sum(jnp.where(assignment == data_group, lengths, 0))

    position = jnp.arange(slab_rows + 2 * HALO, dtype=jnp.int32) + slab_index * slab_rows - HALO
    segment = jnp.sum((position[:, None] >= after[None, 1:]).astype(jnp.int32), axis=1)
    segment = jnp.where(position < 0, -2, jnp.where(position < live, segment, -1))
    segment = jnp.where(position >= group_rows, -2, segment)

    residual_rows = (
        residual.reshape(group_rows // 4, 4, features).reshape(group_rows, features)
    )

    def swap(array, axis):
        return lax.all_to_all(array, axis, split_axis=0, concat_axis=0, tiled=True)

    packed, start = lax.optimization_barrier((into_slots(start, residual_rows), start))
    x_slots = swap(packed, "dp")
    context_slots = swap(attend(start, span, query_rows, key_rows, value_rows), "dp")
    moved = swap(place(after, x_slots, context_slots, slabs, slab_rows, features), "mp")
    carried_slab, context_slab = unplace(moved, features, query_rows.shape[1] * HD)

    core = data_group % 2
    partners = [(group, group + 1 - 2 * (group % 2)) for group in range(groups)]

    def gather(weights):
        half = weights.shape[0] // 2
        own = lax.dynamic_slice_in_dim(weights, core * half, half, 0)
        return lax.all_gather(own, "mp", axis=1, tiled=True)

    def both(own):
        return own, lax.ppermute(own, "dp", partners)

    def project(rows, halves_of):
        own, other = halves_of
        half = rows.shape[1] // 2
        low, high = rows[:, :half], rows[:, half:]
        return jnp.dot(
            jnp.where(core == 0, low, high), own, preferred_element_type=jnp.float32
        ) + jnp.dot(jnp.where(core == 0, high, low), other, preferred_element_type=jnp.float32)

    out_halves, glu_halves = both(gather(out_proj)), both(gather(glu_proj))
    down_own = gather(down_proj)
    carried = carried_slab.astype(jnp.float32) + project(context_slab, out_halves)
    average = jnp.mean(carried, axis=1, keepdims=True)
    centred = carried - average
    variance = jnp.mean(centred * centred, axis=1, keepdims=True)
    normed = (centred * lax.rsqrt(variance + EPS) * norm_gain + norm_bias).astype(jnp.bfloat16)
    halves = project(normed, glu_halves)
    feature_count = halves.shape[1] // 2
    gated_rows = (halves[:, :feature_count] * jax.nn.sigmoid(halves[:, feature_count:])).astype(
        jnp.bfloat16
    )
    down_own, gated_rows = lax.optimization_barrier((down_own, gated_rows))
    down_halves = both(down_own)
    swished = convolve(gated_rows, segment, conv_taps, batch_scale, batch_shift)
    lowered = project(swished, down_halves)
    centre_segment = segment[HALO : HALO + slab_rows]
    own_carried = carried[HALO : HALO + slab_rows]
    return jnp.where((centre_segment >= 0)[:, None], own_carried + lowered, 0.0).astype(
        jnp.bfloat16
    )


def solution(mesh):
    in_specs = (
        P("dp", "mp", None),
        P("dp", "mp", None),
        P("dp", "mp", None),
        P("dp", "mp", None),
        P(),
        P(),
        P(None, "mp"),
        P(),
        P(),
        P(None, "mp"),
        P(),
        P(),
        P(),
        P(None, "mp"),
    )
    out_specs = P(("dp", "mp"), None)
    return jax.shard_map(
        on_device, mesh=mesh, in_specs=in_specs, out_specs=out_specs, check_vma=False
    )
```

```python
import functools

import jax
import jax.numpy as jnp
from jax import lax
from jax.experimental import pallas as pl
from jax.experimental.pallas import tpu as pltpu
from jax.sharding import PartitionSpec as P

HD = 64
KERNEL = 31
HALF = 15
MAXLEN = 256
PIECES = 4
LANES = 128
HALO = 16
CONV_ROWS = 64

EPS = 1e-05
MASKED = -1e30
VMEM_LIMIT = 60 * 1024 * 1024


def params():
    return pltpu.CompilerParams(vmem_limit_bytes=VMEM_LIMIT)


def whole_spec():
    return pl.BlockSpec(memory_space=pltpu.VMEM)


def smem_spec():
    return pl.BlockSpec(memory_space=pltpu.SMEM)


def attention_kernel(
    heads, start_ref, span_ref, q_ref, k_ref, v_ref, out_ref, q_rows, k_rows, v_rows
):
    pairs = q_ref.shape[0]
    step = 256
    lane = lax.broadcasted_iota(jnp.int32, (step, LANES), 1)
    low = lane < HD

    def unpack(chunk, carry):
        first = pl.multiple_of(chunk * step, step)
        for packed, rows in ((q_ref, q_rows), (k_ref, k_rows), (v_ref, v_rows)):
            one = packed[pl.ds(first, step), 0:LANES].astype(jnp.float32)
            if heads == 2:
                two = packed[pl.ds(first, step), LANES : 2 * LANES].astype(jnp.float32)
                even = jnp.where(low, one, pltpu.roll(two, HD, 1))
                odd = jnp.where(low, pltpu.roll(one, HD, 1), two)
            else:
                even = one
                odd = pltpu.roll(one, HD, 1)
            rows[pl.ds(2 * first, step, stride=2), :] = even
            rows[pl.ds(2 * first + 1, step, stride=2), :] = odd
        return carry

    lax.fori_loop(0, pairs // step, unpack, 0)
    for rows in (q_rows, k_rows, v_rows):
        rows[pl.ds(2 * pairs, MAXLEN), :] = jnp.zeros((MAXLEN, LANES), jnp.float32)

    column = lax.broadcasted_iota(jnp.int32, (MAXLEN, MAXLEN), 1)
    head_lane = lax.broadcasted_iota(jnp.int32, (MAXLEN, LANES), 1) // HD

    def slot_body(slot, carry):
        start = start_ref[slot]
        allowed = column < span_ref[slot]
        queries = q_rows[pl.ds(start, MAXLEN), :]
        keys = k_rows[pl.ds(start, MAXLEN), :].astype(jnp.bfloat16)
        values = v_rows[pl.ds(start, MAXLEN), :].astype(jnp.bfloat16)
        result = None
        for head in range(heads):
            own = jnp.where(head_lane == head, queries, 0.0).astype(jnp.bfloat16)
            scores = (
                lax.dot_general(
                    own, keys, (((1,), (1,)), ((), ())), preferred_element_type=jnp.float32
                )
                * HD ** (-0.5)
            )
            scores = jnp.where(allowed, scores, MASKED)
            highest = jnp.max(scores, axis=1, keepdims=True)
            exponentials = jnp.exp(scores - highest)
            denominator = jnp.sum(exponentials, axis=1, keepdims=True)
            weights = (exponentials / denominator).astype(jnp.bfloat16)
            blended = jnp.dot(weights, values, preferred_element_type=jnp.float32)
            result = blended if head == 0 else jnp.where(head_lane == head, blended, result)
        out_ref[slot] = result.astype(jnp.bfloat16)
        return carry

    lax.fori_loop(0, start_ref.shape[0], slot_body, 0)


def attend(start, span, query_rows, key_rows, value_rows):
    pairs, heads, _ = query_rows.shape
    slots = start.shape[0]
    flat = [a.reshape(pairs, heads * LANES) for a in (query_rows, key_rows, value_rows)]
    return pl.pallas_call(
        functools.partial(attention_kernel, heads),
        out_shape=jax.ShapeDtypeStruct((slots, MAXLEN, LANES), jnp.bfloat16),
        in_specs=[smem_spec()] * 2 + [whole_spec()] * 3,
        out_specs=whole_spec(),
        scratch_shapes=[pltpu.VMEM((2 * pairs + MAXLEN, LANES), jnp.float32)] * 3,
        compiler_params=params(),
        cost_estimate=pl.CostEstimate(
            flops=slots * heads * MAXLEN * MAXLEN * LANES * 4,
            bytes_accessed=pairs * heads * LANES * 8,
            transcendentals=slots * heads * MAXLEN * MAXLEN,
        ),
    )(start, span, *flat)


def lane_tiles(width):
    return [(first, min(LANES, width - first)) for first in range(0, width, LANES)]


def pairable(width):
    return width == LANES + LANES // 2


def join_pair(one, two):
    half = LANES // 2
    low = lax.broadcasted_iota(jnp.int32, one[0].shape, 1) < half
    turned = pltpu.roll(two[0], half, 1)
    return (
        one[0],
        jnp.where(low, one[1], turned),
        jnp.where(low, turned, pltpu.roll(two[1], half, 1)),
    )


def split_pair(tiles):
    half = LANES // 2
    low = lax.broadcasted_iota(jnp.int32, tiles[0].shape, 1) < half
    middle = pltpu.roll(tiles[1], half, 1)
    last = pltpu.roll(tiles[2], half, 1)
    return (tiles[0], tiles[1]), (jnp.where(low, middle, last), last)


def slots_kernel(start_ref, rows_ref, out_ref, *held):
    count, width = rows_ref.shape
    for (first, size), rows in zip(lane_tiles(width), held):

        def widen(chunk, carry):
            at = pl.multiple_of(chunk * MAXLEN, MAXLEN)
            rows[pl.ds(at, MAXLEN), 0:size] = rows_ref[
                pl.ds(at, MAXLEN), first : first + size
            ].astype(jnp.float32)
            return carry

        lax.fori_loop(0, count // MAXLEN, widen, 0)
        rows[pl.ds(count, MAXLEN), :] = jnp.zeros((MAXLEN, LANES), jnp.float32)

    def slot_body(slot, carry):
        if pairable(width):
            pair = [
                [rows[pl.ds(start_ref[2 * slot + side], MAXLEN), :] for rows in held]
                for side in range(2)
            ]
            tiles = join_pair(*pair)
        else:
            tiles = [rows[pl.ds(start_ref[slot], MAXLEN), :] for rows in held]
        for index, tile in enumerate(tiles):
            out_ref[slot, :, index * LANES : (index + 1) * LANES] = tile.astype(jnp.bfloat16)
        return carry

    lax.fori_loop(0, out_ref.shape[0], slot_body, 0)


def into_slots(start, rows):
    count, width = rows.shape
    slots = start.shape[0]
    tiles = len(lane_tiles(width))
    shape = (slots, MAXLEN, tiles * LANES)
    if pairable(width):
        shape = (slots // 2, MAXLEN, 2 * width)
    return pl.pallas_call(
        slots_kernel,
        out_shape=jax.ShapeDtypeStruct(shape, jnp.bfloat16),
        in_specs=[smem_spec(), whole_spec()],
        out_specs=whole_spec(),
        scratch_shapes=[pltpu.VMEM((count + MAXLEN, LANES), jnp.float32)] * tiles,
        compiler_params=params(),
    )(start, rows)


def place_kernel(paired, after_ref, x_ref, context_ref, out_ref, context_rows, *x_rows):
    slots = context_ref.shape[0]
    slabs = out_ref.shape[0]
    tall = out_ref.shape[1] * (2 if paired else 1)
    slab_rows = tall - 2 * HALO
    total_rows = context_rows.shape[0]
    held = (context_rows,) + x_rows
    zeros = jnp.zeros((MAXLEN, LANES), jnp.float32)
    for rows in held:
        rows[pl.ds(0, HALO), :] = jnp.zeros((HALO, LANES), jnp.float32)

    def load(ref, slot, tile):
        return ref[slot, :, tile * LANES : (tile + 1) * LANES].astype(jnp.float32)

    def put(step, carry):
        if paired:
            sides = split_pair([load(x_ref, step, tile) for tile in range(3)])
            for side in range(2):
                slot = 2 * step + side
                where = pl.ds(HALO + after_ref[slot], MAXLEN)
                for rows, piece in zip(x_rows, sides[side]):
                    rows[where, :] = piece
                context_rows[where, :] = load(context_ref, slot, 0)
        else:
            where = pl.ds(HALO + after_ref[step], MAXLEN)
            for tile, rows in enumerate(x_rows):
                rows[where, :] = load(x_ref, step, tile)
            context_rows[where, :] = load(context_ref, step, 0)
        return carry

    lax.fori_loop(0, x_ref.shape[0], put, 0)
    live = after_ref[slots]

    def clear(step, carry):
        at = jnp.minimum(HALO + live + step * MAXLEN, total_rows - MAXLEN)
        for rows in held:
            rows[pl.ds(at, MAXLEN), :] = zeros
        return carry

    lax.fori_loop(0, (total_rows - HALO - live + MAXLEN - 1) // MAXLEN, clear, 0)

    def emit(slab, carry):
        at = pl.multiple_of(slab * slab_rows, slab_rows)
        if paired:
            half = tall // 2
            one = pl.ds(at, half)
            two = pl.ds(pl.multiple_of(at + half, 8), half)
            tiles = join_pair([rows[one, :] for rows in x_rows], [rows[two, :] for rows in x_rows])
            tiles = tiles + (context_rows[one, :], context_rows[two, :])
        else:
            tiles = [rows[pl.ds(at, tall), :] for rows in x_rows + (context_rows,)]
        for index, tile in enumerate(tiles):
            out_ref[slab, :, index * LANES : (index + 1) * LANES] = tile.astype(jnp.bfloat16)
        return carry

    lax.fori_loop(0, slabs, emit, 0)


def place(after, x_slots, context_slots, slabs, slab_rows, features):
    count = context_slots.shape[0]
    paired = pairable(features)
    tiles = len(lane_tiles(features))
    tall = slab_rows + 2 * HALO
    shape = (slabs, tall, (tiles + 1) * LANES)
    if paired:
        shape = (slabs, tall // 2, 2 * features + 2 * LANES)
    return pl.pallas_call(
        functools.partial(place_kernel, paired),
        out_shape=jax.ShapeDtypeStruct(shape, jnp.bfloat16),
        in_specs=[smem_spec(), whole_spec(), whole_spec()],
        out_specs=whole_spec(),
        scratch_shapes=[pltpu.VMEM((count * MAXLEN + HALO + MAXLEN, LANES), jnp.float32)]
        * (tiles + 1),
        compiler_params=params(),
    )(after, x_slots, context_slots)


def unplace_kernel(moved_ref, x_ref, context_ref):
    slabs, rows, _ = moved_ref.shape
    step = 16
    span = 3 * LANES

    def chunk(index, carry):
        at = pl.multiple_of(index * step, step)

        def load(slab, tile):
            cells = moved_ref[slab, pl.ds(at, step), tile * LANES : (tile + 1) * LANES]
            return cells.astype(jnp.float32)

        for pair in range(slabs // 2):
            split = [
                split_pair([load(2 * pair + member, tile) for tile in range(3)])
                for member in range(2)
            ]
            for side in range(2):
                to = pl.ds(pl.multiple_of(at + side * rows, step), step)
                for tile, cells in enumerate(join_pair(split[0][side], split[1][side])):
                    first = pair * span + tile * LANES
                    x_ref[to, first : first + LANES] = cells.astype(jnp.bfloat16)
        for slab in range(slabs):
            for side in range(2):
                to = pl.ds(pl.multiple_of(at + side * rows, step), step)
                first = span + side * LANES
                context_ref[to, slab * LANES : (slab + 1) * LANES] = moved_ref[
                    slab, pl.ds(at, step), first : first + LANES
                ]
        return carry

    lax.fori_loop(0, rows // step, chunk, 0)


def unplace(moved, features, context_width):
    slabs, rows, _ = moved.shape
    if not (pairable(features) and context_width == LANES):
        first = len(lane_tiles(features)) * LANES
        x = moved[:, :, :features].transpose(1, 0, 2).reshape(rows, -1)
        context = moved[:, :, first : first + context_width]
        return x, context.transpose(1, 0, 2).reshape(rows, -1)
    return pl.pallas_call(
        unplace_kernel,
        out_shape=(
            jax.ShapeDtypeStruct((2 * rows, slabs * features), jnp.bfloat16),
            jax.ShapeDtypeStruct((2 * rows, slabs * context_width), jnp.bfloat16),
        ),
        in_specs=[whole_spec()],
        out_specs=(whole_spec(), whole_spec()),
        compiler_params=params(),
    )(moved)


def conv_kernel(
    uniform_ref, gated_ref, segment_ref, taps_ref, scale_ref, shift_ref, out_ref, wide
):
    wide[...] = gated_ref[...].astype(jnp.float32)
    edge = HALO - HALF
    scale = scale_ref[...]
    shift = shift_ref[...]
    for chunk in range(out_ref.shape[0] // CONV_ROWS):
        base = chunk * CONV_ROWS

        def finish(total):
            affine = total * scale + shift
            out_ref[base : base + CONV_ROWS, :] = (affine * jax.nn.sigmoid(affine)).astype(
                jnp.bfloat16
            )

        @pl.when(uniform_ref[chunk] == 1)
        def _():
            total = jnp.zeros((CONV_ROWS, LANES), jnp.float32)
            for tap in range(KERNEL):
                total = total + wide[pl.ds(base + edge + tap, CONV_ROWS), :] * taps_ref[
                    tap : tap + 1, :
                ]
            finish(total)

        @pl.when(uniform_ref[chunk] == 0)
        def _():
            centre = segment_ref[pl.ds(base + HALO, CONV_ROWS), :]
            total = jnp.zeros((CONV_ROWS, LANES), jnp.float32)
            for tap in range(KERNEL):
                same = segment_ref[pl.ds(base + edge + tap, CONV_ROWS), :] == centre
                term = jnp.where(same, wide[pl.ds(base + edge + tap, CONV_ROWS), :], 0.0)
                total = total + term * taps_ref[tap : tap + 1, :]
            finish(total)


def convolve(gated_rows, segment, conv_taps, batch_scale, batch_shift):
    tall, width = gated_rows.shape
    rows = tall - 2 * HALO
    chunks = rows // CONV_ROWS
    windows = [segment[c * CONV_ROWS : c * CONV_ROWS + CONV_ROWS + 2 * HALO] for c in range(chunks)]
    windows = jnp.stack(windows)
    uniform = jnp.all(windows == windows[:, :1], axis=1).astype(jnp.int32)
    wide_segment = jnp.broadcast_to(segment[:, None], (tall, LANES))
    return pl.pallas_call(
        conv_kernel,
        grid=(width // LANES,),
        out_shape=jax.ShapeDtypeStruct((rows, width), jnp.bfloat16),
        in_specs=[
            smem_spec(),
            pl.BlockSpec((tall, LANES), lambda i: (0, i)),
            pl.BlockSpec((tall, LANES), lambda i: (0, 0)),
            pl.BlockSpec((KERNEL, LANES), lambda i: (0, i)),
            pl.BlockSpec((1, LANES), lambda i: (0, i)),
            pl.BlockSpec((1, LANES), lambda i: (0, i)),
        ],
        out_specs=pl.BlockSpec((rows, LANES), lambda i: (0, i)),
        scratch_shapes=[pltpu.VMEM((tall, LANES), jnp.float32)],
        compiler_params=params(),
        cost_estimate=pl.CostEstimate(
            flops=2 * rows * width * KERNEL, bytes_accessed=4 * rows * width, transcendentals=0
        ),
    )(
        uniform,
        gated_rows,
        wide_segment,
        conv_taps,
        batch_scale[None, :],
        batch_shift[None, :],
    )


MESH = pl.DeviceIdType.MESH
OUT, GLU_ONE, GLU_TWO, DOWN = range(4)


def any_spec():
    return pl.BlockSpec(memory_space=pl.ANY)


class Place:
    def __init__(self):
        self.dp = lax.axis_index("dp")
        self.mp = lax.axis_index("mp")
        self.y, self.c = self.dp // 2, self.dp % 2
        self.z, self.x = self.mp // 2, self.mp % 2
        self.across = 1 - self.x
        self.near = self.z + 1 - 2 * (self.z % 2)
        self.far_one = 2 - self.z // 2
        self.far_two = 3 - 3 * (self.z // 2)

    def x_side(self):
        return (self.dp, 2 * self.z + self.across)

    def y_side(self):
        return (2 * (1 - self.y) + self.c, self.mp)

    def core_side(self):
        return (2 * self.y + 1 - self.c, self.mp)

    def corner(self):
        return (2 * (1 - self.y) + 1 - self.c, self.mp)

    def above(self):
        return (self.dp, self.mp + 2)

    def below(self):
        return (self.dp, self.mp - 2)


def aligned(index, step):
    return pl.multiple_of(index * step, step)


def piece(weights, kind, z, x, y, c, both_y=False):
    shard = 2 * z + x
    if kind == OUT:
        return weights[0].at[pl.ds(aligned(shard, 192), 192), pl.ds(aligned(c, 512), 512)]
    if kind == GLU_ONE:
        return weights[1].at[pl.ds(aligned(c, 256), 256), pl.ds(aligned(shard, 384), 384)]
    if kind == GLU_TWO:
        if both_y:
            rows = pl.ds(pl.multiple_of(512 + c * 512, 256), 512)
        else:
            rows = pl.ds(pl.multiple_of(512 + (c * 2 + y) * 256, 256), 256)
        return weights[1].at[rows, pl.ds(aligned(shard, 384), 384)]
    if both_y:
        columns = pl.ds(aligned(c, 768), 768)
    else:
        columns = pl.ds(aligned(c * 2 + y, 384), 384)
    return weights[2].at[pl.ds(aligned(shard, 192), 192), columns]


def own_piece(shards, kind, y, c):
    if kind == OUT:
        return shards[0].at[:, pl.ds(aligned(c, 512), 512)]
    if kind == GLU_ONE:
        return shards[1].at[pl.ds(aligned(c, 256), 256), :]
    if kind == GLU_TWO:
        return shards[1].at[pl.ds(pl.multiple_of(512 + (c * 2 + y) * 256, 256), 256), :]
    return shards[2].at[:, pl.ds(aligned(c * 2 + y, 384), 384)]


class Mail:
    def __init__(self, send_sems, recv_sems):
        self.send_sems, self.recv_sems = send_sems, recv_sems
        self.used = 0
        self.sent = []

    def slot(self):
        self.used += 1
        return self.used - 1

    def copy(self, slot, source, target, device):
        return pltpu.make_async_remote_copy(
            src_ref=source,
            dst_ref=target,
            send_sem=self.send_sems.at[slot],
            recv_sem=self.recv_sems.at[slot],
            device_id=device,
            device_id_type=MESH,
        )

    def send(self, slot, source, target, device, when=None):
        copy = self.copy(slot, source, target, device)
        run_if(when, copy.start)
        self.sent.append((copy, when))

    def receive(self, slot, target, device, when=None):
        run_if(when, self.copy(slot, target, target, device).wait_recv)

    def finish(self):
        for copy, when in self.sent:
            run_if(when, copy.wait_send)


def run_if(when, action):
    if when is None:
        action()
    else:
        pl.when(when)(action)


def greet(devices):
    barrier = pltpu.get_barrier_semaphore()

    def hello(device):
        pl.semaphore_signal(barrier, inc=1, device_id=device, device_id_type=MESH)

    count = 0
    for device, when in devices:
        if when is None:
            hello(device)
            count = count + 1
        else:
            pl.when(when)(functools.partial(hello, device))
            count = count + when.astype(jnp.int32)
    pl.semaphore_wait(barrier, count)


KINDS = (GLU_ONE, OUT, GLU_TWO, DOWN)
FIRST = (GLU_TWO, OUT, GLU_ONE)


def find_slots(dp, lengths_ref, assignment_ref, start_ref, span_ref):
    groups = start_ref.shape[0] // PIECES
    per_group = lengths_ref.shape[0] // groups
    zero = jnp.int32(0)
    counts = [zero] * groups
    starts = [zero] * (groups * PIECES)
    spans = [zero] * (groups * PIECES)
    before = zero
    for i in range(per_group):
        target = assignment_ref[dp * per_group + i]
        length = lengths_ref[dp * per_group + i]
        for group in range(groups):
            hit = target == group
            for rank in range(PIECES):
                slot = group * PIECES + rank
                found = hit & (counts[group] == rank)
                starts[slot] = jnp.where(found, before, starts[slot])
                spans[slot] = jnp.where(found, length, spans[slot])
            counts[group] = counts[group] + hit.astype(jnp.int32)
        before = before + length
    for slot in range(groups * PIECES):
        start_ref[slot] = starts[slot]
        span_ref[slot] = spans[slot]


def move_kernel(
    lengths_ref,
    assignment_ref,
    q_ref,
    k_ref,
    v_ref,
    residual_ref,
    out_shard,
    glu_shard,
    down_shard,
    x_got,
    context_got,
    out_all,
    glu_all,
    down_all,
    q_rows,
    k_rows,
    v_rows,
    x_low,
    x_high,
    x_send,
    context_send,
    out_held,
    glu_held,
    down_held,
    mixed,
    start_ref,
    span_ref,
    send_sems,
    recv_sems,
    local_sems,
):
    here = Place()
    z, x, y, c = here.z, here.x, here.y, here.c
    weights = (out_all, glu_all, down_all)
    shards = (out_shard, glu_shard, down_shard)
    held = (out_held, glu_held, down_held)
    mail = Mail(send_sems, recv_sems)
    up, down = z < 3, z > 0
    partners = (here.y_side(), here.corner(), here.core_side())
    greet(
        [(device, None) for device in partners + (here.x_side(),)]
        + [(here.above(), up), (here.below(), down)]
    )

    def spot(kind, zz, xx):
        return piece(weights, kind, zz, xx, y, c)

    own = (
        out_all.at[pl.ds(aligned(here.mp, 192), 192), :],
        glu_all.at[:, pl.ds(aligned(here.mp, 384), 384)],
        down_all.at[pl.ds(aligned(here.mp, 192), 192), :],
    )
    into = [
        pltpu.make_async_copy(shards[i], held[i], local_sems.at[i]) for i in range(3)
    ]
    locals_ = [pltpu.make_async_copy(held[i], own[i], local_sems.at[5 + i]) for i in range(3)]
    slots_up, slots_down, slots_x, slots_near = [
        {kind: mail.slot() for kind in KINDS} for _ in range(4)
    ]
    slots_up_two, slots_down_two = [{kind: mail.slot() for kind in KINDS} for _ in range(2)]
    for kind in KINDS:
        mine = own_piece(shards, kind, y, c)
        mail.send(slots_up[kind], mine, spot(kind, z, x), here.above(), up)
        mail.send(slots_down[kind], mine, spot(kind, z, x), here.below(), down)
        mail.send(slots_x[kind], mine, spot(kind, z, x), here.x_side())
    for copy in into:
        copy.start()
    find_slots(here.dp, lengths_ref, assignment_ref, start_ref, span_ref)

    count = 4 * residual_ref.shape[0]
    step = 128
    low = lax.broadcasted_iota(jnp.int32, (step, LANES), 1) < HD

    def open_rows(chunk, carry):
        first = pl.multiple_of(chunk * step, step)
        cells = [
            residual_ref[pl.ds(first, step), i * LANES : (i + 1) * LANES].astype(jnp.float32)
            for i in range(6)
        ]
        turned = [pltpu.roll(cells[i], HD, 1) for i in (1, 2, 4, 5)]
        frames = (
            (cells[0], cells[1]),
            (jnp.where(low, turned[0], turned[1]), turned[1]),
            (cells[3], cells[4]),
            (jnp.where(low, turned[2], turned[3]), turned[3]),
        )
        for j, (one, two) in enumerate(frames):
            at = pl.ds(4 * first + j, step, stride=4)
            x_low[at, :] = one
            x_high[at, :] = two
        return carry

    lax.fori_loop(0, residual_ref.shape[0] // step, open_rows, 0)
    for rows in (x_low, x_high):
        rows[pl.ds(count, MAXLEN), :] = jnp.zeros((MAXLEN, LANES), jnp.float32)

    def relay(kind):
        mail.receive(slots_up[kind], spot(kind, z - 1, x), here.above(), down)
        mail.send(
            slots_up_two[kind],
            spot(kind, z - 1, x),
            spot(kind, z - 1, x),
            here.above(),
            up & down,
        )
        mail.receive(slots_down[kind], spot(kind, z + 1, x), here.below(), up)
        mail.send(
            slots_down_two[kind],
            spot(kind, z + 1, x),
            spot(kind, z + 1, x),
            here.below(),
            up & down,
        )
        mail.send(
            slots_near[kind],
            spot(kind, here.near, x),
            spot(kind, here.near, x),
            here.x_side(),
        )

    targets = partners + ((here.dp, here.mp),)
    half = PIECES // 2
    x_slots = [mail.slot() for _ in partners]
    context_slots = [mail.slot() for _ in partners]
    for index, target in enumerate(targets):
        group = target[0]

        def fill(pair, carry):
            at = group * half + pair
            both = [
                [
                    rows[pl.ds(start_ref[2 * at + side], MAXLEN), :]
                    for rows in (x_low, x_high)
                ]
                for side in range(2)
            ]
            for tile, cells in enumerate(join_pair(*both)):
                x_send[at, :, tile * LANES : (tile + 1) * LANES] = cells.astype(jnp.bfloat16)
            return carry

        lax.fori_loop(0, half, fill, 0)
        source = x_send.at[pl.ds(group * half, half)]
        landing = x_got.at[pl.ds(here.dp * half, half)]
        if index < 3:
            mail.send(x_slots[index], source, landing, target)
        else:
            copy = pltpu.make_async_copy(source, landing, local_sems.at[3])
            copy.start()
            locals_.append(copy)

    relay(KINDS[0])
    for copy_in, copy_out in zip(into, locals_):
        copy_in.wait()
        copy_out.start()

    pairs = q_ref.shape[0] // 2
    wide_low = lax.broadcasted_iota(jnp.int32, (256, LANES), 1) < HD

    def unpack(chunk, carry):
        first = pl.multiple_of(chunk * 256, 256)
        for i, (packed, rows) in enumerate(((q_ref, q_rows), (k_ref, k_rows), (v_ref, v_rows))):
            mixed[i] = packed[pl.ds(2 * first, 512), :].astype(jnp.float32)
            one = mixed[i, pl.ds(0, 256, stride=2), :]
            two = mixed[i, pl.ds(1, 256, stride=2), :]
            rows[pl.ds(2 * first, 256, stride=2), :] = jnp.where(
                wide_low, one, pltpu.roll(two, HD, 1)
            )
            rows[pl.ds(2 * first + 1, 256, stride=2), :] = jnp.where(
                wide_low, pltpu.roll(one, HD, 1), two
            )
        return carry

    lax.fori_loop(0, pairs // 256, unpack, 0)
    for rows in (q_rows, k_rows, v_rows):
        rows[pl.ds(2 * pairs, MAXLEN), :] = jnp.zeros((MAXLEN, LANES), jnp.float32)

    relay(KINDS[1])
    column = lax.broadcasted_iota(jnp.int32, (MAXLEN, MAXLEN), 1)
    head_lane = lax.broadcasted_iota(jnp.int32, (MAXLEN, LANES), 1) // HD

    def attend_slot(slot):
        start = start_ref[slot]
        allowed = column < span_ref[slot]
        queries = q_rows[pl.ds(start, MAXLEN), :]
        keys = k_rows[pl.ds(start, MAXLEN), :].astype(jnp.bfloat16)
        values = v_rows[pl.ds(start, MAXLEN), :].astype(jnp.bfloat16)
        result = None
        for head in range(2):
            own = jnp.where(head_lane == head, queries, 0.0).astype(jnp.bfloat16)
            scores = (
                lax.dot_general(
                    own, keys, (((1,), (1,)), ((), ())), preferred_element_type=jnp.float32
                )
                * HD ** (-0.5)
            )
            scores = jnp.where(allowed, scores, MASKED)
            highest = jnp.max(scores, axis=1, keepdims=True)
            exponentials = jnp.exp(scores - highest)
            denominator = jnp.sum(exponentials, axis=1, keepdims=True)
            weighing = (exponentials / denominator).astype(jnp.bfloat16)
            blended = jnp.dot(weighing, values, preferred_element_type=jnp.float32)
            result = blended if head == 0 else jnp.where(head_lane == head, blended, result)
        context_send[slot] = result.astype(jnp.bfloat16)

    for index, target in enumerate(targets):
        group = target[0]

        def attend_one(rank, carry):
            attend_slot(group * PIECES + rank)
            return carry

        lax.fori_loop(0, PIECES, attend_one, 0)
        source = context_send.at[pl.ds(group * PIECES, PIECES)]
        landing = context_got.at[pl.ds(here.dp * PIECES, PIECES)]
        if index < 3:
            mail.send(context_slots[index], source, landing, target)
        else:
            copy = pltpu.make_async_copy(source, landing, local_sems.at[4])
            copy.start()
            locals_.append(copy)
        if index < 2:
            relay(KINDS[2 + index])

    for index, source in enumerate(partners):
        mail.receive(x_slots[index], x_got.at[pl.ds(source[0] * half, half)], source)
        mail.receive(
            context_slots[index], context_got.at[pl.ds(source[0] * PIECES, PIECES)], source
        )
    for kind in KINDS:
        mail.receive(slots_x[kind], spot(kind, z, here.across), here.x_side())
        mail.receive(slots_near[kind], spot(kind, here.near, here.across), here.x_side())
        mail.receive(slots_up_two[kind], spot(kind, z - 2, x), here.above(), z > 1)
        mail.receive(slots_down_two[kind], spot(kind, z + 2, x), here.below(), z < 2)
    mail.finish()
    for copy in locals_:
        copy.wait()


def move(lengths, assignment, queries, keys, values, residual, out_shard, glu_shard, down_shard):
    slots = 4 * PIECES
    pairs = queries.shape[0] // 2
    count = 4 * residual.shape[0]
    bf16 = jnp.bfloat16
    return pl.pallas_call(
        move_kernel,
        out_shape=(
            jax.ShapeDtypeStruct((slots // 2, MAXLEN, 3 * LANES), bf16),
            jax.ShapeDtypeStruct((slots, MAXLEN, LANES), bf16),
            jax.ShapeDtypeStruct((1536, 1024), bf16),
            jax.ShapeDtypeStruct((1536, 3072), bf16),
            jax.ShapeDtypeStruct((1536, 1536), bf16),
        ),
        in_specs=[smem_spec()] * 2 + [whole_spec()] * 4 + [any_spec()] * 3,
        out_specs=(any_spec(),) * 5,
        scratch_shapes=[pltpu.VMEM((2 * pairs + MAXLEN, LANES), jnp.float32)] * 3
        + [pltpu.VMEM((count + MAXLEN, LANES), jnp.float32)] * 2
        + [
            pltpu.VMEM((slots // 2, MAXLEN, 3 * LANES), bf16),
            pltpu.VMEM((slots, MAXLEN, LANES), bf16),
            pltpu.VMEM(out_shard.shape, bf16),
            pltpu.VMEM(glu_shard.shape, bf16),
            pltpu.VMEM(down_shard.shape, bf16),
            pltpu.VMEM((3, 512, LANES), jnp.float32),
            pltpu.SMEM((slots,), jnp.int32),
            pltpu.SMEM((slots,), jnp.int32),
            pltpu.SemaphoreType.DMA((30,)),
            pltpu.SemaphoreType.DMA((30,)),
            pltpu.SemaphoreType.DMA((8,)),
        ],
        compiler_params=pltpu.CompilerParams(
            vmem_limit_bytes=VMEM_LIMIT, collective_id=1, has_side_effects=True
        ),
        cost_estimate=pl.CostEstimate(
            flops=slots * 2 * MAXLEN * MAXLEN * LANES * 4,
            bytes_accessed=50 * 1024 * 1024,
            transcendentals=slots * 2 * MAXLEN * MAXLEN,
        ),
    )(lengths, assignment, queries, keys, values, residual, out_shard, glu_shard, down_shard)


SPLIT = 288
PARTS = ((0, SPLIT // 2, 0, SPLIT - 2 * HALO), (SPLIT, 272 - SPLIT // 2, SPLIT - 2 * HALO, 544 - SPLIT))
ROW_STEP = 16
EXCHANGE_ORDER = ((3, 1), (3, 0), (2, 0), (2, 1), (1, 0), (1, 1), (0, 1))


def place_parts_kernel(
    lengths_ref, assignment_ref, x_ref, context_ref, out_ref, after_ref, context_rows, *x_rows
):
    dp = lax.axis_index("dp")
    after_ref[0] = 0

    def seek(u, carry):
        count, total = carry
        hit = assignment_ref[u] == dp
        total = total + jnp.where(hit, lengths_ref[u], 0)
        count = count + hit.astype(jnp.int32)
        after_ref[count] = total
        return count, total

    lax.fori_loop(0, lengths_ref.shape[0], seek, (jnp.int32(0), jnp.int32(0)))
    slots = context_ref.shape[0]
    slabs = out_ref.shape[0]
    tall = out_ref.shape[1] * 2
    slab_rows = tall - 2 * HALO
    total_rows = context_rows.shape[0]
    held = (context_rows,) + x_rows
    zeros = jnp.zeros((MAXLEN, LANES), jnp.float32)
    for rows in held:
        rows[pl.ds(0, HALO), :] = jnp.zeros((HALO, LANES), jnp.float32)

    def load(ref, slot, tile):
        return ref[slot, :, tile * LANES : (tile + 1) * LANES].astype(jnp.float32)

    def put(step, carry):
        sides = split_pair([load(x_ref, step, tile) for tile in range(3)])
        for side in range(2):
            slot = 2 * step + side
            where = pl.ds(HALO + after_ref[slot], MAXLEN)
            for rows, piece in zip(x_rows, sides[side]):
                rows[where, :] = piece
            context_rows[where, :] = load(context_ref, slot, 0)
        return carry

    lax.fori_loop(0, x_ref.shape[0], put, 0)
    live = after_ref[slots]

    def clear(step, carry):
        at = jnp.minimum(HALO + live + step * MAXLEN, total_rows - MAXLEN)
        for rows in held:
            rows[pl.ds(at, MAXLEN), :] = zeros
        return carry

    lax.fori_loop(0, (total_rows - HALO - live + MAXLEN - 1) // MAXLEN, clear, 0)

    def emit(slab, carry):
        at = pl.multiple_of(slab * slab_rows, slab_rows)
        for first, half, *_ in PARTS:
            one = pl.ds(pl.multiple_of(at + first, 16), half)
            two = pl.ds(pl.multiple_of(at + first + half, 16), half)
            tiles = join_pair(
                [rows[one, :] for rows in x_rows], [rows[two, :] for rows in x_rows]
            )
            tiles = tiles + (context_rows[one, :], context_rows[two, :])
            for index, tile in enumerate(tiles):
                lanes = slice(index * LANES, (index + 1) * LANES)
                out_ref[slab, first // 2 : first // 2 + half, lanes] = tile.astype(
                    jnp.bfloat16
                )
        return carry

    lax.fori_loop(0, slabs, emit, 0)


def place_parts(lengths, assignment, x_slots, context_slots, slabs):
    count = context_slots.shape[0]
    return pl.pallas_call(
        place_parts_kernel,
        out_shape=(
            jax.ShapeDtypeStruct((slabs, 272, 5 * LANES), jnp.bfloat16),
            jax.ShapeDtypeStruct((count + 1,), jnp.int32),
        ),
        in_specs=[smem_spec()] * 2 + [whole_spec()] * 2,
        out_specs=(whole_spec(), smem_spec()),
        scratch_shapes=[pltpu.VMEM((count * MAXLEN + HALO + MAXLEN, LANES), jnp.float32)] * 3,
        compiler_params=params(),
    )(lengths, assignment, x_slots, context_slots)


def finish_kernel(
    after_ref,
    slabs_ref,
    gain_ref,
    bias_ref,
    scale_ref,
    shift_ref,
    taps_ref,
    out_in,
    glu_in,
    down_in,
    encoded_ref,
    out_all,
    glu_all,
    down_all,
    moved,
    carried,
    context,
    normed,
    wide,
    swished,
    first_tap,
    last_tap,
    out_held,
    glu_held,
    down_held,
    send_sems,
    recv_sems,
    local_sems,
):
    here = Place()
    z, x, y, c = here.z, here.x, here.y, here.c
    weights = (out_all, glu_all, down_all)
    mail = Mail(send_sems, recv_sems)
    slabs = slabs_ref.shape[0]
    mirrors = (z, here.near, z + 2 - 4 * (z // 2), 3 - z)
    sides = (x, here.across)
    others = [(here.dp, 2 * mirrors[dz] + sides[dx]) for dz, dx in EXCHANGE_ORDER]
    greet([(device, None) for device in others + [here.y_side(), here.core_side()]])

    slab_slots = [[mail.slot() for _ in others] for _ in PARTS]

    def part_rows(part):
        first, half, *_ = PARTS[part]
        return pl.ds(first // 2, half)

    def exchange(part, crossing):
        for index, device in enumerate(others):
            if EXCHANGE_ORDER[index][1] != crossing:
                continue
            mail.send(
                slab_slots[part][index],
                slabs_ref.at[device[1], part_rows(part)],
                moved.at[here.mp, part_rows(part)],
                device,
            )

    def exchanged(part):
        for index in range(len(others)):
            mail.receive(
                slab_slots[part][index],
                moved.at[others[index][1], part_rows(part)],
                others[index],
            )

    tile_width = 768
    tiles = carried.shape[1] // tile_width
    keep = pltpu.make_async_copy(slabs_ref.at[here.mp], moved.at[here.mp], local_sems.at[0])
    keep.start()

    def spot(kind, zz, xx):
        return piece(weights, kind, zz, xx, y, c)

    table = {}

    def slot(*key):
        if key not in table:
            table[key] = mail.slot()
        return table[key]

    def pass_on(name, kind, zz, xx, device, when=None):
        where = spot(kind, zz, xx)
        mail.send(slot(name, kind), where, where, device, when)

    cells = {
        "own near": (here.near, x),
        "own one": (here.far_one, x),
        "own two": (here.far_two, x),
        "other own": (z, here.across),
        "other near": (here.near, here.across),
        "other one": (here.far_one, here.across),
        "other two": (here.far_two, here.across),
    }
    early = ("own near", "own one", "other own", "other near")
    order = early + ("other one", "own two", "other two")

    def after(kind, cell):
        if kind in (OUT, GLU_ONE):
            pass_on("core " + cell, kind, *cells[cell], here.core_side())
        else:
            pass_on("y " + cell, kind, *cells[cell], here.y_side())

    def from_y(kind):
        for cell in order:
            mail.receive(
                slot("y " + cell, kind),
                piece(weights, kind, *cells[cell], 1 - y, c),
                here.y_side(),
            )
            where = piece(weights, kind, *cells[cell], y, c, both_y=True)
            mail.send(slot("core " + cell, kind), where, where, here.core_side())

    def from_core(kind):
        for cell in order:
            where = piece(weights, kind, *cells[cell], y, 1 - c, both_y=kind in (GLU_TWO, DOWN))
            mail.receive(slot("core " + cell, kind), where, here.core_side())

    def start_across(kinds):
        for kind in kinds:
            pass_on("third up", kind, 0, x, here.above(), z == 2)
            pass_on("third down", kind, 3, x, here.below(), z == 1)
            pass_on("x one", kind, here.far_one, x, here.x_side())
        for kind in kinds:
            for cell in early:
                after(kind, cell)

    def across_one(kinds):
        for kind in kinds:
            mail.receive(slot("x one", kind), spot(kind, *cells["other one"]), here.x_side())
            after(kind, "other one")
        for kind in kinds:
            mail.receive(slot("third up", kind), spot(kind, 0, x), here.above(), z == 3)
            mail.receive(slot("third down", kind), spot(kind, 3, x), here.below(), z == 0)
            pass_on("x two", kind, here.far_two, x, here.x_side())
            after(kind, "own two")

    def across_two(kinds):
        for kind in kinds:
            mail.receive(slot("x two", kind), spot(kind, *cells["other two"]), here.x_side())
            after(kind, "other two")

    start_across(FIRST)
    exchange(0, 0)
    live = after_ref[4 * PIECES]

    def bounds(step, carry):
        rows = pl.ds(pl.multiple_of(step * 64, 64), 64)
        position = (
            lax.broadcasted_iota(jnp.int32, (64, LANES), 0)
            + step * 64
            + here.mp * encoded_ref.shape[0]
        )
        begin = jnp.zeros((64, LANES), jnp.int32)
        end = jnp.full((64, LANES), live, jnp.int32)
        for k in range(1, 4 * PIECES):
            begin = jnp.where(position >= after_ref[k], after_ref[k], begin)
        for k in range(4 * PIECES - 1, 0, -1):
            end = jnp.where(position < after_ref[k], after_ref[k], end)
        first_tap[rows, :] = HALF + begin - position
        last_tap[rows, :] = HALF - 1 + end - position
        return carry

    lax.fori_loop(0, encoded_ref.shape[0] // 64, bounds, 0)

    across_one(FIRST)
    exchange(0, 1)
    start_across((DOWN,))
    exchange(1, 0)
    exchange(1, 1)
    across_two(FIRST)
    from_y(GLU_TWO)
    loads = [
        pltpu.make_async_copy(weights[i], (out_held, glu_held, down_held)[i], local_sems.at[1 + i])
        for i in range(3)
    ]

    def glu_load(n, side):
        columns = pl.ds(aligned(n + side * tiles, tile_width), tile_width)
        return pltpu.make_async_copy(
            weights[1].at[:, columns],
            glu_held.at[:, columns],
            local_sems.at[4 + 2 * n + side],
        )

    from_core(OUT)
    loads[0].start()

    def open_part(part):
        first, half, *_ = PARTS[part]

        def chunk(index, carry):
            at = pl.ds(pl.multiple_of(first // 2 + index * 16, 16), 16)

            def load(slab, tile):
                cells_ = moved[slab, at, tile * LANES : (tile + 1) * LANES]
                return cells_.astype(jnp.float32)

            to = [pl.ds(pl.multiple_of(first + s * half + index * 16, 16), 16) for s in range(2)]
            near = [pl.ds(pl.multiple_of(s * half + index * 16, 16), 16) for s in range(2)]
            for pair in range(slabs // 2):
                split = [
                    split_pair([load(2 * pair + member, tile) for tile in range(3)])
                    for member in range(2)
                ]
                for side in range(2):
                    for tile, cells_ in enumerate(join_pair(split[0][side], split[1][side])):
                        begin = (3 * pair + tile) * LANES
                        carried[to[side], begin : begin + LANES] = cells_
            for slab in range(slabs):
                for side in range(2):
                    begin = (3 + side) * LANES
                    context[near[side], slab * LANES : (slab + 1) * LANES] = moved[
                        slab, at, begin : begin + LANES
                    ]
            return carry

        lax.fori_loop(0, half // 16, chunk, 0)

    def attach(part):
        first, half, *_ = PARTS[part]

        def tile(n, carry):
            columns = pl.ds(aligned(n, tile_width), tile_width)
            carried[first : first + 2 * half, columns] += lax.dot_general(
                context[0 : 2 * half, :],
                out_held[columns, :],
                (((1,), (1,)), ((), ())),
                preferred_element_type=jnp.float32,
            )
            return carry

        lax.fori_loop(0, tiles, tile, 0)

        def normalise(index, carry):
            at = pl.ds(pl.multiple_of(first + index * 32, 32), 32)
            to = pl.ds(pl.multiple_of(index * 32, 32), 32)
            cells_ = carried[at, :]
            centred = cells_ - jnp.mean(cells_, axis=1, keepdims=True)
            variance = jnp.mean(centred * centred, axis=1, keepdims=True)
            inverse = lax.rsqrt(variance + EPS)
            for i in range(carried.shape[1] // LANES):
                lanes = slice(i * LANES, (i + 1) * LANES)
                scaled = centred[:, lanes] * inverse * gain_ref[i : i + 1, :] + bias_ref[i : i + 1, :]
                normed[to, lanes] = scaled.astype(jnp.bfloat16)
            return carry

        lax.fori_loop(0, 2 * half // 32, normalise, 0)

    def gate(part):
        first, half, *_ = PARTS[part]

        def tile(n, carry):
            columns = pl.ds(aligned(n, tile_width), tile_width)
            if part == 0:
                for side in range(2):
                    glu_load(n, side).wait()
            rows = normed[0 : 2 * half, :]
            value = jnp.dot(rows, glu_held[:, columns], preferred_element_type=jnp.float32)
            gates = jnp.dot(
                rows,
                glu_held[:, pl.ds(aligned(n + tiles, tile_width), tile_width)],
                preferred_element_type=jnp.float32,
            )
            gated = (value * jax.nn.sigmoid(gates)).astype(jnp.bfloat16)
            for side in range(tile_width // LANES):
                wide[tile_width // LANES * n + side, first : first + 2 * half, :] = gated[
                    :, side * LANES : (side + 1) * LANES
                ].astype(jnp.float32)
            return carry

        lax.fori_loop(0, tiles, tile, 0)

    def convolve_part(part):
        start, count_rows = PARTS[part][2:]
        steps = count_rows // ROW_STEP
        group = 6
        groups = carried.shape[1] // (group * LANES)

        def body(index, carry):
            row = start + lax.rem(index, steps) * ROW_STEP
            column = index // steps * (group * LANES)
            rows = pl.ds(pl.multiple_of(row, ROW_STEP), ROW_STEP)
            low, high = first_tap[rows, :], last_tap[rows, :]
            lanes = [pl.ds(pl.multiple_of(column + i * LANES, LANES), LANES) for i in range(group)]
            totals = [jnp.zeros((ROW_STEP, LANES), jnp.float32) for _ in range(group)]
            for shift in range(8):
                count = ROW_STEP + (24 if shift < 7 else 16)
                at = pl.ds(row + HALO - HALF + shift, count)
                seen = [wide[column // LANES + i, at, :] for i in range(group)]
                for k in range(4 if shift < 7 else 3):
                    tap = shift + 8 * k
                    if tap < HALF:
                        mask = low <= tap
                    else:
                        mask = high >= tap
                    for i in range(group):
                        term = seen[i][8 * k : 8 * k + ROW_STEP] * taps_ref[tap : tap + 1, lanes[i]]
                        if tap != HALF:
                            term = jnp.where(mask, term, 0.0)
                        totals[i] = totals[i] + term
            for i in range(group):
                one = pl.ds(column // LANES + i, 1)
                affine = totals[i] * scale_ref[one, :] + shift_ref[one, :]
                swished[rows, lanes[i]] = (affine * jax.nn.sigmoid(affine)).astype(jnp.bfloat16)
            return carry

        lax.fori_loop(0, steps * groups, body, 0)

    def lower():
        start, count_rows = 0, encoded_ref.shape[0]
        rows = pl.ds(start, count_rows)

        def tile(n, carry):
            columns = pl.ds(aligned(n, tile_width), tile_width)
            total = carried[start + HALO : start + HALO + count_rows, columns] + lax.dot_general(
                swished[rows, :],
                down_held[columns, :],
                (((1,), (1,)), ((), ())),
                preferred_element_type=jnp.float32,
            )
            alive = last_tap[rows, :] >= HALF
            for side in range(tile_width // LANES):
                lane = pl.ds(pl.multiple_of(n * tile_width + side * LANES, LANES), LANES)
                encoded_ref[rows, lane] = jnp.where(
                    alive, total[:, side * LANES : (side + 1) * LANES], 0.0
                ).astype(jnp.bfloat16)
            return carry

        lax.fori_loop(0, tiles, tile, 0)

    keep.wait()
    exchanged(0)
    open_part(0)
    loads[0].wait()
    attach(0)
    from_core(GLU_ONE)
    from_core(GLU_TWO)
    for n in range(tiles):
        for side in range(2):
            glu_load(n, side).start()
    across_one((DOWN,))
    gate(0)
    convolve_part(0)
    exchanged(1)
    open_part(1)
    across_two((DOWN,))
    attach(1)
    from_y(DOWN)
    gate(1)
    from_core(DOWN)
    loads[2].start()
    convolve_part(1)
    loads[2].wait()
    lower()
    mail.finish()


def finish(after, slabs, norm, taps, out_all, glu_all, down_all):
    norm = [a.reshape(-1, LANES) for a in norm]
    bf16, f32 = jnp.bfloat16, jnp.float32
    width = taps.shape[1]
    rows = 512
    tall = rows + 2 * HALO
    weights = (out_all, glu_all, down_all)
    return pl.pallas_call(
        finish_kernel,
        out_shape=(jax.ShapeDtypeStruct((rows, width), bf16),)
        + tuple(jax.ShapeDtypeStruct(a.shape, a.dtype) for a in weights),
        in_specs=[smem_spec(), any_spec()] + [whole_spec()] * 5 + [any_spec()] * 3,
        out_specs=(whole_spec(),) + (any_spec(),) * 3,
        input_output_aliases={7: 1, 8: 2, 9: 3},
        scratch_shapes=[
            pltpu.VMEM(slabs.shape, bf16),
            pltpu.VMEM((tall, width), f32),
            pltpu.VMEM((SPLIT, 1024), bf16),
            pltpu.VMEM((SPLIT, width), bf16),
            pltpu.VMEM((width // LANES, tall, LANES), f32),
            pltpu.VMEM((rows, width), bf16),
            pltpu.VMEM((rows, LANES), jnp.int32),
            pltpu.VMEM((rows, LANES), jnp.int32),
        ]
        + [pltpu.VMEM(a.shape, bf16) for a in weights]
        + [
            pltpu.SemaphoreType.DMA((80,)),
            pltpu.SemaphoreType.DMA((80,)),
            pltpu.SemaphoreType.DMA((16,)),
        ],
        compiler_params=pltpu.CompilerParams(
            vmem_limit_bytes=VMEM_LIMIT, collective_id=2, has_side_effects=True
        ),
    )(after, slabs, *norm, taps, *weights)[0]


def on_device(
    query_rows,
    key_rows,
    value_rows,
    residual,
    lengths,
    assignment,
    out_proj,
    norm_gain,
    norm_bias,
    glu_proj,
    conv_taps,
    batch_scale,
    batch_shift,
    down_proj,
):
    data_group = lax.axis_index("dp")
    slab_index = lax.axis_index("mp")
    groups = lax.axis_size("dp")
    slabs = lax.axis_size("mp")
    group_rows = query_rows.shape[0] * 2
    slab_rows = group_rows // slabs
    total_utterances = lengths.shape[0]
    per_group = total_utterances // groups
    slots = groups * PIECES
    features = residual.shape[2] // 4

    fits = (
        (groups, slabs) == (4, 8)
        and query_rows.shape == (2048, 2, LANES)
        and residual.shape == (1024, 1, 768)
    )
    if fits:
        flat = [a.reshape(4096, LANES) for a in (query_rows, key_rows, value_rows)]
        x_slots, context_slots, *weights = move(
            lengths, assignment, *flat, residual.reshape(1024, 768), out_proj.T, glu_proj, down_proj.T
        )
        placed, after = place_parts(lengths, assignment, x_slots, context_slots, slabs)
        norm = (norm_gain, norm_bias, batch_scale, batch_shift)
        return finish(after, placed, norm, conv_taps, *weights)

    utterance = jnp.arange(total_utterances, dtype=jnp.int32)
    source = utterance // per_group
    earlier = utterance[None, :] < utterance[:, None]
    same_source = source[None, :] == source[:, None]
    same_target = assignment[None, :] == assignment[:, None]
    before = jnp.sum(jnp.where(earlier & same_source, lengths[None, :], 0), axis=1)
    rank = jnp.sum((earlier & same_source & same_target).astype(jnp.int32), axis=1)
    slot = jnp.arange(slots, dtype=jnp.int32)[:, None]
    leaving = (source[None, :] == data_group) & ((assignment * PIECES + rank)[None, :] == slot)
    start = jnp.sum(jnp.where(leaving, before[None, :], 0), axis=1)
    span = jnp.sum(jnp.where(leaving, lengths[None, :], 0), axis=1)
    coming_earlier = (assignment[None, :] == data_group) & (
        (source * PIECES + rank)[None, :] < jnp.arange(slots + 1, dtype=jnp.int32)[:, None]
    )
    after = jnp.sum(jnp.where(coming_earlier, lengths[None, :], 0), axis=1)
    live = jnp.sum(jnp.where(assignment == data_group, lengths, 0))

    position = jnp.arange(slab_rows + 2 * HALO, dtype=jnp.int32) + slab_index * slab_rows - HALO
    segment = jnp.sum((position[:, None] >= after[None, 1:]).astype(jnp.int32), axis=1)
    segment = jnp.where(position < 0, -2, jnp.where(position < live, segment, -1))
    segment = jnp.where(position >= group_rows, -2, segment)

    residual_rows = (
        residual.reshape(group_rows // 4, 4, features).reshape(group_rows, features)
    )

    def swap(array, axis):
        return lax.all_to_all(array, axis, split_axis=0, concat_axis=0, tiled=True)

    packed, start = lax.optimization_barrier((into_slots(start, residual_rows), start))
    x_slots = swap(packed, "dp")
    context_slots = swap(attend(start, span, query_rows, key_rows, value_rows), "dp")
    moved = swap(place(after, x_slots, context_slots, slabs, slab_rows, features), "mp")
    carried_slab, context_slab = unplace(moved, features, query_rows.shape[1] * HD)

    core = data_group % 2
    partners = [(group, group + 1 - 2 * (group % 2)) for group in range(groups)]

    def gather(weights):
        half = weights.shape[0] // 2
        own = lax.dynamic_slice_in_dim(weights, core * half, half, 0)
        return lax.all_gather(own, "mp", axis=1, tiled=True)

    def both(own):
        return own, lax.ppermute(own, "dp", partners)

    def project(rows, halves_of):
        own, other = halves_of
        half = rows.shape[1] // 2
        low, high = rows[:, :half], rows[:, half:]
        return jnp.dot(
            jnp.where(core == 0, low, high), own, preferred_element_type=jnp.float32
        ) + jnp.dot(jnp.where(core == 0, high, low), other, preferred_element_type=jnp.float32)

    out_halves, glu_halves = both(gather(out_proj)), both(gather(glu_proj))
    down_own = gather(down_proj)
    carried = carried_slab.astype(jnp.float32) + project(context_slab, out_halves)
    average = jnp.mean(carried, axis=1, keepdims=True)
    centred = carried - average
    variance = jnp.mean(centred * centred, axis=1, keepdims=True)
    normed = (centred * lax.rsqrt(variance + EPS) * norm_gain + norm_bias).astype(jnp.bfloat16)
    halves = project(normed, glu_halves)
    feature_count = halves.shape[1] // 2
    gated_rows = (halves[:, :feature_count] * jax.nn.sigmoid(halves[:, feature_count:])).astype(
        jnp.bfloat16
    )
    down_own, gated_rows = lax.optimization_barrier((down_own, gated_rows))
    down_halves = both(down_own)
    swished = convolve(gated_rows, segment, conv_taps, batch_scale, batch_shift)
    lowered = project(swished, down_halves)
    centre_segment = segment[HALO : HALO + slab_rows]
    own_carried = carried[HALO : HALO + slab_rows]
    return jnp.where((centre_segment >= 0)[:, None], own_carried + lowered, 0.0).astype(
        jnp.bfloat16
    )


def solution(mesh):
    in_specs = (
        P("dp", "mp", None),
        P("dp", "mp", None),
        P("dp", "mp", None),
        P("dp", "mp", None),
        P(),
        P(),
        P(None, "mp"),
        P(),
        P(),
        P(None, "mp"),
        P(),
        P(),
        P(),
        P(None, "mp"),
    )
    out_specs = P(("dp", "mp"), None)
    return jax.shard_map(
        on_device, mesh=mesh, in_specs=in_specs, out_specs=out_specs, check_vma=False
    )
```
